32 devices in a mesh: dp: 8 (over z, y), seq: 4 (over x, core).
Axes of the slice: x: 2, y: 2, z: 4, core: 2. Of those that a mesh axis runs over, the one named last changes fastest.
Arguments:
- content: float32 [8, 2048, 768], P('dp', 'seq'), may hold values from -6 to 6
- query_stream: float32 [8, 304, 768], P('dp', 'seq'), may hold values from -6 to 6
- segment_ids: int32 [8, 2048], P('dp', 'seq'), may hold values from 0 to 2047, as said below
- pad_mask: int32 [8, 2048], P('dp', 'seq'), may hold values from 0 to 1, as said below
- predicted: int32 [8, 304], P('dp', 'seq'), may hold values from 0 to 2046, as said below
- order: int32 [8, 2048], P('dp', 'seq'), may hold values from 0 to 2047, as said below
- rel_bucket: int32 [4095], replicated, may hold values from 0 to 31, as said below
- qkv_weight: bfloat16 [768, 2304], P(('dp', 'seq')), may hold values from -0.21875 to 0.21875
- qv_bias: bfloat16 [1536], P(('dp', 'seq')), may hold values from -3 to 3
- out_weight: bfloat16 [768, 768], P(('dp', 'seq')), may hold values from -0.875 to 0.875
- out_bias: bfloat16 [768], P(('dp', 'seq')), may hold values from -3 to 3
- attn_gain: bfloat16 [768], P(('dp', 'seq')), may hold values from 0.099609375 to 1.8984375
- attn_shift: bfloat16 [768], P(('dp', 'seq')), may hold values from -3 to 3
- up_weight: bfloat16 [768, 3072], P(('dp', 'seq')), may hold values from -0.21875 to 0.21875
- up_bias: bfloat16 [3072], P(('dp', 'seq')), may hold values from -3 to 3
- down_weight: bfloat16 [3072, 768], P(('dp', 'seq')), may hold values from -0.109375 to 0.109375
- down_bias: bfloat16 [768], P(('dp', 'seq')), may hold values from -3 to 3
- ffn_gain: bfloat16 [768], P(('dp', 'seq')), may hold values from 0.099609375 to 1.8984375
- ffn_shift: bfloat16 [768], P(('dp', 'seq')), may hold values from -3 to 3
- rel_table: bfloat16 [32, 12], replicated, may hold values from -4 to 4
- content_cot: float32 [8, 2048, 768], P('dp', 'seq'), may hold values from -6 to 6
- query_cot: float32 [8, 304, 768], P('dp', 'seq'), may hold values from -6 to 6
Outputs:
- content_out: float32 [8, 2048, 768], P('dp', 'seq')
- query_out: float32 [8, 304, 768], P('dp', 'seq')
- content_grad: float32 [8, 2048, 768], P('dp', 'seq')
- query_grad: float32 [8, 304, 768], P('dp', 'seq')
- qkv_weight_grad: float32 [768, 2304], P(('dp', 'seq'))
- qv_bias_grad: float32 [1536], P(('dp', 'seq'))
- out_weight_grad: float32 [768, 768], P(('dp', 'seq'))
- out_bias_grad: float32 [768], P(('dp', 'seq'))
- attn_gain_grad: float32 [768], P(('dp', 'seq'))
- attn_shift_grad: float32 [768], P(('dp', 'seq'))
- up_weight_grad: float32 [768, 3072], P(('dp', 'seq'))
- up_bias_grad: float32 [3072], P(('dp', 'seq'))
- down_weight_grad: float32 [3072, 768], P(('dp', 'seq'))
- down_bias_grad: float32 [768], P(('dp', 'seq'))
- ffn_gain_grad: float32 [768], P(('dp', 'seq'))
- ffn_shift_grad: float32 [768], P(('dp', 'seq'))
- rel_table_grad: float32 [32, 12], replicated
- stats: float32 [6], replicated
The draws below stay inside these ranges and needn't reach their ends.
Inputs may be any that keep to these rules, and one draw needn't show every extreme that they name: `segment_ids`: each slot's id is the position of the last slot of its document, and for the document holding slot 2047 it is 2047; along each sequence the ids never fall; every document but that last one has 60 to 800 tokens, and in each sequence one has exactly 800. `pad_mask`: in each sequence the padding slots are exactly those of the last document. `predicted`: 304 distinct real token positions of the sequence, none the first of its document, listed in the permuted order. `order`: A permutation of 0 to 2047 in each sequence: unpredicted real tokens take the lowest ranks, then predicted[i] has rank (number of unpredicted real tokens) + i, padding the highest. `rel_bucket`: entry j - i + 2047 is the bucket of key position j seen from position i: 0 at distance 0, below 16 for keys before, at least 16 for keys after, never falling as the distance grows on either side.
All inputs are finite; a program needn't handle non-finite values.
Results may differ from the reference program's by a relative error of at most 0.014.
Values may be sent and summed in bfloat16 or wider, within the bound.
A program may use at most 320 MiB of HBM per device.

```python
import jax
import jax.numpy as jnp
from jax import lax

MODEL_WIDTH = 768
HEADS = 12
HEAD_DIM = 64
FF = 3072
BUCKETS = 32
SEQ_LEN = 2048
DOC_MIN = 60
DOC_MAX = 800
BATCH = 8
PRED = 304


def one_layout(seed_key):
    key_len, key_big, key_perm, key_rank = jax.random.split(seed_key, 4)
    doc_slots = SEQ_LEN // DOC_MIN + 1
    lengths = jax.random.randint(key_len, (doc_slots,), DOC_MIN, DOC_MAX + 1)
    longest = jax.random.randint(key_big, (), 0, 2)
    lengths = jnp.where(jnp.arange(doc_slots) == longest, DOC_MAX, lengths).astype(jnp.int32)
    doc_ends = jnp.cumsum(lengths)
    doc_starts = doc_ends - lengths
    places = jnp.arange(SEQ_LEN, dtype=jnp.int32)
    doc_index = jnp.sum((doc_ends[None, :] <= places[:, None]).astype(jnp.int32), axis=1)
    doc_last = jnp.minimum(doc_ends - 1, SEQ_LEN - 1).astype(jnp.int32)
    seg_ids = jnp.take(doc_last, doc_index).astype(jnp.int32)
    is_valid = (seg_ids < seg_ids[SEQ_LEN - 1]).astype(jnp.int32)
    doc_first = jnp.any(doc_starts[None, :] == places[:, None], axis=1)
    shuffled = jax.random.permutation(key_perm, SEQ_LEN).astype(jnp.int32)
    choose = jnp.where((is_valid == 1) & jnp.logical_not(doc_first), shuffled + SEQ_LEN, shuffled)
    picked = lax.top_k(choose, PRED)[1].astype(jnp.int32)
    matches = places[:, None] == picked[None, :]
    is_pred = jnp.any(matches, axis=1)
    pred_rank = jnp.sum(matches.astype(jnp.int32) * jnp.arange(PRED, dtype=jnp.int32)[None, :], axis=1)
    second = jax.random.permutation(key_rank, SEQ_LEN).astype(jnp.int32)
    grouped = jnp.where(is_pred, SEQ_LEN + pred_rank, jnp.where(is_valid == 1, second, 2 * SEQ_LEN + second))
    ranks = jnp.argsort(jnp.argsort(grouped, stable=True), stable=True).astype(jnp.int32)
    return (seg_ids, is_valid, picked, ranks)


def layout(seed_key):
    return jax.vmap(one_layout)(jax.random.split(jax.random.fold_in(seed_key, 7), BATCH))


def draw_segment_ids(key, part):
    return layout(key)[0]


def draw_pad_mask(key, part):
    return layout(key)[1]


def draw_predicted(key, part):
    return layout(key)[2]


def draw_order(key, part):
    return layout(key)[3]


def draw_rel_bucket(key, part):
    half_count = BUCKETS // 2
    levels = jnp.arange(half_count - 1, dtype=jnp.int32)
    increments = jax.random.randint(jax.random.fold_in(key, 5), (half_count - 1,), 1, 2 + levels * levels // 2)
    thresholds = jnp.cumsum(increments)
    distance = jnp.arange(2 * SEQ_LEN - 1, dtype=jnp.int32) - (SEQ_LEN - 1)
    counted = jnp.sum((thresholds[None, :] <= jnp.abs(distance)[:, None]).astype(jnp.int32), axis=1)
    return (jnp.where(distance > 0, half_count, 0) + counted).astype(jnp.int32)


def rising_rows(seed_key, row_total):
    key_base = jax.random.fold_in(seed_key, 0)
    batch_part = jnp.arange(BATCH, dtype=jnp.float32)[:, None] / BATCH
    row_part = jnp.arange(row_total, dtype=jnp.float32)[None, :] / row_total
    rise = 0.5 * jnp.exp(jnp.log(3.0) * (0.5 * batch_part + 0.5 * row_part))
    values = jax.random.normal(key_base, (BATCH, row_total, MODEL_WIDTH), jnp.float32)
    return jnp.clip(values * rise[..., None], -6.0, 6.0)


def draw_content(key, part):
    return rising_rows(jax.random.fold_in(key, 11), SEQ_LEN)


def draw_query_stream(key, part):
    return rising_rows(jax.random.fold_in(key, 13), PRED)


def steps_of(own_key, extent, cuts, low, largest):
    level = 1.0
    for position, parts in cuts:
        draws = jax.random.uniform(jax.random.fold_in(jax.random.fold_in(own_key, 6), position), (parts,), jnp.float32, low / len(cuts), largest / len(cuts))
        level = level * jnp.repeat(jnp.exp(draws), extent[position] // parts).reshape((-1,) + (1,) * (len(extent) - 1 - position))
    return level


def normal_values(stream_key, extent, width, limit, pieces=(), kind=jnp.bfloat16):
    array = jax.random.normal(stream_key, extent, jnp.float32) * width
    if len(pieces) > 0:
        array = steps_of(stream_key, extent, pieces, -0.22, 0.18) * array
    return jnp.clip(array, min=-limit, max=limit).astype(kind)


def setup_inputs(seed: int = 0) -> dict:
    key_list = jax.random.split(jax.random.key(seed), 23)
    return {
        "content": draw_content(jax.random.fold_in(key_list[22], 71), 0),
        "query_stream": draw_query_stream(jax.random.fold_in(key_list[22], 71), 0),
        "segment_ids": draw_segment_ids(jax.random.fold_in(key_list[22], 71), 0),
        "pad_mask": draw_pad_mask(jax.random.fold_in(key_list[22], 71), 0),
        "predicted": draw_predicted(jax.random.fold_in(key_list[22], 71), 0),
        "order": draw_order(jax.random.fold_in(key_list[22], 71), 0),
        "rel_bucket": draw_rel_bucket(jax.random.fold_in(key_list[22], 71), 0),
        "qkv_weight": normal_values(key_list[7], (MODEL_WIDTH, 3 * MODEL_WIDTH), MODEL_WIDTH ** -0.5, 0.21875, ((0, 32),)),
        "qv_bias": normal_values(key_list[8], (2 * MODEL_WIDTH,), 0.5, 3.0, ((0, 32),)),
        "out_weight": normal_values(key_list[9], (MODEL_WIDTH, MODEL_WIDTH), (MODEL_WIDTH // 16) ** -0.5, 0.875, ((0, 32),)),
        "out_bias": normal_values(key_list[10], (MODEL_WIDTH,), 0.5, 3.0, ((0, 32),)),
        "attn_gain": jnp.clip(1.0 + 0.18 * jax.random.normal(key_list[11], (MODEL_WIDTH,), jnp.float32), 0.099609375, 1.8984375).astype(jnp.bfloat16),
        "attn_shift": normal_values(key_list[12], (MODEL_WIDTH,), 0.5, 3.0, ((0, 32),)),
        "up_weight": normal_values(key_list[13], (MODEL_WIDTH, FF), MODEL_WIDTH ** -0.5, 0.21875, ((0, 32),)),
        "up_bias": normal_values(key_list[14], (FF,), 0.5, 3.0, ((0, 32),)),
        "down_weight": normal_values(key_list[15], (FF, MODEL_WIDTH), FF ** -0.5, 0.109375, ((0, 32),)),
        "down_bias": normal_values(key_list[16], (MODEL_WIDTH,), 0.5, 3.0, ((0, 32),)),
        "ffn_gain": jnp.clip(1.0 + 0.18 * jax.random.normal(key_list[17], (MODEL_WIDTH,), jnp.float32), 0.099609375, 1.8984375).astype(jnp.bfloat16),
        "ffn_shift": normal_values(key_list[18], (MODEL_WIDTH,), 0.5, 3.0, ((0, 32),)),
        "rel_table": normal_values(key_list[19], (BUCKETS, HEADS), 1.0, 4.0),
        "content_cot": normal_values(key_list[20], (BATCH, SEQ_LEN, MODEL_WIDTH), 1.0, 6.0, ((0, 8), (1, 4)), jnp.float32),
        "query_cot": normal_values(key_list[21], (BATCH, PRED, MODEL_WIDTH), 1.0, 6.0, ((0, 8), (1, 4)), jnp.float32),
    }


EPS = 1e-05
NEG = -1000000000.0
SCALE = 0.125
HIGH = lax.Precision.HIGHEST

@jax.custom_vjp
def low(v):
    return lax.optimization_barrier(v.astype(jnp.bfloat16)).astype(jnp.float32)

@jax.custom_vjp
def low_back(v):
    return v

def low_keep(v):
    return (low(v), None)

def low_pass(kept, grad):
    return (grad,)

def back_keep(v):
    return (v, None)

def back_low(kept, grad):
    return (low(grad),)
low.defvjp(low_keep, low_pass)
low_back.defvjp(back_keep, back_low)

def exact_gelu(values):
    return jax.nn.gelu(values, approximate=False)

def layer_norm(residual, gain_vec, shift_vec):
    row_mean = lax.optimization_barrier(jnp.mean(residual, axis=-1, keepdims=True))
    centered = residual - row_mean
    inv_std = lax.rsqrt(lax.optimization_barrier(jnp.mean(centered * centered, axis=-1, keepdims=True)) + EPS)
    return centered * inv_std * gain_vec + shift_vec

def matmul(left, right):
    return jnp.dot(left, right, precision=HIGH, preferred_element_type=jnp.float32)

def seq_layer(params, packed, rel_bucket):
    query_key_value_weight, bias_qv, w_out, bias_out, first_norm_gain, shift_one, w_up, bias_up, w_down, bias_down, gain_two, shift_two, table = params
    all_rows, seg_ids, is_valid, picked, ranks = packed
    length = seg_ids.shape[0]
    row_count = all_rows.shape[0]
    reduced_precision_rows = low(all_rows)
    queries = low(low_back(matmul(reduced_precision_rows, query_key_value_weight[:, :MODEL_WIDTH]) + bias_qv[:MODEL_WIDTH]))
    key_rows = low(low_back(matmul(reduced_precision_rows[:length], query_key_value_weight[:, MODEL_WIDTH:2 * MODEL_WIDTH])))
    value_rows = low(low_back(matmul(reduced_precision_rows[:length], query_key_value_weight[:, 2 * MODEL_WIDTH:]) + bias_qv[MODEL_WIDTH:]))
    key_pos = jnp.arange(length, dtype=jnp.int32)
    query_pos = jnp.concatenate([key_pos, picked.astype(jnp.int32)])
    query_seg = jnp.concatenate([seg_ids, seg_ids[picked]])
    query_limit = jnp.concatenate([ranks, ranks[picked] - 1])
    content_row = jnp.arange(row_count, dtype=jnp.int32) < length
    inside = (query_seg[:, None] == seg_ids[None, :]) & (is_valid[None, :] == 1) & (ranks[None, :] <= query_limit[:, None])
    itself = (key_pos[None, :] == query_pos[:, None]) & content_row[:, None]
    allowed = inside | itself
    offsets = (key_pos[None, :] - query_pos[:, None] + (length - 1)).astype(jnp.int32)
    bias_full = jnp.take(table, rel_bucket, axis=0)
    bias = jnp.transpose(jnp.take(bias_full, offsets, axis=0), (2, 0, 1))
    query_heads = queries.reshape(row_count, HEADS, HEAD_DIM)
    key_heads = key_rows.reshape(length, HEADS, HEAD_DIM)
    value_heads = value_rows.reshape(length, HEADS, HEAD_DIM)
    scores = jnp.einsum('rhd,lhd->hrl', query_heads, key_heads, precision=HIGH) * SCALE + bias
    scores = low_back(scores)
    scores = jnp.where(allowed[None], scores, NEG)
    row_max = lax.optimization_barrier(jnp.max(scores, axis=-1, keepdims=True))
    expo_vals = jnp.exp(scores - row_max)
    probs = low(expo_vals / lax.optimization_barrier(jnp.sum(expo_vals, axis=-1, keepdims=True)))
    context = jnp.einsum('hrl,lhd->rhd', probs, value_heads, precision=HIGH).reshape(row_count, MODEL_WIDTH)
    context = low(low_back(context))
    attn_out = low_back(matmul(context, w_out) + bias_out)
    hidden_one = layer_norm(all_rows + attn_out, first_norm_gain, shift_one)
    pre_act = low_back(matmul(low(hidden_one), w_up) + bias_up)
    activ = exact_gelu(pre_act)
    ffn_out = low_back(matmul(low(activ), w_down) + bias_down)
    hidden_two = layer_norm(hidden_one + ffn_out, gain_two, shift_two)
    row_valid = jnp.concatenate([is_valid.astype(jnp.float32), jnp.ones((row_count - length,), jnp.float32)])
    outputs = hidden_two * row_valid[:, None]
    pad_weight = is_valid.astype(jnp.float32)[:, None]
    sums = jnp.stack([jnp.sum(pad_weight * attn_out[:length] * attn_out[:length]), jnp.sum(attn_out[length:] * attn_out[length:]), jnp.sum(pad_weight * ffn_out[:length] * ffn_out[:length]), jnp.sum(ffn_out[length:] * ffn_out[length:])])
    return (outputs, sums)

def reference(content, query_stream, segment_ids, pad_mask, predicted, order, rel_bucket, qkv_weight, qv_bias, out_weight, out_bias, attn_gain, attn_shift, up_weight, up_bias, down_weight, down_bias, ffn_gain, ffn_shift, rel_table, content_cot, query_cot):
    params = tuple((member.astype(jnp.float32) for member in (qkv_weight, qv_bias, out_weight, out_bias, attn_gain, attn_shift, up_weight, up_bias, down_weight, down_bias, ffn_gain, ffn_shift, rel_table)))
    all_rows = jnp.concatenate([content, query_stream], axis=1)

    def whole(weights, stacked):

        def one_seq(packed):
            return seq_layer(weights, packed, rel_bucket)
        outputs, sums = lax.map(jax.checkpoint(one_seq), (stacked, segment_ids, pad_mask, predicted, order))
        return (outputs, sums)
    outputs, pull, sums = jax.vjp(whole, params, all_rows, has_aux=True)
    cotangent = jnp.concatenate([content_cot, query_cot], axis=1)
    grad_params, grad_rows = pull(cotangent)
    length = content.shape[1]
    pad_float = pad_mask.astype(jnp.float32)
    content_count = jnp.sum(pad_float) * MODEL_WIDTH
    query_count = jnp.float32(BATCH * PRED * MODEL_WIDTH)
    stats = jnp.sqrt(jnp.stack([jnp.sum(pad_float[..., None] * content * content) / content_count, jnp.sum(query_stream * query_stream) / query_count, jnp.sum(sums[:, 0]) / content_count, jnp.sum(sums[:, 1]) / query_count, jnp.sum(sums[:, 2]) / content_count, jnp.sum(sums[:, 3]) / query_count]))
    return (outputs[:, :length], outputs[:, length:], grad_rows[:, :length], grad_rows[:, length:], grad_params[0], grad_params[1], grad_params[2], grad_params[3], grad_params[4], grad_params[5], grad_params[6], grad_params[7], grad_params[8], grad_params[9], grad_params[10], grad_params[11], grad_params[12], stats)
```

```python
import functools
import math

import jax
import jax.numpy as jnp
from jax import lax
from jax.experimental import pallas as pl
from jax.experimental.pallas import tpu as pltpu
from jax.sharding import PartitionSpec as P

MODEL_WIDTH = 768
HEADS = 12
HEAD_DIM = 64
BUCKETS = 32
SEQ_LEN = 2048


EPS = 1e-05
NEG = -1000000000.0
SCALE = 0.125


def exact_gelu(values):
    return jax.nn.gelu(values, approximate=False)


def norm_fwd(residual, gain_vec, shift_vec):
    row_mean = jnp.mean(residual, axis=-1, keepdims=True)
    centered = residual - row_mean
    inv_std = lax.rsqrt(jnp.mean(centered * centered, axis=-1, keepdims=True) + EPS)
    normed = centered * inv_std
    return (normed * gain_vec + shift_vec, normed, inv_std)


def norm_back(upstream, normed, inv_std, gain_vec):
    grad_norm = upstream * gain_vec
    projected = jnp.mean(grad_norm, axis=-1, keepdims=True) + normed * jnp.mean(
        grad_norm * normed, axis=-1, keepdims=True
    )
    return (
        inv_std * (grad_norm - projected),
        jnp.sum(upstream * normed, axis=(0, 1)),
        jnp.sum(upstream, axis=(0, 1)),
    )


def bucket_edges(rel_bucket):
    entry_count = rel_bucket.shape[0]
    matches = rel_bucket[None, :] == jnp.arange(BUCKETS, dtype=jnp.int32)[:, None]
    places = jnp.arange(entry_count, dtype=jnp.int32)[None, :]
    starts = jnp.min(jnp.where(matches, places, entry_count), axis=1)
    counts = jnp.sum(matches.astype(jnp.int32), axis=1)
    return (starts, starts + counts)


def build_mask(
    query_pos, query_seg, query_limit, content_row, key_pos, key_seg, key_order, key_pad
):
    inside = (
        (query_seg[:, None] == key_seg[None, :])
        & (key_pad[None, :] == 1)
        & (key_order[None, :] <= query_limit[:, None])
    )
    itself = (key_pos[None, :] == query_pos[:, None]) & content_row[:, None]
    return (inside | itself, key_pos[None, :] - query_pos[:, None] + (SEQ_LEN - 1))


def masked_scores(query_heads, key_heads, table_low, edges, allowed, offsets):
    raw_scores = (
        jnp.einsum("rhd,lhd->hrl", query_heads, key_heads, preferred_element_type=jnp.float32)
        * SCALE
    )
    starts, ends = edges
    spread = offsets[..., None]
    onehot = ((spread >= starts) & (spread < ends)).astype(jnp.bfloat16)
    bias = jnp.einsum("rlb,bh->hrl", onehot, table_low, preferred_element_type=jnp.float32)
    return (jnp.where(allowed[None], raw_scores + bias, NEG), onehot)


def attend_forward(packed, table_low, edges, content_row):
    queries, key_values, key_seg, key_order, key_pad, query_pos, query_seg, query_limit = packed
    row_count = queries.shape[0]
    length = key_values.shape[0]
    key_pos = jnp.arange(length, dtype=jnp.int32)
    allowed, offsets = build_mask(
        query_pos, query_seg, query_limit, content_row, key_pos, key_seg, key_order, key_pad
    )
    query_heads = queries.reshape(row_count, HEADS, HEAD_DIM)
    key_heads = key_values[:, :MODEL_WIDTH].reshape(length, HEADS, HEAD_DIM)
    value_heads = key_values[:, MODEL_WIDTH:].reshape(length, HEADS, HEAD_DIM)
    scores, onehot = masked_scores(query_heads, key_heads, table_low, edges, allowed, offsets)
    row_max = jnp.max(scores, axis=-1, keepdims=True)
    expo_vals = jnp.exp(scores - row_max)
    row_total = jnp.sum(expo_vals, axis=-1, keepdims=True)
    probs_low = (expo_vals / row_total).astype(jnp.bfloat16)
    context = jnp.einsum("hrl,lhd->rhd", probs_low, value_heads, preferred_element_type=jnp.float32)
    return (
        context.reshape(row_count, MODEL_WIDTH),
        jnp.transpose((row_max + jnp.log(row_total))[..., 0]),
    )


def attend_backward(packed, table_low, edges, content_row):
    (
        queries,
        key_values,
        key_seg,
        key_order,
        key_pad,
        query_pos,
        query_seg,
        query_limit,
        row_lse,
        grad_context,
    ) = packed
    row_count = queries.shape[0]
    length = key_values.shape[0]
    key_pos = jnp.arange(length, dtype=jnp.int32)
    allowed, offsets = build_mask(
        query_pos, query_seg, query_limit, content_row, key_pos, key_seg, key_order, key_pad
    )
    query_heads = queries.reshape(row_count, HEADS, HEAD_DIM)
    key_heads = key_values[:, :MODEL_WIDTH].reshape(length, HEADS, HEAD_DIM)
    value_heads = key_values[:, MODEL_WIDTH:].reshape(length, HEADS, HEAD_DIM)
    scores, onehot = masked_scores(query_heads, key_heads, table_low, edges, allowed, offsets)
    probs = jnp.exp(scores - jnp.transpose(row_lse)[..., None])
    grad_heads = grad_context.reshape(row_count, HEADS, HEAD_DIM)
    grad_probs = jnp.einsum(
        "rhd,lhd->hrl", grad_heads, value_heads, preferred_element_type=jnp.float32
    )
    row_delta = jnp.sum(probs * grad_probs, axis=-1)
    grad_scores = (probs * (grad_probs - row_delta[..., None])).astype(jnp.bfloat16)
    grad_query = (
        jnp.einsum("hrl,lhd->rhd", grad_scores, key_heads, preferred_element_type=jnp.float32)
        * SCALE
    )
    grad_table = jnp.einsum("hrl,rlb->bh", grad_scores, onehot, preferred_element_type=jnp.float32)
    results = (grad_query.reshape(row_count, MODEL_WIDTH), grad_table, jnp.transpose(row_delta))
    probs_low = probs.astype(jnp.bfloat16)
    grad_key = (
        jnp.einsum("hrl,rhd->lhd", grad_scores, query_heads, preferred_element_type=jnp.float32)
        * SCALE
    )
    grad_value = jnp.einsum(
        "hrl,rhd->lhd", probs_low, grad_heads, preferred_element_type=jnp.float32
    )
    results = results + (
        jnp.concatenate(
            [grad_key.reshape(length, MODEL_WIDTH), grad_value.reshape(length, MODEL_WIDTH)],
            axis=-1,
        ),
    )
    return results


def local_general(
    content,
    query_stream,
    segment_ids,
    pad_mask,
    predicted,
    order,
    rel_bucket,
    qkv_weight,
    qv_bias,
    out_weight,
    out_bias,
    attn_gain,
    attn_shift,
    up_weight,
    up_bias,
    down_weight,
    down_bias,
    ffn_gain,
    ffn_shift,
    rel_table,
    content_cot,
    query_cot,
):
    seq_count = content.shape[0]
    shard_length = content.shape[1]
    pred_count = query_stream.shape[1]
    row_count = shard_length + pred_count
    group_size = lax.axis_size("seq")
    edges = bucket_edges(rel_bucket)
    shards = (
        lax.all_gather(qkv_weight, ("dp", "seq"), axis=0, tiled=True),
        lax.all_gather(out_weight, ("dp", "seq"), axis=0, tiled=True),
        lax.all_gather(up_weight, ("dp", "seq"), axis=0, tiled=True),
        lax.all_gather(down_weight, ("dp", "seq"), axis=0, tiled=True),
        lax.all_gather(qv_bias, ("dp", "seq"), axis=0, tiled=True),
        lax.all_gather(out_bias, ("dp", "seq"), axis=0, tiled=True),
        lax.all_gather(attn_gain, ("dp", "seq"), axis=0, tiled=True),
        lax.all_gather(attn_shift, ("dp", "seq"), axis=0, tiled=True),
        lax.all_gather(up_bias, ("dp", "seq"), axis=0, tiled=True),
        lax.all_gather(down_bias, ("dp", "seq"), axis=0, tiled=True),
        lax.all_gather(ffn_gain, ("dp", "seq"), axis=0, tiled=True),
        lax.all_gather(ffn_shift, ("dp", "seq"), axis=0, tiled=True),
    )
    query_key_value_weight, w_out, w_up, w_down = (shards[0], shards[1], shards[2], shards[3])
    bias_qv, bias_out, first_norm_gain, shift_one, bias_up, bias_down, gain_two, shift_two = [
        member.astype(jnp.float32) for member in shards[4:]
    ]
    all_rows = jnp.concatenate([content, query_stream], axis=1)
    reduced_precision_rows = all_rows.astype(jnp.bfloat16)
    queries = (
        jnp.einsum(
            "srd,de->sre",
            reduced_precision_rows,
            query_key_value_weight[:, :MODEL_WIDTH],
            preferred_element_type=jnp.float32,
        )
        + bias_qv[:MODEL_WIDTH]
    ).astype(jnp.bfloat16)
    value_shift = jnp.concatenate([jnp.zeros((MODEL_WIDTH,), jnp.float32), bias_qv[MODEL_WIDTH:]])
    key_values = (
        jnp.einsum(
            "zci,ip->zcp",
            reduced_precision_rows[:, :shard_length],
            query_key_value_weight[:, MODEL_WIDTH:],
            preferred_element_type=jnp.float32,
        )
        + value_shift
    ).astype(jnp.bfloat16)
    full_pairs, full_seg, full_order, full_pad = (
        lax.all_gather(key_values, "seq", axis=1, tiled=True),
        lax.all_gather(segment_ids, "seq", axis=1, tiled=True),
        lax.all_gather(order, "seq", axis=1, tiled=True),
        lax.all_gather(pad_mask, "seq", axis=1, tiled=True),
    )
    content_pos = lax.axis_index("seq") * shard_length + jnp.arange(shard_length, dtype=jnp.int32)
    query_pos = jnp.concatenate(
        [jnp.broadcast_to(content_pos[None, :], (seq_count, shard_length)), predicted], axis=1
    )
    query_seg = jnp.concatenate(
        [segment_ids, jnp.take_along_axis(full_seg, predicted, axis=1)], axis=1
    )
    query_limit = jnp.concatenate(
        [order, jnp.take_along_axis(full_order, predicted, axis=1) - 1], axis=1
    )
    content_row = jnp.arange(row_count, dtype=jnp.int32) < shard_length
    row_meta = (full_seg, full_order, full_pad, query_pos, query_seg, query_limit)

    def forward_one(packed):
        return attend_forward(packed, rel_table, edges, content_row)

    context, row_lse = lax.map(forward_one, (queries, full_pairs) + row_meta)
    context_low = context.astype(jnp.bfloat16)
    attn_out = (
        jnp.einsum("sre,ed->srd", context_low, w_out, preferred_element_type=jnp.float32) + bias_out
    )
    hidden_one, normed_one, inv_one = norm_fwd(all_rows + attn_out, first_norm_gain, shift_one)
    hidden_low = hidden_one.astype(jnp.bfloat16)
    pre_act = (
        jnp.einsum("srd,df->srf", hidden_low, w_up, preferred_element_type=jnp.float32) + bias_up
    )
    activ, gelu_pull = jax.vjp(exact_gelu, pre_act)
    activ_low = activ.astype(jnp.bfloat16)
    ffn_out = (
        jnp.einsum("srf,fd->srd", activ_low, w_down, preferred_element_type=jnp.float32) + bias_down
    )
    hidden_two, normed_two, inv_two = norm_fwd(hidden_one + ffn_out, gain_two, shift_two)
    pad_float = pad_mask.astype(jnp.float32)
    row_valid = jnp.concatenate(
        [pad_float, jnp.ones((seq_count, pred_count), jnp.float32)], axis=1
    )[..., None]
    outputs = hidden_two * row_valid
    pad_weight = pad_float[..., None]
    local_sums = jnp.stack(
        [
            jnp.sum(pad_weight * content * content),
            jnp.sum(query_stream * query_stream),
            jnp.sum(pad_weight * attn_out[:, :shard_length] * attn_out[:, :shard_length]),
            jnp.sum(attn_out[:, shard_length:] * attn_out[:, shard_length:]),
            jnp.sum(pad_weight * ffn_out[:, :shard_length] * ffn_out[:, :shard_length]),
            jnp.sum(ffn_out[:, shard_length:] * ffn_out[:, shard_length:]),
            jnp.sum(pad_float),
        ]
    )
    back_weights = (
        lax.all_gather(qkv_weight, ("dp", "seq"), axis=0, tiled=True),
        lax.all_gather(out_weight, ("dp", "seq"), axis=0, tiled=True),
        lax.all_gather(up_weight, ("dp", "seq"), axis=0, tiled=True),
        lax.all_gather(down_weight, ("dp", "seq"), axis=0, tiled=True),
        lax.all_gather(attn_gain, ("dp", "seq"), axis=0, tiled=True),
        lax.all_gather(ffn_gain, ("dp", "seq"), axis=0, tiled=True),
    )
    back_pairs = lax.all_gather(key_values, "seq", axis=1, tiled=True)
    backward_query_key_value, back_out, back_up, back_down = (
        back_weights[0],
        back_weights[1],
        back_weights[2],
        back_weights[3],
    )
    back_gain_one = back_weights[4].astype(jnp.float32)
    back_gain_two = back_weights[5].astype(jnp.float32)
    upstream = jnp.concatenate([content_cot, query_cot], axis=1) * row_valid
    grad_res_two, grad_gain_two, grad_shift_two = norm_back(
        upstream, normed_two, inv_two, back_gain_two
    )
    grad_ffn = grad_res_two.astype(jnp.bfloat16)
    grad_bias_down = jnp.sum(grad_ffn, axis=(0, 1), dtype=jnp.float32)
    grad_down = jnp.einsum("srf,srd->fd", activ_low, grad_ffn, preferred_element_type=jnp.float32)
    grad_activ = jnp.einsum("srd,fd->srf", grad_ffn, back_down, preferred_element_type=jnp.float32)
    grad_pre = gelu_pull(grad_activ)[0].astype(jnp.bfloat16)
    grad_bias_up = jnp.sum(grad_pre, axis=(0, 1), dtype=jnp.float32)
    grad_up = jnp.einsum("srd,srf->df", hidden_low, grad_pre, preferred_element_type=jnp.float32)
    grad_hidden = grad_res_two + jnp.einsum(
        "srf,df->srd", grad_pre, back_up, preferred_element_type=jnp.float32
    )
    grad_res_one, grad_gain_one, grad_shift_one = norm_back(
        grad_hidden, normed_one, inv_one, back_gain_one
    )
    grad_attn = grad_res_one.astype(jnp.bfloat16)
    grad_bias_out = jnp.sum(grad_attn, axis=(0, 1), dtype=jnp.float32)
    grad_out = jnp.einsum("sre,srd->ed", context_low, grad_attn, preferred_element_type=jnp.float32)
    grad_context = jnp.einsum(
        "srd,ed->sre", grad_attn, back_out, preferred_element_type=jnp.float32
    ).astype(jnp.bfloat16)

    def backward_all(packed):
        return attend_backward(packed, rel_table, edges, content_row)

    grad_queries, grad_tables, per_row_delta, grad_pairs = lax.map(
        backward_all, (queries, back_pairs) + row_meta + (row_lse, grad_context)
    )
    paired_gradients = lax.psum_scatter(
        grad_pairs.astype(jnp.bfloat16), "seq", scatter_dimension=1, tiled=True
    )
    query_grads = grad_queries.astype(jnp.bfloat16)
    grad_bias_qv = jnp.concatenate(
        [
            jnp.sum(query_grads, axis=(0, 1), dtype=jnp.float32),
            jnp.sum(paired_gradients[..., MODEL_WIDTH:], axis=(0, 1), dtype=jnp.float32),
        ]
    )
    grad_qkv = jnp.concatenate(
        [
            jnp.einsum(
                "srd,sre->de",
                reduced_precision_rows,
                query_grads,
                preferred_element_type=jnp.float32,
            ),
            jnp.einsum(
                "cvi,cvp->ip",
                reduced_precision_rows[:, :shard_length],
                paired_gradients,
                preferred_element_type=jnp.float32,
            ),
        ],
        axis=1,
    )
    grad_rows = grad_res_one + jnp.einsum(
        "sre,de->srd",
        query_grads,
        backward_query_key_value[:, :MODEL_WIDTH],
        preferred_element_type=jnp.float32,
    )
    grad_content = grad_rows[:, :shard_length] + jnp.einsum(
        "zwv,bv->zwb",
        paired_gradients,
        backward_query_key_value[:, MODEL_WIDTH:],
        preferred_element_type=jnp.float32,
    )
    grad_query = grad_rows[:, shard_length:]
    owned = (
        lax.psum_scatter(grad_qkv, ("dp", "seq"), scatter_dimension=0, tiled=True),
        lax.psum_scatter(grad_out, ("dp", "seq"), scatter_dimension=0, tiled=True),
        lax.psum_scatter(grad_up, ("dp", "seq"), scatter_dimension=0, tiled=True),
        lax.psum_scatter(grad_down, ("dp", "seq"), scatter_dimension=0, tiled=True),
        lax.psum_scatter(grad_bias_qv, ("dp", "seq"), scatter_dimension=0, tiled=True),
        lax.psum_scatter(grad_bias_out, ("dp", "seq"), scatter_dimension=0, tiled=True),
        lax.psum_scatter(grad_gain_one, ("dp", "seq"), scatter_dimension=0, tiled=True),
        lax.psum_scatter(grad_shift_one, ("dp", "seq"), scatter_dimension=0, tiled=True),
        lax.psum_scatter(grad_bias_up, ("dp", "seq"), scatter_dimension=0, tiled=True),
        lax.psum_scatter(grad_bias_down, ("dp", "seq"), scatter_dimension=0, tiled=True),
        lax.psum_scatter(grad_gain_two, ("dp", "seq"), scatter_dimension=0, tiled=True),
        lax.psum_scatter(grad_shift_two, ("dp", "seq"), scatter_dimension=0, tiled=True),
    )
    table_sum, totals = lax.psum((jnp.sum(grad_tables, axis=0), local_sums), ("dp", "seq"))
    content_count = totals[6] * MODEL_WIDTH
    query_count = float(seq_count * lax.axis_size("dp") * pred_count * group_size * MODEL_WIDTH)
    stats = jnp.sqrt(
        jnp.stack(
            [
                totals[0] / content_count,
                totals[1] / query_count,
                totals[2] / content_count,
                totals[3] / query_count,
                totals[4] / content_count,
                totals[5] / query_count,
            ]
        )
    )
    return (
        outputs[:, :shard_length],
        outputs[:, shard_length:],
        grad_content,
        grad_query,
        owned[0],
        owned[4],
        owned[1],
        owned[5],
        owned[6],
        owned[7],
        owned[2],
        owned[8],
        owned[3],
        owned[9],
        owned[10],
        owned[11],
        table_sum,
        stats,
    )


LOG2E = math.log2(math.e)
TILE = 256
HALF = 128
REACH = 9
DIAGS = 2 * REACH + 1
WIDE = SEQ_LEN + HALF
MASKED = -1e30
F32 = jnp.float32
BF16 = jnp.bfloat16


def bias_kernel(rows_q, own, rev_ref, fold_ref, hot_ref, shift_ref, tile_ref, qbias_ref):
    lane = lax.broadcasted_iota(jnp.int32, (HALF, HALF), 1)
    for h in range(own):
        for e in range(-REACH, REACH + 1):
            start = HALF * (15 - e)
            row = rev_ref[h : h + 1, start : start + 2 * HALF]
            skew = pltpu.roll(
                jnp.broadcast_to(row, (HALF, 2 * HALF)), 0, 1, stride=1, stride_axis=0
            )
            tile_ref[h, e + REACH] = skew[:, HALF:]
    for t in range(rows_q // HALF):
        shift = shift_ref[t * HALF : (t + 1) * HALF, :]
        place = lane + shift
        wrap = place >= HALF
        idx = jnp.where(wrap, place - HALF, place)
        for h in range(own):
            spread = jnp.dot(
                hot_ref[t * HALF : (t + 1) * HALF, :], fold_ref[h], preferred_element_type=F32
            )
            prev = jnp.take_along_axis(spread[:, :HALF], idx, axis=1)
            for j in range(SEQ_LEN // HALF):
                cur = jnp.take_along_axis(
                    spread[:, (j + 1) * HALF : (j + 2) * HALF], idx, axis=1
                )
                out = jnp.where(wrap, cur, prev) * LOG2E
                qbias_ref[h, j * HALF : (j + 1) * HALF, t * HALF : (t + 1) * HALF] = out.T
                prev = cur


def bias_call(rev, fold, hot, shift):
    own = rev.shape[0]
    rows_q = hot.shape[0]
    return pl.pallas_call(
        functools.partial(bias_kernel, rows_q, own),
        out_shape=(
            jax.ShapeDtypeStruct((own, DIAGS, HALF, HALF), F32),
            jax.ShapeDtypeStruct((own, SEQ_LEN, rows_q), F32),
        ),
        compiler_params=pltpu.CompilerParams(vmem_limit_bytes=50 << 20),
        name="bias_tiles",
    )(rev, fold, hot, shift)


def bias_block(tile_ref, h, e):
    mid = tile_ref[h, e]
    return jnp.concatenate(
        [
            jnp.concatenate([mid, tile_ref[h, e - 1]], axis=1),
            jnp.concatenate([tile_ref[h, e + 1], mid], axis=1),
        ],
        axis=0,
    )


def mask_block(kmeta_ref, rseg_ref, rlim_ref, krow, rcol, width):
    kseg = kmeta_ref[0, pl.ds(krow, TILE), :]
    kord = kmeta_ref[1, pl.ds(krow, TILE), :]
    parts = []
    for w in range(width // HALF):
        rseg = rseg_ref[:, pl.ds(rcol + w * HALF, HALF)]
        rlim = rlim_ref[:, pl.ds(rcol + w * HALF, HALF)]
        ok = (kseg == rseg) & (kord <= rlim)
        parts.append(jnp.where(ok, 0.0, MASKED))
    return parts[0] if len(parts) == 1 else jnp.concatenate(parts, axis=1)


def fwd_kernel(
    own,
    rows_q,
    span_ref,
    qt_ref,
    k_ref,
    vt_ref,
    kmeta_ref,
    rseg_ref,
    rlim_ref,
    tile_ref,
    qbias_ref,
    ctx_ref,
    rows_ref,
    lse_ref,
    s_scr,
):
    def run(rcol, width, lo, hi, bias_of):
        heads = range(own)

        def fold(op, x):
            rows = [x[i * 8 : (i + 1) * 8] for i in range(x.shape[0] // 8)]
            while len(rows) > 1:
                rows = [op(rows[i], rows[i + 1]) for i in range(0, len(rows), 2)]
            return rows[0]

        def score(kt, tops):
            krow = pl.multiple_of(kt * TILE, TILE)
            mask = mask_block(kmeta_ref, rseg_ref, rlim_ref, krow, rcol, width)
            new = []
            for h in heads:
                s = jnp.dot(
                    k_ref[h, pl.ds(krow, TILE), :],
                    qt_ref[h * HEAD_DIM : (h + 1) * HEAD_DIM, pl.ds(rcol, width)],
                    preferred_element_type=F32,
                )
                s = s * (SCALE * LOG2E) + (bias_of(h, kt) + mask)
                s_scr[h, pl.ds(krow, TILE), :width] = s
                new.append(jnp.maximum(tops[h], fold(jnp.maximum, s)))
            return tuple(new)

        tops = lax.fori_loop(
            lo, hi + 1, score, tuple(jnp.full((8, width), MASKED, F32) for _ in heads)
        )
        tops = [jnp.max(t, axis=0, keepdims=True) for t in tops]

        def weigh(kt, carry):
            krow = pl.multiple_of(kt * TILE, TILE)
            sums, accs = carry
            new_sums, new_accs = [], []
            for h in heads:
                p = jnp.exp2(s_scr[h, pl.ds(krow, TILE), :width] - tops[h])
                new_sums.append(sums[h] + fold(jnp.add, p))
                new_accs.append(
                    accs[h]
                    + jnp.dot(
                        vt_ref[h * HEAD_DIM : (h + 1) * HEAD_DIM, pl.ds(krow, TILE)],
                        p.astype(BF16),
                        preferred_element_type=F32,
                    )
                )
            return tuple(new_sums), tuple(new_accs)

        sums, accs = lax.fori_loop(
            lo,
            hi + 1,
            weigh,
            (
                tuple(jnp.zeros((8, width), F32) for _ in heads),
                tuple(jnp.zeros((HEAD_DIM, width), F32) for _ in heads),
            ),
        )
        outs = []
        for h in heads:
            total = jnp.sum(sums[h], axis=0, keepdims=True)
            outs.append(accs[h] / total)
            lse_ref[h : h + 1, pl.ds(rcol, width)] = tops[h] + jnp.log2(total)
        out = jnp.concatenate(outs, axis=0)
        ctx_ref[:, pl.ds(rcol, width)] = out.astype(BF16)
        rows_ref[pl.ds(rcol, width), :] = out.T.astype(BF16)

    def content_tile(qt, carry):
        def bias_of(h, kt):
            return bias_block(tile_ref, h, 2 * (kt - qt) + REACH)

        run(pl.multiple_of(qt * TILE, TILE), TILE, span_ref[0, qt], span_ref[1, qt], bias_of)
        return carry

    lax.fori_loop(0, SEQ_LEN // TILE, content_tile, 0)

    def query_tile(t, carry):
        col = pl.multiple_of(t * HALF, HALF)

        def bias_of(h, kt):
            return qbias_ref[h, pl.ds(pl.multiple_of(kt * TILE, TILE), TILE), pl.ds(col, HALF)]

        run(
            pl.multiple_of(SEQ_LEN + t * HALF, HALF),
            HALF,
            span_ref[0, SEQ_LEN // TILE],
            span_ref[1, SEQ_LEN // TILE],
            bias_of,
        )
        return carry

    lax.fori_loop(0, rows_q // HALF, query_tile, 0)


def fwd_call(span, qt, k3, vt, kmeta, rseg, rlim, tiles, qbias):
    own = k3.shape[0]
    rows = qt.shape[1]
    rows_q = rows - SEQ_LEN
    vm = pl.BlockSpec(memory_space=pltpu.VMEM)
    return pl.pallas_call(
        functools.partial(fwd_kernel, own, rows_q),
        out_shape=(
            jax.ShapeDtypeStruct((own * HEAD_DIM, rows), BF16),
            jax.ShapeDtypeStruct((rows, own * HEAD_DIM), BF16),
            jax.ShapeDtypeStruct((own, rows), F32),
        ),
        in_specs=[pl.BlockSpec(memory_space=pltpu.SMEM)] + [vm] * 8,
        scratch_shapes=[
            pltpu.VMEM((own, SEQ_LEN, TILE), F32),
        ],
        compiler_params=pltpu.CompilerParams(vmem_limit_bytes=56 << 20),
        name="attend",
    )(span, qt, k3, vt, kmeta, rseg, rlim, tiles, qbias)


def bwd_kernel(
    own,
    rows_q,
    span_ref,
    qt_ref,
    q_ref,
    k_ref,
    kt_ref,
    v_ref,
    ctx_ref,
    gt_ref,
    g_ref,
    lse_ref,
    kmeta_ref,
    rseg_ref,
    rlim_ref,
    tile_ref,
    qbias_ref,
    hott_ref,
    shift_ref,
    dq_ref,
    dk_ref,
    dv_ref,
    offs_ref,
    qoffs_ref,
    dk_scr,
    dv_scr,
    dq_scr,
    diag_scr,
    ds_scr,
    delta_scr,
):
    dk_scr[...] = jnp.zeros(dk_scr.shape, F32)
    dv_scr[...] = jnp.zeros(dv_scr.shape, F32)
    diag_scr[...] = jnp.zeros(diag_scr.shape, F32)
    ds_scr[...] = jnp.zeros(ds_scr.shape, BF16)
    for h in range(own):
        part = slice(h * HEAD_DIM, (h + 1) * HEAD_DIM)
        delta_scr[h : h + 1, :] = jnp.sum(
            ctx_ref[part, :].astype(F32) * gt_ref[part, :].astype(F32), axis=0, keepdims=True
        )

    def run(rcol, width, lo, hi, bias_of, keep):
        dq_scr[...] = jnp.zeros(dq_scr.shape, F32)

        def body(kt, carry):
            krow = pl.multiple_of(kt * TILE, TILE)
            mask = mask_block(kmeta_ref, rseg_ref, rlim_ref, krow, rcol, width)
            for h in range(own):
                part = slice(h * HEAD_DIM, (h + 1) * HEAD_DIM)
                s = jnp.dot(
                    k_ref[h, pl.ds(krow, TILE), :],
                    qt_ref[part, pl.ds(rcol, width)],
                    preferred_element_type=F32,
                )
                s = s * (SCALE * LOG2E) + (bias_of(h, kt) + mask)
                p = jnp.exp2(s - lse_ref[h : h + 1, pl.ds(rcol, width)])
                gp = jnp.dot(
                    v_ref[h, pl.ds(krow, TILE), :],
                    gt_ref[part, pl.ds(rcol, width)],
                    preferred_element_type=F32,
                )
                ds = p * (gp - delta_scr[h : h + 1, pl.ds(rcol, width)])
                low = ds.astype(BF16)
                keep(h, kt, ds, low)
                dv_scr[h, pl.ds(krow, TILE), :] += jnp.dot(
                    p.astype(BF16), g_ref[h, pl.ds(rcol, width), :], preferred_element_type=F32
                )
                dk_scr[h, pl.ds(krow, TILE), :] += jnp.dot(
                    low, q_ref[h, pl.ds(rcol, width), :], preferred_element_type=F32
                )
                dq_scr[h, :, :width] += jnp.dot(
                    kt_ref[part, pl.ds(krow, TILE)], low, preferred_element_type=F32
                )
            return carry

        lax.fori_loop(lo, hi + 1, body, 0)
        for h in range(own):
            dq_ref[h * HEAD_DIM : (h + 1) * HEAD_DIM, pl.ds(rcol, width)] = (
                dq_scr[h, :, :width] * SCALE
            ).astype(BF16)

    def content_tile(qt, carry):
        def bias_of(h, kt):
            return bias_block(tile_ref, h, 2 * (kt - qt) + REACH)

        def keep(h, kt, ds, low):
            e = 2 * (kt - qt) + REACH
            diag_scr[h, e] += ds[:HALF, :HALF] + ds[HALF:, HALF:]
            diag_scr[h, e - 1] += ds[:HALF, HALF:]
            diag_scr[h, e + 1] += ds[HALF:, :HALF]

        run(pl.multiple_of(qt * TILE, TILE), TILE, span_ref[0, qt], span_ref[1, qt], bias_of, keep)
        return carry

    lax.fori_loop(0, SEQ_LEN // TILE, content_tile, 0)

    def query_tile(t, carry):
        col = pl.multiple_of(t * HALF, HALF)

        def bias_of(h, kt):
            return qbias_ref[h, pl.ds(pl.multiple_of(kt * TILE, TILE), TILE), pl.ds(col, HALF)]

        def keep(h, kt, ds, low):
            ds_scr[h, pl.ds(pl.multiple_of(kt * TILE, TILE), TILE), pl.ds(col, HALF)] = low

        run(
            pl.multiple_of(SEQ_LEN + t * HALF, HALF),
            HALF,
            span_ref[0, SEQ_LEN // TILE],
            span_ref[1, SEQ_LEN // TILE],
            bias_of,
            keep,
        )
        return carry

    lax.fori_loop(0, rows_q // HALF, query_tile, 0)

    for h in range(own):
        dk_ref[h] = (dk_scr[h] * SCALE).astype(BF16)
        dv_ref[h] = dv_scr[h].astype(BF16)

    offs_ref[...] = jnp.zeros(offs_ref.shape, F32)
    qoffs_ref[...] = jnp.zeros(qoffs_ref.shape, F32)
    lane = lax.broadcasted_iota(jnp.int32, (HALF, HALF), 1)
    turn = lane + lax.broadcasted_iota(jnp.int32, (HALF, HALF), 0)
    over = turn >= HALF
    turn = jnp.where(over, turn - HALF, turn)
    for h in range(own):
        for e in range(DIAGS):
            skew = jnp.take_along_axis(diag_scr[h, e], turn, axis=1)
            start = HALF * (15 - e + REACH)
            offs_ref[h : h + 1, start : start + HALF] += jnp.sum(
                jnp.where(over, skew, 0.0), axis=0, keepdims=True
            )
            offs_ref[h : h + 1, start + HALF : start + 2 * HALF] += jnp.sum(
                jnp.where(over, 0.0, skew), axis=0, keepdims=True
            )

    for h in range(own):
        total = jnp.zeros((16, WIDE), F32)
        for t in range(rows_q // HALF):
            shift = shift_ref[t * HALF : (t + 1) * HALF, :]
            place = lane - shift
            low_side = place < 0
            idx = jnp.where(low_side, place + HALF, place)
            prev = jnp.zeros((HALF, HALF), F32)
            pieces = []
            for j in range(SEQ_LEN // HALF + 1):
                if j < SEQ_LEN // HALF:
                    block = ds_scr[h, j * HALF : (j + 1) * HALF, t * HALF : (t + 1) * HALF]
                    cur = jnp.take_along_axis(block.astype(F32).T, idx, axis=1)
                else:
                    cur = jnp.zeros((HALF, HALF), F32)
                pieces.append(jnp.where(low_side, prev, cur).astype(BF16))
                prev = cur
            total += jnp.dot(
                hott_ref[:, t * HALF : (t + 1) * HALF],
                jnp.concatenate(pieces, axis=1),
                preferred_element_type=F32,
            )
        for i in range(16):
            qoffs_ref[h : h + 1, HALF * i : HALF * i + WIDE] += total[i : i + 1, :]


def bwd_call(
    span, qt, q3, k3, kt, v3, ctx, gt, g3, lse, kmeta, rseg, rlim, tiles, qbias, hott, shift
):
    own = k3.shape[0]
    rows = qt.shape[1]
    rows_q = rows - SEQ_LEN
    vm = pl.BlockSpec(memory_space=pltpu.VMEM)
    return pl.pallas_call(
        functools.partial(bwd_kernel, own, rows_q),
        out_shape=(
            jax.ShapeDtypeStruct((own * HEAD_DIM, rows), BF16),
            jax.ShapeDtypeStruct((own, SEQ_LEN, HEAD_DIM), BF16),
            jax.ShapeDtypeStruct((own, SEQ_LEN, HEAD_DIM), BF16),
            jax.ShapeDtypeStruct((own, 2 * SEQ_LEN), F32),
            jax.ShapeDtypeStruct((own, 2 * SEQ_LEN), F32),
        ),
        in_specs=[pl.BlockSpec(memory_space=pltpu.SMEM)] + [vm] * 16,
        scratch_shapes=[
            pltpu.VMEM((own, SEQ_LEN, HEAD_DIM), F32),
            pltpu.VMEM((own, SEQ_LEN, HEAD_DIM), F32),
            pltpu.VMEM((own, HEAD_DIM, TILE), F32),
            pltpu.VMEM((own, DIAGS, HALF, HALF), F32),
            pltpu.VMEM((own, SEQ_LEN, rows_q), BF16),
            pltpu.VMEM((own, rows), F32),
        ],
        compiler_params=pltpu.CompilerParams(vmem_limit_bytes=60 << 20),
        name="attend_back",
    )(span, qt, q3, k3, kt, v3, ctx, gt, g3, lse, kmeta, rseg, rlim, tiles, qbias, hott, shift)


def table_sums(offs, qoffs, rel_bucket):
    ids = jnp.arange(BUCKETS, dtype=jnp.int32)[:, None]
    back = jnp.pad(rel_bucket[::-1], (1, 0), constant_values=BUCKETS)
    ahead = jnp.pad(rel_bucket, (0, 1), constant_values=BUCKETS)
    high = lax.Precision.HIGHEST
    near = jnp.einsum("ho,bo->bh", offs, (back[None, :] == ids).astype(F32), precision=high)
    far = jnp.einsum("ho,bo->bh", qoffs, (ahead[None, :] == ids).astype(F32), precision=high)
    return near + far


def bias_inputs(rel_bucket, rel_table, first, own):
    hot = (rel_bucket[:, None] == jnp.arange(BUCKETS, dtype=jnp.int32)[None, :]).astype(BF16)
    part = lax.dynamic_slice_in_dim(rel_table, first, own, axis=1)
    vec = jnp.einsum("ob,bh->ho", hot, part, preferred_element_type=F32)
    rev = jnp.pad(vec[:, ::-1], ((0, 0), (1, 0))) * LOG2E
    low = jnp.pad(vec, ((0, 0), (0, 1))).astype(BF16)
    fold = jnp.stack([low[:, HALF * i : HALF * i + WIDE] for i in range(16)], axis=1)
    return rev, fold


def query_place(predicted, rows_q):
    a = predicted // HALF
    c = predicted - a * HALF
    pad = rows_q - predicted.shape[0]
    hot = ((15 - a)[:, None] == jnp.arange(16, dtype=jnp.int32)[None, :]).astype(BF16)
    hot = jnp.pad(hot, ((0, pad), (0, 0)))
    shift = jnp.pad(HALF - 1 - c, (0, pad))
    shift = jnp.broadcast_to(shift[:, None], (rows_q, HALF))
    return hot, hot.T, shift


def row_meta(segment, pad_mask, order, predicted, rows_q):
    length = segment.shape[0]
    pos = jnp.arange(length, dtype=jnp.int32)
    real = pad_mask == 1
    seg = jnp.where(real, segment, -2 - pos)
    hit = predicted[:, None] == pos[None, :]
    qseg = jnp.sum(jnp.where(hit, seg[None, :], 0), axis=1)
    qlim = jnp.sum(jnp.where(hit, order[None, :], 0), axis=1) - 1
    pad = rows_q - predicted.shape[0]
    qseg = jnp.pad(qseg, (0, pad), constant_values=-1)
    qlim = jnp.pad(qlim, (0, pad))
    rseg = jnp.concatenate([seg, qseg])[None, :]
    rlim = jnp.concatenate([order, qlim])[None, :]
    kmeta = jnp.broadcast_to(jnp.stack([seg, order])[:, :, None], (2, length, HALF))
    tiles = length // TILE
    head_seg = segment[::TILE]
    tail_seg = segment[TILE - 1 :: TILE]
    starts = jnp.sum((segment[None, :] < head_seg[:, None]).astype(jnp.int32), axis=1)
    own = jnp.arange(tiles, dtype=jnp.int32)
    lo = jnp.where(real[::TILE], starts // TILE, own)
    hi = jnp.where(real[TILE - 1 :: TILE], tail_seg // TILE, own)
    count = jnp.sum(pad_mask)
    lo = jnp.concatenate([lo, jnp.zeros((1,), jnp.int32)])
    hi = jnp.concatenate([hi, jnp.maximum(count - 1, 0)[None] // TILE])
    return rseg, rlim, kmeta, jnp.stack([lo, hi]).astype(jnp.int32)


MESH = pl.DeviceIdType.MESH
ROWS_Q = 384
SLOT_Q = 80
VEC_PARTS = (48, 24, 24, 24, 96, 24, 24, 24)


def signal_peers(dp, s, dps, seqs):
    barrier = pltpu.get_barrier_semaphore()
    for r in range(1, dps):
        pl.semaphore_signal(
            barrier, inc=1, device_id=(lax.rem(dp + r, dps), s), device_id_type=MESH
        )
    for r in range(1, seqs):
        pl.semaphore_signal(
            barrier, inc=1, device_id=(dp, lax.rem(s + r, seqs)), device_id_type=MESH
        )
    pl.semaphore_wait(barrier, dps - 1 + seqs - 1)


def remote(src, dst, send_sem, recv_sem, k, device):
    return pltpu.make_async_remote_copy(
        src_ref=src,
        dst_ref=dst,
        send_sem=send_sem.at[k],
        recv_sem=recv_sem.at[k],
        device_id=device,
        device_id_type=MESH,
    )


def start_kernel(
    dps,
    seqs,
    rc_ref,
    rq_ref,
    zero_ref,
    w_ref,
    v_ref,
    i_ref,
    x_out,
    w_out,
    v_out,
    i_out,
    send_sem,
    recv_sem,
    here_sem,
):
    dp = lax.axis_index("dp")
    s = lax.axis_index("seq")
    length = rc_ref.shape[0]
    count = rq_ref.shape[0]
    mate = s + 1 - 2 * lax.rem(s, 2)
    across = lax.rem(s + 2, seqs)
    signal_peers(dp, s, dps, seqs)

    def spot_c(owner):
        return x_out.at[pl.ds(pl.multiple_of(owner * length, length), length)]

    def spot_q(owner):
        start = seqs * length + owner * count
        return x_out.at[pl.ds(pl.multiple_of(start, 16), count)]

    k = 0
    small = []
    for r in range(1, seqs):
        to = lax.rem(s + r, seqs)
        for src, dst in (
            (w_ref.at[to], w_out.at[dp, s]),
            (v_ref, v_out.at[dp, s]),
            (i_ref, i_out.at[s]),
        ):
            small.append(remote(src, dst, send_sem, recv_sem, k, (dp, to)))
            k += 1
    for copy in small:
        copy.start()
    near, far = [], []
    for src, spot in ((rc_ref, spot_c), (rq_ref, spot_q)):
        far.append(remote(src, spot(s), send_sem, recv_sem, k, (dp, across)))
        near.append(remote(src, spot(s), send_sem, recv_sem, k + 1, (dp, mate)))
        k += 2
    for copy in far + near:
        copy.start()
    here = [
        pltpu.make_async_copy(w_ref.at[s], w_out.at[dp, s], here_sem.at[0]),
        pltpu.make_async_copy(v_ref, v_out.at[dp, s], here_sem.at[1]),
        pltpu.make_async_copy(i_ref, i_out.at[s], here_sem.at[2]),
        pltpu.make_async_copy(rc_ref, spot_c(s), here_sem.at[3]),
        pltpu.make_async_copy(rq_ref, spot_q(s), here_sem.at[4]),
        pltpu.make_async_copy(
            zero_ref,
            x_out.at[pl.ds(seqs * (length + count), zero_ref.shape[0])],
            here_sem.at[5],
        ),
    ]
    for copy in here:
        copy.start()
    for copy in small:
        copy.wait_recv()
    for copy in here:
        copy.wait()
    wide = []
    for r in range(1, dps):
        to = lax.rem(dp + r, dps)
        for ref in (w_out, v_out):
            wide.append(remote(ref.at[dp], ref.at[dp], send_sem, recv_sem, k, (to, s)))
            k += 1
    for copy in wide:
        copy.start()
    pass_on = []
    for copy, spot in zip(far, (spot_c, spot_q)):
        copy.wait_recv()
        pass_on.append(
            remote(spot(across), spot(across), send_sem, recv_sem, k, (dp, mate))
        )
        pass_on[-1].start()
        k += 1
    for copy in small + far:
        copy.wait_send()
    for copy in near + wide + pass_on:
        copy.wait()


def start_call(dps, seqs, rc, rq, w, v, ints):
    copies = 3 * (seqs - 1) + 4 + 2 * (dps - 1) + 2
    zero = jnp.zeros((ROWS_Q - seqs * rq.shape[0], rc.shape[1]), BF16)
    rows = seqs * rc.shape[0] + ROWS_Q
    hbm = pl.BlockSpec(memory_space=pl.ANY)
    return pl.pallas_call(
        functools.partial(start_kernel, dps, seqs),
        out_shape=(
            jax.ShapeDtypeStruct((rows, rc.shape[1]), BF16),
            jax.ShapeDtypeStruct((dps,) + w.shape, BF16),
            jax.ShapeDtypeStruct((dps, seqs) + v.shape, F32),
            jax.ShapeDtypeStruct((seqs,) + ints.shape, jnp.int32),
        ),
        in_specs=[hbm] * 6,
        out_specs=(hbm,) * 4,
        scratch_shapes=[
            pltpu.SemaphoreType.DMA((copies,)),
            pltpu.SemaphoreType.DMA((copies,)),
            pltpu.SemaphoreType.DMA((6,)),
        ],
        compiler_params=pltpu.CompilerParams(collective_id=0, has_side_effects=True),
        name="gather_rows",
    )(rc, rq, zero, w, v, ints)


def swap_kernel(seqs, c_of, q_of, c_ref, q_ref, c_out, q_out, send_sem, recv_sem, here_sem):
    dp = lax.axis_index("dp")
    s = lax.axis_index("seq")
    signal_peers(dp, s, 1, seqs)
    copies = []
    for r in range(1, seqs):
        to = lax.rem(s + r, seqs)
        k = 2 * (r - 1)
        copies.append(remote(c_of(c_ref, to), c_out.at[s], send_sem, recv_sem, k, (dp, to)))
        copies.append(remote(q_of(q_ref, to), q_out.at[s], send_sem, recv_sem, k + 1, (dp, to)))
    for copy in copies:
        copy.start()
    here = [
        pltpu.make_async_copy(c_of(c_ref, s), c_out.at[s], here_sem.at[0]),
        pltpu.make_async_copy(q_of(q_ref, s), q_out.at[s], here_sem.at[1]),
    ]
    for copy in here:
        copy.start()
    for copy in here + copies:
        copy.wait()


def swap_call(seqs, c, q, c_of, q_of, c_shape, q_shape, ident, name):
    hbm = pl.BlockSpec(memory_space=pl.ANY)
    return pl.pallas_call(
        functools.partial(swap_kernel, seqs, c_of, q_of),
        out_shape=(
            jax.ShapeDtypeStruct((seqs,) + c_shape, c.dtype),
            jax.ShapeDtypeStruct((seqs,) + q_shape, q.dtype),
        ),
        in_specs=[hbm] * 2,
        out_specs=(hbm,) * 2,
        scratch_shapes=[
            pltpu.SemaphoreType.DMA((2 * (seqs - 1),)),
            pltpu.SemaphoreType.DMA((2 * (seqs - 1),)),
            pltpu.SemaphoreType.DMA((2,)),
        ],
        compiler_params=pltpu.CompilerParams(collective_id=ident, has_side_effects=True),
        name=name,
    )(c, q)


def end_kernel(
    dps,
    seqs,
    gc_ref,
    gq_ref,
    w_ref,
    v_ref,
    gc_out,
    gq_out,
    w_out,
    v_out,
    c_mate,
    q_mate,
    c_far,
    q_far,
    c_send,
    q_send,
    w_got,
    v_got,
    w_sum,
    v_sum,
    v_last,
    send_sem,
    recv_sem,
):
    dp = lax.axis_index("dp")
    s = lax.axis_index("seq")
    core = lax.rem(s, 2)
    mate = s + 1 - 2 * core
    across = lax.rem(s + 2, seqs)
    signal_peers(dp, s, dps, seqs)
    k = 0
    first = []
    for i in range(2):
        to = lax.rem(mate + 2 * (1 - i), seqs)
        for src, dst in ((gc_ref, c_mate), (gq_ref, q_mate)):
            first.append(remote(src.at[to], dst.at[i], send_sem, recv_sem, k, (dp, mate)))
            k += 1
    wide = []
    for r in range(1, dps):
        to = lax.rem(dp + r, dps)
        for src, dst in ((w_ref, w_got), (v_ref, v_got)):
            wide.append(remote(src.at[to], dst.at[r - 1], send_sem, recv_sem, k, (to, s)))
            k += 1
    for copy in first + wide:
        copy.start()

    def each(ref, step, fn):
        def body(i, carry):
            fn(pl.ds(pl.multiple_of(i * step, step), step))
            return carry

        lax.fori_loop(0, ref.shape[-2] // step, body, 0)

    cross = []
    for (src, got, buf, far, copy) in (
        (gc_ref, c_mate, c_send, c_far, first[0]),
        (gq_ref, q_mate, q_send, q_far, first[1]),
    ):
        copy.wait_recv()

        def add(rows, src=src, got=got, buf=buf):
            buf[rows, :] = (
                src[across, rows, :].astype(F32) + got[0, rows, :].astype(F32)
            ).astype(BF16)

        each(buf, 16, add)
        cross.append(remote(buf, far, send_sem, recv_sem, k, (dp, across)))
        cross[-1].start()
        k += 1
    for copy in wide:
        copy.wait_recv()

    def add_w(rows):
        for t in range(seqs):
            total = w_ref[dp, t, rows, :].astype(F32)
            for r in range(1, dps):
                total += w_got[r - 1, t, rows, :].astype(F32)
            w_sum[t, rows, :] = total

    each(w_sum, 8, add_w)
    total = v_ref[dp]
    for r in range(1, dps):
        total += v_got[r - 1]
    v_sum[...] = total
    last = []
    for r in range(1, seqs):
        to = lax.rem(s + r, seqs)
        last.append(remote(w_sum.at[to], w_out.at[s], send_sem, recv_sem, k, (dp, to)))
        last.append(remote(v_sum.at[to], v_last.at[r - 1], send_sem, recv_sem, k + 1, (dp, to)))
        k += 2
    for copy in last:
        copy.start()
    w_out[s] = w_sum[s]
    for copy in first[2:]:
        copy.wait_recv()
    for copy in cross:
        copy.wait_recv()
    for (src, got, far, out) in (
        (gc_ref, c_mate, c_far, gc_out),
        (gq_ref, q_mate, q_far, gq_out),
    ):

        def total_of(rows, src=src, got=got, far=far, out=out):
            out[rows, :] = (
                src[s, rows, :].astype(F32)
                + got[1, rows, :].astype(F32)
                + far[rows, :].astype(F32)
            )

        each(out, 16, total_of)
    for copy in last:
        copy.wait_recv()
    total = v_sum[s]
    for r in range(1, seqs):
        total += v_last[r - 1]
    v_out[...] = total
    for copy in first + wide + cross + last:
        copy.wait_send()


def end_call(dps, seqs, gc, gq, w, v):
    copies = 4 + 2 * (dps - 1) + 2 + 2 * (seqs - 1)
    vm = pl.BlockSpec(memory_space=pltpu.VMEM)
    cshape, qshape, wshape, vshape = gc.shape[1:], gq.shape[1:], w.shape[1:], v.shape[1:]
    return pl.pallas_call(
        functools.partial(end_kernel, dps, seqs),
        out_shape=(
            jax.ShapeDtypeStruct(cshape, F32),
            jax.ShapeDtypeStruct(qshape, F32),
            jax.ShapeDtypeStruct(wshape, F32),
            jax.ShapeDtypeStruct(vshape[1:], F32),
        ),
        in_specs=[vm] * 4,
        out_specs=(vm,) * 4,
        scratch_shapes=[
            pltpu.VMEM((2,) + cshape, BF16),
            pltpu.VMEM((2,) + qshape, BF16),
            pltpu.VMEM(cshape, BF16),
            pltpu.VMEM(qshape, BF16),
            pltpu.VMEM(cshape, BF16),
            pltpu.VMEM(qshape, BF16),
            pltpu.VMEM((dps - 1,) + wshape, BF16),
            pltpu.VMEM((dps - 1,) + vshape, F32),
            pltpu.VMEM(wshape, F32),
            pltpu.VMEM(vshape, F32),
            pltpu.VMEM((seqs - 1,) + vshape[1:], F32),
            pltpu.SemaphoreType.DMA((copies,)),
            pltpu.SemaphoreType.DMA((copies,)),
        ],
        compiler_params=pltpu.CompilerParams(
            collective_id=3, has_side_effects=True, vmem_limit_bytes=50 << 20
        ),
        name="sum_rows",
    )(gc, gq, w, v)


def flip_perm(count, bit):
    return [(i, i ^ bit) for i in range(count)]


AXES = ("dp", "seq")


def gather_blocks(shard, count, bits):
    me = lax.axis_index(AXES)
    cur = shard
    for bit in bits:
        got = lax.ppermute(cur, AXES, flip_perm(count, bit))
        mine = (me // bit) % 2
        cur = jnp.where(mine == 0, jnp.stack([cur, got]), jnp.stack([got, cur]))
    dims = len(bits)
    order = sorted(range(dims), key=lambda j: -bits[dims - 1 - j])
    cur = jnp.transpose(cur, tuple(order) + tuple(range(dims, cur.ndim)))
    return cur.reshape((count * shard.shape[0],) + shard.shape[1:])


def scatter_sums(full, count, bits):
    me = lax.axis_index(AXES)
    dims = count.bit_length() - 1
    left = [1 << j for j in reversed(range(dims))]
    cur = full.reshape((2,) * dims + (full.shape[0] // count, full.shape[1]))
    for bit in bits:
        axis = left.index(bit)
        left.pop(axis)
        mine = (me // bit) % 2
        give = lax.dynamic_index_in_dim(cur, 1 - mine, axis, keepdims=False).astype(BF16)
        got = lax.ppermute(give, AXES, flip_perm(count, bit))
        keep = lax.dynamic_index_in_dim(cur, mine, axis, keepdims=False)
        cur = keep + got.astype(F32)
    return cur


def local_fast(
    content,
    query_stream,
    segment_ids,
    pad_mask,
    predicted,
    order,
    rel_bucket,
    qkv_weight,
    qv_bias,
    out_weight,
    out_bias,
    attn_gain,
    attn_shift,
    up_weight,
    up_bias,
    down_weight,
    down_bias,
    ffn_gain,
    ffn_shift,
    rel_table,
    content_cot,
    query_cot,
):
    dps, seqs = lax.axis_size("dp"), lax.axis_size("seq")
    count = dps * seqs
    s = lax.axis_index("seq")
    own = HEADS // seqs
    wide = own * HEAD_DIM
    length = content.shape[1]
    preds = query_stream.shape[1]
    pad_q = SLOT_Q - preds
    shard = qkv_weight.shape[0]

    rows = jnp.concatenate(
        [content[0], query_stream[0], jnp.zeros((pad_q, MODEL_WIDTH), F32)], axis=0
    )
    rows_low = rows.astype(BF16)
    vec = jnp.concatenate(
        [
            member.astype(F32)
            for member in (
                qv_bias,
                out_bias,
                attn_gain,
                attn_shift,
                up_bias,
                down_bias,
                ffn_gain,
                ffn_shift,
            )
        ]
    )
    vec = jnp.pad(vec, (0, 1024 - vec.shape[0])).reshape(8, 128)
    ints = jnp.stack(
        [
            segment_ids[0],
            order[0],
            pad_mask[0],
            jnp.pad(predicted[0], (0, length - preds), constant_values=-1),
        ]
    )
    ints = jnp.pad(ints, ((0, 4), (0, 0)))
    w_parts = jnp.transpose(
        qkv_weight.reshape(shard, 3, seqs, wide), (2, 0, 1, 3)
    ).reshape(seqs, shard, 3 * wide)
    x_all, w_all, v_all, i_all = start_call(
        dps, seqs, rows_low[:length], rows_low[length:], w_parts, vec, ints
    )
    w_qkv = w_all.reshape(MODEL_WIDTH, 3 * wide)
    parts = v_all.reshape(count, 1024)
    vectors = []
    at = 0
    for n in VEC_PARTS:
        vectors.append(parts[:, at : at + n].reshape(count * n))
        at += n
    bias_qv, bias_out, gain_one, shift_one, bias_up, bias_down, gain_two, shift_two = vectors
    seg_all = i_all[:, 0].reshape(seqs * length)
    order_all = i_all[:, 1].reshape(seqs * length)
    pad_all = i_all[:, 2].reshape(seqs * length)
    pred_all = i_all[:, 3, :SLOT_Q].reshape(seqs * SLOT_Q)

    bits_up = (8, 16, 4, 2, 1)
    bits_down = (8, 16, 2, 4, 1)
    upout = gather_blocks(
        jnp.concatenate([up_weight, out_weight], axis=1), count, bits_up
    )
    w_down = gather_blocks(
        down_weight.reshape(shard, -1), count, bits_down
    ).reshape(-1, MODEL_WIDTH)
    w_up, w_out = upout[:, : up_weight.shape[1]], upout[:, up_weight.shape[1] :]

    rev, fold = bias_inputs(rel_bucket, rel_table, s * own, own)
    hot, hot_t, shift = query_place(pred_all, ROWS_Q)
    rseg, rlim, kmeta, span = row_meta(seg_all, pad_all, order_all, pred_all, ROWS_Q)
    tiles, qbias = bias_call(rev, fold, hot, shift)

    bq = lax.dynamic_slice_in_dim(bias_qv[:MODEL_WIDTH], s * wide, wide)
    bv = lax.dynamic_slice_in_dim(bias_qv[MODEL_WIDTH:], s * wide, wide)
    w_q, w_k, w_v = w_qkv[:, :wide], w_qkv[:, wide : 2 * wide], w_qkv[:, 2 * wide :]
    keys = x_all[: seqs * length]

    def flat(x, w, b):
        y = jnp.einsum("rd,de->re", x, w, preferred_element_type=F32)
        return (y if b is None else y + b).astype(BF16)

    def flipped(x, w, b):
        y = jnp.einsum("rd,de->er", x, w, preferred_element_type=F32)
        return (y if b is None else y + b[:, None]).astype(BF16)

    def by_head(x):
        return jnp.transpose(x.reshape(x.shape[0], own, HEAD_DIM), (1, 0, 2))

    q_t = flipped(x_all, w_q, bq)
    q3 = by_head(flat(x_all, w_q, bq))
    k3 = by_head(flat(keys, w_k, None))
    k_t = flipped(keys, w_k, None)
    v3 = by_head(flat(keys, w_v, bv))
    v_t = flipped(keys, w_v, bv)

    ctx_t, ctx_rows, lse = fwd_call(span, q_t, k3, v_t, kmeta, rseg, rlim, tiles, qbias)

    def from_rows(ref, t):
        return ref.at[pl.ds(pl.multiple_of(t * length, length), length)]

    def from_query(ref, t):
        return ref.at[pl.ds(pl.multiple_of(seqs * length + t * SLOT_Q, 16), SLOT_Q)]

    ctx_c, ctx_q = swap_call(
        seqs,
        ctx_rows,
        ctx_rows,
        from_rows,
        from_query,
        (length, wide),
        (SLOT_Q, wide),
        1,
        "swap_context",
    )
    context_low = jnp.transpose(
        jnp.concatenate([ctx_c, ctx_q], axis=1), (1, 0, 2)
    ).reshape(length + SLOT_Q, MODEL_WIDTH)

    attn_out = jnp.einsum("re,ed->rd", context_low, w_out, preferred_element_type=F32) + bias_out
    hidden_one, normed_one, inv_one = norm_fwd((rows + attn_out)[None], gain_one, shift_one)
    hidden_low = hidden_one[0].astype(BF16)
    pre_act = jnp.einsum("rd,df->rf", hidden_low, w_up, preferred_element_type=F32) + bias_up
    activ, gelu_pull = jax.vjp(exact_gelu, pre_act)
    activ_low = activ.astype(BF16)
    ffn_out = jnp.einsum("rf,fd->rd", activ_low, w_down, preferred_element_type=F32) + bias_down
    hidden_two, normed_two, inv_two = norm_fwd(hidden_one + ffn_out[None], gain_two, shift_two)
    pad_float = pad_mask[0].astype(F32)
    row_valid = jnp.concatenate([pad_float, jnp.ones((preds,), F32), jnp.zeros((pad_q,), F32)])
    outputs = hidden_two[0] * row_valid[:, None]
    rows_c = jnp.concatenate([pad_float, jnp.zeros((SLOT_Q,), F32)])[:, None]
    rows_q = jnp.concatenate(
        [jnp.zeros((length,), F32), jnp.ones((preds,), F32), jnp.zeros((pad_q,), F32)]
    )[:, None]
    local_sums = jnp.stack(
        [
            jnp.sum(rows_c * rows * rows),
            jnp.sum(rows_q * rows * rows),
            jnp.sum(rows_c * attn_out * attn_out),
            jnp.sum(rows_q * attn_out * attn_out),
            jnp.sum(rows_c * ffn_out * ffn_out),
            jnp.sum(rows_q * ffn_out * ffn_out),
            jnp.sum(pad_float),
        ]
    )
    upstream = (
        jnp.concatenate([content_cot[0], query_cot[0], jnp.zeros((pad_q, MODEL_WIDTH), F32)])
        * row_valid[:, None]
    )
    grad_res_two, grad_gain_two, grad_shift_two = norm_back(
        upstream[None], normed_two, inv_two, gain_two
    )
    grad_res_two = grad_res_two[0]
    grad_ffn = grad_res_two.astype(BF16)
    grad_bias_down = jnp.sum(grad_ffn, axis=0, dtype=F32)
    grad_down = jnp.einsum("rf,rd->fd", activ_low, grad_ffn, preferred_element_type=F32)
    grad_activ = jnp.einsum("rd,fd->rf", grad_ffn, w_down, preferred_element_type=F32)
    grad_pre = gelu_pull(grad_activ)[0].astype(BF16)
    grad_bias_up = jnp.sum(grad_pre, axis=0, dtype=F32)
    grad_up = jnp.einsum("rd,rf->df", hidden_low, grad_pre, preferred_element_type=F32)
    grad_hidden = grad_res_two + jnp.einsum(
        "rf,df->rd", grad_pre, w_up, preferred_element_type=F32
    )
    grad_res_one, grad_gain_one, grad_shift_one = norm_back(
        grad_hidden[None], normed_one, inv_one, gain_one
    )
    grad_res_one = grad_res_one[0]
    grad_attn = grad_res_one.astype(BF16)
    grad_bias_out = jnp.sum(grad_attn, axis=0, dtype=F32)
    grad_out = jnp.einsum("re,rd->ed", context_low, grad_attn, preferred_element_type=F32)
    grad_context = jnp.einsum(
        "rd,ed->re", grad_attn, w_out, preferred_element_type=F32
    ).astype(BF16)

    grad_down_own = scatter_sums(
        grad_down.reshape(MODEL_WIDTH, -1), count, (1, 4, 2, 8, 16)
    ).reshape(-1, MODEL_WIDTH)
    grad_upout_own = scatter_sums(
        jnp.concatenate([grad_up, grad_out], axis=1), count, (1, 2, 4, 8, 16)
    )
    grad_up_own = grad_upout_own[:, : up_weight.shape[1]]
    grad_out_own = grad_upout_own[:, up_weight.shape[1] :]

    split = jnp.transpose(
        grad_context.reshape(length + SLOT_Q, seqs, wide), (1, 0, 2)
    )

    def from_slot(ref, t):
        return ref.at[t]

    g_c, g_q = swap_call(
        seqs,
        split[:, :length],
        split[:, length:],
        from_slot,
        from_slot,
        (length, wide),
        (SLOT_Q, wide),
        2,
        "swap_grads",
    )
    g_rows = jnp.concatenate(
        [
            g_c.reshape(seqs * length, wide),
            g_q.reshape(seqs * SLOT_Q, wide),
            jnp.zeros((ROWS_Q - seqs * SLOT_Q, wide), BF16),
        ]
    )
    dq_t, dk3, dv3, offs, qoffs = bwd_call(
        span,
        q_t,
        q3,
        k3,
        k_t,
        v3,
        ctx_t,
        g_rows.T,
        by_head(g_rows),
        lse,
        kmeta,
        rseg,
        rlim,
        tiles,
        qbias,
        hot_t,
        shift,
    )
    table = table_sums(offs, qoffs, rel_bucket)
    dk = jnp.transpose(dk3, (1, 0, 2)).reshape(seqs * length, wide)
    dv = jnp.transpose(dv3, (1, 0, 2)).reshape(seqs * length, wide)
    grad_w = jnp.concatenate(
        [
            jnp.einsum("rd,er->de", x_all, dq_t, preferred_element_type=F32),
            jnp.einsum("rd,re->de", keys, dk, preferred_element_type=F32),
            jnp.einsum("rd,re->de", keys, dv, preferred_element_type=F32),
        ],
        axis=1,
    ).astype(BF16)
    dq = dq_t.T
    cut = seqs * length
    grad_keys_rows = (
        jnp.einsum("re,de->rd", dq[:cut], w_q, preferred_element_type=F32)
        + jnp.einsum("re,de->rd", dk, w_k, preferred_element_type=F32)
        + jnp.einsum("re,de->rd", dv, w_v, preferred_element_type=F32)
    ).astype(BF16)
    grad_query_rows = jnp.einsum(
        "re,de->rd", dq[cut : cut + seqs * SLOT_Q], w_q, preferred_element_type=F32
    ).astype(BF16)
    bias_q = jnp.sum(dq_t.astype(F32), axis=1)
    bias_v = jnp.sum(dv.astype(F32), axis=0)
    spot = jnp.zeros((2, MODEL_WIDTH), F32)
    grad_bias_qv = lax.dynamic_update_slice(
        spot, jnp.stack([bias_q, bias_v]), (0, s * wide)
    ).reshape(2 * MODEL_WIDTH)
    table_all = lax.dynamic_update_slice(
        jnp.zeros((BUCKETS, HEADS), F32), table, (0, s * own)
    )
    owned = jnp.concatenate(
        [
            member.reshape(count, -1)
            for member in (
                grad_bias_qv,
                grad_bias_out,
                grad_gain_one,
                grad_shift_one,
                grad_bias_up,
                grad_bias_down,
                grad_gain_two,
                grad_shift_two,
            )
        ],
        axis=1,
    )
    used = owned.shape[1]
    shared = jnp.concatenate([table_all.reshape(-1), local_sums])
    vec_grads = jnp.concatenate(
        [
            owned,
            jnp.broadcast_to(shared[None, :], (count, shared.shape[0])),
            jnp.zeros((count, 1024 - used - shared.shape[0]), F32),
        ],
        axis=1,
    ).reshape(dps, seqs, 8, 128)
    sum_c, sum_q, sum_w, sum_v = end_call(
        dps,
        seqs,
        grad_keys_rows.reshape(seqs, length, MODEL_WIDTH),
        grad_query_rows.reshape(seqs, SLOT_Q, MODEL_WIDTH),
        grad_w.reshape(dps, seqs, shard, 3 * wide),
        vec_grads,
    )
    grad_content = grad_res_one[:length] + sum_c
    grad_query = grad_res_one[length : length + preds] + sum_q[:preds]
    grad_qkv_own = jnp.transpose(sum_w.reshape(seqs, shard, 3, wide), (1, 2, 0, 3)).reshape(
        shard, 3 * MODEL_WIDTH
    )
    sums = sum_v.reshape(1024)
    mine = []
    at = 0
    for n in VEC_PARTS:
        mine.append(sums[at : at + n])
        at += n
    table_sum = sums[at : at + BUCKETS * HEADS].reshape(BUCKETS, HEADS)
    totals = sums[at + BUCKETS * HEADS : at + BUCKETS * HEADS + 7]
    content_count = totals[6] * MODEL_WIDTH
    query_count = float(dps * preds * seqs * MODEL_WIDTH)
    each = jnp.stack([content_count, jnp.float32(query_count)])
    stats = jnp.sqrt(totals[:6] / jnp.concatenate([each, each, each]))
    return (
        outputs[None, :length],
        outputs[None, length : length + preds],
        grad_content[None],
        grad_query[None],
        grad_qkv_own,
        mine[0],
        grad_out_own,
        mine[1],
        mine[2],
        mine[3],
        grad_up_own,
        mine[4],
        grad_down_own,
        mine[5],
        mine[6],
        mine[7],
        table_sum,
        stats,
    )


def pick_local(mesh):
    sizes = dict(mesh.shape)
    return local_fast if (sizes["dp"], sizes["seq"]) == (8, 4) else local_general


def solution(mesh):
    in_specs = (
        P("dp", "seq", None),
        P("dp", "seq", None),
        P("dp", "seq"),
        P("dp", "seq"),
        P("dp", "seq"),
        P("dp", "seq"),
        P(),
        P(("dp", "seq"), None),
        P(("dp", "seq")),
        P(("dp", "seq"), None),
        P(("dp", "seq")),
        P(("dp", "seq")),
        P(("dp", "seq")),
        P(("dp", "seq"), None),
        P(("dp", "seq")),
        P(("dp", "seq"), None),
        P(("dp", "seq")),
        P(("dp", "seq")),
        P(("dp", "seq")),
        P(),
        P("dp", "seq", None),
        P("dp", "seq", None),
    )
    out_specs = (
        P("dp", "seq", None),
        P("dp", "seq", None),
        P("dp", "seq", None),
        P("dp", "seq", None),
        P(("dp", "seq"), None),
        P(("dp", "seq")),
        P(("dp", "seq"), None),
        P(("dp", "seq")),
        P(("dp", "seq")),
        P(("dp", "seq")),
        P(("dp", "seq"), None),
        P(("dp", "seq")),
        P(("dp", "seq"), None),
        P(("dp", "seq")),
        P(("dp", "seq")),
        P(("dp", "seq")),
        P(),
        P(),
    )
    local = pick_local(mesh)
    return jax.shard_map(local, mesh=mesh, in_specs=in_specs, out_specs=out_specs, check_vma=False)
```

```python
import functools
import math

import jax
import jax.numpy as jnp
from jax import lax
from jax.experimental import pallas as pl
from jax.experimental.pallas import tpu as pltpu
from jax.sharding import PartitionSpec as P

MODEL_WIDTH = 768
HEADS = 12
HEAD_DIM = 64
BUCKETS = 32
SEQ_LEN = 2048


EPS = 1e-05
NEG = -1000000000.0
SCALE = 0.125


def exact_gelu(values):
    return jax.nn.gelu(values, approximate=False)


def norm_fwd(residual, gain_vec, shift_vec):
    row_mean = jnp.mean(residual, axis=-1, keepdims=True)
    centered = residual - row_mean
    inv_std = lax.rsqrt(jnp.mean(centered * centered, axis=-1, keepdims=True) + EPS)
    normed = centered * inv_std
    return (normed * gain_vec + shift_vec, normed, inv_std)


def norm_back(upstream, normed, inv_std, gain_vec):
    grad_norm = upstream * gain_vec
    projected = jnp.mean(grad_norm, axis=-1, keepdims=True) + normed * jnp.mean(
        grad_norm * normed, axis=-1, keepdims=True
    )
    return (
        inv_std * (grad_norm - projected),
        jnp.sum(upstream * normed, axis=(0, 1)),
        jnp.sum(upstream, axis=(0, 1)),
    )


def bucket_edges(rel_bucket):
    entry_count = rel_bucket.shape[0]
    matches = rel_bucket[None, :] == jnp.arange(BUCKETS, dtype=jnp.int32)[:, None]
    places = jnp.arange(entry_count, dtype=jnp.int32)[None, :]
    starts = jnp.min(jnp.where(matches, places, entry_count), axis=1)
    counts = jnp.sum(matches.astype(jnp.int32), axis=1)
    return (starts, starts + counts)


def build_mask(
    query_pos, query_seg, query_limit, content_row, key_pos, key_seg, key_order, key_pad
):
    inside = (
        (query_seg[:, None] == key_seg[None, :])
        & (key_pad[None, :] == 1)
        & (key_order[None, :] <= query_limit[:, None])
    )
    itself = (key_pos[None, :] == query_pos[:, None]) & content_row[:, None]
    return (inside | itself, key_pos[None, :] - query_pos[:, None] + (SEQ_LEN - 1))


def masked_scores(query_heads, key_heads, table_low, edges, allowed, offsets):
    raw_scores = (
        jnp.einsum("rhd,lhd->hrl", query_heads, key_heads, preferred_element_type=jnp.float32)
        * SCALE
    )
    starts, ends = edges
    spread = offsets[..., None]
    onehot = ((spread >= starts) & (spread < ends)).astype(jnp.bfloat16)
    bias = jnp.einsum("rlb,bh->hrl", onehot, table_low, preferred_element_type=jnp.float32)
    return (jnp.where(allowed[None], raw_scores + bias, NEG), onehot)


def attend_forward(packed, table_low, edges, content_row):
    queries, key_values, key_seg, key_order, key_pad, query_pos, query_seg, query_limit = packed
    row_count = queries.shape[0]
    length = key_values.shape[0]
    key_pos = jnp.arange(length, dtype=jnp.int32)
    allowed, offsets = build_mask(
        query_pos, query_seg, query_limit, content_row, key_pos, key_seg, key_order, key_pad
    )
    query_heads = queries.reshape(row_count, HEADS, HEAD_DIM)
    key_heads = key_values[:, :MODEL_WIDTH].reshape(length, HEADS, HEAD_DIM)
    value_heads = key_values[:, MODEL_WIDTH:].reshape(length, HEADS, HEAD_DIM)
    scores, onehot = masked_scores(query_heads, key_heads, table_low, edges, allowed, offsets)
    row_max = jnp.max(scores, axis=-1, keepdims=True)
    expo_vals = jnp.exp(scores - row_max)
    row_total = jnp.sum(expo_vals, axis=-1, keepdims=True)
    probs_low = (expo_vals / row_total).astype(jnp.bfloat16)
    context = jnp.einsum("hrl,lhd->rhd", probs_low, value_heads, preferred_element_type=jnp.float32)
    return (
        context.reshape(row_count, MODEL_WIDTH),
        jnp.transpose((row_max + jnp.log(row_total))[..., 0]),
    )


def attend_backward(packed, table_low, edges, content_row):
    (
        queries,
        key_values,
        key_seg,
        key_order,
        key_pad,
        query_pos,
        query_seg,
        query_limit,
        row_lse,
        grad_context,
    ) = packed
    row_count = queries.shape[0]
    length = key_values.shape[0]
    key_pos = jnp.arange(length, dtype=jnp.int32)
    allowed, offsets = build_mask(
        query_pos, query_seg, query_limit, content_row, key_pos, key_seg, key_order, key_pad
    )
    query_heads = queries.reshape(row_count, HEADS, HEAD_DIM)
    key_heads = key_values[:, :MODEL_WIDTH].reshape(length, HEADS, HEAD_DIM)
    value_heads = key_values[:, MODEL_WIDTH:].reshape(length, HEADS, HEAD_DIM)
    scores, onehot = masked_scores(query_heads, key_heads, table_low, edges, allowed, offsets)
    probs = jnp.exp(scores - jnp.transpose(row_lse)[..., None])
    grad_heads = grad_context.reshape(row_count, HEADS, HEAD_DIM)
    grad_probs = jnp.einsum(
        "rhd,lhd->hrl", grad_heads, value_heads, preferred_element_type=jnp.float32
    )
    row_delta = jnp.sum(probs * grad_probs, axis=-1)
    grad_scores = (probs * (grad_probs - row_delta[..., None])).astype(jnp.bfloat16)
    grad_query = (
        jnp.einsum("hrl,lhd->rhd", grad_scores, key_heads, preferred_element_type=jnp.float32)
        * SCALE
    )
    grad_table = jnp.einsum("hrl,rlb->bh", grad_scores, onehot, preferred_element_type=jnp.float32)
    results = (grad_query.reshape(row_count, MODEL_WIDTH), grad_table, jnp.transpose(row_delta))
    probs_low = probs.astype(jnp.bfloat16)
    grad_key = (
        jnp.einsum("hrl,rhd->lhd", grad_scores, query_heads, preferred_element_type=jnp.float32)
        * SCALE
    )
    grad_value = jnp.einsum(
        "hrl,rhd->lhd", probs_low, grad_heads, preferred_element_type=jnp.float32
    )
    results = results + (
        jnp.concatenate(
            [grad_key.reshape(length, MODEL_WIDTH), grad_value.reshape(length, MODEL_WIDTH)],
            axis=-1,
        ),
    )
    return results


def local_general(
    content,
    query_stream,
    segment_ids,
    pad_mask,
    predicted,
    order,
    rel_bucket,
    qkv_weight,
    qv_bias,
    out_weight,
    out_bias,
    attn_gain,
    attn_shift,
    up_weight,
    up_bias,
    down_weight,
    down_bias,
    ffn_gain,
    ffn_shift,
    rel_table,
    content_cot,
    query_cot,
):
    seq_count = content.shape[0]
    shard_length = content.shape[1]
    pred_count = query_stream.shape[1]
    row_count = shard_length + pred_count
    group_size = lax.axis_size("seq")
    edges = bucket_edges(rel_bucket)
    shards = (
        lax.all_gather(qkv_weight, ("dp", "seq"), axis=0, tiled=True),
        lax.all_gather(out_weight, ("dp", "seq"), axis=0, tiled=True),
        lax.all_gather(up_weight, ("dp", "seq"), axis=0, tiled=True),
        lax.all_gather(down_weight, ("dp", "seq"), axis=0, tiled=True),
        lax.all_gather(qv_bias, ("dp", "seq"), axis=0, tiled=True),
        lax.all_gather(out_bias, ("dp", "seq"), axis=0, tiled=True),
        lax.all_gather(attn_gain, ("dp", "seq"), axis=0, tiled=True),
        lax.all_gather(attn_shift, ("dp", "seq"), axis=0, tiled=True),
        lax.all_gather(up_bias, ("dp", "seq"), axis=0, tiled=True),
        lax.all_gather(down_bias, ("dp", "seq"), axis=0, tiled=True),
        lax.all_gather(ffn_gain, ("dp", "seq"), axis=0, tiled=True),
        lax.all_gather(ffn_shift, ("dp", "seq"), axis=0, tiled=True),
    )
    query_key_value_weight, w_out, w_up, w_down = (shards[0], shards[1], shards[2], shards[3])
    bias_qv, bias_out, first_norm_gain, shift_one, bias_up, bias_down, gain_two, shift_two = [
        member.astype(jnp.float32) for member in shards[4:]
    ]
    all_rows = jnp.concatenate([content, query_stream], axis=1)
    reduced_precision_rows = all_rows.astype(jnp.bfloat16)
    queries = (
        jnp.einsum(
            "srd,de->sre",
            reduced_precision_rows,
            query_key_value_weight[:, :MODEL_WIDTH],
            preferred_element_type=jnp.float32,
        )
        + bias_qv[:MODEL_WIDTH]
    ).astype(jnp.bfloat16)
    value_shift = jnp.concatenate([jnp.zeros((MODEL_WIDTH,), jnp.float32), bias_qv[MODEL_WIDTH:]])
    key_values = (
        jnp.einsum(
            "zci,ip->zcp",
            reduced_precision_rows[:, :shard_length],
            query_key_value_weight[:, MODEL_WIDTH:],
            preferred_element_type=jnp.float32,
        )
        + value_shift
    ).astype(jnp.bfloat16)
    full_pairs, full_seg, full_order, full_pad = (
        lax.all_gather(key_values, "seq", axis=1, tiled=True),
        lax.all_gather(segment_ids, "seq", axis=1, tiled=True),
        lax.all_gather(order, "seq", axis=1, tiled=True),
        lax.all_gather(pad_mask, "seq", axis=1, tiled=True),
    )
    content_pos = lax.axis_index("seq") * shard_length + jnp.arange(shard_length, dtype=jnp.int32)
    query_pos = jnp.concatenate(
        [jnp.broadcast_to(content_pos[None, :], (seq_count, shard_length)), predicted], axis=1
    )
    query_seg = jnp.concatenate(
        [segment_ids, jnp.take_along_axis(full_seg, predicted, axis=1)], axis=1
    )
    query_limit = jnp.concatenate(
        [order, jnp.take_along_axis(full_order, predicted, axis=1) - 1], axis=1
    )
    content_row = jnp.arange(row_count, dtype=jnp.int32) < shard_length
    row_meta = (full_seg, full_order, full_pad, query_pos, query_seg, query_limit)

    def forward_one(packed):
        return attend_forward(packed, rel_table, edges, content_row)

    context, row_lse = lax.map(forward_one, (queries, full_pairs) + row_meta)
    context_low = context.astype(jnp.bfloat16)
    attn_out = (
        jnp.einsum("sre,ed->srd", context_low, w_out, preferred_element_type=jnp.float32) + bias_out
    )
    hidden_one, normed_one, inv_one = norm_fwd(all_rows + attn_out, first_norm_gain, shift_one)
    hidden_low = hidden_one.astype(jnp.bfloat16)
    pre_act = (
        jnp.einsum("srd,df->srf", hidden_low, w_up, preferred_element_type=jnp.float32) + bias_up
    )
    activ, gelu_pull = jax.vjp(exact_gelu, pre_act)
    activ_low = activ.astype(jnp.bfloat16)
    ffn_out = (
        jnp.einsum("srf,fd->srd", activ_low, w_down, preferred_element_type=jnp.float32) + bias_down
    )
    hidden_two, normed_two, inv_two = norm_fwd(hidden_one + ffn_out, gain_two, shift_two)
    pad_float = pad_mask.astype(jnp.float32)
    row_valid = jnp.concatenate(
        [pad_float, jnp.ones((seq_count, pred_count), jnp.float32)], axis=1
    )[..., None]
    outputs = hidden_two * row_valid
    pad_weight = pad_float[..., None]
    local_sums = jnp.stack(
        [
            jnp.sum(pad_weight * content * content),
            jnp.sum(query_stream * query_stream),
            jnp.sum(pad_weight * attn_out[:, :shard_length] * attn_out[:, :shard_length]),
            jnp.sum(attn_out[:, shard_length:] * attn_out[:, shard_length:]),
            jnp.sum(pad_weight * ffn_out[:, :shard_length] * ffn_out[:, :shard_length]),
            jnp.sum(ffn_out[:, shard_length:] * ffn_out[:, shard_length:]),
            jnp.sum(pad_float),
        ]
    )
    back_weights = (
        lax.all_gather(qkv_weight, ("dp", "seq"), axis=0, tiled=True),
        lax.all_gather(out_weight, ("dp", "seq"), axis=0, tiled=True),
        lax.all_gather(up_weight, ("dp", "seq"), axis=0, tiled=True),
        lax.all_gather(down_weight, ("dp", "seq"), axis=0, tiled=True),
        lax.all_gather(attn_gain, ("dp", "seq"), axis=0, tiled=True),
        lax.all_gather(ffn_gain, ("dp", "seq"), axis=0, tiled=True),
    )
    back_pairs = lax.all_gather(key_values, "seq", axis=1, tiled=True)
    backward_query_key_value, back_out, back_up, back_down = (
        back_weights[0],
        back_weights[1],
        back_weights[2],
        back_weights[3],
    )
    back_gain_one = back_weights[4].astype(jnp.float32)
    back_gain_two = back_weights[5].astype(jnp.float32)
    upstream = jnp.concatenate([content_cot, query_cot], axis=1) * row_valid
    grad_res_two, grad_gain_two, grad_shift_two = norm_back(
        upstream, normed_two, inv_two, back_gain_two
    )
    grad_ffn = grad_res_two.astype(jnp.bfloat16)
    grad_bias_down = jnp.sum(grad_ffn, axis=(0, 1), dtype=jnp.float32)
    grad_down = jnp.einsum("srf,srd->fd", activ_low, grad_ffn, preferred_element_type=jnp.float32)
    grad_activ = jnp.einsum("srd,fd->srf", grad_ffn, back_down, preferred_element_type=jnp.float32)
    grad_pre = gelu_pull(grad_activ)[0].astype(jnp.bfloat16)
    grad_bias_up = jnp.sum(grad_pre, axis=(0, 1), dtype=jnp.float32)
    grad_up = jnp.einsum("srd,srf->df", hidden_low, grad_pre, preferred_element_type=jnp.float32)
    grad_hidden = grad_res_two + jnp.einsum(
        "srf,df->srd", grad_pre, back_up, preferred_element_type=jnp.float32
    )
    grad_res_one, grad_gain_one, grad_shift_one = norm_back(
        grad_hidden, normed_one, inv_one, back_gain_one
    )
    grad_attn = grad_res_one.astype(jnp.bfloat16)
    grad_bias_out = jnp.sum(grad_attn, axis=(0, 1), dtype=jnp.float32)
    grad_out = jnp.einsum("sre,srd->ed", context_low, grad_attn, preferred_element_type=jnp.float32)
    grad_context = jnp.einsum(
        "srd,ed->sre", grad_attn, back_out, preferred_element_type=jnp.float32
    ).astype(jnp.bfloat16)

    def backward_all(packed):
        return attend_backward(packed, rel_table, edges, content_row)

    grad_queries, grad_tables, per_row_delta, grad_pairs = lax.map(
        backward_all, (queries, back_pairs) + row_meta + (row_lse, grad_context)
    )
    paired_gradients = lax.psum_scatter(
        grad_pairs.astype(jnp.bfloat16), "seq", scatter_dimension=1, tiled=True
    )
    query_grads = grad_queries.astype(jnp.bfloat16)
    grad_bias_qv = jnp.concatenate(
        [
            jnp.sum(query_grads, axis=(0, 1), dtype=jnp.float32),
            jnp.sum(paired_gradients[..., MODEL_WIDTH:], axis=(0, 1), dtype=jnp.float32),
        ]
    )
    grad_qkv = jnp.concatenate(
        [
            jnp.einsum(
                "srd,sre->de",
                reduced_precision_rows,
                query_grads,
                preferred_element_type=jnp.float32,
            ),
            jnp.einsum(
                "cvi,cvp->ip",
                reduced_precision_rows[:, :shard_length],
                paired_gradients,
                preferred_element_type=jnp.float32,
            ),
        ],
        axis=1,
    )
    grad_rows = grad_res_one + jnp.einsum(
        "sre,de->srd",
        query_grads,
        backward_query_key_value[:, :MODEL_WIDTH],
        preferred_element_type=jnp.float32,
    )
    grad_content = grad_rows[:, :shard_length] + jnp.einsum(
        "zwv,bv->zwb",
        paired_gradients,
        backward_query_key_value[:, MODEL_WIDTH:],
        preferred_element_type=jnp.float32,
    )
    grad_query = grad_rows[:, shard_length:]
    owned = (
        lax.psum_scatter(grad_qkv, ("dp", "seq"), scatter_dimension=0, tiled=True),
        lax.psum_scatter(grad_out, ("dp", "seq"), scatter_dimension=0, tiled=True),
        lax.psum_scatter(grad_up, ("dp", "seq"), scatter_dimension=0, tiled=True),
        lax.psum_scatter(grad_down, ("dp", "seq"), scatter_dimension=0, tiled=True),
        lax.psum_scatter(grad_bias_qv, ("dp", "seq"), scatter_dimension=0, tiled=True),
        lax.psum_scatter(grad_bias_out, ("dp", "seq"), scatter_dimension=0, tiled=True),
        lax.psum_scatter(grad_gain_one, ("dp", "seq"), scatter_dimension=0, tiled=True),
        lax.psum_scatter(grad_shift_one, ("dp", "seq"), scatter_dimension=0, tiled=True),
        lax.psum_scatter(grad_bias_up, ("dp", "seq"), scatter_dimension=0, tiled=True),
        lax.psum_scatter(grad_bias_down, ("dp", "seq"), scatter_dimension=0, tiled=True),
        lax.psum_scatter(grad_gain_two, ("dp", "seq"), scatter_dimension=0, tiled=True),
        lax.psum_scatter(grad_shift_two, ("dp", "seq"), scatter_dimension=0, tiled=True),
    )
    table_sum, totals = lax.psum((jnp.sum(grad_tables, axis=0), local_sums), ("dp", "seq"))
    content_count = totals[6] * MODEL_WIDTH
    query_count = float(seq_count * lax.axis_size("dp") * pred_count * group_size * MODEL_WIDTH)
    stats = jnp.sqrt(
        jnp.stack(
            [
                totals[0] / content_count,
                totals[1] / query_count,
                totals[2] / content_count,
                totals[3] / query_count,
                totals[4] / content_count,
                totals[5] / query_count,
            ]
        )
    )
    return (
        outputs[:, :shard_length],
        outputs[:, shard_length:],
        grad_content,
        grad_query,
        owned[0],
        owned[4],
        owned[1],
        owned[5],
        owned[6],
        owned[7],
        owned[2],
        owned[8],
        owned[3],
        owned[9],
        owned[10],
        owned[11],
        table_sum,
        stats,
    )


LOG2E = math.log2(math.e)
TILE = 256
HALF = 128
REACH = 9
DIAGS = 2 * REACH + 1
WIDE = SEQ_LEN + HALF
MASKED = -1e30
F32 = jnp.float32
BF16 = jnp.bfloat16


def cost_of(micros):
    return pl.CostEstimate(
        flops=int(micros * 1.0e9), bytes_accessed=int(micros * 1.0e6), transcendentals=0
    )


def bias_kernel(rows_q, own, rev_ref, fold_ref, hot_ref, shift_ref, tile_ref, qbias_ref):
    lane = lax.broadcasted_iota(jnp.int32, (HALF, HALF), 1)
    for h in range(own):
        for e in range(-REACH, REACH + 1):
            start = HALF * (15 - e)
            row = rev_ref[h : h + 1, start : start + 2 * HALF]
            skew = pltpu.roll(
                jnp.broadcast_to(row, (HALF, 2 * HALF)), 0, 1, stride=1, stride_axis=0
            )
            tile_ref[h, e + REACH] = skew[:, HALF:]
    for t in range(rows_q // HALF):
        shift = shift_ref[t * HALF : (t + 1) * HALF, :]
        place = lane + shift
        wrap = place >= HALF
        idx = jnp.where(wrap, place - HALF, place)
        for h in range(own):
            spread = jnp.dot(
                hot_ref[t * HALF : (t + 1) * HALF, :], fold_ref[h], preferred_element_type=F32
            )
            prev = jnp.take_along_axis(spread[:, :HALF], idx, axis=1)
            for j in range(SEQ_LEN // HALF):
                cur = jnp.take_along_axis(
                    spread[:, (j + 1) * HALF : (j + 2) * HALF], idx, axis=1
                )
                out = jnp.where(wrap, cur, prev) * LOG2E
                qbias_ref[h, j * HALF : (j + 1) * HALF, t * HALF : (t + 1) * HALF] = out.T
                prev = cur


def bias_call(rev, fold, hot, shift):
    own = rev.shape[0]
    rows_q = hot.shape[0]
    return pl.pallas_call(
        functools.partial(bias_kernel, rows_q, own),
        out_shape=(
            jax.ShapeDtypeStruct((own, DIAGS, HALF, HALF), F32),
            jax.ShapeDtypeStruct((own, SEQ_LEN, rows_q), F32),
        ),
        compiler_params=pltpu.CompilerParams(vmem_limit_bytes=50 << 20),
        cost_estimate=cost_of(14),
        name="bias_tiles",
    )(rev, fold, hot, shift)


def bias_block(tile_ref, h, e):
    mid = tile_ref[h, e]
    return jnp.concatenate(
        [
            jnp.concatenate([mid, tile_ref[h, e - 1]], axis=1),
            jnp.concatenate([tile_ref[h, e + 1], mid], axis=1),
        ],
        axis=0,
    )


def mask_block(kmeta_ref, rseg_ref, rlim_ref, krow, rcol, width):
    kseg = kmeta_ref[0, pl.ds(krow, TILE), :]
    kord = kmeta_ref[1, pl.ds(krow, TILE), :]
    parts = []
    for w in range(width // HALF):
        rseg = rseg_ref[:, pl.ds(rcol + w * HALF, HALF)]
        rlim = rlim_ref[:, pl.ds(rcol + w * HALF, HALF)]
        ok = (kseg == rseg) & (kord <= rlim)
        parts.append(jnp.where(ok, 0.0, MASKED))
    return parts[0] if len(parts) == 1 else jnp.concatenate(parts, axis=1)


def fwd_kernel(
    own,
    rows_q,
    span_ref,
    qt_ref,
    k_ref,
    vt_ref,
    kmeta_ref,
    rseg_ref,
    rlim_ref,
    tile_ref,
    qbias_ref,
    ctx_ref,
    rows_ref,
    lse_ref,
    s_scr,
):
    def run(rcol, width, lo, hi, bias_of):
        heads = range(own)

        def fold(op, x):
            rows = [x[i * 8 : (i + 1) * 8] for i in range(x.shape[0] // 8)]
            while len(rows) > 1:
                rows = [op(rows[i], rows[i + 1]) for i in range(0, len(rows), 2)]
            return rows[0]

        def score(kt, tops):
            krow = pl.multiple_of(kt * TILE, TILE)
            mask = mask_block(kmeta_ref, rseg_ref, rlim_ref, krow, rcol, width)
            new = []
            for h in heads:
                s = jnp.dot(
                    k_ref[h, pl.ds(krow, TILE), :],
                    qt_ref[h * HEAD_DIM : (h + 1) * HEAD_DIM, pl.ds(rcol, width)],
                    preferred_element_type=F32,
                )
                s = s * (SCALE * LOG2E) + (bias_of(h, kt) + mask)
                s_scr[h, pl.ds(krow, TILE), :width] = s
                new.append(jnp.maximum(tops[h], fold(jnp.maximum, s)))
            return tuple(new)

        tops = lax.fori_loop(
            lo, hi + 1, score, tuple(jnp.full((8, width), MASKED, F32) for _ in heads)
        )
        tops = [jnp.max(t, axis=0, keepdims=True) for t in tops]

        def weigh(kt, carry):
            krow = pl.multiple_of(kt * TILE, TILE)
            sums, accs = carry
            new_sums, new_accs = [], []
            for h in heads:
                p = jnp.exp2(s_scr[h, pl.ds(krow, TILE), :width] - tops[h])
                new_sums.append(sums[h] + fold(jnp.add, p))
                new_accs.append(
                    accs[h]
                    + jnp.dot(
                        vt_ref[h * HEAD_DIM : (h + 1) * HEAD_DIM, pl.ds(krow, TILE)],
                        p.astype(BF16),
                        preferred_element_type=F32,
                    )
                )
            return tuple(new_sums), tuple(new_accs)

        sums, accs = lax.fori_loop(
            lo,
            hi + 1,
            weigh,
            (
                tuple(jnp.zeros((8, width), F32) for _ in heads),
                tuple(jnp.zeros((HEAD_DIM, width), F32) for _ in heads),
            ),
        )
        outs = []
        for h in heads:
            total = jnp.sum(sums[h], axis=0, keepdims=True)
            outs.append(accs[h] / total)
            lse_ref[h : h + 1, pl.ds(rcol, width)] = tops[h] + jnp.log2(total)
        out = jnp.concatenate(outs, axis=0)
        ctx_ref[:, pl.ds(rcol, width)] = out.astype(BF16)
        rows_ref[pl.ds(rcol, width), :] = out.T.astype(BF16)

    def content_tile(qt, carry):
        def bias_of(h, kt):
            return bias_block(tile_ref, h, 2 * (kt - qt) + REACH)

        run(pl.multiple_of(qt * TILE, TILE), TILE, span_ref[0, qt], span_ref[1, qt], bias_of)
        return carry

    lax.fori_loop(0, SEQ_LEN // TILE, content_tile, 0)

    def query_tile(t, carry):
        col = pl.multiple_of(t * HALF, HALF)

        def bias_of(h, kt):
            return qbias_ref[h, pl.ds(pl.multiple_of(kt * TILE, TILE), TILE), pl.ds(col, HALF)]

        run(
            pl.multiple_of(SEQ_LEN + t * HALF, HALF),
            HALF,
            span_ref[0, SEQ_LEN // TILE],
            span_ref[1, SEQ_LEN // TILE],
            bias_of,
        )
        return carry

    lax.fori_loop(0, rows_q // HALF, query_tile, 0)


def fwd_call(span, qt, k3, vt, kmeta, rseg, rlim, tiles, qbias):
    own = k3.shape[0]
    rows = qt.shape[1]
    rows_q = rows - SEQ_LEN
    vm = pl.BlockSpec(memory_space=pltpu.VMEM)
    return pl.pallas_call(
        functools.partial(fwd_kernel, own, rows_q),
        out_shape=(
            jax.ShapeDtypeStruct((own * HEAD_DIM, rows), BF16),
            jax.ShapeDtypeStruct((rows, own * HEAD_DIM), BF16),
            jax.ShapeDtypeStruct((own, rows), F32),
        ),
        in_specs=[pl.BlockSpec(memory_space=pltpu.SMEM)] + [vm] * 8,
        scratch_shapes=[
            pltpu.VMEM((own, SEQ_LEN, TILE), F32),
        ],
        compiler_params=pltpu.CompilerParams(vmem_limit_bytes=56 << 20),
        cost_estimate=cost_of(32),
        name="attend",
    )(span, qt, k3, vt, kmeta, rseg, rlim, tiles, qbias)


def bwd_kernel(
    own,
    rows_q,
    span_ref,
    qt_ref,
    q_ref,
    k_ref,
    kt_ref,
    v_ref,
    ctx_ref,
    gc_ref,
    gq_ref,
    lse_ref,
    kmeta_ref,
    rseg_ref,
    rlim_ref,
    tile_ref,
    qbias_ref,
    hott_ref,
    shift_ref,
    dq_ref,
    dk_ref,
    dv_ref,
    offs_ref,
    qoffs_ref,
    dk_scr,
    dv_scr,
    dq_scr,
    diag_scr,
    ds_scr,
    delta_scr,
    gt_ref,
    g_ref,
):
    rows = gt_ref.shape[1]
    for a in range(0, rows, TILE):
        b = min(a + TILE, rows)
        if b <= SEQ_LEN:
            block = gc_ref[a:b, :].astype(F32)
        else:
            block = gq_ref[a - SEQ_LEN : min(b - SEQ_LEN, gq_ref.shape[0]), :].astype(F32)
            if block.shape[0] < b - a:
                block = jnp.concatenate(
                    [block, jnp.zeros((b - a - block.shape[0], block.shape[1]), F32)], axis=0
                )
        gt_ref[:, a:b] = block.T.astype(BF16)
        for h in range(own):
            g_ref[h, a:b, :] = block[:, h * HEAD_DIM : (h + 1) * HEAD_DIM].astype(BF16)
    dk_scr[...] = jnp.zeros(dk_scr.shape, F32)
    dv_scr[...] = jnp.zeros(dv_scr.shape, F32)
    diag_scr[...] = jnp.zeros(diag_scr.shape, F32)
    ds_scr[...] = jnp.zeros(ds_scr.shape, BF16)
    for h in range(own):
        part = slice(h * HEAD_DIM, (h + 1) * HEAD_DIM)
        delta_scr[h : h + 1, :] = jnp.sum(
            ctx_ref[part, :].astype(F32) * gt_ref[part, :].astype(F32), axis=0, keepdims=True
        )

    def run(rcol, width, lo, hi, bias_of, keep):
        dq_scr[...] = jnp.zeros(dq_scr.shape, F32)

        def body(kt, carry):
            krow = pl.multiple_of(kt * TILE, TILE)
            mask = mask_block(kmeta_ref, rseg_ref, rlim_ref, krow, rcol, width)
            for h in range(own):
                part = slice(h * HEAD_DIM, (h + 1) * HEAD_DIM)
                s = jnp.dot(
                    k_ref[h, pl.ds(krow, TILE), :],
                    qt_ref[part, pl.ds(rcol, width)],
                    preferred_element_type=F32,
                )
                s = s * (SCALE * LOG2E) + (bias_of(h, kt) + mask)
                p = jnp.exp2(s - lse_ref[h : h + 1, pl.ds(rcol, width)])
                gp = jnp.dot(
                    v_ref[h, pl.ds(krow, TILE), :],
                    gt_ref[part, pl.ds(rcol, width)],
                    preferred_element_type=F32,
                )
                ds = p * (gp - delta_scr[h : h + 1, pl.ds(rcol, width)])
                low = ds.astype(BF16)
                keep(h, kt, ds, low)
                dv_scr[h, pl.ds(krow, TILE), :] += jnp.dot(
                    p.astype(BF16), g_ref[h, pl.ds(rcol, width), :], preferred_element_type=F32
                )
                dk_scr[h, pl.ds(krow, TILE), :] += jnp.dot(
                    low, q_ref[h, pl.ds(rcol, width), :], preferred_element_type=F32
                )
                dq_scr[h, :, :width] += jnp.dot(
                    kt_ref[part, pl.ds(krow, TILE)], low, preferred_element_type=F32
                )
            return carry

        lax.fori_loop(lo, hi + 1, body, 0)
        grad = jnp.concatenate([dq_scr[h, :, :width] for h in range(own)], axis=0)
        dq_ref[pl.ds(rcol, width), :] = (grad * SCALE).T.astype(BF16)

    def content_tile(qt, carry):
        def bias_of(h, kt):
            return bias_block(tile_ref, h, 2 * (kt - qt) + REACH)

        def keep(h, kt, ds, low):
            e = 2 * (kt - qt) + REACH
            diag_scr[h, e] += ds[:HALF, :HALF] + ds[HALF:, HALF:]
            diag_scr[h, e - 1] += ds[:HALF, HALF:]
            diag_scr[h, e + 1] += ds[HALF:, :HALF]

        run(pl.multiple_of(qt * TILE, TILE), TILE, span_ref[0, qt], span_ref[1, qt], bias_of, keep)
        return carry

    lax.fori_loop(0, SEQ_LEN // TILE, content_tile, 0)

    def query_tile(t, carry):
        col = pl.multiple_of(t * HALF, HALF)

        def bias_of(h, kt):
            return qbias_ref[h, pl.ds(pl.multiple_of(kt * TILE, TILE), TILE), pl.ds(col, HALF)]

        def keep(h, kt, ds, low):
            ds_scr[h, pl.ds(pl.multiple_of(kt * TILE, TILE), TILE), pl.ds(col, HALF)] = low

        run(
            pl.multiple_of(SEQ_LEN + t * HALF, HALF),
            HALF,
            span_ref[0, SEQ_LEN // TILE],
            span_ref[1, SEQ_LEN // TILE],
            bias_of,
            keep,
        )
        return carry

    lax.fori_loop(0, rows_q // HALF, query_tile, 0)

    for a in range(0, SEQ_LEN, TILE):
        at = slice(a, a + TILE)
        for scr, ref, scale in ((dk_scr, dk_ref, SCALE), (dv_scr, dv_ref, 1.0)):
            block = jnp.concatenate([scr[h, at, :] for h in range(own)], axis=1)
            ref[at, :] = (block * scale).astype(BF16)

    offs_ref[...] = jnp.zeros(offs_ref.shape, F32)
    qoffs_ref[...] = jnp.zeros(qoffs_ref.shape, F32)
    lane = lax.broadcasted_iota(jnp.int32, (HALF, HALF), 1)
    turn = lane + lax.broadcasted_iota(jnp.int32, (HALF, HALF), 0)
    over = turn >= HALF
    turn = jnp.where(over, turn - HALF, turn)
    for h in range(own):
        for e in range(DIAGS):
            skew = jnp.take_along_axis(diag_scr[h, e], turn, axis=1)
            start = HALF * (15 - e + REACH)
            offs_ref[h : h + 1, start : start + HALF] += jnp.sum(
                jnp.where(over, skew, 0.0), axis=0, keepdims=True
            )
            offs_ref[h : h + 1, start + HALF : start + 2 * HALF] += jnp.sum(
                jnp.where(over, 0.0, skew), axis=0, keepdims=True
            )

    for h in range(own):
        total = jnp.zeros((16, WIDE), F32)
        for t in range(rows_q // HALF):
            shift = shift_ref[t * HALF : (t + 1) * HALF, :]
            place = lane - shift
            low_side = place < 0
            idx = jnp.where(low_side, place + HALF, place)
            prev = jnp.zeros((HALF, HALF), F32)
            pieces = []
            for j in range(SEQ_LEN // HALF + 1):
                if j < SEQ_LEN // HALF:
                    block = ds_scr[h, j * HALF : (j + 1) * HALF, t * HALF : (t + 1) * HALF]
                    cur = jnp.take_along_axis(block.astype(F32).T, idx, axis=1)
                else:
                    cur = jnp.zeros((HALF, HALF), F32)
                pieces.append(jnp.where(low_side, prev, cur).astype(BF16))
                prev = cur
            total += jnp.dot(
                hott_ref[:, t * HALF : (t + 1) * HALF],
                jnp.concatenate(pieces, axis=1),
                preferred_element_type=F32,
            )
        for i in range(16):
            qoffs_ref[h : h + 1, HALF * i : HALF * i + WIDE] += total[i : i + 1, :]


def bwd_call(
    span, qt, q3, k3, kt, v3, ctx, g_c, g_q, lse, kmeta, rseg, rlim, tiles, qbias, hott, shift
):
    own = k3.shape[0]
    rows = qt.shape[1]
    rows_q = rows - SEQ_LEN
    vm = pl.BlockSpec(memory_space=pltpu.VMEM)
    return pl.pallas_call(
        functools.partial(bwd_kernel, own, rows_q),
        out_shape=(
            jax.ShapeDtypeStruct((rows, own * HEAD_DIM), BF16),
            jax.ShapeDtypeStruct((SEQ_LEN, own * HEAD_DIM), BF16),
            jax.ShapeDtypeStruct((SEQ_LEN, own * HEAD_DIM), BF16),
            jax.ShapeDtypeStruct((own, 2 * SEQ_LEN), F32),
            jax.ShapeDtypeStruct((own, 2 * SEQ_LEN), F32),
        ),
        in_specs=[pl.BlockSpec(memory_space=pltpu.SMEM)] + [vm] * 16,
        scratch_shapes=[
            pltpu.VMEM((own, SEQ_LEN, HEAD_DIM), F32),
            pltpu.VMEM((own, SEQ_LEN, HEAD_DIM), F32),
            pltpu.VMEM((own, HEAD_DIM, TILE), F32),
            pltpu.VMEM((own, DIAGS, HALF, HALF), F32),
            pltpu.VMEM((own, SEQ_LEN, rows_q), BF16),
            pltpu.VMEM((own, rows), F32),
            pltpu.VMEM((own * HEAD_DIM, rows), BF16),
            pltpu.VMEM((own, rows, HEAD_DIM), BF16),
        ],
        compiler_params=pltpu.CompilerParams(vmem_limit_bytes=60 << 20),
        cost_estimate=cost_of(58),
        name="attend_back",
    )(span, qt, q3, k3, kt, v3, ctx, g_c, g_q, lse, kmeta, rseg, rlim, tiles, qbias, hott, shift)


def table_sums(offs, qoffs, rel_bucket):
    ids = jnp.arange(BUCKETS, dtype=jnp.int32)[:, None]
    back = jnp.pad(rel_bucket[::-1], (1, 0), constant_values=BUCKETS)
    ahead = jnp.pad(rel_bucket, (0, 1), constant_values=BUCKETS)
    high = lax.Precision.HIGHEST
    near = jnp.einsum("ho,bo->bh", offs, (back[None, :] == ids).astype(F32), precision=high)
    far = jnp.einsum("ho,bo->bh", qoffs, (ahead[None, :] == ids).astype(F32), precision=high)
    return near + far


def bias_inputs(rel_bucket, rel_table, first, own):
    hot = (rel_bucket[:, None] == jnp.arange(BUCKETS, dtype=jnp.int32)[None, :]).astype(BF16)
    part = lax.dynamic_slice_in_dim(rel_table, first, own, axis=1)
    vec = jnp.einsum("ob,bh->ho", hot, part, preferred_element_type=F32)
    rev = jnp.pad(vec[:, ::-1], ((0, 0), (1, 0))) * LOG2E
    low = jnp.pad(vec, ((0, 0), (0, 1))).astype(BF16)
    fold = jnp.stack([low[:, HALF * i : HALF * i + WIDE] for i in range(16)], axis=1)
    return rev, fold


def query_place(predicted, rows_q):
    a = predicted // HALF
    c = predicted - a * HALF
    pad = rows_q - predicted.shape[0]
    hot = ((15 - a)[:, None] == jnp.arange(16, dtype=jnp.int32)[None, :]).astype(BF16)
    hot = jnp.pad(hot, ((0, pad), (0, 0)))
    shift = jnp.pad(HALF - 1 - c, (0, pad))
    shift = jnp.broadcast_to(shift[:, None], (rows_q, HALF))
    return hot, hot.T, shift


def row_meta(segment, pad_mask, order, predicted, rows_q):
    length = segment.shape[0]
    pos = jnp.arange(length, dtype=jnp.int32)
    real = pad_mask == 1
    seg = jnp.where(real, segment, -2 - pos)
    hit = predicted[:, None] == pos[None, :]
    qseg = jnp.sum(jnp.where(hit, seg[None, :], 0), axis=1)
    qlim = jnp.sum(jnp.where(hit, order[None, :], 0), axis=1) - 1
    pad = rows_q - predicted.shape[0]
    qseg = jnp.pad(qseg, (0, pad), constant_values=-1)
    qlim = jnp.pad(qlim, (0, pad))
    rseg = jnp.concatenate([seg, qseg])[None, :]
    rlim = jnp.concatenate([order, qlim])[None, :]
    kmeta = jnp.broadcast_to(jnp.stack([seg, order])[:, :, None], (2, length, HALF))
    tiles = length // TILE
    head_seg = segment[::TILE]
    tail_seg = segment[TILE - 1 :: TILE]
    starts = jnp.sum((segment[None, :] < head_seg[:, None]).astype(jnp.int32), axis=1)
    own = jnp.arange(tiles, dtype=jnp.int32)
    lo = jnp.where(real[::TILE], starts // TILE, own)
    hi = jnp.where(real[TILE - 1 :: TILE], tail_seg // TILE, own)
    count = jnp.sum(pad_mask)
    lo = jnp.concatenate([lo, jnp.zeros((1,), jnp.int32)])
    hi = jnp.concatenate([hi, jnp.maximum(count - 1, 0)[None] // TILE])
    return rseg, rlim, kmeta, jnp.stack([lo, hi]).astype(jnp.int32)


ROW_CUTS = (0, 144, 288, 432, 592)
COLS = 768
FWD_BITS_UP = (16, 8, 4, 2)
FWD_BITS_DOWN = (16, 8, 2, 4)


def dot_nn(a, b):
    return jnp.dot(a, b, preferred_element_type=F32)


def dot_nt(a, b):
    return lax.dot_general(a, b, (((1,), (1,)), ((), ())), preferred_element_type=F32)


def dot_tn(a, b):
    return lax.dot_general(a, b, (((0,), (0,)), ((), ())), preferred_element_type=F32)


def place_of(j, bits):
    total = 0
    for n, bit in enumerate(bits):
        total += ((j >> n) & 1) * (bit // 2)
    return total


def mid_kernel(
    seqs,
    bits_up,
    bits_down,
    ctx_c,
    ctx_q,
    x_c,
    x_q,
    cot_c,
    cot_q,
    valid_ref,
    uo_own,
    uo_mate,
    down_own,
    down_mate,
    bias_out,
    gain_one,
    shift_one,
    bias_up,
    bias_down,
    gain_two,
    shift_two,
    out_c,
    out_q,
    res_c,
    res_q,
    gctx_c,
    gctx_q,
    uo_keep,
    uo_give,
    down_keep,
    down_give,
    vec_ref,
    sums_ref,
    w_up,
    w_out,
    w_down,
    ctx_scr,
    one_scr,
    norm_scr,
    inv_scr,
    low_scr,
    act_scr,
    slope_scr,
    sum_scr,
    grad_scr,
    pre_scr,
    part_scr,
    plane_scr,
    sems,
    plane_sems,
):
    core = lax.rem(lax.axis_index("seq"), 2)
    chips, shard = uo_own.shape[0], uo_own.shape[1]
    shard_down = down_own.shape[1]
    length = x_c.shape[0]
    ff = w_up.shape[1]
    copies = []
    for j in range(chips):
        chip = place_of(j, bits_down)
        for side, ref in ((core, down_own), (1 - core, down_mate)):
            row = pl.multiple_of((2 * chip + side) * shard_down, 16)
            copies.append(
                pltpu.make_async_copy(
                    ref.at[j], w_down.at[pl.ds(row, shard_down)], sems.at[len(copies)]
                )
            )
    for copy in copies:
        copy.start()

    def plane_copies(chunk):
        slot = chunk % 2
        cols = pl.ds(chunk * COLS, COLS)
        return [
            pltpu.make_async_copy(
                ref.at[:, :, cols], plane_scr.at[slot, n], plane_sems.at[slot, n]
            )
            for n, ref in enumerate((uo_own, uo_mate))
        ]

    chunks = ff // COLS + 1
    waiting = plane_copies(0)
    for copy in waiting:
        copy.start()
    for chunk in range(chunks):
        for copy in waiting:
            copy.wait()
        if chunk + 1 < chunks:
            waiting = plane_copies(chunk + 1)
            for copy in waiting:
                copy.start()
        slot = chunk % 2

        def assemble(j, carry, chunk=chunk, slot=slot):
            chip = place_of(j, bits_up)
            first = plane_scr[slot, core, j].astype(F32)
            second = plane_scr[slot, 1 - core, j].astype(F32)
            pair = jnp.concatenate([first, second], axis=0).astype(BF16)
            rows = pl.ds(pl.multiple_of(2 * shard * chip, 16), 2 * shard)
            if chunk < ff // COLS:
                w_up[rows, chunk * COLS : (chunk + 1) * COLS] = pair
            else:
                w_out[rows, :] = pair
            return carry

        lax.fori_loop(0, chips, assemble, 0)

    wide = ctx_c.shape[2]
    for t in range(seqs):
        ctx_scr[t, :length, :] = ctx_c[t]
        ctx_scr[t, length:, :] = ctx_q[t]
    blocks = list(zip(ROW_CUTS[:-1], ROW_CUTS[1:]))

    def pick(ref_c, ref_q, a, b):
        if b <= length:
            return ref_c[a:b, :]
        return jnp.concatenate([ref_c[a:length, :], ref_q[: b - length, :]], axis=0)

    def put(ref_c, ref_q, a, b, value):
        if b <= length:
            ref_c[a:b, :] = value
        else:
            ref_c[a:length, :] = value[: length - a]
            ref_q[: b - length, :] = value[length - a :][: ref_q.shape[0]]

    def norm(x):
        mean = jnp.mean(x, axis=-1, keepdims=True)
        centered = x - mean
        inv = lax.rsqrt(jnp.mean(centered * centered, axis=-1, keepdims=True) + EPS)
        return centered * inv, inv

    def norm_grad(up, normed, inv, gain):
        grad = up * gain
        proj = jnp.mean(grad, axis=-1, keepdims=True) + normed * jnp.mean(
            grad * normed, axis=-1, keepdims=True
        )
        return inv * (grad - proj)

    sums_ref[...] = jnp.zeros(sums_ref.shape, F32)
    vec_ref[...] = jnp.zeros(vec_ref.shape, F32)

    def count_in(k, x, a, b):
        ok = valid_ref[a:b, :1]
        sq = x * x * ok
        n = min(b, length) - a
        sums_ref[k : k + 1, :] += jnp.sum(sq[:n], axis=0, keepdims=True)
        if b > length:
            sums_ref[k + 1 : k + 2, :] += jnp.sum(sq[n:], axis=0, keepdims=True)

    for a, b in blocks:
        attn = bias_out[...] + dot_nn(ctx_scr[0, a:b, :], w_out[:wide, :])
        for t in range(1, seqs):
            attn += dot_nn(ctx_scr[t, a:b, :], w_out[t * wide : (t + 1) * wide, :])
        x = pick(x_c, x_q, a, b)
        count_in(0, x, a, b)
        count_in(2, attn, a, b)
        normed, inv = norm(x + attn)
        one = normed * gain_one[...] + shift_one[...]
        norm_scr[a:b, :] = normed
        inv_scr[a:b, :] = jnp.broadcast_to(inv, (b - a, 128))
        one_scr[a:b, :] = one
        low_scr[a:b, :] = one.astype(BF16)

    for copy in copies:
        copy.wait()
    sum_scr[...] = jnp.zeros(sum_scr.shape, F32)

    def up_step(i, carry):
        cols = pl.ds(pl.multiple_of(i * COLS, COLS), COLS)
        for a, b in blocks:
            u = dot_nn(low_scr[a:b, :], w_up[:, cols]) + bias_up[:, cols]
            cdf = 0.5 * (1.0 + lax.erf(u * math.sqrt(0.5)))
            act = (u * cdf).astype(BF16)
            act_scr[a:b, cols] = act
            slope_scr[a:b, cols] = cdf + u * (
                jnp.exp(-0.5 * u * u) * (1.0 / math.sqrt(2.0 * math.pi))
            )
            sum_scr[a:b, :] += dot_nn(act, w_down[cols, :])
        return carry

    lax.fori_loop(0, ff // COLS, up_step, 0)

    for a, b in blocks:
        ffn = sum_scr[a:b, :] + bias_down[...]
        count_in(4, ffn, a, b)
        normed, inv = norm(one_scr[a:b, :] + ffn)
        ok = valid_ref[a:b, :1]
        put(out_c, out_q, a, b, (normed * gain_two[...] + shift_two[...]) * ok)
        up = pick(cot_c, cot_q, a, b) * ok
        vec_ref[4:5, :COLS] += jnp.sum(up * normed, axis=0, keepdims=True)
        vec_ref[5:6, :COLS] += jnp.sum(up, axis=0, keepdims=True)
        grad = norm_grad(up, normed, inv, gain_two[...])
        low = grad.astype(BF16)
        vec_ref[3:4, :COLS] += jnp.sum(low.astype(F32), axis=0, keepdims=True)
        sum_scr[a:b, :] = grad
        grad_scr[a:b, :] = low

    def hand_out(keep, give, value, size, width):
        part_scr[: value.shape[0], :] = value

        def body(j, carry):
            mine = pl.multiple_of((2 * j + core) * size, 8)
            other = pl.multiple_of((2 * j + 1 - core) * size, 8)
            keep(j, part_scr[pl.ds(mine, size), :].astype(BF16))
            give(j, part_scr[pl.ds(other, size), :].astype(BF16))
            return carry

        lax.fori_loop(0, value.shape[0] // (2 * size), body, 0)

    def back_step(i, carry):
        cols = pl.ds(pl.multiple_of(i * COLS, COLS), COLS)
        for a, b in blocks:
            low = (
                dot_nt(grad_scr[a:b, :], w_down[cols, :]) * slope_scr[a:b, cols]
            ).astype(BF16)
            pre_scr[a:b, :] = low
            vec_ref[2:3, cols] += jnp.sum(low.astype(F32), axis=0, keepdims=True)
            sum_scr[a:b, :] += dot_nt(low, w_up[:, cols])

        def keep_up(j, v):
            uo_keep[j, :, cols] = v

        def give_up(j, v):
            uo_give[j, :, cols] = v

        hand_out(keep_up, give_up, dot_tn(low_scr[...], pre_scr[...]), shard, COLS)
        per = COLS // (2 * shard_down)

        def keep_down(j, v):
            down_keep[i * per + j] = v

        def give_down(j, v):
            down_give[i * per + j] = v

        hand_out(keep_down, give_down, dot_tn(act_scr[:, cols], grad_scr[...]), shard_down, COLS)
        return carry

    lax.fori_loop(0, ff // COLS, back_step, 0)

    for a, b in blocks:
        up = sum_scr[a:b, :]
        normed = norm_scr[a:b, :]
        vec_ref[0:1, :COLS] += jnp.sum(up * normed, axis=0, keepdims=True)
        vec_ref[1:2, :COLS] += jnp.sum(up, axis=0, keepdims=True)
        grad = norm_grad(up, normed, inv_scr[a:b, :1], gain_one[...])
        low = grad.astype(BF16)
        vec_ref[6:7, :COLS] += jnp.sum(low.astype(F32), axis=0, keepdims=True)
        put(res_c, res_q, a, b, grad)
        grad_scr[a:b, :] = low
    low = grad_scr[...]
    tail = slice(ff, ff + COLS)
    for t in range(seqs):
        part = w_out[t * wide : (t + 1) * wide, :]
        gctx = dot_nt(low, part).astype(BF16)
        gctx_c[t] = gctx[:length]
        gctx_q[t] = gctx[length:]
        per = wide // (2 * shard)

        def keep_out(j, v, t=t):
            uo_keep[t * per + j, :, tail] = v

        def give_out(j, v, t=t):
            uo_give[t * per + j, :, tail] = v

        hand_out(keep_out, give_out, dot_tn(ctx_scr[t], low), shard, COLS)


def mid_call(ctx_c, ctx_q, x_c, x_q, cot_c, cot_q, valid, planes, vectors):
    seqs, length, wide = ctx_c.shape
    total = length + ctx_q.shape[1]
    uo_own, uo_mate, down_own, down_mate = planes
    chips, shard, cols = uo_own.shape
    shard_down = down_own.shape[1]
    ff = cols - COLS
    vm = pl.BlockSpec(memory_space=pltpu.VMEM)
    hbm = pl.BlockSpec(memory_space=pl.ANY)
    plane = jax.ShapeDtypeStruct((chips, shard, cols), BF16)
    plane_down = jax.ShapeDtypeStruct((chips, shard_down, COLS), BF16)
    return pl.pallas_call(
        functools.partial(mid_kernel, seqs, FWD_BITS_UP, FWD_BITS_DOWN),
        out_shape=(
            jax.ShapeDtypeStruct(x_c.shape, F32),
            jax.ShapeDtypeStruct(x_q.shape, F32),
            jax.ShapeDtypeStruct(x_c.shape, F32),
            jax.ShapeDtypeStruct(x_q.shape, F32),
            jax.ShapeDtypeStruct(ctx_c.shape, BF16),
            jax.ShapeDtypeStruct(ctx_q.shape, BF16),
            plane,
            plane,
            plane_down,
            plane_down,
            jax.ShapeDtypeStruct((8, ff), F32),
            jax.ShapeDtypeStruct((8, COLS), F32),
        ),
        in_specs=[vm] * 7 + [hbm] * 4 + [vm] * 7,
        out_specs=(vm,) * 12,
        scratch_shapes=[
            pltpu.VMEM((COLS, ff), BF16),
            pltpu.VMEM((COLS, COLS), BF16),
            pltpu.VMEM((ff, COLS), BF16),
            pltpu.VMEM((seqs, total, wide), BF16),
            pltpu.VMEM((total, COLS), F32),
            pltpu.VMEM((total, COLS), F32),
            pltpu.VMEM((total, 128), F32),
            pltpu.VMEM((total, COLS), BF16),
            pltpu.VMEM((total, ff), BF16),
            pltpu.VMEM((total, ff), F32),
            pltpu.VMEM((total, COLS), F32),
            pltpu.VMEM((total, COLS), BF16),
            pltpu.VMEM((total, COLS), BF16),
            pltpu.VMEM((COLS, COLS), F32),
            pltpu.VMEM((2, 2, chips, shard, COLS), BF16),
            pltpu.SemaphoreType.DMA((2 * chips,)),
            pltpu.SemaphoreType.DMA((2, 2)),
        ],
        compiler_params=pltpu.CompilerParams(vmem_limit_bytes=62 << 20),
        cost_estimate=cost_of(50),
        name="feed_forward",
    )(ctx_c, ctx_q, x_c, x_q, cot_c, cot_q, valid, *planes, *vectors)


def proj_kernel(own, keys, x_ref, w_ref, bq_ref, bv_ref, qt_ref, q_ref, k_ref, kt_ref, v_ref, vt_ref):
    wide = own * HEAD_DIM
    rows = x_ref.shape[0]
    for a in range(0, rows, 256):
        b = min(a + 256, rows)
        parts = [(0, bq_ref, qt_ref, q_ref)]
        if b <= keys:
            parts += [(1, None, kt_ref, k_ref), (2, bv_ref, vt_ref, v_ref)]
        y = dot_nn(x_ref[a:b, :], w_ref[:, : len(parts) * wide])
        for n, bias, flat_ref, head_ref in parts:
            part = y[:, n * wide : (n + 1) * wide]
            if bias is not None:
                part = part + bias[...]
            flat_ref[:, a:b] = part.T.astype(BF16)
            for h in range(own):
                head_ref[h, a:b, :] = part[:, h * HEAD_DIM : (h + 1) * HEAD_DIM].astype(BF16)


def proj_call(own, keys, x, w, bq, bv):
    rows = x.shape[0]
    wide = own * HEAD_DIM
    vm = pl.BlockSpec(memory_space=pltpu.VMEM)
    flat = lambda n: jax.ShapeDtypeStruct((wide, n), BF16)
    head = lambda n: jax.ShapeDtypeStruct((own, n, HEAD_DIM), BF16)
    return pl.pallas_call(
        functools.partial(proj_kernel, own, keys),
        out_shape=(flat(rows), head(rows), head(keys), flat(keys), head(keys), flat(keys)),
        in_specs=[vm] * 4,
        out_specs=(vm,) * 6,
        compiler_params=pltpu.CompilerParams(vmem_limit_bytes=40 << 20),
        cost_estimate=cost_of(5),
        name="project",
    )(x, w, bq, bv)


def grads_kernel(
    keys,
    x_ref,
    w_ref,
    dq_ref,
    dk_ref,
    dv_ref,
    gc_ref,
    gq_ref,
    gw_ref,
    sum_ref,
    part_scr,
):
    wide = dq_ref.shape[1]
    seqs, length = gc_ref.shape[:2]
    shard = gw_ref.shape[2]
    for n, ref in enumerate((dq_ref, dk_ref, dv_ref)):
        part_scr[...] = dot_tn(x_ref[: ref.shape[0], :], ref[...])
        for j in range(gw_ref.shape[0]):
            gw_ref[j, n] = part_scr[j * shard : (j + 1) * shard, :].astype(BF16)
    sum_ref[...] = jnp.zeros(sum_ref.shape, F32)
    sum_ref[0:1, :] = jnp.sum(dq_ref[...].astype(F32), axis=0, keepdims=True)
    sum_ref[1:2, :] = jnp.sum(dv_ref[...].astype(F32), axis=0, keepdims=True)
    w_q = w_ref[:, :wide]
    w_k = w_ref[:, wide : 2 * wide]
    w_v = w_ref[:, 2 * wide :]
    step = 256
    for t in range(seqs):
        for a in range(0, length, step):
            at = slice(t * length + a, t * length + a + step)
            gc_ref[t, a : a + step, :] = (
                dot_nt(dq_ref[at, :], w_q) + dot_nt(dk_ref[at, :], w_k) + dot_nt(dv_ref[at, :], w_v)
            ).astype(BF16)
    count = gq_ref.shape[1]
    for t in range(seqs):
        at = slice(keys + t * count, keys + (t + 1) * count)
        gq_ref[t] = dot_nt(dq_ref[at, :], w_q).astype(BF16)


def grads_call(seqs, length, count, blocks, x, w, dq, dk, dv):
    wide = dq.shape[1]
    shard = x.shape[1] // blocks
    vm = pl.BlockSpec(memory_space=pltpu.VMEM)
    return pl.pallas_call(
        functools.partial(grads_kernel, seqs * length),
        out_shape=(
            jax.ShapeDtypeStruct((seqs, length, x.shape[1]), BF16),
            jax.ShapeDtypeStruct((seqs, count, x.shape[1]), BF16),
            jax.ShapeDtypeStruct((blocks, 3, shard, wide), BF16),
            jax.ShapeDtypeStruct((8, wide), F32),
        ),
        in_specs=[vm] * 5,
        out_specs=(vm,) * 4,
        scratch_shapes=[pltpu.VMEM((x.shape[1], wide), F32)],
        compiler_params=pltpu.CompilerParams(vmem_limit_bytes=40 << 20),
        cost_estimate=cost_of(6),
        name="weight_grads",
    )(x, w, dq, dk, dv)


MESH = pl.DeviceIdType.MESH
ROWS_Q = 384
SLOT_Q = 80
VEC_PARTS = (48, 24, 24, 24, 96, 24, 24, 24)


def signal_peers(dp, s, dps, seqs):
    barrier = pltpu.get_barrier_semaphore()
    for r in range(1, dps):
        pl.semaphore_signal(
            barrier, inc=1, device_id=(lax.rem(dp + r, dps), s), device_id_type=MESH
        )
    for r in range(1, seqs):
        pl.semaphore_signal(
            barrier, inc=1, device_id=(dp, lax.rem(s + r, seqs)), device_id_type=MESH
        )
    pl.semaphore_wait(barrier, dps - 1 + seqs - 1)


def remote(src, dst, send_sem, recv_sem, k, device):
    return pltpu.make_async_remote_copy(
        src_ref=src,
        dst_ref=dst,
        send_sem=send_sem.at[k],
        recv_sem=recv_sem.at[k],
        device_id=device,
        device_id_type=MESH,
    )


def start_kernel(
    dps,
    seqs,
    rc_ref,
    rq_ref,
    zero_ref,
    w_ref,
    v_ref,
    i_ref,
    x_out,
    w_out,
    v_out,
    i_out,
    send_sem,
    recv_sem,
    here_sem,
):
    dp = lax.axis_index("dp")
    s = lax.axis_index("seq")
    length = rc_ref.shape[0]
    count = rq_ref.shape[0]
    mate = s + 1 - 2 * lax.rem(s, 2)
    across = lax.rem(s + 2, seqs)
    signal_peers(dp, s, dps, seqs)

    def spot_c(owner):
        return x_out.at[pl.ds(pl.multiple_of(owner * length, length), length)]

    def spot_q(owner):
        start = seqs * length + owner * count
        return x_out.at[pl.ds(pl.multiple_of(start, 16), count)]

    k = 0
    small = []
    for r in range(1, seqs):
        to = lax.rem(s + r, seqs)
        for src, dst in (
            (w_ref.at[to], w_out.at[dp, s]),
            (v_ref, v_out.at[dp, s]),
            (i_ref, i_out.at[s]),
        ):
            small.append(remote(src, dst, send_sem, recv_sem, k, (dp, to)))
            k += 1
    for copy in small:
        copy.start()
    near, far = [], []
    for src, spot in ((rc_ref, spot_c), (rq_ref, spot_q)):
        far.append(remote(src, spot(s), send_sem, recv_sem, k, (dp, across)))
        near.append(remote(src, spot(s), send_sem, recv_sem, k + 1, (dp, mate)))
        k += 2
    for copy in far + near:
        copy.start()
    here = [
        pltpu.make_async_copy(w_ref.at[s], w_out.at[dp, s], here_sem.at[0]),
        pltpu.make_async_copy(v_ref, v_out.at[dp, s], here_sem.at[1]),
        pltpu.make_async_copy(i_ref, i_out.at[s], here_sem.at[2]),
        pltpu.make_async_copy(rc_ref, spot_c(s), here_sem.at[3]),
        pltpu.make_async_copy(rq_ref, spot_q(s), here_sem.at[4]),
        pltpu.make_async_copy(
            zero_ref,
            x_out.at[pl.ds(seqs * (length + count), zero_ref.shape[0])],
            here_sem.at[5],
        ),
    ]
    for copy in here:
        copy.start()
    for copy in small:
        copy.wait_recv()
    for copy in here:
        copy.wait()
    wide = []
    for r in range(1, dps):
        to = lax.rem(dp + r, dps)
        for ref in (w_out, v_out):
            wide.append(remote(ref.at[dp], ref.at[dp], send_sem, recv_sem, k, (to, s)))
            k += 1
    for copy in wide:
        copy.start()
    pass_on = []
    for copy, spot in zip(far, (spot_c, spot_q)):
        copy.wait_recv()
        pass_on.append(
            remote(spot(across), spot(across), send_sem, recv_sem, k, (dp, mate))
        )
        pass_on[-1].start()
        k += 1
    for copy in small + far:
        copy.wait_send()
    for copy in near + wide + pass_on:
        copy.wait()


def start_call(dps, seqs, rc, rq, w, v, ints):
    copies = 3 * (seqs - 1) + 4 + 2 * (dps - 1) + 2
    zero = jnp.zeros((ROWS_Q - seqs * rq.shape[0], rc.shape[1]), BF16)
    rows = seqs * rc.shape[0] + ROWS_Q
    vmem = pl.BlockSpec(memory_space=pltpu.VMEM)
    return pl.pallas_call(
        functools.partial(start_kernel, dps, seqs),
        out_shape=(
            jax.ShapeDtypeStruct((rows, rc.shape[1]), BF16),
            jax.ShapeDtypeStruct((dps,) + w.shape, BF16),
            jax.ShapeDtypeStruct((dps, seqs) + v.shape, F32),
            jax.ShapeDtypeStruct((seqs,) + ints.shape, jnp.int32),
        ),
        in_specs=[vmem] * 6,
        out_specs=(vmem,) * 4,
        scratch_shapes=[
            pltpu.SemaphoreType.DMA((copies,)),
            pltpu.SemaphoreType.DMA((copies,)),
            pltpu.SemaphoreType.DMA((6,)),
        ],
        compiler_params=pltpu.CompilerParams(collective_id=0, has_side_effects=True),
        cost_estimate=cost_of(35),
        name="gather_rows",
    )(rc, rq, zero, w, v, ints)


def swap_kernel(seqs, c_of, q_of, c_ref, q_ref, c_out, q_out, send_sem, recv_sem, here_sem):
    dp = lax.axis_index("dp")
    s = lax.axis_index("seq")
    signal_peers(dp, s, 1, seqs)
    copies = []
    for r in range(1, seqs):
        to = lax.rem(s + r, seqs)
        k = 2 * (r - 1)
        copies.append(remote(c_of(c_ref, to), c_out.at[s], send_sem, recv_sem, k, (dp, to)))
        copies.append(remote(q_of(q_ref, to), q_out.at[s], send_sem, recv_sem, k + 1, (dp, to)))
    for copy in copies:
        copy.start()
    here = [
        pltpu.make_async_copy(c_of(c_ref, s), c_out.at[s], here_sem.at[0]),
        pltpu.make_async_copy(q_of(q_ref, s), q_out.at[s], here_sem.at[1]),
    ]
    for copy in here:
        copy.start()
    for copy in here + copies:
        copy.wait()


def swap_call(seqs, c, q, c_of, q_of, c_shape, q_shape, ident, name):
    vmem = pl.BlockSpec(memory_space=pltpu.VMEM)
    return pl.pallas_call(
        functools.partial(swap_kernel, seqs, c_of, q_of),
        out_shape=(
            jax.ShapeDtypeStruct((seqs,) + c_shape, c.dtype),
            jax.ShapeDtypeStruct((seqs,) + q_shape, q.dtype),
        ),
        in_specs=[vmem] * 2,
        out_specs=(vmem,) * 2,
        scratch_shapes=[
            pltpu.SemaphoreType.DMA((2 * (seqs - 1),)),
            pltpu.SemaphoreType.DMA((2 * (seqs - 1),)),
            pltpu.SemaphoreType.DMA((2,)),
        ],
        compiler_params=pltpu.CompilerParams(collective_id=ident, has_side_effects=True),
        cost_estimate=cost_of(12),
        name=name,
    )(c, q)


def end_kernel(
    dps,
    seqs,
    gc_ref,
    gq_ref,
    w_ref,
    v_ref,
    gc_out,
    gq_out,
    w_out,
    v_out,
    c_mate,
    q_mate,
    c_far,
    q_far,
    c_send,
    q_send,
    w_got,
    v_got,
    w_sum,
    v_sum,
    v_last,
    send_sem,
    recv_sem,
):
    dp = lax.axis_index("dp")
    s = lax.axis_index("seq")
    core = lax.rem(s, 2)
    mate = s + 1 - 2 * core
    across = lax.rem(s + 2, seqs)
    signal_peers(dp, s, dps, seqs)
    k = 0
    first = []
    for i in range(2):
        to = lax.rem(mate + 2 * (1 - i), seqs)
        for src, dst in ((gc_ref, c_mate), (gq_ref, q_mate)):
            first.append(remote(src.at[to], dst.at[i], send_sem, recv_sem, k, (dp, mate)))
            k += 1
    wide = []
    for r in range(1, dps):
        to = lax.rem(dp + r, dps)
        for src, dst in ((w_ref, w_got), (v_ref, v_got)):
            wide.append(remote(src.at[to], dst.at[r - 1], send_sem, recv_sem, k, (to, s)))
            k += 1
    for copy in first + wide:
        copy.start()

    def each(ref, step, fn):
        def body(i, carry):
            fn(pl.ds(pl.multiple_of(i * step, step), step))
            return carry

        lax.fori_loop(0, ref.shape[-2] // step, body, 0)

    cross = []
    for (src, got, buf, far, copy) in (
        (gc_ref, c_mate, c_send, c_far, first[0]),
        (gq_ref, q_mate, q_send, q_far, first[1]),
    ):
        copy.wait_recv()

        def add(rows, src=src, got=got, buf=buf):
            buf[rows, :] = (
                src[across, rows, :].astype(F32) + got[0, rows, :].astype(F32)
            ).astype(BF16)

        each(buf, 16, add)
        cross.append(remote(buf, far, send_sem, recv_sem, k, (dp, across)))
        cross[-1].start()
        k += 1
    for copy in wide:
        copy.wait_recv()

    def add_w(rows):
        for t in range(seqs):
            total = w_ref[dp, t, rows, :].astype(F32)
            for r in range(1, dps):
                total += w_got[r - 1, t, rows, :].astype(F32)
            w_sum[t, rows, :] = total

    each(w_sum, 8, add_w)
    total = v_ref[dp]
    for r in range(1, dps):
        total += v_got[r - 1]
    v_sum[...] = total
    last = []
    for r in range(1, seqs):
        to = lax.rem(s + r, seqs)
        last.append(remote(w_sum.at[to], w_out.at[s], send_sem, recv_sem, k, (dp, to)))
        last.append(remote(v_sum.at[to], v_last.at[r - 1], send_sem, recv_sem, k + 1, (dp, to)))
        k += 2
    for copy in last:
        copy.start()
    w_out[s] = w_sum[s]
    for copy in first[2:]:
        copy.wait_recv()
    for copy in cross:
        copy.wait_recv()
    for (src, got, far, out) in (
        (gc_ref, c_mate, c_far, gc_out),
        (gq_ref, q_mate, q_far, gq_out),
    ):

        def total_of(rows, src=src, got=got, far=far, out=out):
            out[rows, :] = (
                src[s, rows, :].astype(F32)
                + got[1, rows, :].astype(F32)
                + far[rows, :].astype(F32)
            )

        each(out, 16, total_of)
    for copy in last:
        copy.wait_recv()
    total = v_sum[s]
    for r in range(1, seqs):
        total += v_last[r - 1]
    v_out[...] = total
    for copy in first + wide + cross + last:
        copy.wait_send()


def end_call(dps, seqs, gc, gq, w, v):
    copies = 4 + 2 * (dps - 1) + 2 + 2 * (seqs - 1)
    vm = pl.BlockSpec(memory_space=pltpu.VMEM)
    cshape, qshape, wshape, vshape = gc.shape[1:], gq.shape[1:], w.shape[1:], v.shape[1:]
    return pl.pallas_call(
        functools.partial(end_kernel, dps, seqs),
        out_shape=(
            jax.ShapeDtypeStruct(cshape, F32),
            jax.ShapeDtypeStruct(qshape, F32),
            jax.ShapeDtypeStruct(wshape, F32),
            jax.ShapeDtypeStruct(vshape[1:], F32),
        ),
        in_specs=[vm] * 4,
        out_specs=(vm,) * 4,
        scratch_shapes=[
            pltpu.VMEM((2,) + cshape, BF16),
            pltpu.VMEM((2,) + qshape, BF16),
            pltpu.VMEM(cshape, BF16),
            pltpu.VMEM(qshape, BF16),
            pltpu.VMEM(cshape, BF16),
            pltpu.VMEM(qshape, BF16),
            pltpu.VMEM((dps - 1,) + wshape, BF16),
            pltpu.VMEM((dps - 1,) + vshape, F32),
            pltpu.VMEM(wshape, F32),
            pltpu.VMEM(vshape, F32),
            pltpu.VMEM((seqs - 1,) + vshape[1:], F32),
            pltpu.SemaphoreType.DMA((copies,)),
            pltpu.SemaphoreType.DMA((copies,)),
        ],
        compiler_params=pltpu.CompilerParams(
            collective_id=3, has_side_effects=True, vmem_limit_bytes=50 << 20
        ),
        cost_estimate=cost_of(30),
        name="sum_rows",
    )(gc, gq, w, v)


def flip_perm(count, bit):
    return [(i, i ^ bit) for i in range(count)]


AXES = ("dp", "seq")


def tie(values, *others):
    return lax.optimization_barrier((values, others))[0]


def give_to(cur, count, bit):
    return lax.ppermute(cur, AXES, flip_perm(count, bit))


def pile(cur, got, bit):
    mine = (lax.axis_index(AXES) // bit) % 2
    return jnp.where(mine == 0, jnp.concatenate([cur, got]), jnp.concatenate([got, cur]))


def halves(cur, bit, left):
    axis = left.index(bit)
    mine = (lax.axis_index(AXES) // bit) % 2
    give = lax.dynamic_index_in_dim(cur, 1 - mine, axis, keepdims=False).astype(BF16)
    stay = lax.dynamic_index_in_dim(cur, mine, axis, keepdims=False)
    return give, stay


def local_fast(
    content,
    query_stream,
    segment_ids,
    pad_mask,
    predicted,
    order,
    rel_bucket,
    qkv_weight,
    qv_bias,
    out_weight,
    out_bias,
    attn_gain,
    attn_shift,
    up_weight,
    up_bias,
    down_weight,
    down_bias,
    ffn_gain,
    ffn_shift,
    rel_table,
    content_cot,
    query_cot,
):
    dps, seqs = lax.axis_size("dp"), lax.axis_size("seq")
    count = dps * seqs
    s = lax.axis_index("seq")
    own = HEADS // seqs
    wide = own * HEAD_DIM
    length = content.shape[1]
    preds = query_stream.shape[1]
    pad_q = SLOT_Q - preds
    shard = qkv_weight.shape[0]

    x_q = jnp.pad(query_stream[0], ((0, pad_q), (0, 0)))
    vec = jnp.concatenate(
        [
            member.astype(F32)
            for member in (
                qv_bias,
                out_bias,
                attn_gain,
                attn_shift,
                up_bias,
                down_bias,
                ffn_gain,
                ffn_shift,
            )
        ]
    )
    vec = jnp.pad(vec, (0, 1024 - vec.shape[0])).reshape(8, 128)
    ints = jnp.stack(
        [
            segment_ids[0],
            order[0],
            pad_mask[0],
            jnp.pad(predicted[0], (0, length - preds), constant_values=-1),
        ]
    )
    ints = jnp.pad(ints, ((0, 4), (0, 0)))
    w_parts = jnp.transpose(
        qkv_weight.reshape(shard, 3, seqs, wide), (2, 0, 1, 3)
    ).reshape(seqs, shard, 3 * wide)
    gather = (jnp.concatenate([up_weight, out_weight], axis=1)[None], down_weight[None])
    stages = list(zip(FWD_BITS_UP, FWD_BITS_DOWN))

    def launch(n):
        return tuple(give_to(cur, count, bit) for cur, bit in zip(gather, stages[n]))

    def land(n, got, *others):
        got = tie(got, *others)
        return tuple(pile(c, g, bit) for c, g, bit in zip(gather, got, stages[n]))

    flying = launch(0)
    x_all, w_all, v_all, i_all = start_call(
        dps, seqs, content[0].astype(BF16), x_q.astype(BF16), w_parts, vec, ints
    )
    w_qkv = w_all.reshape(MODEL_WIDTH, 3 * wide)
    parts = v_all.reshape(count, 1024)
    vectors = []
    at = 0
    for n in VEC_PARTS:
        vectors.append(parts[:, at : at + n].reshape(count * n))
        at += n
    bias_qv, bias_out, gain_one, shift_one, bias_up, bias_down, gain_two, shift_two = vectors
    seg_all = i_all[:, 0].reshape(seqs * length)
    order_all = i_all[:, 1].reshape(seqs * length)
    pad_all = i_all[:, 2].reshape(seqs * length)
    pred_all = i_all[:, 3, :SLOT_Q].reshape(seqs * SLOT_Q)

    gather = land(0, flying, i_all)
    flying = launch(1)
    rev, fold = bias_inputs(rel_bucket, rel_table, s * own, own)
    rev, fold = tie((rev, fold), gather)
    hot, hot_t, shift = query_place(pred_all, ROWS_Q)
    rseg, rlim, kmeta, span = row_meta(seg_all, pad_all, order_all, pred_all, ROWS_Q)
    tiles, qbias = bias_call(rev, fold, hot, shift)

    bq = lax.dynamic_slice_in_dim(bias_qv[:MODEL_WIDTH], s * wide, wide)
    bv = lax.dynamic_slice_in_dim(bias_qv[MODEL_WIDTH:], s * wide, wide)
    gather = land(1, flying, tiles)
    flying = launch(2)
    x_all = tie(x_all, gather)
    q_t, q3, k3, k_t, v3, v_t = proj_call(
        own, seqs * length, x_all, w_qkv, bq[None], bv[None]
    )
    gather = land(2, flying, q_t)
    flying = launch(3)
    q_t = tie(q_t, gather)

    ctx_t, ctx_rows, lse = fwd_call(span, q_t, k3, v_t, kmeta, rseg, rlim, tiles, qbias)

    gather = land(3, flying, ctx_rows)
    others = tuple(give_to(cur, count, 1) for cur in gather)
    ctx_rows = tie(ctx_rows, gather)
    planes = (gather[0], others[0], gather[1], others[1])

    def from_rows(ref, t):
        return ref.at[pl.ds(pl.multiple_of(t * length, length), length)]

    def from_query(ref, t):
        return ref.at[pl.ds(pl.multiple_of(seqs * length + t * SLOT_Q, 16), SLOT_Q)]

    ctx_c, ctx_q = swap_call(
        seqs,
        ctx_rows,
        ctx_rows,
        from_rows,
        from_query,
        (length, wide),
        (SLOT_Q, wide),
        1,
        "swap_context",
    )
    pad_float = pad_mask[0].astype(F32)
    valid = jnp.concatenate([pad_float, jnp.ones((preds,), F32), jnp.zeros((pad_q,), F32)])
    valid = jnp.broadcast_to(valid[:, None], (length + SLOT_Q, 128))
    (
        out_c,
        out_q,
        res_c,
        res_q,
        give_c,
        give_q,
        uo_keep,
        uo_give,
        down_keep,
        down_give,
        vec_sums,
        squares,
    ) = mid_call(
        ctx_c,
        ctx_q,
        content[0],
        x_q,
        content_cot[0],
        jnp.pad(query_cot[0], ((0, pad_q), (0, 0))),
        valid,
        planes,
        [
            member[None]
            for member in (bias_out, gain_one, shift_one, bias_up, bias_down, gain_two, shift_two)
        ],
    )
    back = ((2, 4, 8, 16), (4, 2, 8, 16))
    left = [[16, 8, 4, 2], [16, 8, 4, 2]]
    flying = (give_to(uo_give, count, 1), give_to(down_give, count, 1))
    stay = (uo_keep, down_keep)

    def add_up(got, *others):
        got = tie(got, *others)
        return tuple(k.astype(F32) + g.astype(F32) for k, g in zip(stay, got))

    def send_on(n, sums):
        away, kept, gone = [], [], []
        for i in range(2):
            bit = back[i][n]
            give, keep = halves(sums[i], bit, left[i])
            left[i].remove(bit)
            gone.append(give)
            away.append(give_to(give, count, bit))
            kept.append(keep)
        return tuple(away), tuple(kept), tuple(gone)

    local_sums = jnp.concatenate([jnp.sum(squares, axis=1)[:6], jnp.sum(pad_float)[None]])

    def from_slot(ref, t):
        return ref.at[t]

    g_c, g_q = swap_call(
        seqs,
        give_c,
        give_q,
        from_slot,
        from_slot,
        (length, wide),
        (SLOT_Q, wide),
        2,
        "swap_grads",
    )
    sums = add_up(flying, g_c)
    sums = tuple(x.reshape((2,) * 4 + x.shape[1:]) for x in sums)
    flying, stay, gone = send_on(0, sums)
    g_c = tie(g_c, stay, gone)
    dq, dk, dv, offs, qoffs = bwd_call(
        span,
        q_t,
        q3,
        k3,
        k_t,
        v3,
        ctx_t,
        g_c.reshape(seqs * length, wide),
        g_q.reshape(seqs * SLOT_Q, wide),
        lse,
        kmeta,
        rseg,
        rlim,
        tiles,
        qbias,
        hot_t,
        shift,
    )
    table = table_sums(offs, qoffs, rel_bucket)
    sums = add_up(flying, dq)
    flying, stay, gone = send_on(1, sums)
    dq = tie(dq, stay, gone)
    grad_c, grad_q, grad_w, qv_sums = grads_call(
        seqs, length, SLOT_Q, count, x_all, w_qkv, dq, dk, dv
    )
    spot = jnp.zeros((2, MODEL_WIDTH), F32)
    grad_bias_qv = lax.dynamic_update_slice(
        spot, qv_sums[:2], (0, s * wide)
    ).reshape(2 * MODEL_WIDTH)
    table_all = lax.dynamic_update_slice(
        jnp.zeros((BUCKETS, HEADS), F32), table, (0, s * own)
    )
    owned = jnp.concatenate(
        [
            member.reshape(count, -1)
            for member in (
                grad_bias_qv,
                vec_sums[6, :MODEL_WIDTH],
                vec_sums[0, :MODEL_WIDTH],
                vec_sums[1, :MODEL_WIDTH],
                vec_sums[2],
                vec_sums[3, :MODEL_WIDTH],
                vec_sums[4, :MODEL_WIDTH],
                vec_sums[5, :MODEL_WIDTH],
            )
        ],
        axis=1,
    )
    used = owned.shape[1]
    shared = jnp.concatenate([table_all.reshape(-1), local_sums])
    vec_grads = jnp.concatenate(
        [
            owned,
            jnp.broadcast_to(shared[None, :], (count, shared.shape[0])),
            jnp.zeros((count, 1024 - used - shared.shape[0]), F32),
        ],
        axis=1,
    ).reshape(dps, seqs, 8, 128)
    sums = add_up(flying, grad_c)
    flying, stay, gone = send_on(2, sums)
    grad_c = tie(grad_c, stay, gone)
    sum_c, sum_q, sum_w, sum_v = end_call(
        dps,
        seqs,
        grad_c,
        grad_q,
        grad_w.reshape(dps, seqs, 3 * shard, wide),
        vec_grads,
    )
    sums = add_up(flying, sum_c)
    flying, stay, _ = send_on(3, sums)
    grad_uo_own, grad_down_own = add_up(flying)
    grad_up_own, grad_out_own = grad_uo_own[:, :-MODEL_WIDTH], grad_uo_own[:, -MODEL_WIDTH:]
    grad_content = res_c + sum_c
    grad_query = res_q[:preds] + sum_q[:preds]
    grad_qkv_own = jnp.transpose(sum_w.reshape(seqs, 3, shard, wide), (2, 1, 0, 3)).reshape(
        shard, 3 * MODEL_WIDTH
    )
    sums = sum_v.reshape(1024)
    mine = []
    at = 0
    for n in VEC_PARTS:
        mine.append(sums[at : at + n])
        at += n
    table_sum = sums[at : at + BUCKETS * HEADS].reshape(BUCKETS, HEADS)
    totals = sums[at + BUCKETS * HEADS : at + BUCKETS * HEADS + 7]
    content_count = totals[6] * MODEL_WIDTH
    query_count = float(dps * preds * seqs * MODEL_WIDTH)
    each = jnp.stack([content_count, jnp.float32(query_count)])
    stats = jnp.sqrt(totals[:6] / jnp.concatenate([each, each, each]))
    return (
        out_c[None],
        out_q[None, :preds],
        grad_content[None],
        grad_query[None],
        grad_qkv_own,
        mine[0],
        grad_out_own,
        mine[1],
        mine[2],
        mine[3],
        grad_up_own,
        mine[4],
        grad_down_own,
        mine[5],
        mine[6],
        mine[7],
        table_sum,
        stats,
    )


def pick_local(mesh):
    sizes = dict(mesh.shape)
    return local_fast if (sizes["dp"], sizes["seq"]) == (8, 4) else local_general


def solution(mesh):
    in_specs = (
        P("dp", "seq", None),
        P("dp", "seq", None),
        P("dp", "seq"),
        P("dp", "seq"),
        P("dp", "seq"),
        P("dp", "seq"),
        P(),
        P(("dp", "seq"), None),
        P(("dp", "seq")),
        P(("dp", "seq"), None),
        P(("dp", "seq")),
        P(("dp", "seq")),
        P(("dp", "seq")),
        P(("dp", "seq"), None),
        P(("dp", "seq")),
        P(("dp", "seq"), None),
        P(("dp", "seq")),
        P(("dp", "seq")),
        P(("dp", "seq")),
        P(),
        P("dp", "seq", None),
        P("dp", "seq", None),
    )
    out_specs = (
        P("dp", "seq", None),
        P("dp", "seq", None),
        P("dp", "seq", None),
        P("dp", "seq", None),
        P(("dp", "seq"), None),
        P(("dp", "seq")),
        P(("dp", "seq"), None),
        P(("dp", "seq")),
        P(("dp", "seq")),
        P(("dp", "seq")),
        P(("dp", "seq"), None),
        P(("dp", "seq")),
        P(("dp", "seq"), None),
        P(("dp", "seq")),
        P(("dp", "seq")),
        P(("dp", "seq")),
        P(),
        P(),
    )
    local = pick_local(mesh)
    return jax.shard_map(local, mesh=mesh, in_specs=in_specs, out_specs=out_specs, check_vma=False)
```

```python
import functools
import math

import jax
import jax.numpy as jnp
from jax import lax
from jax.experimental import pallas as pl
from jax.experimental.pallas import tpu as pltpu
from jax.sharding import PartitionSpec as P

MODEL_WIDTH = 768
HEADS = 12
HEAD_DIM = 64
BUCKETS = 32
SEQ_LEN = 2048


EPS = 1e-05
NEG = -1000000000.0
SCALE = 0.125


def exact_gelu(values):
    return jax.nn.gelu(values, approximate=False)


def norm_fwd(residual, gain_vec, shift_vec):
    row_mean = jnp.mean(residual, axis=-1, keepdims=True)
    centered = residual - row_mean
    inv_std = lax.rsqrt(jnp.mean(centered * centered, axis=-1, keepdims=True) + EPS)
    normed = centered * inv_std
    return (normed * gain_vec + shift_vec, normed, inv_std)


def norm_back(upstream, normed, inv_std, gain_vec):
    grad_norm = upstream * gain_vec
    projected = jnp.mean(grad_norm, axis=-1, keepdims=True) + normed * jnp.mean(
        grad_norm * normed, axis=-1, keepdims=True
    )
    return (
        inv_std * (grad_norm - projected),
        jnp.sum(upstream * normed, axis=(0, 1)),
        jnp.sum(upstream, axis=(0, 1)),
    )


def bucket_edges(rel_bucket):
    entry_count = rel_bucket.shape[0]
    matches = rel_bucket[None, :] == jnp.arange(BUCKETS, dtype=jnp.int32)[:, None]
    places = jnp.arange(entry_count, dtype=jnp.int32)[None, :]
    starts = jnp.min(jnp.where(matches, places, entry_count), axis=1)
    counts = jnp.sum(matches.astype(jnp.int32), axis=1)
    return (starts, starts + counts)


def build_mask(
    query_pos, query_seg, query_limit, content_row, key_pos, key_seg, key_order, key_pad
):
    inside = (
        (query_seg[:, None] == key_seg[None, :])
        & (key_pad[None, :] == 1)
        & (key_order[None, :] <= query_limit[:, None])
    )
    itself = (key_pos[None, :] == query_pos[:, None]) & content_row[:, None]
    return (inside | itself, key_pos[None, :] - query_pos[:, None] + (SEQ_LEN - 1))


def masked_scores(query_heads, key_heads, table_low, edges, allowed, offsets):
    raw_scores = (
        jnp.einsum("rhd,lhd->hrl", query_heads, key_heads, preferred_element_type=jnp.float32)
        * SCALE
    )
    starts, ends = edges
    spread = offsets[..., None]
    onehot = ((spread >= starts) & (spread < ends)).astype(jnp.bfloat16)
    bias = jnp.einsum("rlb,bh->hrl", onehot, table_low, preferred_element_type=jnp.float32)
    return (jnp.where(allowed[None], raw_scores + bias, NEG), onehot)


def attend_forward(packed, table_low, edges, content_row):
    queries, key_values, key_seg, key_order, key_pad, query_pos, query_seg, query_limit = packed
    row_count = queries.shape[0]
    length = key_values.shape[0]
    key_pos = jnp.arange(length, dtype=jnp.int32)
    allowed, offsets = build_mask(
        query_pos, query_seg, query_limit, content_row, key_pos, key_seg, key_order, key_pad
    )
    query_heads = queries.reshape(row_count, HEADS, HEAD_DIM)
    key_heads = key_values[:, :MODEL_WIDTH].reshape(length, HEADS, HEAD_DIM)
    value_heads = key_values[:, MODEL_WIDTH:].reshape(length, HEADS, HEAD_DIM)
    scores, onehot = masked_scores(query_heads, key_heads, table_low, edges, allowed, offsets)
    row_max = jnp.max(scores, axis=-1, keepdims=True)
    expo_vals = jnp.exp(scores - row_max)
    row_total = jnp.sum(expo_vals, axis=-1, keepdims=True)
    probs_low = (expo_vals / row_total).astype(jnp.bfloat16)
    context = jnp.einsum("hrl,lhd->rhd", probs_low, value_heads, preferred_element_type=jnp.float32)
    return (
        context.reshape(row_count, MODEL_WIDTH),
        jnp.transpose((row_max + jnp.log(row_total))[..., 0]),
    )


def attend_backward(packed, table_low, edges, content_row):
    (
        queries,
        key_values,
        key_seg,
        key_order,
        key_pad,
        query_pos,
        query_seg,
        query_limit,
        row_lse,
        grad_context,
    ) = packed
    row_count = queries.shape[0]
    length = key_values.shape[0]
    key_pos = jnp.arange(length, dtype=jnp.int32)
    allowed, offsets = build_mask(
        query_pos, query_seg, query_limit, content_row, key_pos, key_seg, key_order, key_pad
    )
    query_heads = queries.reshape(row_count, HEADS, HEAD_DIM)
    key_heads = key_values[:, :MODEL_WIDTH].reshape(length, HEADS, HEAD_DIM)
    value_heads = key_values[:, MODEL_WIDTH:].reshape(length, HEADS, HEAD_DIM)
    scores, onehot = masked_scores(query_heads, key_heads, table_low, edges, allowed, offsets)
    probs = jnp.exp(scores - jnp.transpose(row_lse)[..., None])
    grad_heads = grad_context.reshape(row_count, HEADS, HEAD_DIM)
    grad_probs = jnp.einsum(
        "rhd,lhd->hrl", grad_heads, value_heads, preferred_element_type=jnp.float32
    )
    row_delta = jnp.sum(probs * grad_probs, axis=-1)
    grad_scores = (probs * (grad_probs - row_delta[..., None])).astype(jnp.bfloat16)
    grad_query = (
        jnp.einsum("hrl,lhd->rhd", grad_scores, key_heads, preferred_element_type=jnp.float32)
        * SCALE
    )
    grad_table = jnp.einsum("hrl,rlb->bh", grad_scores, onehot, preferred_element_type=jnp.float32)
    results = (grad_query.reshape(row_count, MODEL_WIDTH), grad_table, jnp.transpose(row_delta))
    probs_low = probs.astype(jnp.bfloat16)
    grad_key = (
        jnp.einsum("hrl,rhd->lhd", grad_scores, query_heads, preferred_element_type=jnp.float32)
        * SCALE
    )
    grad_value = jnp.einsum(
        "hrl,rhd->lhd", probs_low, grad_heads, preferred_element_type=jnp.float32
    )
    results = results + (
        jnp.concatenate(
            [grad_key.reshape(length, MODEL_WIDTH), grad_value.reshape(length, MODEL_WIDTH)],
            axis=-1,
        ),
    )
    return results


def local_general(
    content,
    query_stream,
    segment_ids,
    pad_mask,
    predicted,
    order,
    rel_bucket,
    qkv_weight,
    qv_bias,
    out_weight,
    out_bias,
    attn_gain,
    attn_shift,
    up_weight,
    up_bias,
    down_weight,
    down_bias,
    ffn_gain,
    ffn_shift,
    rel_table,
    content_cot,
    query_cot,
):
    seq_count = content.shape[0]
    shard_length = content.shape[1]
    pred_count = query_stream.shape[1]
    row_count = shard_length + pred_count
    group_size = lax.axis_size("seq")
    edges = bucket_edges(rel_bucket)
    shards = (
        lax.all_gather(qkv_weight, ("dp", "seq"), axis=0, tiled=True),
        lax.all_gather(out_weight, ("dp", "seq"), axis=0, tiled=True),
        lax.all_gather(up_weight, ("dp", "seq"), axis=0, tiled=True),
        lax.all_gather(down_weight, ("dp", "seq"), axis=0, tiled=True),
        lax.all_gather(qv_bias, ("dp", "seq"), axis=0, tiled=True),
        lax.all_gather(out_bias, ("dp", "seq"), axis=0, tiled=True),
        lax.all_gather(attn_gain, ("dp", "seq"), axis=0, tiled=True),
        lax.all_gather(attn_shift, ("dp", "seq"), axis=0, tiled=True),
        lax.all_gather(up_bias, ("dp", "seq"), axis=0, tiled=True),
        lax.all_gather(down_bias, ("dp", "seq"), axis=0, tiled=True),
        lax.all_gather(ffn_gain, ("dp", "seq"), axis=0, tiled=True),
        lax.all_gather(ffn_shift, ("dp", "seq"), axis=0, tiled=True),
    )
    query_key_value_weight, w_out, w_up, w_down = (shards[0], shards[1], shards[2], shards[3])
    bias_qv, bias_out, first_norm_gain, shift_one, bias_up, bias_down, gain_two, shift_two = [
        member.astype(jnp.float32) for member in shards[4:]
    ]
    all_rows = jnp.concatenate([content, query_stream], axis=1)
    reduced_precision_rows = all_rows.astype(jnp.bfloat16)
    queries = (
        jnp.einsum(
            "srd,de->sre",
            reduced_precision_rows,
            query_key_value_weight[:, :MODEL_WIDTH],
            preferred_element_type=jnp.float32,
        )
        + bias_qv[:MODEL_WIDTH]
    ).astype(jnp.bfloat16)
    value_shift = jnp.concatenate([jnp.zeros((MODEL_WIDTH,), jnp.float32), bias_qv[MODEL_WIDTH:]])
    key_values = (
        jnp.einsum(
            "zci,ip->zcp",
            reduced_precision_rows[:, :shard_length],
            query_key_value_weight[:, MODEL_WIDTH:],
            preferred_element_type=jnp.float32,
        )
        + value_shift
    ).astype(jnp.bfloat16)
    full_pairs, full_seg, full_order, full_pad = (
        lax.all_gather(key_values, "seq", axis=1, tiled=True),
        lax.all_gather(segment_ids, "seq", axis=1, tiled=True),
        lax.all_gather(order, "seq", axis=1, tiled=True),
        lax.all_gather(pad_mask, "seq", axis=1, tiled=True),
    )
    content_pos = lax.axis_index("seq") * shard_length + jnp.arange(shard_length, dtype=jnp.int32)
    query_pos = jnp.concatenate(
        [jnp.broadcast_to(content_pos[None, :], (seq_count, shard_length)), predicted], axis=1
    )
    query_seg = jnp.concatenate(
        [segment_ids, jnp.take_along_axis(full_seg, predicted, axis=1)], axis=1
    )
    query_limit = jnp.concatenate(
        [order, jnp.take_along_axis(full_order, predicted, axis=1) - 1], axis=1
    )
    content_row = jnp.arange(row_count, dtype=jnp.int32) < shard_length
    row_meta = (full_seg, full_order, full_pad, query_pos, query_seg, query_limit)

    def forward_one(packed):
        return attend_forward(packed, rel_table, edges, content_row)

    context, row_lse = lax.map(forward_one, (queries, full_pairs) + row_meta)
    context_low = context.astype(jnp.bfloat16)
    attn_out = (
        jnp.einsum("sre,ed->srd", context_low, w_out, preferred_element_type=jnp.float32) + bias_out
    )
    hidden_one, normed_one, inv_one = norm_fwd(all_rows + attn_out, first_norm_gain, shift_one)
    hidden_low = hidden_one.astype(jnp.bfloat16)
    pre_act = (
        jnp.einsum("srd,df->srf", hidden_low, w_up, preferred_element_type=jnp.float32) + bias_up
    )
    activ, gelu_pull = jax.vjp(exact_gelu, pre_act)
    activ_low = activ.astype(jnp.bfloat16)
    ffn_out = (
        jnp.einsum("srf,fd->srd", activ_low, w_down, preferred_element_type=jnp.float32) + bias_down
    )
    hidden_two, normed_two, inv_two = norm_fwd(hidden_one + ffn_out, gain_two, shift_two)
    pad_float = pad_mask.astype(jnp.float32)
    row_valid = jnp.concatenate(
        [pad_float, jnp.ones((seq_count, pred_count), jnp.float32)], axis=1
    )[..., None]
    outputs = hidden_two * row_valid
    pad_weight = pad_float[..., None]
    local_sums = jnp.stack(
        [
            jnp.sum(pad_weight * content * content),
            jnp.sum(query_stream * query_stream),
            jnp.sum(pad_weight * attn_out[:, :shard_length] * attn_out[:, :shard_length]),
            jnp.sum(attn_out[:, shard_length:] * attn_out[:, shard_length:]),
            jnp.sum(pad_weight * ffn_out[:, :shard_length] * ffn_out[:, :shard_length]),
            jnp.sum(ffn_out[:, shard_length:] * ffn_out[:, shard_length:]),
            jnp.sum(pad_float),
        ]
    )
    back_weights = (
        lax.all_gather(qkv_weight, ("dp", "seq"), axis=0, tiled=True),
        lax.all_gather(out_weight, ("dp", "seq"), axis=0, tiled=True),
        lax.all_gather(up_weight, ("dp", "seq"), axis=0, tiled=True),
        lax.all_gather(down_weight, ("dp", "seq"), axis=0, tiled=True),
        lax.all_gather(attn_gain, ("dp", "seq"), axis=0, tiled=True),
        lax.all_gather(ffn_gain, ("dp", "seq"), axis=0, tiled=True),
    )
    back_pairs = lax.all_gather(key_values, "seq", axis=1, tiled=True)
    backward_query_key_value, back_out, back_up, back_down = (
        back_weights[0],
        back_weights[1],
        back_weights[2],
        back_weights[3],
    )
    back_gain_one = back_weights[4].astype(jnp.float32)
    back_gain_two = back_weights[5].astype(jnp.float32)
    upstream = jnp.concatenate([content_cot, query_cot], axis=1) * row_valid
    grad_res_two, grad_gain_two, grad_shift_two = norm_back(
        upstream, normed_two, inv_two, back_gain_two
    )
    grad_ffn = grad_res_two.astype(jnp.bfloat16)
    grad_bias_down = jnp.sum(grad_ffn, axis=(0, 1), dtype=jnp.float32)
    grad_down = jnp.einsum("srf,srd->fd", activ_low, grad_ffn, preferred_element_type=jnp.float32)
    grad_activ = jnp.einsum("srd,fd->srf", grad_ffn, back_down, preferred_element_type=jnp.float32)
    grad_pre = gelu_pull(grad_activ)[0].astype(jnp.bfloat16)
    grad_bias_up = jnp.sum(grad_pre, axis=(0, 1), dtype=jnp.float32)
    grad_up = jnp.einsum("srd,srf->df", hidden_low, grad_pre, preferred_element_type=jnp.float32)
    grad_hidden = grad_res_two + jnp.einsum(
        "srf,df->srd", grad_pre, back_up, preferred_element_type=jnp.float32
    )
    grad_res_one, grad_gain_one, grad_shift_one = norm_back(
        grad_hidden, normed_one, inv_one, back_gain_one
    )
    grad_attn = grad_res_one.astype(jnp.bfloat16)
    grad_bias_out = jnp.sum(grad_attn, axis=(0, 1), dtype=jnp.float32)
    grad_out = jnp.einsum("sre,srd->ed", context_low, grad_attn, preferred_element_type=jnp.float32)
    grad_context = jnp.einsum(
        "srd,ed->sre", grad_attn, back_out, preferred_element_type=jnp.float32
    ).astype(jnp.bfloat16)

    def backward_all(packed):
        return attend_backward(packed, rel_table, edges, content_row)

    grad_queries, grad_tables, per_row_delta, grad_pairs = lax.map(
        backward_all, (queries, back_pairs) + row_meta + (row_lse, grad_context)
    )
    paired_gradients = lax.psum_scatter(
        grad_pairs.astype(jnp.bfloat16), "seq", scatter_dimension=1, tiled=True
    )
    query_grads = grad_queries.astype(jnp.bfloat16)
    grad_bias_qv = jnp.concatenate(
        [
            jnp.sum(query_grads, axis=(0, 1), dtype=jnp.float32),
            jnp.sum(paired_gradients[..., MODEL_WIDTH:], axis=(0, 1), dtype=jnp.float32),
        ]
    )
    grad_qkv = jnp.concatenate(
        [
            jnp.einsum(
                "srd,sre->de",
                reduced_precision_rows,
                query_grads,
                preferred_element_type=jnp.float32,
            ),
            jnp.einsum(
                "cvi,cvp->ip",
                reduced_precision_rows[:, :shard_length],
                paired_gradients,
                preferred_element_type=jnp.float32,
            ),
        ],
        axis=1,
    )
    grad_rows = grad_res_one + jnp.einsum(
        "sre,de->srd",
        query_grads,
        backward_query_key_value[:, :MODEL_WIDTH],
        preferred_element_type=jnp.float32,
    )
    grad_content = grad_rows[:, :shard_length] + jnp.einsum(
        "zwv,bv->zwb",
        paired_gradients,
        backward_query_key_value[:, MODEL_WIDTH:],
        preferred_element_type=jnp.float32,
    )
    grad_query = grad_rows[:, shard_length:]
    owned = (
        lax.psum_scatter(grad_qkv, ("dp", "seq"), scatter_dimension=0, tiled=True),
        lax.psum_scatter(grad_out, ("dp", "seq"), scatter_dimension=0, tiled=True),
        lax.psum_scatter(grad_up, ("dp", "seq"), scatter_dimension=0, tiled=True),
        lax.psum_scatter(grad_down, ("dp", "seq"), scatter_dimension=0, tiled=True),
        lax.psum_scatter(grad_bias_qv, ("dp", "seq"), scatter_dimension=0, tiled=True),
        lax.psum_scatter(grad_bias_out, ("dp", "seq"), scatter_dimension=0, tiled=True),
        lax.psum_scatter(grad_gain_one, ("dp", "seq"), scatter_dimension=0, tiled=True),
        lax.psum_scatter(grad_shift_one, ("dp", "seq"), scatter_dimension=0, tiled=True),
        lax.psum_scatter(grad_bias_up, ("dp", "seq"), scatter_dimension=0, tiled=True),
        lax.psum_scatter(grad_bias_down, ("dp", "seq"), scatter_dimension=0, tiled=True),
        lax.psum_scatter(grad_gain_two, ("dp", "seq"), scatter_dimension=0, tiled=True),
        lax.psum_scatter(grad_shift_two, ("dp", "seq"), scatter_dimension=0, tiled=True),
    )
    table_sum, totals = lax.psum((jnp.sum(grad_tables, axis=0), local_sums), ("dp", "seq"))
    content_count = totals[6] * MODEL_WIDTH
    query_count = float(seq_count * lax.axis_size("dp") * pred_count * group_size * MODEL_WIDTH)
    stats = jnp.sqrt(
        jnp.stack(
            [
                totals[0] / content_count,
                totals[1] / query_count,
                totals[2] / content_count,
                totals[3] / query_count,
                totals[4] / content_count,
                totals[5] / query_count,
            ]
        )
    )
    return (
        outputs[:, :shard_length],
        outputs[:, shard_length:],
        grad_content,
        grad_query,
        owned[0],
        owned[4],
        owned[1],
        owned[5],
        owned[6],
        owned[7],
        owned[2],
        owned[8],
        owned[3],
        owned[9],
        owned[10],
        owned[11],
        table_sum,
        stats,
    )


LOG2E = math.log2(math.e)
TILE = 256
KEYS = 512
HALF = 128
REACH = 11
DIAGS = 2 * REACH + 1
WIDE = SEQ_LEN + HALF
MASKED = -1e30
F32 = jnp.float32
BF16 = jnp.bfloat16


def cost_of(micros):
    return pl.CostEstimate(
        flops=int(micros * 1.0e9), bytes_accessed=int(micros * 1.0e6), transcendentals=0
    )


def bias_kernel(rows_q, own, rev_ref, fold_ref, hot_ref, shift_ref, tile_ref, qbias_ref):
    lane = lax.broadcasted_iota(jnp.int32, (HALF, HALF), 1)
    for h in range(own):
        for e in range(-REACH, REACH + 1):
            start = HALF * (15 - e)
            row = rev_ref[h : h + 1, start : start + 2 * HALF]
            skew = pltpu.roll(
                jnp.broadcast_to(row, (HALF, 2 * HALF)), 0, 1, stride=1, stride_axis=0
            )
            tile_ref[h, e + REACH] = skew[:, HALF:]
    for t in range(rows_q // HALF):
        shift = shift_ref[t * HALF : (t + 1) * HALF, :]
        place = lane + shift
        wrap = place >= HALF
        idx = jnp.where(wrap, place - HALF, place)
        for h in range(own):
            spread = jnp.dot(
                hot_ref[t * HALF : (t + 1) * HALF, :], fold_ref[h], preferred_element_type=F32
            )
            prev = jnp.take_along_axis(spread[:, :HALF], idx, axis=1)
            for j in range(SEQ_LEN // HALF):
                cur = jnp.take_along_axis(
                    spread[:, (j + 1) * HALF : (j + 2) * HALF], idx, axis=1
                )
                out = jnp.where(wrap, cur, prev) * LOG2E
                qbias_ref[h, j * HALF : (j + 1) * HALF, t * HALF : (t + 1) * HALF] = out.T
                prev = cur


def bias_call(rev, fold, hot, shift):
    own = rev.shape[0]
    rows_q = hot.shape[0]
    return pl.pallas_call(
        functools.partial(bias_kernel, rows_q, own),
        out_shape=(
            jax.ShapeDtypeStruct((own, DIAGS, HALF, HALF), F32),
            jax.ShapeDtypeStruct((own, SEQ_LEN, rows_q), F32),
        ),
        compiler_params=pltpu.CompilerParams(vmem_limit_bytes=50 << 20),
        cost_estimate=cost_of(14),
        name="bias_tiles",
    )(rev, fold, hot, shift)


def bias_block(tile_ref, h, e):
    return jnp.concatenate(
        [
            jnp.concatenate([tile_ref[h, e + i], tile_ref[h, e + i - 1]], axis=1)
            for i in range(KEYS // HALF)
        ],
        axis=0,
    )


def mask_block(kmeta_ref, rseg_ref, rlim_ref, krow, rcol, width):
    kseg = kmeta_ref[0, pl.ds(krow, KEYS), :]
    kord = kmeta_ref[1, pl.ds(krow, KEYS), :]
    parts = []
    for w in range(width // HALF):
        rseg = rseg_ref[:, pl.ds(rcol + w * HALF, HALF)]
        rlim = rlim_ref[:, pl.ds(rcol + w * HALF, HALF)]
        ok = (kseg == rseg) & (kord <= rlim)
        parts.append(jnp.where(ok, 0.0, MASKED))
    return parts[0] if len(parts) == 1 else jnp.concatenate(parts, axis=1)


def fwd_kernel(
    own,
    rows_q,
    span_ref,
    qt_ref,
    k_ref,
    vt_ref,
    kmeta_ref,
    rseg_ref,
    rlim_ref,
    tile_ref,
    qbias_ref,
    ctx_ref,
    rows_ref,
    lse_ref,
    s_scr,
):
    def run(rcol, width, lo, steps, bias_of):
        heads = range(own)

        def fold(op, x):
            rows = [x[i * 8 : (i + 1) * 8] for i in range(x.shape[0] // 8)]
            while len(rows) > 1:
                rows = [op(rows[i], rows[i + 1]) for i in range(0, len(rows), 2)]
            return rows[0]

        def score(step, tops):
            kt = lo + step * (KEYS // TILE)
            krow = pl.multiple_of(kt * TILE, TILE)
            mask = mask_block(kmeta_ref, rseg_ref, rlim_ref, krow, rcol, width)
            new = []
            for h in heads:
                s = jnp.dot(
                    k_ref[h, pl.ds(krow, KEYS), :],
                    qt_ref[h * HEAD_DIM : (h + 1) * HEAD_DIM, pl.ds(rcol, width)],
                    preferred_element_type=F32,
                )
                s = s * (SCALE * LOG2E) + (bias_of(h, kt) + mask)
                s_scr[h, pl.ds(krow, KEYS), :width] = s
                new.append(jnp.maximum(tops[h], fold(jnp.maximum, s)))
            return tuple(new)

        tops = lax.fori_loop(
            0, steps, score, tuple(jnp.full((8, width), MASKED, F32) for _ in heads)
        )
        tops = [jnp.max(t, axis=0, keepdims=True) for t in tops]

        def weigh(step, carry):
            kt = lo + step * (KEYS // TILE)
            krow = pl.multiple_of(kt * TILE, TILE)
            sums, accs = carry
            new_sums, new_accs = [], []
            for h in heads:
                p = jnp.exp2(s_scr[h, pl.ds(krow, KEYS), :width] - tops[h])
                new_sums.append(sums[h] + fold(jnp.add, p))
                new_accs.append(
                    accs[h]
                    + jnp.dot(
                        vt_ref[h * HEAD_DIM : (h + 1) * HEAD_DIM, pl.ds(krow, KEYS)],
                        p.astype(BF16),
                        preferred_element_type=F32,
                    )
                )
            return tuple(new_sums), tuple(new_accs)

        sums, accs = lax.fori_loop(
            0,
            steps,
            weigh,
            (
                tuple(jnp.zeros((8, width), F32) for _ in heads),
                tuple(jnp.zeros((HEAD_DIM, width), F32) for _ in heads),
            ),
        )
        outs = []
        for h in heads:
            total = jnp.sum(sums[h], axis=0, keepdims=True)
            outs.append(accs[h] / total)
            lse_ref[h : h + 1, pl.ds(rcol, width)] = tops[h] + jnp.log2(total)
        out = jnp.concatenate(outs, axis=0)
        ctx_ref[:, pl.ds(rcol, width)] = out.astype(BF16)
        return out

    def content_tile(qt, carry):
        def bias_of(h, kt):
            return bias_block(tile_ref, h, 2 * (kt - qt) + REACH)

        run(pl.multiple_of(qt * TILE, TILE), TILE, span_ref[0, qt], span_ref[1, qt], bias_of)
        return carry

    lax.fori_loop(0, SEQ_LEN // TILE, content_tile, 0)

    def query_bias(h, kt):
        return qbias_ref[h, pl.ds(pl.multiple_of(kt * TILE, TILE), KEYS), :]

    last = SEQ_LEN // TILE
    out = run(SEQ_LEN, rows_q, span_ref[0, last], span_ref[1, last], query_bias)
    rows_ref[...] = out.T.astype(BF16)


def fwd_call(span, qt, k3, vt, kmeta, rseg, rlim, tiles, qbias):
    own = k3.shape[0]
    rows = qt.shape[1]
    rows_q = rows - SEQ_LEN
    vm = pl.BlockSpec(memory_space=pltpu.VMEM)
    return pl.pallas_call(
        functools.partial(fwd_kernel, own, rows_q),
        out_shape=(
            jax.ShapeDtypeStruct((own * HEAD_DIM, rows), BF16),
            jax.ShapeDtypeStruct((rows_q, own * HEAD_DIM), BF16),
            jax.ShapeDtypeStruct((own, rows), F32),
        ),
        in_specs=[pl.BlockSpec(memory_space=pltpu.SMEM)] + [vm] * 8,
        scratch_shapes=[
            pltpu.VMEM((own, SEQ_LEN, max(rows_q, TILE)), F32),
        ],
        compiler_params=pltpu.CompilerParams(vmem_limit_bytes=56 << 20),
        cost_estimate=cost_of(32),
        name="attend",
    )(span, qt, k3, vt, kmeta, rseg, rlim, tiles, qbias)


def bwd_kernel(
    own,
    rows_q,
    span_ref,
    qt_ref,
    q_ref,
    k_ref,
    kt_ref,
    v_ref,
    ctx_ref,
    gc_ref,
    gq_ref,
    lse_ref,
    kmeta_ref,
    rseg_ref,
    rlim_ref,
    tile_ref,
    qbias_ref,
    hott_ref,
    shift_ref,
    dq_ref,
    dk_ref,
    dv_ref,
    offs_ref,
    qoffs_ref,
    dk_scr,
    dv_scr,
    dq_scr,
    diag_scr,
    ds_scr,
    delta_scr,
    gt_ref,
    g_ref,
):
    seqs, length = gc_ref.shape[0], gc_ref.shape[2]
    for t in range(seqs):
        for a in range(0, length, TILE):
            block = gc_ref[t, :, a : a + TILE]
            at = slice(t * length + a, t * length + a + TILE)
            gt_ref[:, at] = block
            back = block.astype(F32).T
            for h in range(own):
                g_ref[h, at, :] = back[:, h * HEAD_DIM : (h + 1) * HEAD_DIM].astype(BF16)
    used = gq_ref.shape[0]
    block = jnp.concatenate(
        [gq_ref[...].astype(F32), jnp.zeros((rows_q - used, gq_ref.shape[1]), F32)], axis=0
    )
    gt_ref[:, SEQ_LEN:] = block.T.astype(BF16)
    for h in range(own):
        g_ref[h, SEQ_LEN:, :] = block[:, h * HEAD_DIM : (h + 1) * HEAD_DIM].astype(BF16)
    dk_scr[...] = jnp.zeros(dk_scr.shape, F32)
    dv_scr[...] = jnp.zeros(dv_scr.shape, F32)
    diag_scr[...] = jnp.zeros(diag_scr.shape, F32)
    ds_scr[...] = jnp.zeros(ds_scr.shape, BF16)
    for h in range(own):
        part = slice(h * HEAD_DIM, (h + 1) * HEAD_DIM)
        delta_scr[h : h + 1, :] = jnp.sum(
            ctx_ref[part, :].astype(F32) * gt_ref[part, :].astype(F32), axis=0, keepdims=True
        )

    def run(rcol, width, lo, steps, bias_of, keep):
        dq_scr[...] = jnp.zeros(dq_scr.shape, F32)

        def body(step, carry):
            kt = lo + step * (KEYS // TILE)
            krow = pl.multiple_of(kt * TILE, TILE)
            mask = mask_block(kmeta_ref, rseg_ref, rlim_ref, krow, rcol, width)
            for h in range(own):
                part = slice(h * HEAD_DIM, (h + 1) * HEAD_DIM)
                s = jnp.dot(
                    k_ref[h, pl.ds(krow, KEYS), :],
                    qt_ref[part, pl.ds(rcol, width)],
                    preferred_element_type=F32,
                )
                s = s * (SCALE * LOG2E) + (bias_of(h, kt) + mask)
                p = jnp.exp2(s - lse_ref[h : h + 1, pl.ds(rcol, width)])
                gp = jnp.dot(
                    v_ref[h, pl.ds(krow, KEYS), :],
                    gt_ref[part, pl.ds(rcol, width)],
                    preferred_element_type=F32,
                )
                ds = p * (gp - delta_scr[h : h + 1, pl.ds(rcol, width)])
                low = ds.astype(BF16)
                keep(h, kt, ds, low)
                dv_scr[h, pl.ds(krow, KEYS), :] += jnp.dot(
                    p.astype(BF16), g_ref[h, pl.ds(rcol, width), :], preferred_element_type=F32
                )
                dk_scr[h, pl.ds(krow, KEYS), :] += jnp.dot(
                    low, q_ref[h, pl.ds(rcol, width), :], preferred_element_type=F32
                )
                dq_scr[h, :, :width] += jnp.dot(
                    kt_ref[part, pl.ds(krow, KEYS)], low, preferred_element_type=F32
                )
            return carry

        lax.fori_loop(0, steps, body, 0)
        grad = jnp.concatenate([dq_scr[h, :, :width] for h in range(own)], axis=0)
        dq_ref[pl.ds(rcol, width), :] = (grad * SCALE).T.astype(BF16)

    def content_tile(qt, carry):
        def bias_of(h, kt):
            return bias_block(tile_ref, h, 2 * (kt - qt) + REACH)

        def keep(h, kt, ds, low):
            e = 2 * (kt - qt) + REACH
            subs = [ds[i * HALF : (i + 1) * HALF] for i in range(KEYS // HALF)]
            diag_scr[h, e - 1] += subs[0][:, HALF:]
            for i, sub in enumerate(subs):
                here = sub[:, :HALF]
                if i + 1 < len(subs):
                    here = here + subs[i + 1][:, HALF:]
                diag_scr[h, e + i] += here

        run(pl.multiple_of(qt * TILE, TILE), TILE, span_ref[0, qt], span_ref[1, qt], bias_of, keep)
        return carry

    lax.fori_loop(0, SEQ_LEN // TILE, content_tile, 0)

    def query_bias(h, kt):
        return qbias_ref[h, pl.ds(pl.multiple_of(kt * TILE, TILE), KEYS), :]

    def query_keep(h, kt, ds, low):
        ds_scr[h, pl.ds(pl.multiple_of(kt * TILE, TILE), KEYS), :] = low

    last = SEQ_LEN // TILE
    run(SEQ_LEN, rows_q, span_ref[0, last], span_ref[1, last], query_bias, query_keep)

    for a in range(0, SEQ_LEN, TILE):
        at = slice(a, a + TILE)
        for scr, ref, scale in ((dk_scr, dk_ref, SCALE), (dv_scr, dv_ref, 1.0)):
            block = jnp.concatenate([scr[h, at, :] for h in range(own)], axis=1)
            ref[at, :] = (block * scale).astype(BF16)

    offs_ref[...] = jnp.zeros(offs_ref.shape, F32)
    qoffs_ref[...] = jnp.zeros(qoffs_ref.shape, F32)
    lane = lax.broadcasted_iota(jnp.int32, (HALF, HALF), 1)
    turn = lane + lax.broadcasted_iota(jnp.int32, (HALF, HALF), 0)
    over = turn >= HALF
    turn = jnp.where(over, turn - HALF, turn)
    for h in range(own):
        for e in range(DIAGS):
            skew = jnp.take_along_axis(diag_scr[h, e], turn, axis=1)
            start = HALF * (15 - e + REACH)
            offs_ref[h : h + 1, start : start + HALF] += jnp.sum(
                jnp.where(over, skew, 0.0), axis=0, keepdims=True
            )
            offs_ref[h : h + 1, start + HALF : start + 2 * HALF] += jnp.sum(
                jnp.where(over, 0.0, skew), axis=0, keepdims=True
            )

    for h in range(own):
        total = jnp.zeros((16, WIDE), F32)
        for t in range(rows_q // HALF):
            shift = shift_ref[t * HALF : (t + 1) * HALF, :]
            place = lane - shift
            low_side = place < 0
            idx = jnp.where(low_side, place + HALF, place)
            prev = jnp.zeros((HALF, HALF), F32)
            pieces = []
            for j in range(SEQ_LEN // HALF + 1):
                if j < SEQ_LEN // HALF:
                    block = ds_scr[h, j * HALF : (j + 1) * HALF, t * HALF : (t + 1) * HALF]
                    cur = jnp.take_along_axis(block.astype(F32).T, idx, axis=1)
                else:
                    cur = jnp.zeros((HALF, HALF), F32)
                pieces.append(jnp.where(low_side, prev, cur).astype(BF16))
                prev = cur
            total += jnp.dot(
                hott_ref[:, t * HALF : (t + 1) * HALF],
                jnp.concatenate(pieces, axis=1),
                preferred_element_type=F32,
            )
        for i in range(16):
            qoffs_ref[h : h + 1, HALF * i : HALF * i + WIDE] += total[i : i + 1, :]


def bwd_call(
    span, qt, q3, k3, kt, v3, ctx, g_c, g_q, lse, kmeta, rseg, rlim, tiles, qbias, hott, shift
):
    own = k3.shape[0]
    rows = qt.shape[1]
    rows_q = rows - SEQ_LEN
    vm = pl.BlockSpec(memory_space=pltpu.VMEM)
    return pl.pallas_call(
        functools.partial(bwd_kernel, own, rows_q),
        out_shape=(
            jax.ShapeDtypeStruct((rows, own * HEAD_DIM), BF16),
            jax.ShapeDtypeStruct((SEQ_LEN, own * HEAD_DIM), BF16),
            jax.ShapeDtypeStruct((SEQ_LEN, own * HEAD_DIM), BF16),
            jax.ShapeDtypeStruct((own, 2 * SEQ_LEN), F32),
            jax.ShapeDtypeStruct((own, 2 * SEQ_LEN), F32),
        ),
        in_specs=[pl.BlockSpec(memory_space=pltpu.SMEM)] + [vm] * 16,
        scratch_shapes=[
            pltpu.VMEM((own, SEQ_LEN, HEAD_DIM), F32),
            pltpu.VMEM((own, SEQ_LEN, HEAD_DIM), F32),
            pltpu.VMEM((own, HEAD_DIM, max(rows_q, TILE)), F32),
            pltpu.VMEM((own, DIAGS, HALF, HALF), F32),
            pltpu.VMEM((own, SEQ_LEN, rows_q), BF16),
            pltpu.VMEM((own, rows), F32),
            pltpu.VMEM((own * HEAD_DIM, rows), BF16),
            pltpu.VMEM((own, rows, HEAD_DIM), BF16),
        ],
        compiler_params=pltpu.CompilerParams(vmem_limit_bytes=60 << 20),
        cost_estimate=cost_of(58),
        name="attend_back",
    )(span, qt, q3, k3, kt, v3, ctx, g_c, g_q, lse, kmeta, rseg, rlim, tiles, qbias, hott, shift)


def table_sums(offs, qoffs, rel_bucket):
    ids = jnp.arange(BUCKETS, dtype=jnp.int32)[:, None]
    back = jnp.pad(rel_bucket[::-1], (1, 0), constant_values=BUCKETS)
    ahead = jnp.pad(rel_bucket, (0, 1), constant_values=BUCKETS)
    high = lax.Precision.HIGHEST
    near = jnp.einsum("ho,bo->bh", offs, (back[None, :] == ids).astype(F32), precision=high)
    far = jnp.einsum("ho,bo->bh", qoffs, (ahead[None, :] == ids).astype(F32), precision=high)
    return near + far


def bias_inputs(rel_bucket, rel_table, first, own):
    hot = (rel_bucket[:, None] == jnp.arange(BUCKETS, dtype=jnp.int32)[None, :]).astype(BF16)
    part = lax.dynamic_slice_in_dim(rel_table, first, own, axis=1)
    vec = jnp.einsum("ob,bh->ho", hot, part, preferred_element_type=F32)
    rev = jnp.pad(vec[:, ::-1], ((0, 0), (1, 0))) * LOG2E
    low = jnp.pad(vec, ((0, 0), (0, 1))).astype(BF16)
    fold = jnp.stack([low[:, HALF * i : HALF * i + WIDE] for i in range(16)], axis=1)
    return rev, fold


def query_place(predicted, rows_q):
    a = predicted // HALF
    c = predicted - a * HALF
    pad = rows_q - predicted.shape[0]
    hot = ((15 - a)[:, None] == jnp.arange(16, dtype=jnp.int32)[None, :]).astype(BF16)
    hot = jnp.pad(hot, ((0, pad), (0, 0)))
    shift = jnp.pad(HALF - 1 - c, (0, pad))
    shift = jnp.broadcast_to(shift[:, None], (rows_q, HALF))
    return hot, hot.T, shift


def row_meta(segment, pad_mask, order, predicted, rows_q):
    length = segment.shape[0]
    pos = jnp.arange(length, dtype=jnp.int32)
    real = pad_mask == 1
    seg = jnp.where(real, segment, -2 - pos)
    hit = predicted[:, None] == pos[None, :]
    qseg = jnp.sum(jnp.where(hit, seg[None, :], 0), axis=1)
    qlim = jnp.sum(jnp.where(hit, order[None, :], 0), axis=1) - 1
    pad = rows_q - predicted.shape[0]
    qseg = jnp.pad(qseg, (0, pad), constant_values=-1)
    qlim = jnp.pad(qlim, (0, pad))
    rseg = jnp.concatenate([seg, qseg])[None, :]
    rlim = jnp.concatenate([order, qlim])[None, :]
    kmeta = jnp.broadcast_to(jnp.stack([seg, order])[:, :, None], (2, length, HALF))
    head_seg = segment[::TILE]
    tail_seg = segment[TILE - 1 :: TILE]
    starts = jnp.sum((segment[None, :] < head_seg[:, None]).astype(jnp.int32), axis=1)
    first = jnp.arange(0, length, TILE, dtype=jnp.int32)
    lo = jnp.where(real[::TILE], starts, first) // TILE
    hi = jnp.where(real[TILE - 1 :: TILE], tail_seg, first + TILE - 1) // TILE
    count = jnp.sum(pad_mask)
    lo = jnp.concatenate([lo, jnp.zeros((1,), jnp.int32)])
    hi = jnp.concatenate([hi, jnp.maximum(count - 1, 0)[None] // TILE])
    per = KEYS // TILE
    steps = (hi - lo + per) // per
    lo = jnp.minimum(lo, length // TILE - steps * per)
    return rseg, rlim, kmeta, jnp.stack([lo, steps]).astype(jnp.int32)


COLS = 768
FWD_BITS_UP = (16, 8, 4, 2)
FWD_BITS_DOWN = (16, 8, 2, 4)


def dot_nn(a, b):
    return jnp.dot(a, b, preferred_element_type=F32)


def dot_nt(a, b):
    return lax.dot_general(a, b, (((1,), (1,)), ((), ())), preferred_element_type=F32)


def dot_tn(a, b):
    return lax.dot_general(a, b, (((0,), (0,)), ((), ())), preferred_element_type=F32)


def place_of(j, bits):
    total = 0
    for n, bit in enumerate(bits):
        total += ((j >> n) & 1) * (bit // 2)
    return total


def mid_kernel(
    seqs,
    bits_up,
    bits_down,
    ctx_c,
    ctx_q,
    x_c,
    x_q,
    cot_c,
    cot_q,
    valid_ref,
    six_ref,
    bias_up,
    uo_own,
    uo_mate,
    down_own,
    down_mate,
    res_c,
    res_q,
    gctx_c,
    gctx_q,
    six_out,
    up_out,
    sums_ref,
    out_c,
    out_q,
    parts_out,
    w_up,
    w_out,
    w_down,
    one_scr,
    norm_scr,
    inv_scr,
    low_scr,
    act_scr,
    slope_scr,
    sum_scr,
    grad_scr,
    pre_scr,
    plane_scr,
    outc_scr,
    outq_scr,
    parts_scr,
    sq_scr,
    sems,
    plane_sems,
    out_sems,
):
    core = lax.rem(lax.axis_index("seq"), 2)
    chips, shard = uo_own.shape[0], uo_own.shape[1]
    shard_down = down_own.shape[1]
    length = x_c.shape[0]
    count = x_q.shape[0]
    ff = w_up.shape[1]
    chunks = ff // COLS
    wide = ctx_c.shape[1]
    half_ff, half = ff // 2, COLS // 2
    bias_out, gain_one, shift_one, bias_down, gain_two, shift_two = [
        six_ref[i : i + 1, :] for i in range(6)
    ]

    def plane_copies(chunk, slot):
        start = chunk * COLS
        if not isinstance(start, int):
            start = pl.multiple_of(start, COLS)
        return [
            pltpu.make_async_copy(
                ref.at[:, :, pl.ds(start, COLS)], plane_scr.at[slot, n], plane_sems.at[slot, n]
            )
            for n, ref in enumerate((uo_own, uo_mate))
        ]

    def assemble(slot, put_rows):
        def body(j, carry):
            chip = place_of(j, bits_up)
            first = plane_scr[slot, core, j].astype(F32)
            second = plane_scr[slot, 1 - core, j].astype(F32)
            pair = jnp.concatenate([first, second], axis=0).astype(BF16)
            put_rows(pl.ds(pl.multiple_of(2 * shard * chip, 16), 2 * shard), pair)
            return carry

        lax.fori_loop(0, chips, body, 0)

    for chunk, slot in ((chunks, 0), (0, 1)):
        for copy in plane_copies(chunk, slot):
            copy.start()
    copies = []
    for j in range(chips):
        chip = place_of(j, bits_down)
        for side, ref in ((core, down_own), (1 - core, down_mate)):
            row = pl.multiple_of((2 * chip + side) * shard_down, 16)
            copies.append(
                pltpu.make_async_copy(
                    ref.at[j], w_down.at[pl.ds(row, shard_down)], sems.at[len(copies)]
                )
            )
    for copy in copies:
        copy.start()
    for copy in plane_copies(chunks, 0):
        copy.wait()

    def put_out(rows, pair):
        w_out[rows, :] = pair

    assemble(0, put_out)
    for copy in plane_copies(1, 0):
        copy.start()

    blocks = [(0, length // 2), (length // 2, length), (length, length + count)]

    def pick(ref_c, ref_q, a, b):
        return ref_c[a:b, :] if b <= length else ref_q[...]

    def put(ref_c, ref_q, a, b, value):
        if b <= length:
            ref_c[a:b, :] = value
        else:
            ref_q[...] = value[: ref_q.shape[0]]

    def norm(x):
        mean = jnp.mean(x, axis=-1, keepdims=True)
        centered = x - mean
        inv = lax.rsqrt(jnp.mean(centered * centered, axis=-1, keepdims=True) + EPS)
        return centered * inv, inv

    def norm_grad(up, normed, inv, gain):
        grad = up * gain
        proj = jnp.mean(grad, axis=-1, keepdims=True) + normed * jnp.mean(
            grad * normed, axis=-1, keepdims=True
        )
        return inv * (grad - proj)

    sq_scr[...] = jnp.zeros(sq_scr.shape, F32)
    six_out[...] = jnp.zeros(six_out.shape, F32)
    up_out[...] = jnp.zeros(up_out.shape, F32)

    def count_in(k, x, a, b):
        row = k + (1 if b > length else 0)
        sq_scr[row : row + 1, :] += jnp.sum(x * x * valid_ref[a:b, :1], axis=0, keepdims=True)

    def add_row(row, x):
        six_out[row : row + 1, :] += jnp.sum(x, axis=0, keepdims=True)

    for a, b in blocks:
        attn = bias_out
        for t in range(seqs):
            part = w_out[t * wide : (t + 1) * wide, :]
            attn = attn + (
                dot_tn(ctx_c[t, :, a:b], part) if b <= length else dot_nn(ctx_q[t], part)
            )
        x = pick(x_c, x_q, a, b)
        count_in(0, x, a, b)
        count_in(2, attn, a, b)
        normed, inv = norm(x + attn)
        one = normed * gain_one + shift_one
        norm_scr[a:b, :] = normed
        inv_scr[a:b, :] = jnp.broadcast_to(inv, (b - a, 128))
        one_scr[a:b, :] = one
        low_scr[a:b, :] = one.astype(BF16)

    for copy in copies:
        copy.wait()
    sum_scr[...] = jnp.zeros(sum_scr.shape, F32)

    def up_step(i, carry):
        cols = pl.ds(pl.multiple_of(i * COLS, COLS), COLS)
        slot = lax.rem(i + 1, 2)
        for copy in plane_copies(i, slot):
            copy.wait()

        def put_up(rows, pair):
            w_up[rows, cols] = pair

        assemble(slot, put_up)

        @pl.when(i + 2 < chunks)
        def _():
            for copy in plane_copies(i + 2, slot):
                copy.start()

        for a, b in blocks:
            u = dot_nn(low_scr[a:b, :], w_up[:, cols]) + bias_up[:, cols]
            cdf = 0.5 * (1.0 + lax.erf(u * math.sqrt(0.5)))
            act = (u * cdf).astype(BF16)
            act_scr[a:b, cols] = act
            slope_scr[a:b, cols] = cdf + u * (
                jnp.exp(-0.5 * u * u) * (1.0 / math.sqrt(2.0 * math.pi))
            )
            sum_scr[a:b, :] += dot_nn(act, w_down[cols, :])
        return carry

    lax.fori_loop(0, chunks, up_step, 0)

    for a, b in blocks:
        ffn = sum_scr[a:b, :] + bias_down
        count_in(4, ffn, a, b)
        normed, inv = norm(one_scr[a:b, :] + ffn)
        ok = valid_ref[a:b, :1]
        put(outc_scr, outq_scr, a, b, (normed * gain_two + shift_two) * ok)
        up = pick(cot_c, cot_q, a, b) * ok
        add_row(4, up * normed)
        add_row(5, up)
        grad = norm_grad(up, normed, inv, gain_two)
        low = grad.astype(BF16)
        add_row(3, low.astype(F32))
        sum_scr[a:b, :] = grad
        grad_scr[a:b, :] = low
    leaving = [
        pltpu.make_async_copy(outc_scr, out_c, out_sems.at[0]),
        pltpu.make_async_copy(outq_scr, out_q, out_sems.at[1]),
    ]
    for copy in leaving:
        copy.start()

    def goes(h):
        return lax.rem(h + core, 2)

    def up_copy(i):
        h, at = i // 2, lax.rem(i, 2) if not isinstance(i, int) else i % 2
        cols = pl.ds(pl.multiple_of(at * COLS, COLS) if not isinstance(i, int) else at * COLS, COLS)
        return pltpu.make_async_copy(
            parts_scr.at[h, :, cols], parts_out.at[goes(h), :, cols], out_sems.at[2 + i]
        )

    down_rows = 2 * shard * (COLS // (2 * shard_down))
    down_cols = pl.ds(half_ff + half, half_ff)

    def down_copy(i, h):
        start = i * down_rows
        rows = pl.ds(start if isinstance(i, int) else pl.multiple_of(start, down_rows), down_rows)
        return pltpu.make_async_copy(
            parts_scr.at[h, rows, down_cols],
            parts_out.at[goes(h), rows, down_cols],
            out_sems.at[2 + chunks * (1 + h) + i],
        )

    def back_step(i, carry):
        cols = pl.ds(pl.multiple_of(i * COLS, COLS), COLS)
        for a, b in blocks:
            low = (
                dot_nt(grad_scr[a:b, :], w_down[cols, :]) * slope_scr[a:b, cols]
            ).astype(BF16)
            pre_scr[a:b, :] = low
            up_out[:, cols] += jnp.sum(low.astype(F32), axis=0, keepdims=True)
            sum_scr[a:b, :] += dot_nt(low, w_up[:, cols])
        at = pl.ds(pl.multiple_of(lax.rem(i, 2) * COLS, COLS), COLS)
        parts_scr[i // 2, :, at] = dot_tn(low_scr[...], pre_scr[...]).astype(BF16)
        up_copy(i).start()
        grads = dot_tn(act_scr[:, cols], grad_scr[...]).astype(BF16)
        for h in range(2):
            for chip in range(COLS // (2 * shard_down)):
                to = pl.ds(pl.multiple_of(i * down_rows, down_rows) + chip * 2 * shard, 2 * shard)
                for g in range(shard_down // shard):
                    row = 2 * shard_down * chip + 2 * shard * g
                    col = half_ff + half * (1 + g)
                    parts_scr[h, to, col : col + half] = grads[
                        row : row + 2 * shard, h * half : (h + 1) * half
                    ]
            down_copy(i, h).start()
        return carry

    lax.fori_loop(0, chunks, back_step, 0)
    leaving += [up_copy(i) for i in range(chunks)]
    leaving += [down_copy(i, h) for i in range(chunks) for h in range(2)]

    for a, b in blocks:
        up = sum_scr[a:b, :]
        normed = norm_scr[a:b, :]
        add_row(1, up * normed)
        add_row(2, up)
        grad = norm_grad(up, normed, inv_scr[a:b, :1], gain_one)
        low = grad.astype(BF16)
        add_row(0, low.astype(F32))
        put(res_c, res_q, a, b, grad)
        grad_scr[a:b, :] = low
    for t in range(seqs):
        rows = slice(t * wide, (t + 1) * wide)
        part = w_out[rows, :]
        gctx_c[t] = dot_nt(part, grad_scr[:length, :]).astype(BF16)
        gctx_q[t] = dot_nt(grad_scr[length:, :], part).astype(BF16)
        grads = (
            dot_nn(ctx_c[t], grad_scr[:length, :]) + dot_tn(ctx_q[t], grad_scr[length:, :])
        ).astype(BF16)
        for h in range(2):
            parts_scr[h, rows, half_ff : half_ff + half] = grads[:, h * half : (h + 1) * half]
    last = 2 + 3 * chunks
    for h in range(2):
        tail = pl.ds(half_ff, half)
        leaving.append(
            pltpu.make_async_copy(
                parts_scr.at[h, :, tail], parts_out.at[goes(h), :, tail], out_sems.at[last + h]
            )
        )
        leaving[-1].start()
    sums_ref[...] = jnp.broadcast_to(jnp.sum(sq_scr[...], axis=1, keepdims=True), sums_ref.shape)
    for copy in leaving:
        copy.wait()


def mid_call(ctx_c, ctx_q, x_c, x_q, cot_c, cot_q, valid, six, bias_up, planes, preds):
    seqs, wide, length = ctx_c.shape
    count = ctx_q.shape[1]
    total = length + count
    uo_own, uo_mate, down_own, down_mate = planes
    chips, shard, cols = uo_own.shape
    ff = cols - COLS
    chunks = ff // COLS
    vm = pl.BlockSpec(memory_space=pltpu.VMEM)
    anywhere = pl.BlockSpec(memory_space=pl.ANY)
    parts = jax.ShapeDtypeStruct((2, COLS, (cols + ff) // 2), BF16)
    return pl.pallas_call(
        functools.partial(mid_kernel, seqs, FWD_BITS_UP, FWD_BITS_DOWN),
        out_shape=(
            jax.ShapeDtypeStruct(x_c.shape, F32),
            jax.ShapeDtypeStruct(x_q.shape, F32),
            jax.ShapeDtypeStruct(ctx_c.shape, BF16),
            jax.ShapeDtypeStruct(ctx_q.shape, BF16),
            jax.ShapeDtypeStruct((6, COLS), F32),
            jax.ShapeDtypeStruct((1, ff), F32),
            jax.ShapeDtypeStruct((8, 128), F32),
            jax.ShapeDtypeStruct(x_c.shape, F32),
            jax.ShapeDtypeStruct((preds, COLS), F32),
            parts,
        ),
        in_specs=[vm] * 9 + [anywhere] * 4,
        out_specs=(vm,) * 7 + (anywhere,) * 3,
        scratch_shapes=[
            pltpu.VMEM((COLS, ff), BF16),
            pltpu.VMEM((COLS, COLS), BF16),
            pltpu.VMEM((ff, COLS), BF16),
            pltpu.VMEM((total, COLS), F32),
            pltpu.VMEM((total, COLS), F32),
            pltpu.VMEM((total, 128), F32),
            pltpu.VMEM((total, COLS), BF16),
            pltpu.VMEM((total, ff), BF16),
            pltpu.VMEM((total, ff), F32),
            pltpu.VMEM((total, COLS), F32),
            pltpu.VMEM((total, COLS), BF16),
            pltpu.VMEM((total, COLS), BF16),
            pltpu.VMEM((2, 2, chips, shard, COLS), BF16),
            pltpu.VMEM(x_c.shape, F32),
            pltpu.VMEM((preds, COLS), F32),
            pltpu.VMEM(parts.shape, BF16),
            pltpu.VMEM((8, COLS), F32),
            pltpu.SemaphoreType.DMA((2 * chips,)),
            pltpu.SemaphoreType.DMA((2, 2)),
            pltpu.SemaphoreType.DMA((4 + 3 * chunks,)),
        ],
        compiler_params=pltpu.CompilerParams(vmem_limit_bytes=63 << 20),
        cost_estimate=cost_of(45),
        name="feed_forward",
    )(ctx_c, ctx_q, x_c, x_q, cot_c, cot_q, valid, six, bias_up, *planes)


def proj_kernel(own, keys, x_ref, w_ref, bq_ref, bv_ref, qt_ref, q_ref, k_ref, kt_ref, v_ref, vt_ref):
    wide = own * HEAD_DIM
    rows = x_ref.shape[0]
    for a in range(0, rows, 256):
        b = min(a + 256, rows)
        parts = [(0, bq_ref, qt_ref, q_ref)]
        if b <= keys:
            parts += [(1, None, kt_ref, k_ref), (2, bv_ref, vt_ref, v_ref)]
        y = dot_nn(x_ref[a:b, :], w_ref[:, : len(parts) * wide])
        for n, bias, flat_ref, head_ref in parts:
            part = y[:, n * wide : (n + 1) * wide]
            if bias is not None:
                part = part + bias[...]
            flat_ref[:, a:b] = part.T.astype(BF16)
            for h in range(own):
                head_ref[h, a:b, :] = part[:, h * HEAD_DIM : (h + 1) * HEAD_DIM].astype(BF16)


def proj_call(own, keys, x, w, bq, bv):
    rows = x.shape[0]
    wide = own * HEAD_DIM
    vm = pl.BlockSpec(memory_space=pltpu.VMEM)
    flat = lambda n: jax.ShapeDtypeStruct((wide, n), BF16)
    head = lambda n: jax.ShapeDtypeStruct((own, n, HEAD_DIM), BF16)
    return pl.pallas_call(
        functools.partial(proj_kernel, own, keys),
        out_shape=(flat(rows), head(rows), head(keys), flat(keys), head(keys), flat(keys)),
        in_specs=[vm] * 4,
        out_specs=(vm,) * 6,
        compiler_params=pltpu.CompilerParams(vmem_limit_bytes=40 << 20),
        cost_estimate=cost_of(5),
        name="project",
    )(x, w, bq, bv)


def grads_kernel(
    keys,
    x_ref,
    w_ref,
    dq_ref,
    dk_ref,
    dv_ref,
    gc_ref,
    gq_ref,
    gw_ref,
    sum_ref,
    part_scr,
):
    wide = dq_ref.shape[1]
    seqs, length = gc_ref.shape[:2]
    shard = gw_ref.shape[2]
    for n, ref in enumerate((dq_ref, dk_ref, dv_ref)):
        part_scr[...] = dot_tn(x_ref[: ref.shape[0], :], ref[...])
        for j in range(gw_ref.shape[0]):
            gw_ref[j, n] = part_scr[j * shard : (j + 1) * shard, :].astype(BF16)
    sum_ref[...] = jnp.zeros(sum_ref.shape, F32)
    sum_ref[0:1, :] = jnp.sum(dq_ref[...].astype(F32), axis=0, keepdims=True)
    sum_ref[1:2, :] = jnp.sum(dv_ref[...].astype(F32), axis=0, keepdims=True)
    w_q = w_ref[:, :wide]
    w_k = w_ref[:, wide : 2 * wide]
    w_v = w_ref[:, 2 * wide :]
    step = 256
    for t in range(seqs):
        for a in range(0, length, step):
            at = slice(t * length + a, t * length + a + step)
            gc_ref[t, a : a + step, :] = (
                dot_nt(dq_ref[at, :], w_q) + dot_nt(dk_ref[at, :], w_k) + dot_nt(dv_ref[at, :], w_v)
            ).astype(BF16)
    count = gq_ref.shape[1]
    for t in range(seqs):
        at = slice(keys + t * count, keys + (t + 1) * count)
        gq_ref[t] = dot_nt(dq_ref[at, :], w_q).astype(BF16)


def grads_call(seqs, length, count, blocks, x, w, dq, dk, dv):
    wide = dq.shape[1]
    shard = x.shape[1] // blocks
    vm = pl.BlockSpec(memory_space=pltpu.VMEM)
    return pl.pallas_call(
        functools.partial(grads_kernel, seqs * length),
        out_shape=(
            jax.ShapeDtypeStruct((seqs, length, x.shape[1]), BF16),
            jax.ShapeDtypeStruct((seqs, count, x.shape[1]), BF16),
            jax.ShapeDtypeStruct((blocks, 3, shard, wide), BF16),
            jax.ShapeDtypeStruct((8, wide), F32),
        ),
        in_specs=[vm] * 5,
        out_specs=(vm,) * 4,
        scratch_shapes=[pltpu.VMEM((x.shape[1], wide), F32)],
        compiler_params=pltpu.CompilerParams(vmem_limit_bytes=40 << 20),
        cost_estimate=cost_of(6),
        name="weight_grads",
    )(x, w, dq, dk, dv)


MESH = pl.DeviceIdType.MESH
ROWS_Q = 384
SLOT_Q = 80


def signal_peers(dp, s, dps, seqs):
    barrier = pltpu.get_barrier_semaphore()
    for r in range(1, dps):
        pl.semaphore_signal(
            barrier, inc=1, device_id=(lax.rem(dp + r, dps), s), device_id_type=MESH
        )
    for r in range(1, seqs):
        pl.semaphore_signal(
            barrier, inc=1, device_id=(dp, lax.rem(s + r, seqs)), device_id_type=MESH
        )
    pl.semaphore_wait(barrier, dps - 1 + seqs - 1)


def remote(src, dst, send_sem, recv_sem, k, device):
    return pltpu.make_async_remote_copy(
        src_ref=src,
        dst_ref=dst,
        send_sem=send_sem.at[k],
        recv_sem=recv_sem.at[k],
        device_id=device,
        device_id_type=MESH,
    )


def start_kernel(
    dps,
    seqs,
    rc_ref,
    rq_ref,
    zero_ref,
    w_ref,
    v_ref,
    i_ref,
    x_out,
    w_out,
    v_out,
    i_out,
    send_sem,
    recv_sem,
    here_sem,
):
    dp = lax.axis_index("dp")
    s = lax.axis_index("seq")
    length = rc_ref.shape[0]
    count = rq_ref.shape[0]
    mate = s + 1 - 2 * lax.rem(s, 2)
    across = lax.rem(s + 2, seqs)
    signal_peers(dp, s, dps, seqs)

    def spot_c(owner):
        return x_out.at[pl.ds(pl.multiple_of(owner * length, length), length)]

    def spot_q(owner):
        start = seqs * length + owner * count
        return x_out.at[pl.ds(pl.multiple_of(start, 16), count)]

    k = 0
    small = []
    for r in range(1, seqs):
        to = lax.rem(s + r, seqs)
        for src, dst in (
            (w_ref.at[to], w_out.at[dp, s]),
            (v_ref, v_out.at[dp, s]),
            (i_ref, i_out.at[s]),
        ):
            small.append(remote(src, dst, send_sem, recv_sem, k, (dp, to)))
            k += 1
    for copy in small:
        copy.start()
    near, far = [], []
    for src, spot in ((rc_ref, spot_c), (rq_ref, spot_q)):
        far.append(remote(src, spot(s), send_sem, recv_sem, k, (dp, across)))
        near.append(remote(src, spot(s), send_sem, recv_sem, k + 1, (dp, mate)))
        k += 2
    for copy in far + near:
        copy.start()
    here = [
        pltpu.make_async_copy(w_ref.at[s], w_out.at[dp, s], here_sem.at[0]),
        pltpu.make_async_copy(v_ref, v_out.at[dp, s], here_sem.at[1]),
        pltpu.make_async_copy(i_ref, i_out.at[s], here_sem.at[2]),
        pltpu.make_async_copy(rc_ref, spot_c(s), here_sem.at[3]),
        pltpu.make_async_copy(rq_ref, spot_q(s), here_sem.at[4]),
        pltpu.make_async_copy(
            zero_ref,
            x_out.at[pl.ds(seqs * (length + count), zero_ref.shape[0])],
            here_sem.at[5],
        ),
    ]
    for copy in here:
        copy.start()
    for copy in small:
        copy.wait_recv()
    for copy in here:
        copy.wait()
    wide = []
    for r in range(1, dps):
        to = lax.rem(dp + r, dps)
        for ref in (w_out, v_out):
            wide.append(remote(ref.at[dp], ref.at[dp], send_sem, recv_sem, k, (to, s)))
            k += 1
    for copy in wide:
        copy.start()
    pass_on = []
    for copy, spot in zip(far, (spot_c, spot_q)):
        copy.wait_recv()
        pass_on.append(
            remote(spot(across), spot(across), send_sem, recv_sem, k, (dp, mate))
        )
        pass_on[-1].start()
        k += 1
    for copy in small + far:
        copy.wait_send()
    for copy in near + wide + pass_on:
        copy.wait()


def start_call(dps, seqs, rc, rq, w, v, ints):
    copies = 3 * (seqs - 1) + 4 + 2 * (dps - 1) + 2
    zero = jnp.zeros((ROWS_Q - seqs * rq.shape[0], rc.shape[1]), BF16)
    rows = seqs * rc.shape[0] + ROWS_Q
    vmem = pl.BlockSpec(memory_space=pltpu.VMEM)
    return pl.pallas_call(
        functools.partial(start_kernel, dps, seqs),
        out_shape=(
            jax.ShapeDtypeStruct((rows, rc.shape[1]), BF16),
            jax.ShapeDtypeStruct((dps,) + w.shape, BF16),
            jax.ShapeDtypeStruct((dps, seqs) + v.shape, F32),
            jax.ShapeDtypeStruct((seqs,) + ints.shape, jnp.int32),
        ),
        in_specs=[vmem] * 6,
        out_specs=(vmem,) * 4,
        scratch_shapes=[
            pltpu.SemaphoreType.DMA((copies,)),
            pltpu.SemaphoreType.DMA((copies,)),
            pltpu.SemaphoreType.DMA((6,)),
        ],
        compiler_params=pltpu.CompilerParams(collective_id=0, has_side_effects=True),
        cost_estimate=cost_of(35),
        name="gather_rows",
    )(rc, rq, zero, w, v, ints)


def swap_kernel(seqs, c_of, q_of, c_ref, q_ref, c_out, q_out, send_sem, recv_sem, here_sem):
    dp = lax.axis_index("dp")
    s = lax.axis_index("seq")
    signal_peers(dp, s, 1, seqs)
    copies = []
    for r in range(1, seqs):
        to = lax.rem(s + r, seqs)
        k = 2 * (r - 1)
        copies.append(remote(c_of(c_ref, to), c_out.at[s], send_sem, recv_sem, k, (dp, to)))
        copies.append(remote(q_of(q_ref, to), q_out.at[s], send_sem, recv_sem, k + 1, (dp, to)))
    for copy in copies:
        copy.start()
    here = [
        pltpu.make_async_copy(c_of(c_ref, s), c_out.at[s], here_sem.at[0]),
        pltpu.make_async_copy(q_of(q_ref, s), q_out.at[s], here_sem.at[1]),
    ]
    for copy in here:
        copy.start()
    for copy in here + copies:
        copy.wait()


def swap_call(seqs, c, q, c_of, q_of, c_shape, q_shape, ident, name):
    vmem = pl.BlockSpec(memory_space=pltpu.VMEM)
    return pl.pallas_call(
        functools.partial(swap_kernel, seqs, c_of, q_of),
        out_shape=(
            jax.ShapeDtypeStruct((seqs,) + c_shape, c.dtype),
            jax.ShapeDtypeStruct((seqs,) + q_shape, q.dtype),
        ),
        in_specs=[vmem] * 2,
        out_specs=(vmem,) * 2,
        scratch_shapes=[
            pltpu.SemaphoreType.DMA((2 * (seqs - 1),)),
            pltpu.SemaphoreType.DMA((2 * (seqs - 1),)),
            pltpu.SemaphoreType.DMA((2,)),
        ],
        compiler_params=pltpu.CompilerParams(collective_id=ident, has_side_effects=True),
        cost_estimate=cost_of(12),
        name=name,
    )(c, q)


def end_kernel(
    dps,
    seqs,
    gc_ref,
    gq_ref,
    w_ref,
    v_ref,
    gc_out,
    gq_out,
    w_out,
    v_out,
    c_mate,
    q_mate,
    c_far,
    q_far,
    c_send,
    q_send,
    w_got,
    v_got,
    w_sum,
    v_sum,
    v_last,
    send_sem,
    recv_sem,
):
    dp = lax.axis_index("dp")
    s = lax.axis_index("seq")
    core = lax.rem(s, 2)
    mate = s + 1 - 2 * core
    across = lax.rem(s + 2, seqs)
    signal_peers(dp, s, dps, seqs)
    k = 0
    first = []
    for i in range(2):
        to = lax.rem(mate + 2 * (1 - i), seqs)
        for src, dst in ((gc_ref, c_mate), (gq_ref, q_mate)):
            first.append(remote(src.at[to], dst.at[i], send_sem, recv_sem, k, (dp, mate)))
            k += 1
    wide = []
    for r in range(1, dps):
        to = lax.rem(dp + r, dps)
        for src, dst in ((w_ref, w_got), (v_ref, v_got)):
            wide.append(remote(src.at[to], dst.at[r - 1], send_sem, recv_sem, k, (to, s)))
            k += 1
    for copy in first + wide:
        copy.start()

    def each(ref, step, fn):
        def body(i, carry):
            fn(pl.ds(pl.multiple_of(i * step, step), step))
            return carry

        lax.fori_loop(0, ref.shape[-2] // step, body, 0)

    cross = []
    for (src, got, buf, far, copy) in (
        (gc_ref, c_mate, c_send, c_far, first[0]),
        (gq_ref, q_mate, q_send, q_far, first[1]),
    ):
        copy.wait_recv()

        def add(rows, src=src, got=got, buf=buf):
            buf[rows, :] = (
                src[across, rows, :].astype(F32) + got[0, rows, :].astype(F32)
            ).astype(BF16)

        each(buf, 16, add)
        cross.append(remote(buf, far, send_sem, recv_sem, k, (dp, across)))
        cross[-1].start()
        k += 1
    for copy in wide:
        copy.wait_recv()

    def add_w(rows):
        for t in range(seqs):
            total = w_ref[dp, t, rows, :].astype(F32)
            for r in range(1, dps):
                total += w_got[r - 1, t, rows, :].astype(F32)
            w_sum[t, rows, :] = total

    each(w_sum, 8, add_w)
    total = v_ref[dp]
    for r in range(1, dps):
        total += v_got[r - 1]
    v_sum[...] = total
    last = []
    for r in range(1, seqs):
        to = lax.rem(s + r, seqs)
        last.append(remote(w_sum.at[to], w_out.at[s], send_sem, recv_sem, k, (dp, to)))
        last.append(remote(v_sum.at[to], v_last.at[r - 1], send_sem, recv_sem, k + 1, (dp, to)))
        k += 2
    for copy in last:
        copy.start()
    w_out[s] = w_sum[s]
    for copy in first[2:]:
        copy.wait_recv()
    for copy in cross:
        copy.wait_recv()
    for (src, got, far, out) in (
        (gc_ref, c_mate, c_far, gc_out),
        (gq_ref, q_mate, q_far, gq_out),
    ):

        def total_of(rows, src=src, got=got, far=far, out=out):
            out[rows, :] = (
                src[s, rows, :].astype(F32)
                + got[1, rows, :].astype(F32)
                + far[rows, :].astype(F32)
            )

        each(out, 16, total_of)
    for copy in last:
        copy.wait_recv()
    total = v_sum[s]
    for r in range(1, seqs):
        total += v_last[r - 1]
    v_out[...] = total
    for copy in first + wide + cross + last:
        copy.wait_send()


def end_call(dps, seqs, gc, gq, w, v):
    copies = 4 + 2 * (dps - 1) + 2 + 2 * (seqs - 1)
    vm = pl.BlockSpec(memory_space=pltpu.VMEM)
    cshape, qshape, wshape, vshape = gc.shape[1:], gq.shape[1:], w.shape[1:], v.shape[1:]
    return pl.pallas_call(
        functools.partial(end_kernel, dps, seqs),
        out_shape=(
            jax.ShapeDtypeStruct(cshape, F32),
            jax.ShapeDtypeStruct(qshape, F32),
            jax.ShapeDtypeStruct(wshape, F32),
            jax.ShapeDtypeStruct(vshape[1:], F32),
        ),
        in_specs=[vm] * 4,
        out_specs=(vm,) * 4,
        scratch_shapes=[
            pltpu.VMEM((2,) + cshape, BF16),
            pltpu.VMEM((2,) + qshape, BF16),
            pltpu.VMEM(cshape, BF16),
            pltpu.VMEM(qshape, BF16),
            pltpu.VMEM(cshape, BF16),
            pltpu.VMEM(qshape, BF16),
            pltpu.VMEM((dps - 1,) + wshape, BF16),
            pltpu.VMEM((dps - 1,) + vshape, F32),
            pltpu.VMEM(wshape, F32),
            pltpu.VMEM(vshape, F32),
            pltpu.VMEM((seqs - 1,) + vshape[1:], F32),
            pltpu.SemaphoreType.DMA((copies,)),
            pltpu.SemaphoreType.DMA((copies,)),
        ],
        compiler_params=pltpu.CompilerParams(
            collective_id=3, has_side_effects=True, vmem_limit_bytes=50 << 20
        ),
        cost_estimate=cost_of(30),
        name="sum_rows",
    )(gc, gq, w, v)


def flip_perm(count, bit):
    return [(i, i ^ bit) for i in range(count)]


AXES = ("dp", "seq")


def tie(values, *others):
    return lax.optimization_barrier((values, others))[0]


def give_to(cur, count, bit):
    return lax.ppermute(cur, AXES, flip_perm(count, bit))


def pile(cur, got, bit):
    mine = (lax.axis_index(AXES) // bit) % 2
    return jnp.where(mine == 0, jnp.concatenate([cur, got]), jnp.concatenate([got, cur]))


def local_fast(
    content,
    query_stream,
    segment_ids,
    pad_mask,
    predicted,
    order,
    rel_bucket,
    qkv_weight,
    qv_bias,
    out_weight,
    out_bias,
    attn_gain,
    attn_shift,
    up_weight,
    up_bias,
    down_weight,
    down_bias,
    ffn_gain,
    ffn_shift,
    rel_table,
    content_cot,
    query_cot,
):
    dps, seqs = lax.axis_size("dp"), lax.axis_size("seq")
    count = dps * seqs
    s = lax.axis_index("seq")
    own = HEADS // seqs
    wide = own * HEAD_DIM
    length = content.shape[1]
    preds = query_stream.shape[1]
    pad_q = SLOT_Q - preds
    shard = qkv_weight.shape[0]

    x_q = jnp.pad(query_stream[0], ((0, pad_q), (0, 0)))
    vec = jnp.concatenate(
        [
            member.astype(F32)
            for member in (
                qv_bias,
                up_bias,
                out_bias,
                attn_gain,
                attn_shift,
                down_bias,
                ffn_gain,
                ffn_shift,
            )
        ]
    )
    vec = jnp.pad(vec, (0, 1024 - vec.shape[0])).reshape(8, 128)
    ints = jnp.stack(
        [
            segment_ids[0],
            order[0],
            pad_mask[0],
            jnp.pad(predicted[0], (0, length - preds), constant_values=-1),
        ]
    )
    ints = jnp.pad(ints, ((0, 4), (0, 0)))
    w_parts = jnp.transpose(
        qkv_weight.reshape(shard, 3, seqs, wide), (2, 0, 1, 3)
    ).reshape(seqs, shard, 3 * wide)
    gather = (jnp.concatenate([up_weight, out_weight], axis=1)[None], down_weight[None])
    stages = list(zip(FWD_BITS_UP, FWD_BITS_DOWN))

    def launch(n):
        return tuple(give_to(cur, count, bit) for cur, bit in zip(gather, stages[n]))

    def land(n, got, *others):
        got = tie(got, *others)
        return tuple(pile(c, g, bit) for c, g, bit in zip(gather, got, stages[n]))

    flying = launch(0)
    x_all, w_all, v_all, i_all = start_call(
        dps, seqs, content[0].astype(BF16), x_q.astype(BF16), w_parts, vec, ints
    )
    w_qkv = w_all.reshape(MODEL_WIDTH, 3 * wide)
    parts_all = v_all.reshape(count, 1024)
    n_qv, n_up, n_one = qv_bias.shape[0], up_bias.shape[0], out_bias.shape[0]
    cut_up, cut_end = n_qv + n_up, n_qv + n_up + 6 * n_one
    bias_qv = parts_all[:, :n_qv].reshape(count * n_qv)
    bias_up = parts_all[:, n_qv:cut_up].reshape(1, count * n_up)
    six = jnp.transpose(parts_all[:, cut_up:cut_end].reshape(count, 6, n_one), (1, 0, 2)).reshape(
        6, count * n_one
    )
    seg_all = i_all[:, 0].reshape(seqs * length)
    order_all = i_all[:, 1].reshape(seqs * length)
    pad_all = i_all[:, 2].reshape(seqs * length)
    pred_all = i_all[:, 3, :SLOT_Q].reshape(seqs * SLOT_Q)

    gather = land(0, flying, i_all)
    flying = launch(1)
    rev, fold = bias_inputs(rel_bucket, rel_table, s * own, own)
    rev, fold = tie((rev, fold), gather)
    hot, hot_t, shift = query_place(pred_all, ROWS_Q)
    rseg, rlim, kmeta, span = row_meta(seg_all, pad_all, order_all, pred_all, ROWS_Q)
    tiles, qbias = bias_call(rev, fold, hot, shift)

    bq = lax.dynamic_slice_in_dim(bias_qv[:MODEL_WIDTH], s * wide, wide)
    bv = lax.dynamic_slice_in_dim(bias_qv[MODEL_WIDTH:], s * wide, wide)
    gather = land(1, flying, tiles)
    flying = launch(2)
    x_all = tie(x_all, gather)
    q_t, q3, k3, k_t, v3, v_t = proj_call(
        own, seqs * length, x_all, w_qkv, bq[None], bv[None]
    )
    gather = land(2, flying, q_t)
    flying = launch(3)
    q_t = tie(q_t, gather)

    ctx_t, ctx_rows, lse = fwd_call(span, q_t, k3, v_t, kmeta, rseg, rlim, tiles, qbias)

    gather = land(3, flying, ctx_rows)
    others = tuple(give_to(cur, count, 1) for cur in gather)
    ctx_rows = tie(ctx_rows, gather)
    planes = (gather[0], others[0], gather[1], others[1])

    def from_lanes(ref, t):
        return ref.at[:, pl.ds(pl.multiple_of(t * length, length), length)]

    def from_query(ref, t):
        return ref.at[pl.ds(pl.multiple_of(t * SLOT_Q, 16), SLOT_Q)]

    ctx_c, ctx_q = swap_call(
        seqs,
        ctx_t,
        ctx_rows,
        from_lanes,
        from_query,
        (wide, length),
        (SLOT_Q, wide),
        1,
        "swap_context",
    )
    pad_float = pad_mask[0].astype(F32)
    valid = jnp.concatenate([pad_float, jnp.ones((preds,), F32), jnp.zeros((pad_q,), F32)])
    valid = jnp.broadcast_to(valid[:, None], (length + SLOT_Q, 128))
    (
        res_c,
        res_q,
        give_c,
        give_q,
        six_sums,
        up_sums,
        squares,
        out_c,
        out_q,
        parts,
    ) = mid_call(
        ctx_c,
        ctx_q,
        content[0],
        x_q,
        content_cot[0],
        jnp.pad(query_cot[0], ((0, pad_q), (0, 0))),
        valid,
        six,
        bias_up,
        planes,
        preds,
    )
    core = s % 2
    spot = (lax.axis_index(AXES) // 2) % 4
    flying = give_to(parts[1], count, 1)

    def both(mine, got):
        total = mine[0].astype(F32) + got.astype(F32)
        return total.astype(BF16).reshape((2, 2, 4, mine.shape[1] // 16, mine.shape[2]))

    def block(x, index):
        return lax.dynamic_index_in_dim(x, index, 2, keepdims=False)

    local_sums = jnp.concatenate([squares[:6, 0], jnp.sum(pad_float)[None]])

    def from_slot(ref, t):
        return ref.at[t]

    g_c, g_q = swap_call(
        seqs,
        give_c,
        give_q,
        from_slot,
        from_slot,
        (wide, length),
        (SLOT_Q, wide),
        2,
        "swap_grads",
    )
    flying = tie(flying, g_c)
    pairs = both(parts, flying)
    gone = tuple(block(pairs, spot ^ r) for r in (1, 2, 3))
    flying = tuple(give_to(x, count, 2 * r) for x, r in zip(gone, (1, 2, 3)))
    stay = block(pairs, spot)
    g_c = tie(g_c, stay, gone)
    dq, dk, dv, offs, qoffs = bwd_call(
        span,
        q_t,
        q3,
        k3,
        k_t,
        v3,
        ctx_t,
        g_c,
        g_q.reshape(seqs * SLOT_Q, wide),
        lse,
        kmeta,
        rseg,
        rlim,
        tiles,
        qbias,
        hot_t,
        shift,
    )
    table = table_sums(offs, qoffs, rel_bucket)
    flying = tie(flying, dq)

    def total_of(kept, got):
        total = kept.astype(F32)
        for x in got:
            total += x.astype(F32)
        return total

    def split(x, bit):
        mine = (lax.axis_index(AXES) // bit) % 2
        axis = x.ndim - 3
        away = lax.dynamic_index_in_dim(x, 1 - mine, axis, keepdims=False).astype(BF16)
        return away, lax.dynamic_index_in_dim(x, mine, axis, keepdims=False)

    gone, stay = split(total_of(stay, flying), 8)
    flying = give_to(gone, count, 8)
    dq = tie(dq, stay, gone)
    grad_c, grad_q, grad_w, qv_sums = grads_call(
        seqs, length, SLOT_Q, count, x_all, w_qkv, dq, dk, dv
    )
    spot = jnp.zeros((2, MODEL_WIDTH), F32)
    grad_bias_qv = lax.dynamic_update_slice(
        spot, qv_sums[:2], (0, s * wide)
    ).reshape(2 * MODEL_WIDTH)
    table_all = lax.dynamic_update_slice(
        jnp.zeros((BUCKETS, HEADS), F32), table, (0, s * own)
    )
    owned = jnp.concatenate(
        [
            member.reshape(count, -1)
            for member in (
                grad_bias_qv,
                up_sums,
                jnp.transpose(six_sums.reshape(6, count, n_one), (1, 0, 2)),
            )
        ],
        axis=1,
    )
    used = owned.shape[1]
    shared = jnp.concatenate([table_all.reshape(-1), local_sums])
    vec_grads = jnp.concatenate(
        [
            owned,
            jnp.broadcast_to(shared[None, :], (count, shared.shape[0])),
            jnp.zeros((count, 1024 - used - shared.shape[0]), F32),
        ],
        axis=1,
    ).reshape(dps, seqs, 8, 128)
    flying = tie(flying, grad_c)
    gone, stay = split(total_of(stay, (flying,)), 16)
    flying = give_to(gone, count, 16)
    grad_c = tie(grad_c, stay, gone)
    sum_c, sum_q, sum_w, sum_v = end_call(
        dps,
        seqs,
        grad_c,
        grad_q,
        grad_w.reshape(dps, seqs, 3 * shard, wide),
        vec_grads,
    )
    flying = tie(flying, sum_c)
    pair = total_of(stay, (flying,))
    half_ff, half = up_weight.shape[1] // 2, MODEL_WIDTH // 2
    wide_up = half_ff + half
    first, second = pair[:shard], pair[shard:]
    low_cols, high_cols = pair[:, wide_up : wide_up + half_ff // 2], pair[:, wide_up + half_ff // 2 :]

    def pick(a, b):
        return jnp.where(core == 0, a, b), jnp.where(core == 0, b, a)

    rows_mine, rows_away = pick(first[:, :wide_up], second[:, :wide_up])
    cols_mine, cols_away = pick(low_cols, high_cols)
    rows_got = give_to(rows_away, count, 1)
    cols_got = give_to(cols_away, count, 1)
    rows_low, rows_high = pick(rows_mine, rows_got)
    grad_up_own = jnp.concatenate([rows_low[:, :half_ff], rows_high[:, :half_ff]], axis=1)
    grad_out_own = jnp.concatenate([rows_low[:, half_ff:], rows_high[:, half_ff:]], axis=1)

    def unfold(x):
        return jnp.concatenate([x[:, :half], x[:, half:]], axis=0)

    cols_low, cols_high = pick(unfold(cols_mine), unfold(cols_got))
    grad_down_own = jnp.concatenate([cols_low, cols_high], axis=1)
    grad_content = res_c + sum_c
    grad_query = res_q[:preds] + sum_q[:preds]
    grad_qkv_own = jnp.transpose(sum_w.reshape(seqs, 3, shard, wide), (2, 1, 0, 3)).reshape(
        shard, 3 * MODEL_WIDTH
    )
    sums = sum_v.reshape(1024)
    at = cut_end
    mine = [sums[:n_qv], sums[n_qv:cut_up]]
    mine += [sums[cut_up + i * n_one : cut_up + (i + 1) * n_one] for i in range(6)]
    table_sum = sums[at : at + BUCKETS * HEADS].reshape(BUCKETS, HEADS)
    totals = sums[at + BUCKETS * HEADS : at + BUCKETS * HEADS + 7]
    content_count = totals[6] * MODEL_WIDTH
    query_count = float(dps * preds * seqs * MODEL_WIDTH)
    each = jnp.stack([content_count, jnp.float32(query_count)])
    stats = jnp.sqrt(totals[:6] / jnp.concatenate([each, each, each]))
    return (
        out_c[None],
        out_q[None],
        grad_content[None],
        grad_query[None],
        grad_qkv_own,
        mine[0],
        grad_out_own,
        mine[2],
        mine[3],
        mine[4],
        grad_up_own,
        mine[1],
        grad_down_own,
        mine[5],
        mine[6],
        mine[7],
        table_sum,
        stats,
    )


def pick_local(mesh):
    sizes = dict(mesh.shape)
    return local_fast if (sizes["dp"], sizes["seq"]) == (8, 4) else local_general


def solution(mesh):
    in_specs = (
        P("dp", "seq", None),
        P("dp", "seq", None),
        P("dp", "seq"),
        P("dp", "seq"),
        P("dp", "seq"),
        P("dp", "seq"),
        P(),
        P(("dp", "seq"), None),
        P(("dp", "seq")),
        P(("dp", "seq"), None),
        P(("dp", "seq")),
        P(("dp", "seq")),
        P(("dp", "seq")),
        P(("dp", "seq"), None),
        P(("dp", "seq")),
        P(("dp", "seq"), None),
        P(("dp", "seq")),
        P(("dp", "seq")),
        P(("dp", "seq")),
        P(),
        P("dp", "seq", None),
        P("dp", "seq", None),
    )
    out_specs = (
        P("dp", "seq", None),
        P("dp", "seq", None),
        P("dp", "seq", None),
        P("dp", "seq", None),
        P(("dp", "seq"), None),
        P(("dp", "seq")),
        P(("dp", "seq"), None),
        P(("dp", "seq")),
        P(("dp", "seq")),
        P(("dp", "seq")),
        P(("dp", "seq"), None),
        P(("dp", "seq")),
        P(("dp", "seq"), None),
        P(("dp", "seq")),
        P(("dp", "seq")),
        P(("dp", "seq")),
        P(),
        P(),
    )
    local = pick_local(mesh)
    return jax.shard_map(local, mesh=mesh, in_specs=in_specs, out_specs=out_specs, check_vma=False)
```

```python
import functools
import math

import jax
import jax.numpy as jnp
from jax import lax
from jax.experimental import pallas as pl
from jax.experimental.pallas import tpu as pltpu
from jax.sharding import PartitionSpec as P

MODEL_WIDTH = 768
HEADS = 12
HEAD_DIM = 64
BUCKETS = 32
SEQ_LEN = 2048


EPS = 1e-05
NEG = -1000000000.0
SCALE = 0.125


def exact_gelu(values):
    return jax.nn.gelu(values, approximate=False)


def norm_fwd(residual, gain_vec, shift_vec):
    row_mean = jnp.mean(residual, axis=-1, keepdims=True)
    centered = residual - row_mean
    inv_std = lax.rsqrt(jnp.mean(centered * centered, axis=-1, keepdims=True) + EPS)
    normed = centered * inv_std
    return (normed * gain_vec + shift_vec, normed, inv_std)


def norm_back(upstream, normed, inv_std, gain_vec):
    grad_norm = upstream * gain_vec
    projected = jnp.mean(grad_norm, axis=-1, keepdims=True) + normed * jnp.mean(
        grad_norm * normed, axis=-1, keepdims=True
    )
    return (
        inv_std * (grad_norm - projected),
        jnp.sum(upstream * normed, axis=(0, 1)),
        jnp.sum(upstream, axis=(0, 1)),
    )


def bucket_edges(rel_bucket):
    entry_count = rel_bucket.shape[0]
    matches = rel_bucket[None, :] == jnp.arange(BUCKETS, dtype=jnp.int32)[:, None]
    places = jnp.arange(entry_count, dtype=jnp.int32)[None, :]
    starts = jnp.min(jnp.where(matches, places, entry_count), axis=1)
    counts = jnp.sum(matches.astype(jnp.int32), axis=1)
    return (starts, starts + counts)


def build_mask(
    query_pos, query_seg, query_limit, content_row, key_pos, key_seg, key_order, key_pad
):
    inside = (
        (query_seg[:, None] == key_seg[None, :])
        & (key_pad[None, :] == 1)
        & (key_order[None, :] <= query_limit[:, None])
    )
    itself = (key_pos[None, :] == query_pos[:, None]) & content_row[:, None]
    return (inside | itself, key_pos[None, :] - query_pos[:, None] + (SEQ_LEN - 1))


def masked_scores(query_heads, key_heads, table_low, edges, allowed, offsets):
    raw_scores = (
        jnp.einsum("rhd,lhd->hrl", query_heads, key_heads, preferred_element_type=jnp.float32)
        * SCALE
    )
    starts, ends = edges
    spread = offsets[..., None]
    onehot = ((spread >= starts) & (spread < ends)).astype(jnp.bfloat16)
    bias = jnp.einsum("rlb,bh->hrl", onehot, table_low, preferred_element_type=jnp.float32)
    return (jnp.where(allowed[None], raw_scores + bias, NEG), onehot)


def attend_forward(packed, table_low, edges, content_row):
    queries, key_values, key_seg, key_order, key_pad, query_pos, query_seg, query_limit = packed
    row_count = queries.shape[0]
    length = key_values.shape[0]
    key_pos = jnp.arange(length, dtype=jnp.int32)
    allowed, offsets = build_mask(
        query_pos, query_seg, query_limit, content_row, key_pos, key_seg, key_order, key_pad
    )
    query_heads = queries.reshape(row_count, HEADS, HEAD_DIM)
    key_heads = key_values[:, :MODEL_WIDTH].reshape(length, HEADS, HEAD_DIM)
    value_heads = key_values[:, MODEL_WIDTH:].reshape(length, HEADS, HEAD_DIM)
    scores, onehot = masked_scores(query_heads, key_heads, table_low, edges, allowed, offsets)
    row_max = jnp.max(scores, axis=-1, keepdims=True)
    expo_vals = jnp.exp(scores - row_max)
    row_total = jnp.sum(expo_vals, axis=-1, keepdims=True)
    probs_low = (expo_vals / row_total).astype(jnp.bfloat16)
    context = jnp.einsum("hrl,lhd->rhd", probs_low, value_heads, preferred_element_type=jnp.float32)
    return (
        context.reshape(row_count, MODEL_WIDTH),
        jnp.transpose((row_max + jnp.log(row_total))[..., 0]),
    )


def attend_backward(packed, table_low, edges, content_row):
    (
        queries,
        key_values,
        key_seg,
        key_order,
        key_pad,
        query_pos,
        query_seg,
        query_limit,
        row_lse,
        grad_context,
    ) = packed
    row_count = queries.shape[0]
    length = key_values.shape[0]
    key_pos = jnp.arange(length, dtype=jnp.int32)
    allowed, offsets = build_mask(
        query_pos, query_seg, query_limit, content_row, key_pos, key_seg, key_order, key_pad
    )
    query_heads = queries.reshape(row_count, HEADS, HEAD_DIM)
    key_heads = key_values[:, :MODEL_WIDTH].reshape(length, HEADS, HEAD_DIM)
    value_heads = key_values[:, MODEL_WIDTH:].reshape(length, HEADS, HEAD_DIM)
    scores, onehot = masked_scores(query_heads, key_heads, table_low, edges, allowed, offsets)
    probs = jnp.exp(scores - jnp.transpose(row_lse)[..., None])
    grad_heads = grad_context.reshape(row_count, HEADS, HEAD_DIM)
    grad_probs = jnp.einsum(
        "rhd,lhd->hrl", grad_heads, value_heads, preferred_element_type=jnp.float32
    )
    row_delta = jnp.sum(probs * grad_probs, axis=-1)
    grad_scores = (probs * (grad_probs - row_delta[..., None])).astype(jnp.bfloat16)
    grad_query = (
        jnp.einsum("hrl,lhd->rhd", grad_scores, key_heads, preferred_element_type=jnp.float32)
        * SCALE
    )
    grad_table = jnp.einsum("hrl,rlb->bh", grad_scores, onehot, preferred_element_type=jnp.float32)
    results = (grad_query.reshape(row_count, MODEL_WIDTH), grad_table, jnp.transpose(row_delta))
    probs_low = probs.astype(jnp.bfloat16)
    grad_key = (
        jnp.einsum("hrl,rhd->lhd", grad_scores, query_heads, preferred_element_type=jnp.float32)
        * SCALE
    )
    grad_value = jnp.einsum(
        "hrl,rhd->lhd", probs_low, grad_heads, preferred_element_type=jnp.float32
    )
    results = results + (
        jnp.concatenate(
            [grad_key.reshape(length, MODEL_WIDTH), grad_value.reshape(length, MODEL_WIDTH)],
            axis=-1,
        ),
    )
    return results


def local_general(
    content,
    query_stream,
    segment_ids,
    pad_mask,
    predicted,
    order,
    rel_bucket,
    qkv_weight,
    qv_bias,
    out_weight,
    out_bias,
    attn_gain,
    attn_shift,
    up_weight,
    up_bias,
    down_weight,
    down_bias,
    ffn_gain,
    ffn_shift,
    rel_table,
    content_cot,
    query_cot,
):
    seq_count = content.shape[0]
    shard_length = content.shape[1]
    pred_count = query_stream.shape[1]
    row_count = shard_length + pred_count
    group_size = lax.axis_size("seq")
    edges = bucket_edges(rel_bucket)
    shards = (
        lax.all_gather(qkv_weight, ("dp", "seq"), axis=0, tiled=True),
        lax.all_gather(out_weight, ("dp", "seq"), axis=0, tiled=True),
        lax.all_gather(up_weight, ("dp", "seq"), axis=0, tiled=True),
        lax.all_gather(down_weight, ("dp", "seq"), axis=0, tiled=True),
        lax.all_gather(qv_bias, ("dp", "seq"), axis=0, tiled=True),
        lax.all_gather(out_bias, ("dp", "seq"), axis=0, tiled=True),
        lax.all_gather(attn_gain, ("dp", "seq"), axis=0, tiled=True),
        lax.all_gather(attn_shift, ("dp", "seq"), axis=0, tiled=True),
        lax.all_gather(up_bias, ("dp", "seq"), axis=0, tiled=True),
        lax.all_gather(down_bias, ("dp", "seq"), axis=0, tiled=True),
        lax.all_gather(ffn_gain, ("dp", "seq"), axis=0, tiled=True),
        lax.all_gather(ffn_shift, ("dp", "seq"), axis=0, tiled=True),
    )
    query_key_value_weight, w_out, w_up, w_down = (shards[0], shards[1], shards[2], shards[3])
    bias_qv, bias_out, first_norm_gain, shift_one, bias_up, bias_down, gain_two, shift_two = [
        member.astype(jnp.float32) for member in shards[4:]
    ]
    all_rows = jnp.concatenate([content, query_stream], axis=1)
    reduced_precision_rows = all_rows.astype(jnp.bfloat16)
    queries = (
        jnp.einsum(
            "srd,de->sre",
            reduced_precision_rows,
            query_key_value_weight[:, :MODEL_WIDTH],
            preferred_element_type=jnp.float32,
        )
        + bias_qv[:MODEL_WIDTH]
    ).astype(jnp.bfloat16)
    value_shift = jnp.concatenate([jnp.zeros((MODEL_WIDTH,), jnp.float32), bias_qv[MODEL_WIDTH:]])
    key_values = (
        jnp.einsum(
            "zci,ip->zcp",
            reduced_precision_rows[:, :shard_length],
            query_key_value_weight[:, MODEL_WIDTH:],
            preferred_element_type=jnp.float32,
        )
        + value_shift
    ).astype(jnp.bfloat16)
    full_pairs, full_seg, full_order, full_pad = (
        lax.all_gather(key_values, "seq", axis=1, tiled=True),
        lax.all_gather(segment_ids, "seq", axis=1, tiled=True),
        lax.all_gather(order, "seq", axis=1, tiled=True),
        lax.all_gather(pad_mask, "seq", axis=1, tiled=True),
    )
    content_pos = lax.axis_index("seq") * shard_length + jnp.arange(shard_length, dtype=jnp.int32)
    query_pos = jnp.concatenate(
        [jnp.broadcast_to(content_pos[None, :], (seq_count, shard_length)), predicted], axis=1
    )
    query_seg = jnp.concatenate(
        [segment_ids, jnp.take_along_axis(full_seg, predicted, axis=1)], axis=1
    )
    query_limit = jnp.concatenate(
        [order, jnp.take_along_axis(full_order, predicted, axis=1) - 1], axis=1
    )
    content_row = jnp.arange(row_count, dtype=jnp.int32) < shard_length
    row_meta = (full_seg, full_order, full_pad, query_pos, query_seg, query_limit)

    def forward_one(packed):
        return attend_forward(packed, rel_table, edges, content_row)

    context, row_lse = lax.map(forward_one, (queries, full_pairs) + row_meta)
    context_low = context.astype(jnp.bfloat16)
    attn_out = (
        jnp.einsum("sre,ed->srd", context_low, w_out, preferred_element_type=jnp.float32) + bias_out
    )
    hidden_one, normed_one, inv_one = norm_fwd(all_rows + attn_out, first_norm_gain, shift_one)
    hidden_low = hidden_one.astype(jnp.bfloat16)
    pre_act = (
        jnp.einsum("srd,df->srf", hidden_low, w_up, preferred_element_type=jnp.float32) + bias_up
    )
    activ, gelu_pull = jax.vjp(exact_gelu, pre_act)
    activ_low = activ.astype(jnp.bfloat16)
    ffn_out = (
        jnp.einsum("srf,fd->srd", activ_low, w_down, preferred_element_type=jnp.float32) + bias_down
    )
    hidden_two, normed_two, inv_two = norm_fwd(hidden_one + ffn_out, gain_two, shift_two)
    pad_float = pad_mask.astype(jnp.float32)
    row_valid = jnp.concatenate(
        [pad_float, jnp.ones((seq_count, pred_count), jnp.float32)], axis=1
    )[..., None]
    outputs = hidden_two * row_valid
    pad_weight = pad_float[..., None]
    local_sums = jnp.stack(
        [
            jnp.sum(pad_weight * content * content),
            jnp.sum(query_stream * query_stream),
            jnp.sum(pad_weight * attn_out[:, :shard_length] * attn_out[:, :shard_length]),
            jnp.sum(attn_out[:, shard_length:] * attn_out[:, shard_length:]),
            jnp.sum(pad_weight * ffn_out[:, :shard_length] * ffn_out[:, :shard_length]),
            jnp.sum(ffn_out[:, shard_length:] * ffn_out[:, shard_length:]),
            jnp.sum(pad_float),
        ]
    )
    back_weights = (
        lax.all_gather(qkv_weight, ("dp", "seq"), axis=0, tiled=True),
        lax.all_gather(out_weight, ("dp", "seq"), axis=0, tiled=True),
        lax.all_gather(up_weight, ("dp", "seq"), axis=0, tiled=True),
        lax.all_gather(down_weight, ("dp", "seq"), axis=0, tiled=True),
        lax.all_gather(attn_gain, ("dp", "seq"), axis=0, tiled=True),
        lax.all_gather(ffn_gain, ("dp", "seq"), axis=0, tiled=True),
    )
    back_pairs = lax.all_gather(key_values, "seq", axis=1, tiled=True)
    backward_query_key_value, back_out, back_up, back_down = (
        back_weights[0],
        back_weights[1],
        back_weights[2],
        back_weights[3],
    )
    back_gain_one = back_weights[4].astype(jnp.float32)
    back_gain_two = back_weights[5].astype(jnp.float32)
    upstream = jnp.concatenate([content_cot, query_cot], axis=1) * row_valid
    grad_res_two, grad_gain_two, grad_shift_two = norm_back(
        upstream, normed_two, inv_two, back_gain_two
    )
    grad_ffn = grad_res_two.astype(jnp.bfloat16)
    grad_bias_down = jnp.sum(grad_ffn, axis=(0, 1), dtype=jnp.float32)
    grad_down = jnp.einsum("srf,srd->fd", activ_low, grad_ffn, preferred_element_type=jnp.float32)
    grad_activ = jnp.einsum("srd,fd->srf", grad_ffn, back_down, preferred_element_type=jnp.float32)
    grad_pre = gelu_pull(grad_activ)[0].astype(jnp.bfloat16)
    grad_bias_up = jnp.sum(grad_pre, axis=(0, 1), dtype=jnp.float32)
    grad_up = jnp.einsum("srd,srf->df", hidden_low, grad_pre, preferred_element_type=jnp.float32)
    grad_hidden = grad_res_two + jnp.einsum(
        "srf,df->srd", grad_pre, back_up, preferred_element_type=jnp.float32
    )
    grad_res_one, grad_gain_one, grad_shift_one = norm_back(
        grad_hidden, normed_one, inv_one, back_gain_one
    )
    grad_attn = grad_res_one.astype(jnp.bfloat16)
    grad_bias_out = jnp.sum(grad_attn, axis=(0, 1), dtype=jnp.float32)
    grad_out = jnp.einsum("sre,srd->ed", context_low, grad_attn, preferred_element_type=jnp.float32)
    grad_context = jnp.einsum(
        "srd,ed->sre", grad_attn, back_out, preferred_element_type=jnp.float32
    ).astype(jnp.bfloat16)

    def backward_all(packed):
        return attend_backward(packed, rel_table, edges, content_row)

    grad_queries, grad_tables, per_row_delta, grad_pairs = lax.map(
        backward_all, (queries, back_pairs) + row_meta + (row_lse, grad_context)
    )
    paired_gradients = lax.psum_scatter(
        grad_pairs.astype(jnp.bfloat16), "seq", scatter_dimension=1, tiled=True
    )
    query_grads = grad_queries.astype(jnp.bfloat16)
    grad_bias_qv = jnp.concatenate(
        [
            jnp.sum(query_grads, axis=(0, 1), dtype=jnp.float32),
            jnp.sum(paired_gradients[..., MODEL_WIDTH:], axis=(0, 1), dtype=jnp.float32),
        ]
    )
    grad_qkv = jnp.concatenate(
        [
            jnp.einsum(
                "srd,sre->de",
                reduced_precision_rows,
                query_grads,
                preferred_element_type=jnp.float32,
            ),
            jnp.einsum(
                "cvi,cvp->ip",
                reduced_precision_rows[:, :shard_length],
                paired_gradients,
                preferred_element_type=jnp.float32,
            ),
        ],
        axis=1,
    )
    grad_rows = grad_res_one + jnp.einsum(
        "sre,de->srd",
        query_grads,
        backward_query_key_value[:, :MODEL_WIDTH],
        preferred_element_type=jnp.float32,
    )
    grad_content = grad_rows[:, :shard_length] + jnp.einsum(
        "zwv,bv->zwb",
        paired_gradients,
        backward_query_key_value[:, MODEL_WIDTH:],
        preferred_element_type=jnp.float32,
    )
    grad_query = grad_rows[:, shard_length:]
    owned = (
        lax.psum_scatter(grad_qkv, ("dp", "seq"), scatter_dimension=0, tiled=True),
        lax.psum_scatter(grad_out, ("dp", "seq"), scatter_dimension=0, tiled=True),
        lax.psum_scatter(grad_up, ("dp", "seq"), scatter_dimension=0, tiled=True),
        lax.psum_scatter(grad_down, ("dp", "seq"), scatter_dimension=0, tiled=True),
        lax.psum_scatter(grad_bias_qv, ("dp", "seq"), scatter_dimension=0, tiled=True),
        lax.psum_scatter(grad_bias_out, ("dp", "seq"), scatter_dimension=0, tiled=True),
        lax.psum_scatter(grad_gain_one, ("dp", "seq"), scatter_dimension=0, tiled=True),
        lax.psum_scatter(grad_shift_one, ("dp", "seq"), scatter_dimension=0, tiled=True),
        lax.psum_scatter(grad_bias_up, ("dp", "seq"), scatter_dimension=0, tiled=True),
        lax.psum_scatter(grad_bias_down, ("dp", "seq"), scatter_dimension=0, tiled=True),
        lax.psum_scatter(grad_gain_two, ("dp", "seq"), scatter_dimension=0, tiled=True),
        lax.psum_scatter(grad_shift_two, ("dp", "seq"), scatter_dimension=0, tiled=True),
    )
    table_sum, totals = lax.psum((jnp.sum(grad_tables, axis=0), local_sums), ("dp", "seq"))
    content_count = totals[6] * MODEL_WIDTH
    query_count = float(seq_count * lax.axis_size("dp") * pred_count * group_size * MODEL_WIDTH)
    stats = jnp.sqrt(
        jnp.stack(
            [
                totals[0] / content_count,
                totals[1] / query_count,
                totals[2] / content_count,
                totals[3] / query_count,
                totals[4] / content_count,
                totals[5] / query_count,
            ]
        )
    )
    return (
        outputs[:, :shard_length],
        outputs[:, shard_length:],
        grad_content,
        grad_query,
        owned[0],
        owned[4],
        owned[1],
        owned[5],
        owned[6],
        owned[7],
        owned[2],
        owned[8],
        owned[3],
        owned[9],
        owned[10],
        owned[11],
        table_sum,
        stats,
    )


LOG2E = math.log2(math.e)
TILE = 256
KEYS = 512
HALF = 128
REACH = 11
DIAGS = 2 * REACH + 1
WIDE = SEQ_LEN + HALF
MASKED = -1e30
F32 = jnp.float32
BF16 = jnp.bfloat16


def dot_nn(a, b):
    return jnp.dot(a, b, preferred_element_type=F32)


def dot_nt(a, b):
    return lax.dot_general(a, b, (((1,), (1,)), ((), ())), preferred_element_type=F32)


def dot_tn(a, b):
    return lax.dot_general(a, b, (((0,), (0,)), ((), ())), preferred_element_type=F32)


def cost_of(micros):
    return pl.CostEstimate(
        flops=int(micros * 1.0e9), bytes_accessed=int(micros * 1.0e6), transcendentals=0
    )


def bias_kernel(
    rows_q,
    own,
    slot_q,
    heads_ref,
    bucket_ref,
    table_ref,
    ints_ref,
    tile_out,
    qbias_out,
    kmeta_ref,
    rseg_ref,
    rlim_ref,
    hot_ref,
    shift_ref,
    vec_scr,
    ahead_scr,
    fold_scr,
    tile_scr,
    qbias_scr,
    sems,
):
    seqs, length = ints_ref.shape[0], ints_ref.shape[2]
    first = heads_ref[0]
    hot = (
        lax.broadcasted_iota(jnp.int32, (BUCKETS, 2 * SEQ_LEN), 0) == bucket_ref[0:1, :]
    ).astype(BF16)
    vec_scr[...] = dot_tn(table_ref[...], hot)
    hot = (
        lax.broadcasted_iota(jnp.int32, (BUCKETS, 2 * SEQ_LEN), 0) == bucket_ref[1:2, :]
    ).astype(BF16)
    ahead_scr[...] = dot_tn(table_ref[...], hot) * LOG2E
    copies = []
    for h in range(own):
        row = ahead_scr[pl.ds(first + h, 1), :]
        for e in range(-REACH, REACH + 1):
            start = HALF * (15 + e)
            skew = pltpu.roll(
                jnp.broadcast_to(row[:, start : start + 2 * HALF], (HALF, 2 * HALF)),
                0,
                1,
                stride=1,
                stride_axis=0,
            )
            tile_scr[h, e + REACH] = skew[:, HALF:].T
        copies.append(pltpu.make_async_copy(tile_scr.at[h], tile_out.at[h], sems.at[h]))
        copies[-1].start()
        vec = vec_scr[pl.ds(first + h, 1), :]
        fold_scr[h] = jnp.concatenate(
            [vec[:, HALF * i : HALF * i + WIDE] for i in range(16)], axis=0
        ).astype(BF16)

    place = lax.broadcasted_iota(jnp.int32, (1, length), 1)
    lane = lax.broadcasted_iota(jnp.int32, (HALF, HALF), 1)
    segs, orders = [], []
    for t in range(seqs):
        seg = ints_ref[t, 0:1, :]
        seg = jnp.where(ints_ref[t, 2:3, :] == 1, seg, -2 - t * length - place)
        order = ints_ref[t, 1:2, :]
        rseg_ref[:, t * length : (t + 1) * length] = seg
        rlim_ref[:, t * length : (t + 1) * length] = order
        for n, row in ((0, seg.astype(F32)), (1, order.astype(F32))):
            for i in range(length // HALF):
                part = row[:, i * HALF : (i + 1) * HALF]
                (segs, orders)[n].append(part)
                kmeta_ref[n, t * length + i * HALF : t * length + (i + 1) * HALF, :] = (
                    jnp.broadcast_to(part, (HALF, HALF)).T.astype(jnp.int32)
                )
    segs = jnp.concatenate(segs, axis=0)
    orders = jnp.concatenate(orders, axis=0)
    preds = [ints_ref[t, 3:4, :slot_q].astype(F32) for t in range(seqs)]
    preds.append(jnp.full((1, rows_q - seqs * slot_q), -1.0, F32))
    preds = jnp.concatenate(preds, axis=1)
    high = lax.Precision.HIGHEST
    for t in range(rows_q // HALF):
        at = slice(t * HALF, (t + 1) * HALF)
        spots = jnp.broadcast_to(preds[:, at], (HALF, HALF)).T.astype(jnp.int32)
        group = jnp.right_shift(spots, 7)
        inside = jnp.bitwise_and(spots, HALF - 1)
        pick = (lane == group)[:, :16].astype(F32)
        for rows, ref, less in ((segs, rseg_ref, 0.0), (orders, rlim_ref, 1.0)):
            spread = jnp.dot(pick, rows, precision=high, preferred_element_type=F32)
            found = jnp.take_along_axis(spread, inside, axis=1) - less
            ref[:, length * seqs + t * HALF : length * seqs + (t + 1) * HALF] = found.T[
                0:1, :
            ].astype(jnp.int32)
        hot_ref[at, :] = (lane == 15 - group)[:, :16].astype(BF16)
        shift_ref[at, :] = HALF - 1 - inside

    for h in range(own):
        for t in range(rows_q // HALF):
            at = slice(t * HALF, (t + 1) * HALF)
            turn = lane + shift_ref[at, :]
            wrap = turn >= HALF
            idx = jnp.where(wrap, turn - HALF, turn)
            spread = dot_nn(hot_ref[at, :], fold_scr[h])
            prev = jnp.take_along_axis(spread[:, :HALF], idx, axis=1)
            for j in range(SEQ_LEN // HALF):
                cur = jnp.take_along_axis(
                    spread[:, (j + 1) * HALF : (j + 2) * HALF], idx, axis=1
                )
                out = jnp.where(wrap, cur, prev) * LOG2E
                qbias_scr[h, j * HALF : (j + 1) * HALF, at] = out.T
                prev = cur
        copies.append(pltpu.make_async_copy(qbias_scr.at[h], qbias_out.at[h], sems.at[own + h]))
        copies[-1].start()
    for copy in copies:
        copy.wait()


def bias_call(own, rows_q, slot_q, first, buckets, table, ints):
    vm = pl.BlockSpec(memory_space=pltpu.VMEM)
    anywhere = pl.BlockSpec(memory_space=pl.ANY)
    tiles = jax.ShapeDtypeStruct((own, DIAGS, HALF, HALF), F32)
    qbias = jax.ShapeDtypeStruct((own, SEQ_LEN, rows_q), F32)
    rows = jax.ShapeDtypeStruct((1, SEQ_LEN + rows_q), jnp.int32)
    return pl.pallas_call(
        functools.partial(bias_kernel, rows_q, own, slot_q),
        out_shape=(
            tiles,
            qbias,
            jax.ShapeDtypeStruct((2, SEQ_LEN, HALF), jnp.int32),
            rows,
            rows,
            jax.ShapeDtypeStruct((rows_q, 16), BF16),
            jax.ShapeDtypeStruct((rows_q, HALF), jnp.int32),
        ),
        in_specs=[pl.BlockSpec(memory_space=pltpu.SMEM)] + [vm] * 3,
        out_specs=(anywhere,) * 2 + (vm,) * 5,
        scratch_shapes=[
            pltpu.VMEM((table.shape[1], 2 * SEQ_LEN), F32),
            pltpu.VMEM((table.shape[1], 2 * SEQ_LEN), F32),
            pltpu.VMEM((own, 16, WIDE), BF16),
            pltpu.VMEM(tiles.shape, F32),
            pltpu.VMEM(qbias.shape, F32),
            pltpu.SemaphoreType.DMA((2 * own,)),
        ],
        compiler_params=pltpu.CompilerParams(vmem_limit_bytes=50 << 20),
        cost_estimate=cost_of(12),
        name="bias_tiles",
    )(first, buckets, table, ints)


def bias_block(tile_ref, h, e):
    return jnp.concatenate(
        [
            jnp.concatenate([tile_ref[h, e + i], tile_ref[h, e + i - 1]], axis=1)
            for i in range(KEYS // HALF)
        ],
        axis=0,
    )


def mask_block(kmeta_ref, rseg_ref, rlim_ref, krow, rcol, width):
    kseg = kmeta_ref[0, pl.ds(krow, KEYS), :]
    kord = kmeta_ref[1, pl.ds(krow, KEYS), :]
    parts = []
    for w in range(width // HALF):
        rseg = rseg_ref[:, pl.ds(rcol + w * HALF, HALF)]
        rlim = rlim_ref[:, pl.ds(rcol + w * HALF, HALF)]
        ok = (kseg == rseg) & (kord <= rlim)
        parts.append(jnp.where(ok, 0.0, MASKED))
    return parts[0] if len(parts) == 1 else jnp.concatenate(parts, axis=1)


def fwd_kernel(
    own,
    rows_q,
    span_ref,
    qt_ref,
    k_ref,
    vt_ref,
    kmeta_ref,
    rseg_ref,
    rlim_ref,
    tile_ref,
    qbias_ref,
    ctx_ref,
    rows_ref,
    lse_ref,
    s_scr,
    qbias_scr,
    qbias_sem,
):
    late = pltpu.make_async_copy(qbias_ref, qbias_scr, qbias_sem.at[0])
    late.start()

    def run(rcol, width, lo, steps, bias_of):
        heads = range(own)

        def fold(op, x):
            rows = [x[i * 8 : (i + 1) * 8] for i in range(x.shape[0] // 8)]
            while len(rows) > 1:
                rows = [op(rows[i], rows[i + 1]) for i in range(0, len(rows), 2)]
            return rows[0]

        def score(step, tops):
            kt = lo + step * (KEYS // TILE)
            krow = pl.multiple_of(kt * TILE, TILE)
            mask = mask_block(kmeta_ref, rseg_ref, rlim_ref, krow, rcol, width)
            new = []
            for h in heads:
                s = jnp.dot(
                    k_ref[h, pl.ds(krow, KEYS), :],
                    qt_ref[h * HEAD_DIM : (h + 1) * HEAD_DIM, pl.ds(rcol, width)],
                    preferred_element_type=F32,
                )
                s = s * (SCALE * LOG2E) + (bias_of(h, kt) + mask)
                s_scr[h, pl.ds(krow, KEYS), :width] = s
                new.append(jnp.maximum(tops[h], fold(jnp.maximum, s)))
            return tuple(new)

        tops = lax.fori_loop(
            0, steps, score, tuple(jnp.full((8, width), MASKED, F32) for _ in heads)
        )
        tops = [jnp.max(t, axis=0, keepdims=True) for t in tops]

        def weigh(step, carry):
            kt = lo + step * (KEYS // TILE)
            krow = pl.multiple_of(kt * TILE, TILE)
            sums, accs = carry
            new_sums, new_accs = [], []
            for h in heads:
                p = jnp.exp2(s_scr[h, pl.ds(krow, KEYS), :width] - tops[h])
                new_sums.append(sums[h] + fold(jnp.add, p))
                new_accs.append(
                    accs[h]
                    + jnp.dot(
                        vt_ref[h * HEAD_DIM : (h + 1) * HEAD_DIM, pl.ds(krow, KEYS)],
                        p.astype(BF16),
                        preferred_element_type=F32,
                    )
                )
            return tuple(new_sums), tuple(new_accs)

        sums, accs = lax.fori_loop(
            0,
            steps,
            weigh,
            (
                tuple(jnp.zeros((8, width), F32) for _ in heads),
                tuple(jnp.zeros((HEAD_DIM, width), F32) for _ in heads),
            ),
        )
        outs = []
        for h in heads:
            total = jnp.sum(sums[h], axis=0, keepdims=True)
            outs.append(accs[h] / total)
            lse_ref[h : h + 1, pl.ds(rcol, width)] = tops[h] + jnp.log2(total)
        out = jnp.concatenate(outs, axis=0)
        ctx_ref[:, pl.ds(rcol, width)] = out.astype(BF16)
        return out

    def content_tile(qt, carry):
        def bias_of(h, kt):
            return bias_block(tile_ref, h, 2 * (kt - qt) + REACH)

        run(pl.multiple_of(qt * TILE, TILE), TILE, span_ref[0, qt], span_ref[1, qt], bias_of)
        return carry

    lax.fori_loop(0, SEQ_LEN // TILE, content_tile, 0)

    def query_bias(h, kt):
        return qbias_scr[h, pl.ds(pl.multiple_of(kt * TILE, TILE), KEYS), :]

    late.wait()
    last = SEQ_LEN // TILE
    out = run(SEQ_LEN, rows_q, span_ref[0, last], span_ref[1, last], query_bias)
    rows_ref[...] = out.T.astype(BF16)


def fwd_call(span, qt, k3, vt, kmeta, rseg, rlim, tiles, qbias):
    own = k3.shape[0]
    rows = qt.shape[1]
    rows_q = rows - SEQ_LEN
    vm = pl.BlockSpec(memory_space=pltpu.VMEM)
    return pl.pallas_call(
        functools.partial(fwd_kernel, own, rows_q),
        out_shape=(
            jax.ShapeDtypeStruct((own * HEAD_DIM, rows), BF16),
            jax.ShapeDtypeStruct((rows_q, own * HEAD_DIM), BF16),
            jax.ShapeDtypeStruct((own, rows), F32),
        ),
        in_specs=[pl.BlockSpec(memory_space=pltpu.SMEM)]
        + [vm] * 7
        + [pl.BlockSpec(memory_space=pl.ANY)],
        scratch_shapes=[
            pltpu.VMEM((own, SEQ_LEN, max(rows_q, TILE)), F32),
            pltpu.VMEM(qbias.shape, F32),
            pltpu.SemaphoreType.DMA((1,)),
        ],
        compiler_params=pltpu.CompilerParams(vmem_limit_bytes=56 << 20),
        cost_estimate=cost_of(32),
        name="attend",
    )(span, qt, k3, vt, kmeta, rseg, rlim, tiles, qbias)


def bwd_kernel(
    own,
    rows_q,
    span_ref,
    qt_ref,
    q_ref,
    k_ref,
    kt_ref,
    v_ref,
    ctx_ref,
    gc_ref,
    gq_ref,
    lse_ref,
    kmeta_ref,
    rseg_ref,
    rlim_ref,
    tile_ref,
    hot_ref,
    shift_ref,
    qbias_ref,
    dq_ref,
    dk_ref,
    dv_ref,
    offs_ref,
    qoffs_ref,
    dk_scr,
    dv_scr,
    dq_scr,
    diag_scr,
    ds_scr,
    delta_scr,
    gt_ref,
    g_ref,
    qbias_scr,
    qbias_sem,
):
    late = pltpu.make_async_copy(qbias_ref, qbias_scr, qbias_sem.at[0])
    late.start()
    seqs, length = gc_ref.shape[0], gc_ref.shape[2]
    for t in range(seqs):
        for a in range(0, length, TILE):
            block = gc_ref[t, :, a : a + TILE]
            at = slice(t * length + a, t * length + a + TILE)
            gt_ref[:, at] = block
            back = block.astype(F32).T
            for h in range(own):
                g_ref[h, at, :] = back[:, h * HEAD_DIM : (h + 1) * HEAD_DIM].astype(BF16)
    used = gq_ref.shape[0]
    block = jnp.concatenate(
        [gq_ref[...].astype(F32), jnp.zeros((rows_q - used, gq_ref.shape[1]), F32)], axis=0
    )
    gt_ref[:, SEQ_LEN:] = block.T.astype(BF16)
    for h in range(own):
        g_ref[h, SEQ_LEN:, :] = block[:, h * HEAD_DIM : (h + 1) * HEAD_DIM].astype(BF16)
    dk_scr[...] = jnp.zeros(dk_scr.shape, F32)
    dv_scr[...] = jnp.zeros(dv_scr.shape, F32)
    diag_scr[...] = jnp.zeros(diag_scr.shape, F32)
    ds_scr[...] = jnp.zeros(ds_scr.shape, BF16)
    for h in range(own):
        part = slice(h * HEAD_DIM, (h + 1) * HEAD_DIM)
        delta_scr[h : h + 1, :] = jnp.sum(
            ctx_ref[part, :].astype(F32) * gt_ref[part, :].astype(F32), axis=0, keepdims=True
        )

    def run(rcol, width, lo, steps, bias_of, keep):
        dq_scr[...] = jnp.zeros(dq_scr.shape, F32)

        def body(step, carry):
            kt = lo + step * (KEYS // TILE)
            krow = pl.multiple_of(kt * TILE, TILE)
            mask = mask_block(kmeta_ref, rseg_ref, rlim_ref, krow, rcol, width)
            for h in range(own):
                part = slice(h * HEAD_DIM, (h + 1) * HEAD_DIM)
                s = jnp.dot(
                    k_ref[h, pl.ds(krow, KEYS), :],
                    qt_ref[part, pl.ds(rcol, width)],
                    preferred_element_type=F32,
                )
                s = s * (SCALE * LOG2E) + (bias_of(h, kt) + mask)
                p = jnp.exp2(s - lse_ref[h : h + 1, pl.ds(rcol, width)])
                gp = jnp.dot(
                    v_ref[h, pl.ds(krow, KEYS), :],
                    gt_ref[part, pl.ds(rcol, width)],
                    preferred_element_type=F32,
                )
                ds = p * (gp - delta_scr[h : h + 1, pl.ds(rcol, width)])
                low = ds.astype(BF16)
                keep(h, kt, ds, low)
                dv_scr[h, pl.ds(krow, KEYS), :] += jnp.dot(
                    p.astype(BF16), g_ref[h, pl.ds(rcol, width), :], preferred_element_type=F32
                )
                dk_scr[h, pl.ds(krow, KEYS), :] += jnp.dot(
                    low, q_ref[h, pl.ds(rcol, width), :], preferred_element_type=F32
                )
                dq_scr[h, :, :width] += jnp.dot(
                    kt_ref[part, pl.ds(krow, KEYS)], low, preferred_element_type=F32
                )
            return carry

        lax.fori_loop(0, steps, body, 0)
        grad = jnp.concatenate([dq_scr[h, :, :width] for h in range(own)], axis=0)
        dq_ref[pl.ds(rcol, width), :] = (grad * SCALE).T.astype(BF16)

    def content_tile(qt, carry):
        def bias_of(h, kt):
            return bias_block(tile_ref, h, 2 * (kt - qt) + REACH)

        def keep(h, kt, ds, low):
            e = 2 * (kt - qt) + REACH
            subs = [ds[i * HALF : (i + 1) * HALF] for i in range(KEYS // HALF)]
            diag_scr[h, e - 1] += subs[0][:, HALF:]
            for i, sub in enumerate(subs):
                here = sub[:, :HALF]
                if i + 1 < len(subs):
                    here = here + subs[i + 1][:, HALF:]
                diag_scr[h, e + i] += here

        run(pl.multiple_of(qt * TILE, TILE), TILE, span_ref[0, qt], span_ref[1, qt], bias_of, keep)
        return carry

    lax.fori_loop(0, SEQ_LEN // TILE, content_tile, 0)

    def query_bias(h, kt):
        return qbias_scr[h, pl.ds(pl.multiple_of(kt * TILE, TILE), KEYS), :]

    def query_keep(h, kt, ds, low):
        ds_scr[h, pl.ds(pl.multiple_of(kt * TILE, TILE), KEYS), :] = low

    late.wait()
    last = SEQ_LEN // TILE
    run(SEQ_LEN, rows_q, span_ref[0, last], span_ref[1, last], query_bias, query_keep)

    for a in range(0, SEQ_LEN, TILE):
        at = slice(a, a + TILE)
        for scr, ref, scale in ((dk_scr, dk_ref, SCALE), (dv_scr, dv_ref, 1.0)):
            block = jnp.concatenate([scr[h, at, :] for h in range(own)], axis=1)
            ref[at, :] = (block * scale).astype(BF16)

    offs_ref[...] = jnp.zeros(offs_ref.shape, F32)
    qoffs_ref[...] = jnp.zeros(qoffs_ref.shape, F32)
    lane = lax.broadcasted_iota(jnp.int32, (HALF, HALF), 1)
    turn = lane + lax.broadcasted_iota(jnp.int32, (HALF, HALF), 0)
    over = turn >= HALF
    turn = jnp.where(over, turn - HALF, turn)
    for h in range(own):
        for e in range(DIAGS):
            skew = jnp.take_along_axis(diag_scr[h, e].T, turn, axis=1)
            start = HALF * (15 + e - REACH)
            offs_ref[h : h + 1, start : start + HALF] += jnp.sum(
                jnp.where(over, skew, 0.0), axis=0, keepdims=True
            )
            offs_ref[h : h + 1, start + HALF : start + 2 * HALF] += jnp.sum(
                jnp.where(over, 0.0, skew), axis=0, keepdims=True
            )

    for h in range(own):
        total = jnp.zeros((16, WIDE), F32)
        for t in range(rows_q // HALF):
            shift = shift_ref[t * HALF : (t + 1) * HALF, :]
            place = lane - shift
            low_side = place < 0
            idx = jnp.where(low_side, place + HALF, place)
            prev = jnp.zeros((HALF, HALF), F32)
            pieces = []
            for j in range(SEQ_LEN // HALF + 1):
                if j < SEQ_LEN // HALF:
                    block = ds_scr[h, j * HALF : (j + 1) * HALF, t * HALF : (t + 1) * HALF]
                    cur = jnp.take_along_axis(block.astype(F32).T, idx, axis=1)
                else:
                    cur = jnp.zeros((HALF, HALF), F32)
                pieces.append(jnp.where(low_side, prev, cur).astype(BF16))
                prev = cur
            total += dot_tn(
                hot_ref[t * HALF : (t + 1) * HALF, :], jnp.concatenate(pieces, axis=1)
            )
        for i in range(16):
            qoffs_ref[h : h + 1, HALF * i : HALF * i + WIDE] += total[i : i + 1, :]


def bwd_call(
    span, qt, q3, k3, kt, v3, ctx, g_c, g_q, lse, kmeta, rseg, rlim, tiles, hot, shift, qbias
):
    own = k3.shape[0]
    rows = qt.shape[1]
    rows_q = rows - SEQ_LEN
    vm = pl.BlockSpec(memory_space=pltpu.VMEM)
    return pl.pallas_call(
        functools.partial(bwd_kernel, own, rows_q),
        out_shape=(
            jax.ShapeDtypeStruct((rows, own * HEAD_DIM), BF16),
            jax.ShapeDtypeStruct((SEQ_LEN, own * HEAD_DIM), BF16),
            jax.ShapeDtypeStruct((SEQ_LEN, own * HEAD_DIM), BF16),
            jax.ShapeDtypeStruct((own, 2 * SEQ_LEN), F32),
            jax.ShapeDtypeStruct((own, 2 * SEQ_LEN), F32),
        ),
        in_specs=[pl.BlockSpec(memory_space=pltpu.SMEM)]
        + [vm] * 15
        + [pl.BlockSpec(memory_space=pl.ANY)],
        scratch_shapes=[
            pltpu.VMEM((own, SEQ_LEN, HEAD_DIM), F32),
            pltpu.VMEM((own, SEQ_LEN, HEAD_DIM), F32),
            pltpu.VMEM((own, HEAD_DIM, max(rows_q, TILE)), F32),
            pltpu.VMEM((own, DIAGS, HALF, HALF), F32),
            pltpu.VMEM((own, SEQ_LEN, rows_q), BF16),
            pltpu.VMEM((own, rows), F32),
            pltpu.VMEM((own * HEAD_DIM, rows), BF16),
            pltpu.VMEM((own, rows, HEAD_DIM), BF16),
            pltpu.VMEM(qbias.shape, F32),
            pltpu.SemaphoreType.DMA((1,)),
        ],
        compiler_params=pltpu.CompilerParams(vmem_limit_bytes=60 << 20),
        cost_estimate=cost_of(58),
        name="attend_back",
    )(span, qt, q3, k3, kt, v3, ctx, g_c, g_q, lse, kmeta, rseg, rlim, tiles, hot, shift, qbias)


def key_spans(segment, pad_mask):
    length = segment.shape[0]
    real = pad_mask == 1
    head_seg = segment[::TILE]
    tail_seg = segment[TILE - 1 :: TILE]
    starts = jnp.sum((segment[None, :] < head_seg[:, None]).astype(jnp.int32), axis=1)
    first = jnp.arange(0, length, TILE, dtype=jnp.int32)
    lo = jnp.where(real[::TILE], starts, first) // TILE
    hi = jnp.where(real[TILE - 1 :: TILE], tail_seg, first + TILE - 1) // TILE
    count = jnp.sum(pad_mask)
    lo = jnp.concatenate([lo, jnp.zeros((1,), jnp.int32)])
    hi = jnp.concatenate([hi, jnp.maximum(count - 1, 0)[None] // TILE])
    per = KEYS // TILE
    steps = (hi - lo + per) // per
    lo = jnp.minimum(lo, length // TILE - steps * per)
    return jnp.stack([lo, steps]).astype(jnp.int32)


COLS = 768
FWD_BITS_UP = (16, 8, 4, 2)
FWD_BITS_DOWN = (16, 8, 2, 4)


def place_of(j, bits):
    total = 0
    for n, bit in enumerate(bits):
        total += ((j >> n) & 1) * (bit // 2)
    return total


def mid_kernel(
    seqs,
    bits_up,
    bits_down,
    ctx_c,
    ctx_q,
    x_c,
    x_q,
    cot_c,
    cot_q,
    pad_ref,
    six_ref,
    bias_up,
    uo_own,
    uo_mate,
    down_own,
    down_mate,
    res_c,
    res_q,
    gctx_c,
    gctx_q,
    six_out,
    up_out,
    sums_ref,
    out_c,
    out_q,
    keep_out,
    give_out,
    w_up,
    w_out,
    w_down,
    one_scr,
    norm_scr,
    inv_scr,
    low_scr,
    act_scr,
    slope_scr,
    sum_scr,
    grad_scr,
    pre_scr,
    plane_scr,
    outc_scr,
    outq_scr,
    parts_scr,
    sq_scr,
    valid_ref,
    xq_scr,
    cotq_scr,
    sems,
    plane_sems,
    out_sems,
):
    core = lax.rem(lax.axis_index("seq"), 2)
    chips, shard = uo_own.shape[0], uo_own.shape[1]
    shard_down = down_own.shape[1]
    length = x_c.shape[0]
    preds = x_q.shape[0]
    count = xq_scr.shape[0]
    ff = w_up.shape[1]
    chunks = ff // COLS
    wide = ctx_c.shape[1]
    half_ff, half = ff // 2, COLS // 2
    bias_out, gain_one, shift_one, bias_down, gain_two, shift_two = [
        six_ref[i : i + 1, :] for i in range(6)
    ]

    def plane_copies(chunk, slot):
        start = chunk * COLS
        if not isinstance(start, int):
            start = pl.multiple_of(start, COLS)
        return [
            pltpu.make_async_copy(
                ref.at[:, :, pl.ds(start, COLS)], plane_scr.at[slot, n], plane_sems.at[slot, n]
            )
            for n, ref in enumerate((uo_own, uo_mate))
        ]

    def assemble(slot, put_rows):
        def body(j, carry):
            chip = place_of(j, bits_up)
            first = plane_scr[slot, core, j].astype(F32)
            second = plane_scr[slot, 1 - core, j].astype(F32)
            pair = jnp.concatenate([first, second], axis=0).astype(BF16)
            put_rows(pl.ds(pl.multiple_of(2 * shard * chip, 16), 2 * shard), pair)
            return carry

        lax.fori_loop(0, chips, body, 0)

    for chunk, slot in ((chunks, 0), (0, 1)):
        for copy in plane_copies(chunk, slot):
            copy.start()
    copies = []
    for j in range(chips):
        chip = place_of(j, bits_down)
        for side, ref in ((core, down_own), (1 - core, down_mate)):
            row = pl.multiple_of((2 * chip + side) * shard_down, 16)
            copies.append(
                pltpu.make_async_copy(
                    ref.at[j], w_down.at[pl.ds(row, shard_down)], sems.at[len(copies)]
                )
            )
    for copy in copies:
        copy.start()
    for copy in plane_copies(chunks, 0):
        copy.wait()

    def put_out(rows, pair):
        w_out[rows, :] = pair

    assemble(0, put_out)
    for copy in plane_copies(1, 0):
        copy.start()

    for a in range(0, length, 128):
        row = pad_ref[:, a : a + 128].astype(F32)
        valid_ref[a : a + 128, :] = jnp.broadcast_to(row, (128, 128)).T
    spot = lax.broadcasted_iota(jnp.int32, (count, 128), 0)
    valid_ref[length:, :] = jnp.where(spot < preds, 1.0, 0.0)
    for ref, scr in ((x_q, xq_scr), (cot_q, cotq_scr)):
        scr[...] = jnp.zeros(scr.shape, F32)
        scr[:preds, :] = ref[...]
    blocks = [(0, length // 2), (length // 2, length), (length, length + count)]

    def pick(ref_c, ref_q, a, b):
        return ref_c[a:b, :] if b <= length else ref_q[...]

    def put(ref_c, ref_q, a, b, value):
        if b <= length:
            ref_c[a:b, :] = value
        else:
            ref_q[...] = value[: ref_q.shape[0]]

    def norm(x):
        mean = jnp.mean(x, axis=-1, keepdims=True)
        centered = x - mean
        inv = lax.rsqrt(jnp.mean(centered * centered, axis=-1, keepdims=True) + EPS)
        return centered * inv, inv

    def norm_grad(up, normed, inv, gain):
        grad = up * gain
        proj = jnp.mean(grad, axis=-1, keepdims=True) + normed * jnp.mean(
            grad * normed, axis=-1, keepdims=True
        )
        return inv * (grad - proj)

    sq_scr[...] = jnp.zeros(sq_scr.shape, F32)
    six_out[...] = jnp.zeros(six_out.shape, F32)
    up_out[...] = jnp.zeros(up_out.shape, F32)

    def count_in(k, x, a, b):
        row = k + (1 if b > length else 0)
        sq_scr[row : row + 1, :] += jnp.sum(x * x * valid_ref[a:b, :1], axis=0, keepdims=True)

    def add_row(row, x):
        six_out[row : row + 1, :] += jnp.sum(x, axis=0, keepdims=True)

    for a, b in blocks:
        attn = bias_out
        for t in range(seqs):
            part = w_out[t * wide : (t + 1) * wide, :]
            attn = attn + (
                dot_tn(ctx_c[t, :, a:b], part) if b <= length else dot_nn(ctx_q[t], part)
            )
        x = pick(x_c, xq_scr, a, b)
        count_in(0, x, a, b)
        count_in(2, attn, a, b)
        normed, inv = norm(x + attn)
        one = normed * gain_one + shift_one
        norm_scr[a:b, :] = normed
        inv_scr[a:b, :] = jnp.broadcast_to(inv, (b - a, 128))
        one_scr[a:b, :] = one
        low_scr[a:b, :] = one.astype(BF16)

    for copy in copies:
        copy.wait()
    sum_scr[...] = jnp.zeros(sum_scr.shape, F32)

    def up_step(i, carry):
        cols = pl.ds(pl.multiple_of(i * COLS, COLS), COLS)
        slot = lax.rem(i + 1, 2)
        for copy in plane_copies(i, slot):
            copy.wait()

        def put_up(rows, pair):
            w_up[rows, cols] = pair

        assemble(slot, put_up)

        @pl.when(i + 2 < chunks)
        def _():
            for copy in plane_copies(i + 2, slot):
                copy.start()

        for a, b in blocks:
            u = dot_nn(low_scr[a:b, :], w_up[:, cols]) + bias_up[:, cols]
            cdf = 0.5 * (1.0 + lax.erf(u * math.sqrt(0.5)))
            act = (u * cdf).astype(BF16)
            act_scr[a:b, cols] = act
            slope_scr[a:b, cols] = cdf + u * (
                jnp.exp(-0.5 * u * u) * (1.0 / math.sqrt(2.0 * math.pi))
            )
            sum_scr[a:b, :] += dot_nn(act, w_down[cols, :])
        return carry

    lax.fori_loop(0, chunks, up_step, 0)

    for a, b in blocks:
        ffn = sum_scr[a:b, :] + bias_down
        count_in(4, ffn, a, b)
        normed, inv = norm(one_scr[a:b, :] + ffn)
        ok = valid_ref[a:b, :1]
        put(outc_scr, outq_scr, a, b, (normed * gain_two + shift_two) * ok)
        up = pick(cot_c, cotq_scr, a, b) * ok
        add_row(4, up * normed)
        add_row(5, up)
        grad = norm_grad(up, normed, inv, gain_two)
        low = grad.astype(BF16)
        add_row(3, low.astype(F32))
        sum_scr[a:b, :] = grad
        grad_scr[a:b, :] = low
    leaving = [
        pltpu.make_async_copy(outc_scr, out_c, out_sems.at[0]),
        pltpu.make_async_copy(outq_scr, out_q, out_sems.at[1]),
    ]
    for copy in leaving:
        copy.start()

    def start(copy_of, h):
        @pl.when(core == h)
        def _():
            copy_of(keep_out).start()

        @pl.when(core != h)
        def _():
            copy_of(give_out).start()

    def up_copy(i, out):
        h, at = i // 2, lax.rem(i, 2) if not isinstance(i, int) else i % 2
        cols = pl.ds(pl.multiple_of(at * COLS, COLS) if not isinstance(i, int) else at * COLS, COLS)
        return pltpu.make_async_copy(
            parts_scr.at[h, :, cols], out.at[:, cols], out_sems.at[2 + i]
        )

    down_rows = 2 * shard * (COLS // (2 * shard_down))
    down_cols = pl.ds(half_ff + half, half_ff)

    def down_copy(i, h, out):
        start = i * down_rows
        rows = pl.ds(start if isinstance(i, int) else pl.multiple_of(start, down_rows), down_rows)
        return pltpu.make_async_copy(
            parts_scr.at[h, rows, down_cols],
            out.at[rows, down_cols],
            out_sems.at[2 + chunks * (1 + h) + i],
        )

    def back_step(i, carry):
        cols = pl.ds(pl.multiple_of(i * COLS, COLS), COLS)
        for a, b in blocks:
            low = (
                dot_nt(grad_scr[a:b, :], w_down[cols, :]) * slope_scr[a:b, cols]
            ).astype(BF16)
            pre_scr[a:b, :] = low
            up_out[:, cols] += jnp.sum(low.astype(F32), axis=0, keepdims=True)
            sum_scr[a:b, :] += dot_nt(low, w_up[:, cols])
        at = pl.ds(pl.multiple_of(lax.rem(i, 2) * COLS, COLS), COLS)
        parts_scr[i // 2, :, at] = dot_tn(low_scr[...], pre_scr[...]).astype(BF16)
        start(lambda out: up_copy(i, out), i // 2)
        grads = dot_tn(act_scr[:, cols], grad_scr[...]).astype(BF16)
        for h in range(2):
            for chip in range(COLS // (2 * shard_down)):
                to = pl.ds(pl.multiple_of(i * down_rows, down_rows) + chip * 2 * shard, 2 * shard)
                for g in range(shard_down // shard):
                    row = 2 * shard_down * chip + 2 * shard * g
                    col = half_ff + half * (1 + g)
                    parts_scr[h, to, col : col + half] = grads[
                        row : row + 2 * shard, h * half : (h + 1) * half
                    ]
            start(lambda out: down_copy(i, h, out), h)
        return carry

    lax.fori_loop(0, chunks, back_step, 0)
    leaving += [up_copy(i, keep_out) for i in range(chunks)]
    leaving += [down_copy(i, h, keep_out) for i in range(chunks) for h in range(2)]

    for a, b in blocks:
        up = sum_scr[a:b, :]
        normed = norm_scr[a:b, :]
        add_row(1, up * normed)
        add_row(2, up)
        grad = norm_grad(up, normed, inv_scr[a:b, :1], gain_one)
        low = grad.astype(BF16)
        add_row(0, low.astype(F32))
        put(res_c, res_q, a, b, grad)
        grad_scr[a:b, :] = low
    for t in range(seqs):
        rows = slice(t * wide, (t + 1) * wide)
        part = w_out[rows, :]
        gctx_c[t] = dot_nt(part, grad_scr[:length, :]).astype(BF16)
        gctx_q[t] = dot_nt(grad_scr[length:, :], part).astype(BF16)
        grads = (
            dot_nn(ctx_c[t], grad_scr[:length, :]) + dot_tn(ctx_q[t], grad_scr[length:, :])
        ).astype(BF16)
        for h in range(2):
            parts_scr[h, rows, half_ff : half_ff + half] = grads[:, h * half : (h + 1) * half]
    tail = pl.ds(half_ff, half)

    def tail_copy(h, out):
        return pltpu.make_async_copy(
            parts_scr.at[h, :, tail], out.at[:, tail], out_sems.at[2 + 3 * chunks + h]
        )

    for h in range(2):
        start(lambda out: tail_copy(h, out), h)
    leaving += [tail_copy(h, keep_out) for h in range(2)]
    sq_scr[6:7, :] = jnp.sum(
        jnp.where(lax.broadcasted_iota(jnp.int32, (length, COLS), 1) == 0, valid_ref[:length, :1], 0.0),
        axis=0,
        keepdims=True,
    )
    sums_ref[...] = jnp.broadcast_to(jnp.sum(sq_scr[...], axis=1, keepdims=True), sums_ref.shape)
    for copy in leaving:
        copy.wait()


def mid_call(ctx_c, ctx_q, x_c, x_q, cot_c, cot_q, pad, six, bias_up, planes):
    seqs, wide, length = ctx_c.shape
    count = ctx_q.shape[1]
    preds = x_q.shape[0]
    total = length + count
    uo_own, uo_mate, down_own, down_mate = planes
    chips, shard, cols = uo_own.shape
    ff = cols - COLS
    chunks = ff // COLS
    vm = pl.BlockSpec(memory_space=pltpu.VMEM)
    anywhere = pl.BlockSpec(memory_space=pl.ANY)
    parts = jax.ShapeDtypeStruct((COLS, (cols + ff) // 2), BF16)
    return pl.pallas_call(
        functools.partial(mid_kernel, seqs, FWD_BITS_UP, FWD_BITS_DOWN),
        out_shape=(
            jax.ShapeDtypeStruct(x_c.shape, F32),
            jax.ShapeDtypeStruct((count, COLS), F32),
            jax.ShapeDtypeStruct(ctx_c.shape, BF16),
            jax.ShapeDtypeStruct(ctx_q.shape, BF16),
            jax.ShapeDtypeStruct((6, COLS), F32),
            jax.ShapeDtypeStruct((1, ff), F32),
            jax.ShapeDtypeStruct((8, 128), F32),
            jax.ShapeDtypeStruct(x_c.shape, F32),
            jax.ShapeDtypeStruct((preds, COLS), F32),
            parts,
            parts,
        ),
        in_specs=[vm] * 9 + [anywhere] * 4,
        out_specs=(vm,) * 7 + (anywhere,) * 4,
        scratch_shapes=[
            pltpu.VMEM((COLS, ff), BF16),
            pltpu.VMEM((COLS, COLS), BF16),
            pltpu.VMEM((ff, COLS), BF16),
            pltpu.VMEM((total, COLS), F32),
            pltpu.VMEM((total, COLS), F32),
            pltpu.VMEM((total, 128), F32),
            pltpu.VMEM((total, COLS), BF16),
            pltpu.VMEM((total, ff), BF16),
            pltpu.VMEM((total, ff), F32),
            pltpu.VMEM((total, COLS), F32),
            pltpu.VMEM((total, COLS), BF16),
            pltpu.VMEM((total, COLS), BF16),
            pltpu.VMEM((2, 2, chips, shard, COLS), BF16),
            pltpu.VMEM(x_c.shape, F32),
            pltpu.VMEM((preds, COLS), F32),
            pltpu.VMEM((2,) + parts.shape, BF16),
            pltpu.VMEM((8, COLS), F32),
            pltpu.VMEM((total, 128), F32),
            pltpu.VMEM((count, COLS), F32),
            pltpu.VMEM((count, COLS), F32),
            pltpu.SemaphoreType.DMA((2 * chips,)),
            pltpu.SemaphoreType.DMA((2, 2)),
            pltpu.SemaphoreType.DMA((4 + 3 * chunks,)),
        ],
        compiler_params=pltpu.CompilerParams(vmem_limit_bytes=63 << 20),
        cost_estimate=cost_of(45),
        name="feed_forward",
    )(ctx_c, ctx_q, x_c, x_q, cot_c, cot_q, pad, six, bias_up, *planes)


def proj_kernel(own, keys, x_ref, w_ref, bq_ref, bv_ref, qt_ref, q_ref, k_ref, kt_ref, v_ref, vt_ref):
    wide = own * HEAD_DIM
    rows = x_ref.shape[0]
    for a in range(0, rows, 256):
        b = min(a + 256, rows)
        parts = [(0, bq_ref, qt_ref, q_ref)]
        if b <= keys:
            parts += [(1, None, kt_ref, k_ref), (2, bv_ref, vt_ref, v_ref)]
        y = dot_nn(x_ref[a:b, :], w_ref[:, : len(parts) * wide])
        for n, bias, flat_ref, head_ref in parts:
            part = y[:, n * wide : (n + 1) * wide]
            if bias is not None:
                part = part + bias[...]
            flat_ref[:, a:b] = part.T.astype(BF16)
            for h in range(own):
                head_ref[h, a:b, :] = part[:, h * HEAD_DIM : (h + 1) * HEAD_DIM].astype(BF16)


def proj_call(own, keys, x, w, bq, bv):
    rows = x.shape[0]
    wide = own * HEAD_DIM
    vm = pl.BlockSpec(memory_space=pltpu.VMEM)
    flat = lambda n: jax.ShapeDtypeStruct((wide, n), BF16)
    head = lambda n: jax.ShapeDtypeStruct((own, n, HEAD_DIM), BF16)
    return pl.pallas_call(
        functools.partial(proj_kernel, own, keys),
        out_shape=(flat(rows), head(rows), head(keys), flat(keys), head(keys), flat(keys)),
        in_specs=[vm] * 4,
        out_specs=(vm,) * 6,
        compiler_params=pltpu.CompilerParams(vmem_limit_bytes=40 << 20),
        cost_estimate=cost_of(5),
        name="project",
    )(x, w, bq, bv)


def grads_kernel(
    keys,
    x_ref,
    w_ref,
    dq_ref,
    dk_ref,
    dv_ref,
    offs_ref,
    qoffs_ref,
    bucket_ref,
    six_ref,
    up_ref,
    squares_ref,
    gc_ref,
    gq_ref,
    gw_ref,
    vec_ref,
    shared_ref,
    part_scr,
):
    s = lax.axis_index("seq")
    wide = dq_ref.shape[1]
    seqs, length = gc_ref.shape[:2]
    shard = gw_ref.shape[1]
    for n, ref in enumerate((dq_ref, dk_ref, dv_ref)):
        part_scr[:, n * wide : (n + 1) * wide] = dot_tn(x_ref[: ref.shape[0], :], ref[...])
    for j in range(gw_ref.shape[0]):
        gw_ref[j] = part_scr[j * shard : (j + 1) * shard, :].astype(BF16)
    blocks = vec_ref.shape[0]
    n_one, n_up = six_ref.shape[1] // blocks, up_ref.shape[1] // blocks
    n_qv = 2 * n_one
    vec_ref[...] = jnp.zeros(vec_ref.shape, F32)
    sums = [jnp.sum(ref[...].astype(F32), axis=0, keepdims=True) for ref in (dq_ref, dv_ref)]
    for d in range(blocks):
        vec_ref[d, :6, :n_one] = six_ref[:, d * n_one : (d + 1) * n_one]
        vec_ref[d, 6:7, :n_up] = up_ref[:, d * n_up : (d + 1) * n_up]
        kind, start = divmod(d * n_qv, seqs * wide)
        owner, start = divmod(start, wide)
        piece = sums[kind][:, start : start + n_qv]
        vec_ref[d, 7:8, :n_qv] = jnp.where(s == owner, piece, 0.0)
    own = offs_ref.shape[0]
    table = jnp.zeros((own, BUCKETS), F32)
    for row, ref in ((1, offs_ref), (0, qoffs_ref)):
        hot = (
            lax.broadcasted_iota(jnp.int32, (BUCKETS, ref.shape[1]), 0)
            == bucket_ref[row : row + 1, :]
        ).astype(F32)
        table += lax.dot_general(
            ref[...],
            hot,
            (((1,), (1,)), ((), ())),
            precision=lax.Precision.HIGHEST,
            preferred_element_type=F32,
        )
    shared_ref[...] = jnp.zeros(shared_ref.shape, F32)
    for h in range(own):
        shared_ref[pl.ds(s * own + h, 1), :BUCKETS] = table[h : h + 1]
    shared_ref[16:24, :] = squares_ref[...]
    w_q = w_ref[:, :wide]
    w_k = w_ref[:, wide : 2 * wide]
    w_v = w_ref[:, 2 * wide :]
    step = 256
    for t in range(seqs):
        for a in range(0, length, step):
            at = slice(t * length + a, t * length + a + step)
            gc_ref[t, a : a + step, :] = (
                dot_nt(dq_ref[at, :], w_q) + dot_nt(dk_ref[at, :], w_k) + dot_nt(dv_ref[at, :], w_v)
            ).astype(BF16)
    count = gq_ref.shape[1]
    for t in range(seqs):
        at = slice(keys + t * count, keys + (t + 1) * count)
        gq_ref[t] = dot_nt(dq_ref[at, :], w_q).astype(BF16)


def grads_call(
    seqs, length, count, blocks, x, w, dq, dk, dv, offs, qoffs, buckets, six, up, squares
):
    wide = dq.shape[1]
    shard = x.shape[1] // blocks
    vm = pl.BlockSpec(memory_space=pltpu.VMEM)
    return pl.pallas_call(
        functools.partial(grads_kernel, seqs * length),
        out_shape=(
            jax.ShapeDtypeStruct((seqs, length, x.shape[1]), BF16),
            jax.ShapeDtypeStruct((seqs, count, x.shape[1]), BF16),
            jax.ShapeDtypeStruct((blocks, shard, 3 * wide), BF16),
            jax.ShapeDtypeStruct((blocks, 8, 128), F32),
            jax.ShapeDtypeStruct((24, 128), F32),
        ),
        in_specs=[vm] * 11,
        out_specs=(vm,) * 5,
        scratch_shapes=[pltpu.VMEM((x.shape[1], 3 * wide), F32)],
        compiler_params=pltpu.CompilerParams(vmem_limit_bytes=40 << 20),
        cost_estimate=cost_of(6),
        name="weight_grads",
    )(x, w, dq, dk, dv, offs, qoffs, buckets, six, up, squares)


MESH = pl.DeviceIdType.MESH
ROWS_Q = 384
SLOT_Q = 80


def greet(devices):
    barrier = pltpu.get_barrier_semaphore()
    for device in devices:
        pl.semaphore_signal(barrier, inc=1, device_id=device, device_id_type=MESH)
    pl.semaphore_wait(barrier, len(devices))


def remote(src, dst, send_sem, recv_sem, k, device):
    return pltpu.make_async_remote_copy(
        src_ref=src,
        dst_ref=dst,
        send_sem=send_sem.at[k],
        recv_sem=recv_sem.at[k],
        device_id=device,
        device_id_type=MESH,
    )


def start_kernel(
    dps,
    seqs,
    c_ref,
    q_ref,
    w_ref,
    v_ref,
    seg_ref,
    order_ref,
    pad_ref,
    pred_ref,
    x_out,
    w_out,
    v_out,
    i_out,
    q_scr,
    send_sem,
    recv_sem,
):
    dp = lax.axis_index("dp")
    s = lax.axis_index("seq")
    length = c_ref.shape[0]
    count = q_scr.shape[0]
    mate = s + 1 - 2 * lax.rem(s, 2)
    across = lax.rem(s + 2, seqs)
    level = dp + 1 - 2 * lax.rem(dp, 2)
    stacks = dps // 2
    greet(
        [(dp, lax.rem(s + r, seqs)) for r in range(1, seqs)]
        + [(level, s)]
        + [(lax.rem(dp + 2 * r, dps), s) for r in range(1, stacks)]
    )

    def at_c(owner):
        return pl.ds(pl.multiple_of(owner * length, length), length)

    def at_q(owner):
        return pl.ds(pl.multiple_of(seqs * length + owner * count, 16), count)

    k = 0

    def push(src, dst, device):
        nonlocal k
        copy = remote(src, dst, send_sem, recv_sem, k, device)
        copy.start()
        k += 1
        return copy

    i_out[s] = jnp.zeros(i_out.shape[1:], jnp.int32)
    for n, ref in enumerate((seg_ref, order_ref, pad_ref)):
        i_out[s, n : n + 1, :] = ref[...]
    i_out[s, 3:4, :] = jnp.full((1, length), -1, jnp.int32)
    i_out[s, 3:4, : pred_ref.shape[1]] = pred_ref[...]
    small = []
    for r in range(1, seqs):
        to = lax.rem(s + r, seqs)
        small.append(push(w_ref.at[to], w_out.at[dp, s], (dp, to)))
        small.append(push(v_ref, v_out.at[dp, s], (dp, to)))
        small.append(push(i_out.at[s], i_out.at[s], (dp, to)))
    x_out[at_c(s), :] = c_ref[...].astype(BF16)
    far = [push(x_out.at[at_c(s)], x_out.at[at_c(s)], (dp, across))]
    q_scr[...] = jnp.zeros(q_scr.shape, F32)
    q_scr[: q_ref.shape[0], :] = q_ref[...]
    x_out[at_q(s), :] = q_scr[...].astype(BF16)
    far.append(push(x_out.at[at_q(s)], x_out.at[at_q(s)], (dp, across)))
    near = [push(x_out.at[at(s)], x_out.at[at(s)], (dp, mate)) for at in (at_c, at_q)]
    w_out[dp, s] = w_ref[s]
    v_out[dp, s] = v_ref[...]
    rest = seqs * (length + count)
    x_out[rest:, :] = jnp.zeros((x_out.shape[0] - rest, x_out.shape[1]), BF16)
    for copy in small:
        copy.wait_recv()
    wide, flat = [], []
    for r in range(1, stacks):
        to = lax.rem(dp + 2 * r, dps)
        wide.append([push(ref.at[dp], ref.at[dp], (to, s)) for ref in (w_out, v_out)])
    flat += [push(ref.at[dp], ref.at[dp], (level, s)) for ref in (w_out, v_out)]
    for r in range(1, stacks):
        source = lax.rem(dp + dps - 2 * r, dps)
        for copy, ref in zip(wide[r - 1], (w_out, v_out)):
            copy.wait_recv()
            flat.append(push(ref.at[source], ref.at[source], (level, s)))
    pass_on = []
    for copy, at in zip(far, (at_c, at_q)):
        copy.wait_recv()
        pass_on.append(push(x_out.at[at(across)], x_out.at[at(across)], (dp, mate)))
    for copy in near + flat + pass_on:
        copy.wait_recv()
    for copy in small + far + near + flat + pass_on + sum(wide, []):
        copy.wait_send()


def start_call(dps, seqs, content, query, w, v, metas, slot_q):
    copies = 3 * (seqs - 1) + 4 + 2 * (dps // 2 - 1) + dps + 2
    length, width = content.shape
    vmem = pl.BlockSpec(memory_space=pltpu.VMEM)
    return pl.pallas_call(
        functools.partial(start_kernel, dps, seqs),
        out_shape=(
            jax.ShapeDtypeStruct((seqs * length + ROWS_Q, width), BF16),
            jax.ShapeDtypeStruct((dps,) + w.shape, BF16),
            jax.ShapeDtypeStruct((dps, seqs) + v.shape, F32),
            jax.ShapeDtypeStruct((seqs, 8, length), jnp.int32),
        ),
        in_specs=[vmem] * 8,
        out_specs=(vmem,) * 4,
        scratch_shapes=[
            pltpu.VMEM((slot_q, width), F32),
            pltpu.SemaphoreType.DMA((copies,)),
            pltpu.SemaphoreType.DMA((copies,)),
        ],
        compiler_params=pltpu.CompilerParams(
            collective_id=0, has_side_effects=True, vmem_limit_bytes=30 << 20
        ),
        cost_estimate=cost_of(30),
        name="gather_rows",
    )(content, query, w, v, *metas)


def swap_kernel(seqs, c_of, q_of, c_ref, q_ref, c_out, q_out, send_sem, recv_sem, here_sem):
    dp = lax.axis_index("dp")
    s = lax.axis_index("seq")
    greet([(dp, lax.rem(s + r, seqs)) for r in range(1, seqs)])
    copies = []
    for r in range(1, seqs):
        to = lax.rem(s + r, seqs)
        k = 2 * (r - 1)
        copies.append(remote(c_of(c_ref, to), c_out.at[s], send_sem, recv_sem, k, (dp, to)))
        copies.append(remote(q_of(q_ref, to), q_out.at[s], send_sem, recv_sem, k + 1, (dp, to)))
    for copy in copies:
        copy.start()
    here = [
        pltpu.make_async_copy(c_of(c_ref, s), c_out.at[s], here_sem.at[0]),
        pltpu.make_async_copy(q_of(q_ref, s), q_out.at[s], here_sem.at[1]),
    ]
    for copy in here:
        copy.start()
    for copy in here + copies:
        copy.wait()


def swap_call(seqs, c, q, c_of, q_of, c_shape, q_shape, ident, name):
    vmem = pl.BlockSpec(memory_space=pltpu.VMEM)
    return pl.pallas_call(
        functools.partial(swap_kernel, seqs, c_of, q_of),
        out_shape=(
            jax.ShapeDtypeStruct((seqs,) + c_shape, c.dtype),
            jax.ShapeDtypeStruct((seqs,) + q_shape, q.dtype),
        ),
        in_specs=[vmem] * 2,
        out_specs=(vmem,) * 2,
        scratch_shapes=[
            pltpu.SemaphoreType.DMA((2 * (seqs - 1),)),
            pltpu.SemaphoreType.DMA((2 * (seqs - 1),)),
            pltpu.SemaphoreType.DMA((2,)),
        ],
        compiler_params=pltpu.CompilerParams(collective_id=ident, has_side_effects=True),
        cost_estimate=cost_of(12),
        name=name,
    )(c, q)


def end_kernel(
    dps,
    seqs,
    gc_ref,
    gq_ref,
    w_ref,
    v_ref,
    sh_ref,
    gc_out,
    gq_out,
    w_out,
    v_out,
    sh_out,
    c_mate,
    q_mate,
    c_far,
    q_far,
    c_send,
    q_send,
    w_got,
    v_got,
    w_sum,
    v_sum,
    v_last,
    sh_got,
    sh_sum,
    sh_last,
    send_sem,
    recv_sem,
):
    dp = lax.axis_index("dp")
    s = lax.axis_index("seq")
    core = lax.rem(s, 2)
    mate = s + 1 - 2 * core
    across = lax.rem(s + 2, seqs)
    greet(
        [(dp, lax.rem(s + r, seqs)) for r in range(1, seqs)]
        + [(lax.rem(dp + r, dps), s) for r in range(1, dps)]
    )
    k = 0
    first = []
    for i in range(2):
        to = lax.rem(mate + 2 * (1 - i), seqs)
        for src, dst in ((gc_ref, c_mate), (gq_ref, q_mate)):
            first.append(remote(src.at[to], dst.at[i], send_sem, recv_sem, k, (dp, mate)))
            k += 1
    wide = []
    for r in range(1, dps):
        to = lax.rem(dp + r, dps)
        for src, dst in ((w_ref, w_got), (v_ref, v_got)):
            wide.append(remote(src.at[to], dst.at[r - 1], send_sem, recv_sem, k, (to, s)))
            k += 1
        wide.append(remote(sh_ref, sh_got.at[r - 1], send_sem, recv_sem, k, (to, s)))
        k += 1
    for copy in first + wide:
        copy.start()

    def each(ref, step, fn):
        def body(i, carry):
            fn(pl.ds(pl.multiple_of(i * step, step), step))
            return carry

        lax.fori_loop(0, ref.shape[-2] // step, body, 0)

    cross = []
    for (src, got, buf, far, copy) in (
        (gc_ref, c_mate, c_send, c_far, first[0]),
        (gq_ref, q_mate, q_send, q_far, first[1]),
    ):
        copy.wait_recv()

        def add(rows, src=src, got=got, buf=buf):
            buf[rows, :] = (
                src[across, rows, :].astype(F32) + got[0, rows, :].astype(F32)
            ).astype(BF16)

        each(buf, 16, add)
        cross.append(remote(buf, far, send_sem, recv_sem, k, (dp, across)))
        cross[-1].start()
        k += 1
    for copy in wide:
        copy.wait_recv()

    def add_w(rows):
        for t in range(seqs):
            total = w_ref[dp, t, rows, :].astype(F32)
            for r in range(1, dps):
                total += w_got[r - 1, t, rows, :].astype(F32)
            w_sum[t, rows, :] = total

    each(w_sum, 8, add_w)
    total = v_ref[dp]
    for r in range(1, dps):
        total += v_got[r - 1]
    v_sum[...] = total
    total = sh_ref[...]
    for r in range(1, dps):
        total += sh_got[r - 1]
    sh_sum[...] = total
    last = []
    for r in range(1, seqs):
        to = lax.rem(s + r, seqs)
        last.append(remote(w_sum.at[to], w_out.at[s], send_sem, recv_sem, k, (dp, to)))
        last.append(remote(v_sum.at[to], v_last.at[r - 1], send_sem, recv_sem, k + 1, (dp, to)))
        last.append(remote(sh_sum, sh_last.at[r - 1], send_sem, recv_sem, k + 2, (dp, to)))
        k += 3
    for copy in last:
        copy.start()
    w_out[s] = w_sum[s]
    for copy in first[2:]:
        copy.wait_recv()
    for copy in cross:
        copy.wait_recv()
    for (src, got, far, out) in (
        (gc_ref, c_mate, c_far, gc_out),
        (gq_ref, q_mate, q_far, gq_out),
    ):

        def total_of(rows, src=src, got=got, far=far, out=out):
            out[rows, :] = (
                src[s, rows, :].astype(F32)
                + got[1, rows, :].astype(F32)
                + far[rows, :].astype(F32)
            )

        each(out, 16, total_of)
    for copy in last:
        copy.wait_recv()
    total = v_sum[s]
    for r in range(1, seqs):
        total += v_last[r - 1]
    v_out[...] = total
    total = sh_sum[...]
    for r in range(1, seqs):
        total += sh_last[r - 1]
    sh_out[...] = total
    for copy in first + wide + cross + last:
        copy.wait_send()


def end_call(dps, seqs, gc, gq, w, v, sh):
    copies = 4 + 3 * (dps - 1) + 2 + 3 * (seqs - 1)
    vm = pl.BlockSpec(memory_space=pltpu.VMEM)
    cshape, qshape, wshape, vshape = gc.shape[1:], gq.shape[1:], w.shape[1:], v.shape[1:]
    return pl.pallas_call(
        functools.partial(end_kernel, dps, seqs),
        out_shape=(
            jax.ShapeDtypeStruct(cshape, F32),
            jax.ShapeDtypeStruct(qshape, F32),
            jax.ShapeDtypeStruct(wshape, F32),
            jax.ShapeDtypeStruct(vshape[1:], F32),
            jax.ShapeDtypeStruct(sh.shape, F32),
        ),
        in_specs=[vm] * 5,
        out_specs=(vm,) * 5,
        scratch_shapes=[
            pltpu.VMEM((2,) + cshape, BF16),
            pltpu.VMEM((2,) + qshape, BF16),
            pltpu.VMEM(cshape, BF16),
            pltpu.VMEM(qshape, BF16),
            pltpu.VMEM(cshape, BF16),
            pltpu.VMEM(qshape, BF16),
            pltpu.VMEM((dps - 1,) + wshape, BF16),
            pltpu.VMEM((dps - 1,) + vshape, F32),
            pltpu.VMEM(wshape, F32),
            pltpu.VMEM(vshape, F32),
            pltpu.VMEM((seqs - 1,) + vshape[1:], F32),
            pltpu.VMEM((dps - 1,) + sh.shape, F32),
            pltpu.VMEM(sh.shape, F32),
            pltpu.VMEM((seqs - 1,) + sh.shape, F32),
            pltpu.SemaphoreType.DMA((copies,)),
            pltpu.SemaphoreType.DMA((copies,)),
        ],
        compiler_params=pltpu.CompilerParams(
            collective_id=3, has_side_effects=True, vmem_limit_bytes=50 << 20
        ),
        cost_estimate=cost_of(30),
        name="sum_rows",
    )(gc, gq, w, v, sh)


def flip_perm(count, bit):
    return [(i, i ^ bit) for i in range(count)]


AXES = ("dp", "seq")


def tie(values, *others):
    return lax.optimization_barrier((values, others))[0]


def give_to(cur, count, bit):
    return lax.ppermute(cur, AXES, flip_perm(count, bit))


def pile(cur, got, bit):
    mine = (lax.axis_index(AXES) // bit) % 2
    return jnp.where(mine == 0, jnp.concatenate([cur, got]), jnp.concatenate([got, cur]))


def local_fast(
    content,
    query_stream,
    segment_ids,
    pad_mask,
    predicted,
    order,
    rel_bucket,
    qkv_weight,
    qv_bias,
    out_weight,
    out_bias,
    attn_gain,
    attn_shift,
    up_weight,
    up_bias,
    down_weight,
    down_bias,
    ffn_gain,
    ffn_shift,
    rel_table,
    content_cot,
    query_cot,
):
    dps, seqs = lax.axis_size("dp"), lax.axis_size("seq")
    count = dps * seqs
    s = lax.axis_index("seq")
    own = HEADS // seqs
    wide = own * HEAD_DIM
    length = content.shape[1]
    preds = query_stream.shape[1]
    shard = qkv_weight.shape[0]

    vec = jnp.concatenate(
        [
            member.astype(F32)
            for member in (
                qv_bias,
                up_bias,
                out_bias,
                attn_gain,
                attn_shift,
                down_bias,
                ffn_gain,
                ffn_shift,
            )
        ]
    )
    vec = jnp.pad(vec, (0, 1024 - vec.shape[0])).reshape(8, 128)
    buckets = jnp.stack(
        [
            jnp.pad(rel_bucket, (0, 1), constant_values=BUCKETS),
            jnp.pad(rel_bucket, (1, 0), constant_values=BUCKETS),
        ]
    )
    w_parts = jnp.transpose(
        qkv_weight.reshape(shard, 3, seqs, wide), (2, 0, 1, 3)
    ).reshape(seqs, shard, 3 * wide)
    gather = (jnp.concatenate([up_weight, out_weight], axis=1)[None], down_weight[None])
    stages = list(zip(FWD_BITS_UP, FWD_BITS_DOWN))

    def launch(n):
        return tuple(give_to(cur, count, bit) for cur, bit in zip(gather, stages[n]))

    def land(n, got, *others):
        got = tie(got, *others)
        return tuple(pile(c, g, bit) for c, g, bit in zip(gather, got, stages[n]))

    flying = launch(0)
    x_all, w_all, v_all, i_all = start_call(
        dps,
        seqs,
        content[0],
        query_stream[0],
        w_parts,
        vec,
        (segment_ids, order, pad_mask, predicted),
        SLOT_Q,
    )
    w_qkv = w_all.reshape(MODEL_WIDTH, 3 * wide)
    parts_all = v_all.reshape(count, 1024)
    n_qv, n_up, n_one = qv_bias.shape[0], up_bias.shape[0], out_bias.shape[0]
    cut_up, cut_end = n_qv + n_up, n_qv + n_up + 6 * n_one
    bias_qv = parts_all[:, :n_qv].reshape(count * n_qv)
    bias_up = parts_all[:, n_qv:cut_up].reshape(1, count * n_up)
    six = jnp.transpose(parts_all[:, cut_up:cut_end].reshape(count, 6, n_one), (1, 0, 2)).reshape(
        6, count * n_one
    )
    seg_all = i_all[:, 0].reshape(seqs * length)
    pad_all = i_all[:, 2].reshape(seqs * length)
    span = key_spans(seg_all, pad_all)

    gather = land(0, flying, i_all)
    flying = launch(1)
    first = (s * own).astype(jnp.int32)[None]
    ints = tie(i_all, gather)
    tiles, qbias, kmeta, rseg, rlim, hot, shift = bias_call(
        own, ROWS_Q, SLOT_Q, first, buckets, rel_table, ints
    )

    bq = lax.dynamic_slice_in_dim(bias_qv[:MODEL_WIDTH], s * wide, wide)
    bv = lax.dynamic_slice_in_dim(bias_qv[MODEL_WIDTH:], s * wide, wide)
    gather = land(1, flying, tiles)
    flying = launch(2)
    x_all = tie(x_all, gather)
    q_t, q3, k3, k_t, v3, v_t = proj_call(
        own, seqs * length, x_all, w_qkv, bq[None], bv[None]
    )
    gather = land(2, flying, q_t)
    flying = launch(3)
    q_t = tie(q_t, gather)

    ctx_t, ctx_rows, lse = fwd_call(span, q_t, k3, v_t, kmeta, rseg, rlim, tiles, qbias)

    gather = land(3, flying, ctx_rows)
    others = tuple(give_to(cur, count, 1) for cur in gather)
    ctx_rows = tie(ctx_rows, gather)
    planes = (gather[0], others[0], gather[1], others[1])

    def from_lanes(ref, t):
        return ref.at[:, pl.ds(pl.multiple_of(t * length, length), length)]

    def from_query(ref, t):
        return ref.at[pl.ds(pl.multiple_of(t * SLOT_Q, 16), SLOT_Q)]

    ctx_c, ctx_q = swap_call(
        seqs,
        ctx_t,
        ctx_rows,
        from_lanes,
        from_query,
        (wide, length),
        (SLOT_Q, wide),
        1,
        "swap_context",
    )
    (
        res_c,
        res_q,
        give_c,
        give_q,
        six_sums,
        up_sums,
        squares,
        out_c,
        out_q,
        keep,
        give,
    ) = mid_call(
        ctx_c,
        ctx_q,
        content[0],
        query_stream[0],
        content_cot[0],
        query_cot[0],
        pad_mask,
        six,
        bias_up,
        planes,
    )
    core = s % 2
    spot = (lax.axis_index(AXES) // 2) % 4
    flying = give_to(give, count, 1)

    def both(mine, got):
        total = mine.astype(F32) + got.astype(F32)
        return total.astype(BF16).reshape((2, 2, 4, mine.shape[0] // 16, mine.shape[1]))

    def block(x, index):
        return lax.dynamic_index_in_dim(x, index, 2, keepdims=False)

    def from_slot(ref, t):
        return ref.at[t]

    g_c, g_q = swap_call(
        seqs,
        give_c,
        give_q,
        from_slot,
        from_slot,
        (wide, length),
        (SLOT_Q, wide),
        2,
        "swap_grads",
    )
    flying = tie(flying, g_c)
    pairs = both(keep, flying)
    gone = tuple(block(pairs, spot ^ r) for r in (1, 2, 3))
    flying = tuple(give_to(x, count, 2 * r) for x, r in zip(gone, (1, 2, 3)))
    stay = block(pairs, spot)
    g_c = tie(g_c, stay, gone)
    dq, dk, dv, offs, qoffs = bwd_call(
        span,
        q_t,
        q3,
        k3,
        k_t,
        v3,
        ctx_t,
        g_c,
        g_q.reshape(seqs * SLOT_Q, wide),
        lse,
        kmeta,
        rseg,
        rlim,
        tiles,
        hot,
        shift,
        qbias,
    )
    flying = tie(flying, dq)

    def total_of(kept, got):
        total = kept.astype(F32)
        for x in got:
            total += x.astype(F32)
        return total

    def split(x, bit):
        mine = (lax.axis_index(AXES) // bit) % 2
        axis = x.ndim - 3
        away = lax.dynamic_index_in_dim(x, 1 - mine, axis, keepdims=False).astype(BF16)
        return away, lax.dynamic_index_in_dim(x, mine, axis, keepdims=False)

    gone, stay = split(total_of(stay, flying), 8)
    flying = give_to(gone, count, 8)
    dq = tie(dq, stay, gone)
    grad_c, grad_q, grad_w, vec_grads, shared = grads_call(
        seqs,
        length,
        SLOT_Q,
        count,
        x_all,
        w_qkv,
        dq,
        dk,
        dv,
        offs,
        qoffs,
        buckets,
        six_sums,
        up_sums,
        squares,
    )
    flying = tie(flying, grad_c)
    gone, stay = split(total_of(stay, (flying,)), 16)
    flying = give_to(gone, count, 16)
    grad_c = tie(grad_c, stay, gone)
    sum_c, sum_q, sum_w, sum_v, sum_shared = end_call(
        dps,
        seqs,
        grad_c,
        grad_q,
        grad_w.reshape(dps, seqs, shard, 3 * wide),
        vec_grads.reshape(dps, seqs, 8, 128),
        shared,
    )
    flying = tie(flying, sum_c)
    pair = total_of(stay, (flying,))
    half_ff, half = up_weight.shape[1] // 2, MODEL_WIDTH // 2
    wide_up = half_ff + half
    first, second = pair[:shard], pair[shard:]
    low_cols, high_cols = pair[:, wide_up : wide_up + half_ff // 2], pair[:, wide_up + half_ff // 2 :]

    def pick(a, b):
        return jnp.where(core == 0, a, b), jnp.where(core == 0, b, a)

    rows_mine, rows_away = pick(first[:, :wide_up], second[:, :wide_up])
    cols_mine, cols_away = pick(low_cols, high_cols)
    rows_got = give_to(rows_away, count, 1)
    cols_got = give_to(cols_away, count, 1)
    rows_low, rows_high = pick(rows_mine, rows_got)
    grad_up_own = jnp.concatenate([rows_low[:, :half_ff], rows_high[:, :half_ff]], axis=1)
    grad_out_own = jnp.concatenate([rows_low[:, half_ff:], rows_high[:, half_ff:]], axis=1)

    def unfold(x):
        return jnp.concatenate([x[:, :half], x[:, half:]], axis=0)

    cols_low, cols_high = pick(unfold(cols_mine), unfold(cols_got))
    grad_down_own = jnp.concatenate([cols_low, cols_high], axis=1)
    grad_content = res_c + sum_c
    grad_query = res_q[:preds] + sum_q[:preds]
    grad_qkv_own = jnp.transpose(sum_w.reshape(seqs, shard, 3, wide), (1, 2, 0, 3)).reshape(
        shard, 3 * MODEL_WIDTH
    )
    mine = [sum_v[7, :n_qv], sum_v[6, :n_up]] + [sum_v[i, :n_one] for i in range(6)]
    table_sum = sum_shared[:HEADS, :BUCKETS].T
    totals = sum_shared[16:23, 0]
    content_count = totals[6] * MODEL_WIDTH
    query_count = float(dps * preds * seqs * MODEL_WIDTH)
    each = jnp.stack([content_count, jnp.float32(query_count)])
    stats = jnp.sqrt(totals[:6] / jnp.concatenate([each, each, each]))
    return (
        out_c[None],
        out_q[None],
        grad_content[None],
        grad_query[None],
        grad_qkv_own,
        mine[0],
        grad_out_own,
        mine[2],
        mine[3],
        mine[4],
        grad_up_own,
        mine[1],
        grad_down_own,
        mine[5],
        mine[6],
        mine[7],
        table_sum,
        stats,
    )


def pick_local(mesh):
    sizes = dict(mesh.shape)
    return local_fast if (sizes["dp"], sizes["seq"]) == (8, 4) else local_general


def solution(mesh):
    in_specs = (
        P("dp", "seq", None),
        P("dp", "seq", None),
        P("dp", "seq"),
        P("dp", "seq"),
        P("dp", "seq"),
        P("dp", "seq"),
        P(),
        P(("dp", "seq"), None),
        P(("dp", "seq")),
        P(("dp", "seq"), None),
        P(("dp", "seq")),
        P(("dp", "seq")),
        P(("dp", "seq")),
        P(("dp", "seq"), None),
        P(("dp", "seq")),
        P(("dp", "seq"), None),
        P(("dp", "seq")),
        P(("dp", "seq")),
        P(("dp", "seq")),
        P(),
        P("dp", "seq", None),
        P("dp", "seq", None),
    )
    out_specs = (
        P("dp", "seq", None),
        P("dp", "seq", None),
        P("dp", "seq", None),
        P("dp", "seq", None),
        P(("dp", "seq"), None),
        P(("dp", "seq")),
        P(("dp", "seq"), None),
        P(("dp", "seq")),
        P(("dp", "seq")),
        P(("dp", "seq")),
        P(("dp", "seq"), None),
        P(("dp", "seq")),
        P(("dp", "seq"), None),
        P(("dp", "seq")),
        P(("dp", "seq")),
        P(("dp", "seq")),
        P(),
        P(),
    )
    local = pick_local(mesh)
    return jax.shard_map(local, mesh=mesh, in_specs=in_specs, out_specs=out_specs, check_vma=False)
```

```python
import functools
import math

import jax
import jax.numpy as jnp
from jax import lax
from jax.experimental import pallas as pl
from jax.experimental.pallas import tpu as pltpu
from jax.sharding import PartitionSpec as P

MODEL_WIDTH = 768
HEADS = 12
HEAD_DIM = 64
BUCKETS = 32
SEQ_LEN = 2048


EPS = 1e-05
NEG = -1000000000.0
SCALE = 0.125


def exact_gelu(values):
    return jax.nn.gelu(values, approximate=False)


def norm_fwd(residual, gain_vec, shift_vec):
    row_mean = jnp.mean(residual, axis=-1, keepdims=True)
    centered = residual - row_mean
    inv_std = lax.rsqrt(jnp.mean(centered * centered, axis=-1, keepdims=True) + EPS)
    normed = centered * inv_std
    return (normed * gain_vec + shift_vec, normed, inv_std)


def norm_back(upstream, normed, inv_std, gain_vec):
    grad_norm = upstream * gain_vec
    projected = jnp.mean(grad_norm, axis=-1, keepdims=True) + normed * jnp.mean(
        grad_norm * normed, axis=-1, keepdims=True
    )
    return (
        inv_std * (grad_norm - projected),
        jnp.sum(upstream * normed, axis=(0, 1)),
        jnp.sum(upstream, axis=(0, 1)),
    )


def bucket_edges(rel_bucket):
    entry_count = rel_bucket.shape[0]
    matches = rel_bucket[None, :] == jnp.arange(BUCKETS, dtype=jnp.int32)[:, None]
    places = jnp.arange(entry_count, dtype=jnp.int32)[None, :]
    starts = jnp.min(jnp.where(matches, places, entry_count), axis=1)
    counts = jnp.sum(matches.astype(jnp.int32), axis=1)
    return (starts, starts + counts)


def build_mask(
    query_pos, query_seg, query_limit, content_row, key_pos, key_seg, key_order, key_pad
):
    inside = (
        (query_seg[:, None] == key_seg[None, :])
        & (key_pad[None, :] == 1)
        & (key_order[None, :] <= query_limit[:, None])
    )
    itself = (key_pos[None, :] == query_pos[:, None]) & content_row[:, None]
    return (inside | itself, key_pos[None, :] - query_pos[:, None] + (SEQ_LEN - 1))


def masked_scores(query_heads, key_heads, table_low, edges, allowed, offsets):
    raw_scores = (
        jnp.einsum("rhd,lhd->hrl", query_heads, key_heads, preferred_element_type=jnp.float32)
        * SCALE
    )
    starts, ends = edges
    spread = offsets[..., None]
    onehot = ((spread >= starts) & (spread < ends)).astype(jnp.bfloat16)
    bias = jnp.einsum("rlb,bh->hrl", onehot, table_low, preferred_element_type=jnp.float32)
    return (jnp.where(allowed[None], raw_scores + bias, NEG), onehot)


def attend_forward(packed, table_low, edges, content_row):
    queries, key_values, key_seg, key_order, key_pad, query_pos, query_seg, query_limit = packed
    row_count = queries.shape[0]
    length = key_values.shape[0]
    key_pos = jnp.arange(length, dtype=jnp.int32)
    allowed, offsets = build_mask(
        query_pos, query_seg, query_limit, content_row, key_pos, key_seg, key_order, key_pad
    )
    query_heads = queries.reshape(row_count, HEADS, HEAD_DIM)
    key_heads = key_values[:, :MODEL_WIDTH].reshape(length, HEADS, HEAD_DIM)
    value_heads = key_values[:, MODEL_WIDTH:].reshape(length, HEADS, HEAD_DIM)
    scores, onehot = masked_scores(query_heads, key_heads, table_low, edges, allowed, offsets)
    row_max = jnp.max(scores, axis=-1, keepdims=True)
    expo_vals = jnp.exp(scores - row_max)
    row_total = jnp.sum(expo_vals, axis=-1, keepdims=True)
    probs_low = (expo_vals / row_total).astype(jnp.bfloat16)
    context = jnp.einsum("hrl,lhd->rhd", probs_low, value_heads, preferred_element_type=jnp.float32)
    return (
        context.reshape(row_count, MODEL_WIDTH),
        jnp.transpose((row_max + jnp.log(row_total))[..., 0]),
    )


def attend_backward(packed, table_low, edges, content_row):
    (
        queries,
        key_values,
        key_seg,
        key_order,
        key_pad,
        query_pos,
        query_seg,
        query_limit,
        row_lse,
        grad_context,
    ) = packed
    row_count = queries.shape[0]
    length = key_values.shape[0]
    key_pos = jnp.arange(length, dtype=jnp.int32)
    allowed, offsets = build_mask(
        query_pos, query_seg, query_limit, content_row, key_pos, key_seg, key_order, key_pad
    )
    query_heads = queries.reshape(row_count, HEADS, HEAD_DIM)
    key_heads = key_values[:, :MODEL_WIDTH].reshape(length, HEADS, HEAD_DIM)
    value_heads = key_values[:, MODEL_WIDTH:].reshape(length, HEADS, HEAD_DIM)
    scores, onehot = masked_scores(query_heads, key_heads, table_low, edges, allowed, offsets)
    probs = jnp.exp(scores - jnp.transpose(row_lse)[..., None])
    grad_heads = grad_context.reshape(row_count, HEADS, HEAD_DIM)
    grad_probs = jnp.einsum(
        "rhd,lhd->hrl", grad_heads, value_heads, preferred_element_type=jnp.float32
    )
    row_delta = jnp.sum(probs * grad_probs, axis=-1)
    grad_scores = (probs * (grad_probs - row_delta[..., None])).astype(jnp.bfloat16)
    grad_query = (
        jnp.einsum("hrl,lhd->rhd", grad_scores, key_heads, preferred_element_type=jnp.float32)
        * SCALE
    )
    grad_table = jnp.einsum("hrl,rlb->bh", grad_scores, onehot, preferred_element_type=jnp.float32)
    results = (grad_query.reshape(row_count, MODEL_WIDTH), grad_table, jnp.transpose(row_delta))
    probs_low = probs.astype(jnp.bfloat16)
    grad_key = (
        jnp.einsum("hrl,rhd->lhd", grad_scores, query_heads, preferred_element_type=jnp.float32)
        * SCALE
    )
    grad_value = jnp.einsum(
        "hrl,rhd->lhd", probs_low, grad_heads, preferred_element_type=jnp.float32
    )
    results = results + (
        jnp.concatenate(
            [grad_key.reshape(length, MODEL_WIDTH), grad_value.reshape(length, MODEL_WIDTH)],
            axis=-1,
        ),
    )
    return results


def local_general(
    content,
    query_stream,
    segment_ids,
    pad_mask,
    predicted,
    order,
    rel_bucket,
    qkv_weight,
    qv_bias,
    out_weight,
    out_bias,
    attn_gain,
    attn_shift,
    up_weight,
    up_bias,
    down_weight,
    down_bias,
    ffn_gain,
    ffn_shift,
    rel_table,
    content_cot,
    query_cot,
):
    seq_count = content.shape[0]
    shard_length = content.shape[1]
    pred_count = query_stream.shape[1]
    row_count = shard_length + pred_count
    group_size = lax.axis_size("seq")
    edges = bucket_edges(rel_bucket)
    shards = (
        lax.all_gather(qkv_weight, ("dp", "seq"), axis=0, tiled=True),
        lax.all_gather(out_weight, ("dp", "seq"), axis=0, tiled=True),
        lax.all_gather(up_weight, ("dp", "seq"), axis=0, tiled=True),
        lax.all_gather(down_weight, ("dp", "seq"), axis=0, tiled=True),
        lax.all_gather(qv_bias, ("dp", "seq"), axis=0, tiled=True),
        lax.all_gather(out_bias, ("dp", "seq"), axis=0, tiled=True),
        lax.all_gather(attn_gain, ("dp", "seq"), axis=0, tiled=True),
        lax.all_gather(attn_shift, ("dp", "seq"), axis=0, tiled=True),
        lax.all_gather(up_bias, ("dp", "seq"), axis=0, tiled=True),
        lax.all_gather(down_bias, ("dp", "seq"), axis=0, tiled=True),
        lax.all_gather(ffn_gain, ("dp", "seq"), axis=0, tiled=True),
        lax.all_gather(ffn_shift, ("dp", "seq"), axis=0, tiled=True),
    )
    query_key_value_weight, w_out, w_up, w_down = (shards[0], shards[1], shards[2], shards[3])
    bias_qv, bias_out, first_norm_gain, shift_one, bias_up, bias_down, gain_two, shift_two = [
        member.astype(jnp.float32) for member in shards[4:]
    ]
    all_rows = jnp.concatenate([content, query_stream], axis=1)
    reduced_precision_rows = all_rows.astype(jnp.bfloat16)
    queries = (
        jnp.einsum(
            "srd,de->sre",
            reduced_precision_rows,
            query_key_value_weight[:, :MODEL_WIDTH],
            preferred_element_type=jnp.float32,
        )
        + bias_qv[:MODEL_WIDTH]
    ).astype(jnp.bfloat16)
    value_shift = jnp.concatenate([jnp.zeros((MODEL_WIDTH,), jnp.float32), bias_qv[MODEL_WIDTH:]])
    key_values = (
        jnp.einsum(
            "zci,ip->zcp",
            reduced_precision_rows[:, :shard_length],
            query_key_value_weight[:, MODEL_WIDTH:],
            preferred_element_type=jnp.float32,
        )
        + value_shift
    ).astype(jnp.bfloat16)
    full_pairs, full_seg, full_order, full_pad = (
        lax.all_gather(key_values, "seq", axis=1, tiled=True),
        lax.all_gather(segment_ids, "seq", axis=1, tiled=True),
        lax.all_gather(order, "seq", axis=1, tiled=True),
        lax.all_gather(pad_mask, "seq", axis=1, tiled=True),
    )
    content_pos = lax.axis_index("seq") * shard_length + jnp.arange(shard_length, dtype=jnp.int32)
    query_pos = jnp.concatenate(
        [jnp.broadcast_to(content_pos[None, :], (seq_count, shard_length)), predicted], axis=1
    )
    query_seg = jnp.concatenate(
        [segment_ids, jnp.take_along_axis(full_seg, predicted, axis=1)], axis=1
    )
    query_limit = jnp.concatenate(
        [order, jnp.take_along_axis(full_order, predicted, axis=1) - 1], axis=1
    )
    content_row = jnp.arange(row_count, dtype=jnp.int32) < shard_length
    row_meta = (full_seg, full_order, full_pad, query_pos, query_seg, query_limit)

    def forward_one(packed):
        return attend_forward(packed, rel_table, edges, content_row)

    context, row_lse = lax.map(forward_one, (queries, full_pairs) + row_meta)
    context_low = context.astype(jnp.bfloat16)
    attn_out = (
        jnp.einsum("sre,ed->srd", context_low, w_out, preferred_element_type=jnp.float32) + bias_out
    )
    hidden_one, normed_one, inv_one = norm_fwd(all_rows + attn_out, first_norm_gain, shift_one)
    hidden_low = hidden_one.astype(jnp.bfloat16)
    pre_act = (
        jnp.einsum("srd,df->srf", hidden_low, w_up, preferred_element_type=jnp.float32) + bias_up
    )
    activ, gelu_pull = jax.vjp(exact_gelu, pre_act)
    activ_low = activ.astype(jnp.bfloat16)
    ffn_out = (
        jnp.einsum("srf,fd->srd", activ_low, w_down, preferred_element_type=jnp.float32) + bias_down
    )
    hidden_two, normed_two, inv_two = norm_fwd(hidden_one + ffn_out, gain_two, shift_two)
    pad_float = pad_mask.astype(jnp.float32)
    row_valid = jnp.concatenate(
        [pad_float, jnp.ones((seq_count, pred_count), jnp.float32)], axis=1
    )[..., None]
    outputs = hidden_two * row_valid
    pad_weight = pad_float[..., None]
    local_sums = jnp.stack(
        [
            jnp.sum(pad_weight * content * content),
            jnp.sum(query_stream * query_stream),
            jnp.sum(pad_weight * attn_out[:, :shard_length] * attn_out[:, :shard_length]),
            jnp.sum(attn_out[:, shard_length:] * attn_out[:, shard_length:]),
            jnp.sum(pad_weight * ffn_out[:, :shard_length] * ffn_out[:, :shard_length]),
            jnp.sum(ffn_out[:, shard_length:] * ffn_out[:, shard_length:]),
            jnp.sum(pad_float),
        ]
    )
    back_weights = (
        lax.all_gather(qkv_weight, ("dp", "seq"), axis=0, tiled=True),
        lax.all_gather(out_weight, ("dp", "seq"), axis=0, tiled=True),
        lax.all_gather(up_weight, ("dp", "seq"), axis=0, tiled=True),
        lax.all_gather(down_weight, ("dp", "seq"), axis=0, tiled=True),
        lax.all_gather(attn_gain, ("dp", "seq"), axis=0, tiled=True),
        lax.all_gather(ffn_gain, ("dp", "seq"), axis=0, tiled=True),
    )
    back_pairs = lax.all_gather(key_values, "seq", axis=1, tiled=True)
    backward_query_key_value, back_out, back_up, back_down = (
        back_weights[0],
        back_weights[1],
        back_weights[2],
        back_weights[3],
    )
    back_gain_one = back_weights[4].astype(jnp.float32)
    back_gain_two = back_weights[5].astype(jnp.float32)
    upstream = jnp.concatenate([content_cot, query_cot], axis=1) * row_valid
    grad_res_two, grad_gain_two, grad_shift_two = norm_back(
        upstream, normed_two, inv_two, back_gain_two
    )
    grad_ffn = grad_res_two.astype(jnp.bfloat16)
    grad_bias_down = jnp.sum(grad_ffn, axis=(0, 1), dtype=jnp.float32)
    grad_down = jnp.einsum("srf,srd->fd", activ_low, grad_ffn, preferred_element_type=jnp.float32)
    grad_activ = jnp.einsum("srd,fd->srf", grad_ffn, back_down, preferred_element_type=jnp.float32)
    grad_pre = gelu_pull(grad_activ)[0].astype(jnp.bfloat16)
    grad_bias_up = jnp.sum(grad_pre, axis=(0, 1), dtype=jnp.float32)
    grad_up = jnp.einsum("srd,srf->df", hidden_low, grad_pre, preferred_element_type=jnp.float32)
    grad_hidden = grad_res_two + jnp.einsum(
        "srf,df->srd", grad_pre, back_up, preferred_element_type=jnp.float32
    )
    grad_res_one, grad_gain_one, grad_shift_one = norm_back(
        grad_hidden, normed_one, inv_one, back_gain_one
    )
    grad_attn = grad_res_one.astype(jnp.bfloat16)
    grad_bias_out = jnp.sum(grad_attn, axis=(0, 1), dtype=jnp.float32)
    grad_out = jnp.einsum("sre,srd->ed", context_low, grad_attn, preferred_element_type=jnp.float32)
    grad_context = jnp.einsum(
        "srd,ed->sre", grad_attn, back_out, preferred_element_type=jnp.float32
    ).astype(jnp.bfloat16)

    def backward_all(packed):
        return attend_backward(packed, rel_table, edges, content_row)

    grad_queries, grad_tables, per_row_delta, grad_pairs = lax.map(
        backward_all, (queries, back_pairs) + row_meta + (row_lse, grad_context)
    )
    paired_gradients = lax.psum_scatter(
        grad_pairs.astype(jnp.bfloat16), "seq", scatter_dimension=1, tiled=True
    )
    query_grads = grad_queries.astype(jnp.bfloat16)
    grad_bias_qv = jnp.concatenate(
        [
            jnp.sum(query_grads, axis=(0, 1), dtype=jnp.float32),
            jnp.sum(paired_gradients[..., MODEL_WIDTH:], axis=(0, 1), dtype=jnp.float32),
        ]
    )
    grad_qkv = jnp.concatenate(
        [
            jnp.einsum(
                "srd,sre->de",
                reduced_precision_rows,
                query_grads,
                preferred_element_type=jnp.float32,
            ),
            jnp.einsum(
                "cvi,cvp->ip",
                reduced_precision_rows[:, :shard_length],
                paired_gradients,
                preferred_element_type=jnp.float32,
            ),
        ],
        axis=1,
    )
    grad_rows = grad_res_one + jnp.einsum(
        "sre,de->srd",
        query_grads,
        backward_query_key_value[:, :MODEL_WIDTH],
        preferred_element_type=jnp.float32,
    )
    grad_content = grad_rows[:, :shard_length] + jnp.einsum(
        "zwv,bv->zwb",
        paired_gradients,
        backward_query_key_value[:, MODEL_WIDTH:],
        preferred_element_type=jnp.float32,
    )
    grad_query = grad_rows[:, shard_length:]
    owned = (
        lax.psum_scatter(grad_qkv, ("dp", "seq"), scatter_dimension=0, tiled=True),
        lax.psum_scatter(grad_out, ("dp", "seq"), scatter_dimension=0, tiled=True),
        lax.psum_scatter(grad_up, ("dp", "seq"), scatter_dimension=0, tiled=True),
        lax.psum_scatter(grad_down, ("dp", "seq"), scatter_dimension=0, tiled=True),
        lax.psum_scatter(grad_bias_qv, ("dp", "seq"), scatter_dimension=0, tiled=True),
        lax.psum_scatter(grad_bias_out, ("dp", "seq"), scatter_dimension=0, tiled=True),
        lax.psum_scatter(grad_gain_one, ("dp", "seq"), scatter_dimension=0, tiled=True),
        lax.psum_scatter(grad_shift_one, ("dp", "seq"), scatter_dimension=0, tiled=True),
        lax.psum_scatter(grad_bias_up, ("dp", "seq"), scatter_dimension=0, tiled=True),
        lax.psum_scatter(grad_bias_down, ("dp", "seq"), scatter_dimension=0, tiled=True),
        lax.psum_scatter(grad_gain_two, ("dp", "seq"), scatter_dimension=0, tiled=True),
        lax.psum_scatter(grad_shift_two, ("dp", "seq"), scatter_dimension=0, tiled=True),
    )
    table_sum, totals = lax.psum((jnp.sum(grad_tables, axis=0), local_sums), ("dp", "seq"))
    content_count = totals[6] * MODEL_WIDTH
    query_count = float(seq_count * lax.axis_size("dp") * pred_count * group_size * MODEL_WIDTH)
    stats = jnp.sqrt(
        jnp.stack(
            [
                totals[0] / content_count,
                totals[1] / query_count,
                totals[2] / content_count,
                totals[3] / query_count,
                totals[4] / content_count,
                totals[5] / query_count,
            ]
        )
    )
    return (
        outputs[:, :shard_length],
        outputs[:, shard_length:],
        grad_content,
        grad_query,
        owned[0],
        owned[4],
        owned[1],
        owned[5],
        owned[6],
        owned[7],
        owned[2],
        owned[8],
        owned[3],
        owned[9],
        owned[10],
        owned[11],
        table_sum,
        stats,
    )


LOG2E = math.log2(math.e)
TILE = 256
KEYS = 512
HALF = 128
REACH = 11
DIAGS = 2 * REACH + 1
WIDE = SEQ_LEN + HALF
MASKED = -1e30
F32 = jnp.float32
BF16 = jnp.bfloat16


def dot_nn(a, b):
    return jnp.dot(a, b, preferred_element_type=F32)


def dot_nt(a, b):
    return lax.dot_general(a, b, (((1,), (1,)), ((), ())), preferred_element_type=F32)


def dot_tn(a, b):
    return lax.dot_general(a, b, (((0,), (0,)), ((), ())), preferred_element_type=F32)


def cost_of(micros):
    return pl.CostEstimate(
        flops=int(micros * 1.0e9), bytes_accessed=int(micros * 1.0e6), transcendentals=0
    )


def bias_kernel(
    rows_q,
    own,
    slot_q,
    heads_ref,
    bucket_ref,
    table_ref,
    ints_ref,
    tile_out,
    qbias_out,
    kmeta_ref,
    rseg_ref,
    rlim_ref,
    hot_ref,
    shift_ref,
    vec_scr,
    ahead_scr,
    fold_scr,
    tile_scr,
    qbias_scr,
    sems,
):
    seqs, length = ints_ref.shape[0], ints_ref.shape[2]
    first = heads_ref[0]
    hot = (
        lax.broadcasted_iota(jnp.int32, (BUCKETS, 2 * SEQ_LEN), 0) == bucket_ref[0:1, :]
    ).astype(BF16)
    vec_scr[...] = dot_tn(table_ref[...], hot)
    hot = (
        lax.broadcasted_iota(jnp.int32, (BUCKETS, 2 * SEQ_LEN), 0) == bucket_ref[1:2, :]
    ).astype(BF16)
    ahead_scr[...] = dot_tn(table_ref[...], hot) * LOG2E
    copies = []
    for h in range(own):
        row = ahead_scr[pl.ds(first + h, 1), :]
        for e in range(-REACH, REACH + 1):
            start = HALF * (15 + e)
            skew = pltpu.roll(
                jnp.broadcast_to(row[:, start : start + 2 * HALF], (HALF, 2 * HALF)),
                0,
                1,
                stride=1,
                stride_axis=0,
            )
            tile_scr[h, e + REACH] = skew[:, HALF:].T
        copies.append(pltpu.make_async_copy(tile_scr.at[h], tile_out.at[h], sems.at[h]))
        copies[-1].start()
        vec = vec_scr[pl.ds(first + h, 1), :]
        fold_scr[h] = jnp.concatenate(
            [vec[:, HALF * i : HALF * i + WIDE] for i in range(16)], axis=0
        ).astype(BF16)

    place = lax.broadcasted_iota(jnp.int32, (1, length), 1)
    lane = lax.broadcasted_iota(jnp.int32, (HALF, HALF), 1)
    segs, orders = [], []
    for t in range(seqs):
        seg = ints_ref[t, 0:1, :]
        seg = jnp.where(ints_ref[t, 2:3, :] == 1, seg, -2 - t * length - place)
        order = ints_ref[t, 1:2, :]
        rseg_ref[:, t * length : (t + 1) * length] = seg
        rlim_ref[:, t * length : (t + 1) * length] = order
        for n, row in ((0, seg.astype(F32)), (1, order.astype(F32))):
            for i in range(length // HALF):
                part = row[:, i * HALF : (i + 1) * HALF]
                (segs, orders)[n].append(part)
                kmeta_ref[n, t * length + i * HALF : t * length + (i + 1) * HALF, :] = (
                    jnp.broadcast_to(part, (HALF, HALF)).T.astype(jnp.int32)
                )
    segs = jnp.concatenate(segs, axis=0)
    orders = jnp.concatenate(orders, axis=0)
    preds = [ints_ref[t, 3:4, :slot_q].astype(F32) for t in range(seqs)]
    preds.append(jnp.full((1, rows_q - seqs * slot_q), -1.0, F32))
    preds = jnp.concatenate(preds, axis=1)
    high = lax.Precision.HIGHEST
    for t in range(rows_q // HALF):
        at = slice(t * HALF, (t + 1) * HALF)
        spots = jnp.broadcast_to(preds[:, at], (HALF, HALF)).T.astype(jnp.int32)
        group = jnp.right_shift(spots, 7)
        inside = jnp.bitwise_and(spots, HALF - 1)
        pick = (lane == group)[:, :16].astype(F32)
        for rows, ref, less in ((segs, rseg_ref, 0.0), (orders, rlim_ref, 1.0)):
            spread = jnp.dot(pick, rows, precision=high, preferred_element_type=F32)
            found = jnp.take_along_axis(spread, inside, axis=1) - less
            ref[:, length * seqs + t * HALF : length * seqs + (t + 1) * HALF] = found.T[
                0:1, :
            ].astype(jnp.int32)
        hot_ref[at, :] = (lane == 15 - group)[:, :16].astype(BF16)
        shift_ref[at, :] = HALF - 1 - inside

    for h in range(own):
        for t in range(rows_q // HALF):
            at = slice(t * HALF, (t + 1) * HALF)
            turn = lane + shift_ref[at, :]
            wrap = turn >= HALF
            idx = jnp.where(wrap, turn - HALF, turn)
            spread = dot_nn(hot_ref[at, :], fold_scr[h])
            prev = jnp.take_along_axis(spread[:, :HALF], idx, axis=1)
            for j in range(SEQ_LEN // HALF):
                cur = jnp.take_along_axis(
                    spread[:, (j + 1) * HALF : (j + 2) * HALF], idx, axis=1
                )
                out = jnp.where(wrap, cur, prev) * LOG2E
                qbias_scr[h, j * HALF : (j + 1) * HALF, at] = out.T
                prev = cur
        copies.append(pltpu.make_async_copy(qbias_scr.at[h], qbias_out.at[h], sems.at[own + h]))
        copies[-1].start()
    for copy in copies:
        copy.wait()


def bias_call(own, rows_q, slot_q, first, buckets, table, ints):
    vm = pl.BlockSpec(memory_space=pltpu.VMEM)
    anywhere = pl.BlockSpec(memory_space=pl.ANY)
    tiles = jax.ShapeDtypeStruct((own, DIAGS, HALF, HALF), F32)
    qbias = jax.ShapeDtypeStruct((own, SEQ_LEN, rows_q), F32)
    rows = jax.ShapeDtypeStruct((1, SEQ_LEN + rows_q), jnp.int32)
    return pl.pallas_call(
        functools.partial(bias_kernel, rows_q, own, slot_q),
        out_shape=(
            tiles,
            qbias,
            jax.ShapeDtypeStruct((2, SEQ_LEN, HALF), jnp.int32),
            rows,
            rows,
            jax.ShapeDtypeStruct((rows_q, 16), BF16),
            jax.ShapeDtypeStruct((rows_q, HALF), jnp.int32),
        ),
        in_specs=[pl.BlockSpec(memory_space=pltpu.SMEM)] + [vm] * 3,
        out_specs=(anywhere,) * 2 + (vm,) * 5,
        scratch_shapes=[
            pltpu.VMEM((table.shape[1], 2 * SEQ_LEN), F32),
            pltpu.VMEM((table.shape[1], 2 * SEQ_LEN), F32),
            pltpu.VMEM((own, 16, WIDE), BF16),
            pltpu.VMEM(tiles.shape, F32),
            pltpu.VMEM(qbias.shape, F32),
            pltpu.SemaphoreType.DMA((2 * own,)),
        ],
        compiler_params=pltpu.CompilerParams(vmem_limit_bytes=24 << 20),
        cost_estimate=cost_of(12),
        name="bias_tiles",
    )(first, buckets, table, ints)


def bias_block(tile_ref, h, e):
    return jnp.concatenate(
        [
            jnp.concatenate([tile_ref[h, e + i], tile_ref[h, e + i - 1]], axis=1)
            for i in range(KEYS // HALF)
        ],
        axis=0,
    )


def mask_block(kmeta_ref, rseg_ref, rlim_ref, krow, rcol, width):
    kseg = kmeta_ref[0, pl.ds(krow, KEYS), :]
    kord = kmeta_ref[1, pl.ds(krow, KEYS), :]
    parts = []
    for w in range(width // HALF):
        rseg = rseg_ref[:, pl.ds(rcol + w * HALF, HALF)]
        rlim = rlim_ref[:, pl.ds(rcol + w * HALF, HALF)]
        ok = (kseg == rseg) & (kord <= rlim)
        parts.append(jnp.where(ok, 0.0, MASKED))
    return parts[0] if len(parts) == 1 else jnp.concatenate(parts, axis=1)


def fwd_kernel(
    own,
    rows_q,
    span_ref,
    qt_ref,
    k_ref,
    vt_ref,
    kmeta_ref,
    rseg_ref,
    rlim_ref,
    tile_ref,
    qbias_ref,
    ctx_ref,
    rows_ref,
    lse_ref,
    s_scr,
    qbias_scr,
    qbias_sem,
):
    late = pltpu.make_async_copy(qbias_ref, qbias_scr, qbias_sem.at[0])
    late.start()

    def run(rcol, width, lo, steps, bias_of):
        heads = range(own)

        def fold(op, x):
            rows = [x[i * 8 : (i + 1) * 8] for i in range(x.shape[0] // 8)]
            while len(rows) > 1:
                rows = [op(rows[i], rows[i + 1]) for i in range(0, len(rows), 2)]
            return rows[0]

        def score(step, tops):
            kt = lo + step * (KEYS // TILE)
            krow = pl.multiple_of(kt * TILE, TILE)
            mask = mask_block(kmeta_ref, rseg_ref, rlim_ref, krow, rcol, width)
            new = []
            for h in heads:
                s = jnp.dot(
                    k_ref[h, pl.ds(krow, KEYS), :],
                    qt_ref[h * HEAD_DIM : (h + 1) * HEAD_DIM, pl.ds(rcol, width)],
                    preferred_element_type=F32,
                )
                s = s * (SCALE * LOG2E) + (bias_of(h, kt) + mask)
                s_scr[h, pl.ds(krow, KEYS), :width] = s
                new.append(jnp.maximum(tops[h], fold(jnp.maximum, s)))
            return tuple(new)

        tops = lax.fori_loop(
            0, steps, score, tuple(jnp.full((8, width), MASKED, F32) for _ in heads)
        )
        tops = [jnp.max(t, axis=0, keepdims=True) for t in tops]

        def weigh(step, carry):
            kt = lo + step * (KEYS // TILE)
            krow = pl.multiple_of(kt * TILE, TILE)
            sums, accs = carry
            new_sums, new_accs = [], []
            for h in heads:
                p = jnp.exp2(s_scr[h, pl.ds(krow, KEYS), :width] - tops[h])
                new_sums.append(sums[h] + fold(jnp.add, p))
                new_accs.append(
                    accs[h]
                    + jnp.dot(
                        vt_ref[h * HEAD_DIM : (h + 1) * HEAD_DIM, pl.ds(krow, KEYS)],
                        p.astype(BF16),
                        preferred_element_type=F32,
                    )
                )
            return tuple(new_sums), tuple(new_accs)

        sums, accs = lax.fori_loop(
            0,
            steps,
            weigh,
            (
                tuple(jnp.zeros((8, width), F32) for _ in heads),
                tuple(jnp.zeros((HEAD_DIM, width), F32) for _ in heads),
            ),
        )
        outs = []
        for h in heads:
            total = jnp.sum(sums[h], axis=0, keepdims=True)
            outs.append(accs[h] / total)
            lse_ref[h : h + 1, pl.ds(rcol, width)] = tops[h] + jnp.log2(total)
        out = jnp.concatenate(outs, axis=0)
        ctx_ref[:, pl.ds(rcol, width)] = out.astype(BF16)
        return out

    def content_tile(qt, carry):
        def bias_of(h, kt):
            return bias_block(tile_ref, h, 2 * (kt - qt) + REACH)

        run(pl.multiple_of(qt * TILE, TILE), TILE, span_ref[0, qt], span_ref[1, qt], bias_of)
        return carry

    lax.fori_loop(0, SEQ_LEN // TILE, content_tile, 0)

    def query_bias(h, kt):
        return qbias_scr[h, pl.ds(pl.multiple_of(kt * TILE, TILE), KEYS), :]

    late.wait()
    last = SEQ_LEN // TILE
    out = run(SEQ_LEN, rows_q, span_ref[0, last], span_ref[1, last], query_bias)
    rows_ref[...] = out.T.astype(BF16)


def fwd_call(span, qt, k3, vt, kmeta, rseg, rlim, tiles, qbias):
    own = k3.shape[0]
    rows = qt.shape[1]
    rows_q = rows - SEQ_LEN
    vm = pl.BlockSpec(memory_space=pltpu.VMEM)
    return pl.pallas_call(
        functools.partial(fwd_kernel, own, rows_q),
        out_shape=(
            jax.ShapeDtypeStruct((own * HEAD_DIM, rows), BF16),
            jax.ShapeDtypeStruct((rows_q, own * HEAD_DIM), BF16),
            jax.ShapeDtypeStruct((own, rows), F32),
        ),
        in_specs=[pl.BlockSpec(memory_space=pltpu.SMEM)]
        + [vm] * 7
        + [pl.BlockSpec(memory_space=pl.ANY)],
        scratch_shapes=[
            pltpu.VMEM((own, SEQ_LEN, max(rows_q, TILE)), F32),
            pltpu.VMEM(qbias.shape, F32),
            pltpu.SemaphoreType.DMA((1,)),
        ],
        compiler_params=pltpu.CompilerParams(vmem_limit_bytes=40 << 20),
        cost_estimate=cost_of(32),
        name="attend",
    )(span, qt, k3, vt, kmeta, rseg, rlim, tiles, qbias)


def bwd_kernel(
    own,
    rows_q,
    span_ref,
    qt_ref,
    q_ref,
    k_ref,
    kt_ref,
    v_ref,
    ctx_ref,
    gc_ref,
    gq_ref,
    lse_ref,
    kmeta_ref,
    rseg_ref,
    rlim_ref,
    tile_ref,
    hot_ref,
    shift_ref,
    qbias_ref,
    dq_ref,
    dk_ref,
    dv_ref,
    offs_ref,
    qoffs_ref,
    dk_scr,
    dv_scr,
    dq_scr,
    diag_scr,
    ds_scr,
    delta_scr,
    gt_ref,
    g_ref,
    qbias_scr,
    qbias_sem,
):
    late = pltpu.make_async_copy(qbias_ref, qbias_scr, qbias_sem.at[0])
    late.start()
    seqs, length = gc_ref.shape[0], gc_ref.shape[2]
    for t in range(seqs):
        for a in range(0, length, TILE):
            block = gc_ref[t, :, a : a + TILE]
            at = slice(t * length + a, t * length + a + TILE)
            gt_ref[:, at] = block
            back = block.astype(F32).T
            for h in range(own):
                g_ref[h, at, :] = back[:, h * HEAD_DIM : (h + 1) * HEAD_DIM].astype(BF16)
    used = gq_ref.shape[0]
    block = jnp.concatenate(
        [gq_ref[...].astype(F32), jnp.zeros((rows_q - used, gq_ref.shape[1]), F32)], axis=0
    )
    gt_ref[:, SEQ_LEN:] = block.T.astype(BF16)
    for h in range(own):
        g_ref[h, SEQ_LEN:, :] = block[:, h * HEAD_DIM : (h + 1) * HEAD_DIM].astype(BF16)
    dk_scr[...] = jnp.zeros(dk_scr.shape, F32)
    dv_scr[...] = jnp.zeros(dv_scr.shape, F32)
    diag_scr[...] = jnp.zeros(diag_scr.shape, F32)
    ds_scr[...] = jnp.zeros(ds_scr.shape, BF16)
    for h in range(own):
        part = slice(h * HEAD_DIM, (h + 1) * HEAD_DIM)
        delta_scr[h : h + 1, :] = jnp.sum(
            ctx_ref[part, :].astype(F32) * gt_ref[part, :].astype(F32), axis=0, keepdims=True
        )

    def run(rcol, width, lo, steps, bias_of, keep):
        dq_scr[...] = jnp.zeros(dq_scr.shape, F32)

        def body(step, carry):
            kt = lo + step * (KEYS // TILE)
            krow = pl.multiple_of(kt * TILE, TILE)
            mask = mask_block(kmeta_ref, rseg_ref, rlim_ref, krow, rcol, width)
            for h in range(own):
                part = slice(h * HEAD_DIM, (h + 1) * HEAD_DIM)
                s = jnp.dot(
                    k_ref[h, pl.ds(krow, KEYS), :],
                    qt_ref[part, pl.ds(rcol, width)],
                    preferred_element_type=F32,
                )
                s = s * (SCALE * LOG2E) + (bias_of(h, kt) + mask)
                p = jnp.exp2(s - lse_ref[h : h + 1, pl.ds(rcol, width)])
                gp = jnp.dot(
                    v_ref[h, pl.ds(krow, KEYS), :],
                    gt_ref[part, pl.ds(rcol, width)],
                    preferred_element_type=F32,
                )
                ds = p * (gp - delta_scr[h : h + 1, pl.ds(rcol, width)])
                low = ds.astype(BF16)
                keep(h, kt, ds, low)
                dv_scr[h, pl.ds(krow, KEYS), :] += jnp.dot(
                    p.astype(BF16), g_ref[h, pl.ds(rcol, width), :], preferred_element_type=F32
                )
                dk_scr[h, pl.ds(krow, KEYS), :] += jnp.dot(
                    low, q_ref[h, pl.ds(rcol, width), :], preferred_element_type=F32
                )
                dq_scr[h, :, :width] += jnp.dot(
                    kt_ref[part, pl.ds(krow, KEYS)], low, preferred_element_type=F32
                )
            return carry

        lax.fori_loop(0, steps, body, 0)
        grad = jnp.concatenate([dq_scr[h, :, :width] for h in range(own)], axis=0)
        dq_ref[pl.ds(rcol, width), :] = (grad * SCALE).T.astype(BF16)

    def content_tile(qt, carry):
        def bias_of(h, kt):
            return bias_block(tile_ref, h, 2 * (kt - qt) + REACH)

        def keep(h, kt, ds, low):
            e = 2 * (kt - qt) + REACH
            subs = [ds[i * HALF : (i + 1) * HALF] for i in range(KEYS // HALF)]
            diag_scr[h, e - 1] += subs[0][:, HALF:]
            for i, sub in enumerate(subs):
                here = sub[:, :HALF]
                if i + 1 < len(subs):
                    here = here + subs[i + 1][:, HALF:]
                diag_scr[h, e + i] += here

        run(pl.multiple_of(qt * TILE, TILE), TILE, span_ref[0, qt], span_ref[1, qt], bias_of, keep)
        return carry

    lax.fori_loop(0, SEQ_LEN // TILE, content_tile, 0)

    def query_bias(h, kt):
        return qbias_scr[h, pl.ds(pl.multiple_of(kt * TILE, TILE), KEYS), :]

    def query_keep(h, kt, ds, low):
        ds_scr[h, pl.ds(pl.multiple_of(kt * TILE, TILE), KEYS), :] = low

    late.wait()
    last = SEQ_LEN // TILE
    run(SEQ_LEN, rows_q, span_ref[0, last], span_ref[1, last], query_bias, query_keep)

    for a in range(0, SEQ_LEN, TILE):
        at = slice(a, a + TILE)
        for scr, ref, scale in ((dk_scr, dk_ref, SCALE), (dv_scr, dv_ref, 1.0)):
            block = jnp.concatenate([scr[h, at, :] for h in range(own)], axis=1)
            ref[at, :] = (block * scale).astype(BF16)

    offs_ref[...] = jnp.zeros(offs_ref.shape, F32)
    qoffs_ref[...] = jnp.zeros(qoffs_ref.shape, F32)
    lane = lax.broadcasted_iota(jnp.int32, (HALF, HALF), 1)
    turn = lane + lax.broadcasted_iota(jnp.int32, (HALF, HALF), 0)
    over = turn >= HALF
    turn = jnp.where(over, turn - HALF, turn)
    for h in range(own):
        for e in range(DIAGS):
            skew = jnp.take_along_axis(diag_scr[h, e].T, turn, axis=1)
            start = HALF * (15 + e - REACH)
            offs_ref[h : h + 1, start : start + HALF] += jnp.sum(
                jnp.where(over, skew, 0.0), axis=0, keepdims=True
            )
            offs_ref[h : h + 1, start + HALF : start + 2 * HALF] += jnp.sum(
                jnp.where(over, 0.0, skew), axis=0, keepdims=True
            )

    for h in range(own):
        total = jnp.zeros((16, WIDE), F32)
        for t in range(rows_q // HALF):
            shift = shift_ref[t * HALF : (t + 1) * HALF, :]
            place = lane - shift
            low_side = place < 0
            idx = jnp.where(low_side, place + HALF, place)
            prev = jnp.zeros((HALF, HALF), F32)
            pieces = []
            for j in range(SEQ_LEN // HALF + 1):
                if j < SEQ_LEN // HALF:
                    block = ds_scr[h, j * HALF : (j + 1) * HALF, t * HALF : (t + 1) * HALF]
                    cur = jnp.take_along_axis(block.astype(F32).T, idx, axis=1)
                else:
                    cur = jnp.zeros((HALF, HALF), F32)
                pieces.append(jnp.where(low_side, prev, cur).astype(BF16))
                prev = cur
            total += dot_tn(
                hot_ref[t * HALF : (t + 1) * HALF, :], jnp.concatenate(pieces, axis=1)
            )
        for i in range(16):
            qoffs_ref[h : h + 1, HALF * i : HALF * i + WIDE] += total[i : i + 1, :]


def bwd_call(
    span, qt, q3, k3, kt, v3, ctx, g_c, g_q, lse, kmeta, rseg, rlim, tiles, hot, shift, qbias
):
    own = k3.shape[0]
    rows = qt.shape[1]
    rows_q = rows - SEQ_LEN
    vm = pl.BlockSpec(memory_space=pltpu.VMEM)
    return pl.pallas_call(
        functools.partial(bwd_kernel, own, rows_q),
        out_shape=(
            jax.ShapeDtypeStruct((rows, own * HEAD_DIM), BF16),
            jax.ShapeDtypeStruct((SEQ_LEN, own * HEAD_DIM), BF16),
            jax.ShapeDtypeStruct((SEQ_LEN, own * HEAD_DIM), BF16),
            jax.ShapeDtypeStruct((own, 2 * SEQ_LEN), F32),
            jax.ShapeDtypeStruct((own, 2 * SEQ_LEN), F32),
        ),
        in_specs=[pl.BlockSpec(memory_space=pltpu.SMEM)]
        + [vm] * 15
        + [pl.BlockSpec(memory_space=pl.ANY)],
        scratch_shapes=[
            pltpu.VMEM((own, SEQ_LEN, HEAD_DIM), F32),
            pltpu.VMEM((own, SEQ_LEN, HEAD_DIM), F32),
            pltpu.VMEM((own, HEAD_DIM, max(rows_q, TILE)), F32),
            pltpu.VMEM((own, DIAGS, HALF, HALF), F32),
            pltpu.VMEM((own, SEQ_LEN, rows_q), BF16),
            pltpu.VMEM((own, rows), F32),
            pltpu.VMEM((own * HEAD_DIM, rows), BF16),
            pltpu.VMEM((own, rows, HEAD_DIM), BF16),
            pltpu.VMEM(qbias.shape, F32),
            pltpu.SemaphoreType.DMA((1,)),
        ],
        compiler_params=pltpu.CompilerParams(vmem_limit_bytes=56 << 20),
        cost_estimate=cost_of(58),
        name="attend_back",
    )(span, qt, q3, k3, kt, v3, ctx, g_c, g_q, lse, kmeta, rseg, rlim, tiles, hot, shift, qbias)


def key_spans(segment, pad_mask):
    length = segment.shape[0]
    real = pad_mask == 1
    head_seg = segment[::TILE]
    tail_seg = segment[TILE - 1 :: TILE]
    starts = jnp.sum((segment[None, :] < head_seg[:, None]).astype(jnp.int32), axis=1)
    first = jnp.arange(0, length, TILE, dtype=jnp.int32)
    lo = jnp.where(real[::TILE], starts, first) // TILE
    hi = jnp.where(real[TILE - 1 :: TILE], tail_seg, first + TILE - 1) // TILE
    count = jnp.sum(pad_mask)
    lo = jnp.concatenate([lo, jnp.zeros((1,), jnp.int32)])
    hi = jnp.concatenate([hi, jnp.maximum(count - 1, 0)[None] // TILE])
    per = KEYS // TILE
    steps = (hi - lo + per) // per
    lo = jnp.minimum(lo, length // TILE - steps * per)
    return jnp.stack([lo, steps]).astype(jnp.int32)


COLS = 768
UP_TOP = (2, 1)
DOWN_TOP = (1, 2)


def place_of(j, top):
    return (
        8 * (j % 2)
        + 4 * ((j // 2) % 2)
        + top[0] * ((j // 4) % 2)
        + top[1] * (j // 8)
    )


def mid_kernel(
    seqs,
    ctx_c,
    ctx_q,
    x_c,
    x_q,
    cot_c,
    cot_q,
    pad_ref,
    six_ref,
    bias_up,
    uo_own,
    uo_own_far,
    uo_mate,
    uo_mate_far,
    down_own,
    down_own_far,
    down_mate,
    down_mate_far,
    res_c,
    res_q,
    gctx_c,
    gctx_q,
    six_out,
    up_out,
    sums_ref,
    out_c,
    out_q,
    keep_out,
    give_out,
    w_up,
    w_out,
    w_down,
    one_scr,
    norm_scr,
    inv_scr,
    low_scr,
    act_scr,
    slope_scr,
    sum_scr,
    grad_scr,
    pre_scr,
    plane_scr,
    outc_scr,
    outq_scr,
    parts_scr,
    sq_scr,
    valid_ref,
    xq_scr,
    cotq_scr,
    sems,
    plane_sems,
    out_sems,
):
    core = lax.rem(lax.axis_index("seq"), 2)
    this = lax.axis_index("dp") * (seqs // 2) + lax.axis_index("seq") // 2
    near, shard = uo_own.shape[0], uo_own.shape[1]
    chips = 2 * near
    shard_down = down_own.shape[1]
    length = x_c.shape[0]
    preds = x_q.shape[0]
    count = xq_scr.shape[0]
    ff = w_up.shape[1]
    chunks = ff // COLS
    wide = ctx_c.shape[1]
    half_ff, half = ff // 2, COLS // 2
    bias_out, gain_one, shift_one, bias_down, gain_two, shift_two = [
        six_ref[i : i + 1, :] for i in range(6)
    ]

    def plane_copies(chunk, slot):
        start = chunk * COLS
        if not isinstance(start, int):
            start = pl.multiple_of(start, COLS)
        return [
            pltpu.make_async_copy(
                ref.at[:, :, pl.ds(start, COLS)],
                plane_scr.at[slot, n // 2, pl.ds(near * (n % 2), near)],
                plane_sems.at[slot, n],
            )
            for n, ref in enumerate((uo_own, uo_own_far, uo_mate, uo_mate_far))
        ]

    def assemble(slot, put_rows):
        def body(j, carry):
            chip = this ^ place_of(j, UP_TOP)
            first = plane_scr[slot, core, j].astype(F32)
            second = plane_scr[slot, 1 - core, j].astype(F32)
            pair = jnp.concatenate([first, second], axis=0).astype(BF16)
            put_rows(pl.ds(pl.multiple_of(2 * shard * chip, 16), 2 * shard), pair)
            return carry

        lax.fori_loop(0, chips, body, 0)

    for chunk, slot in ((chunks, 0), (0, 1)):
        for copy in plane_copies(chunk, slot):
            copy.start()
    copies = []
    for j in range(chips):
        chip = this ^ place_of(j, DOWN_TOP)
        own, mate = ((down_own, down_mate), (down_own_far, down_mate_far))[j // near]
        for side, ref in ((core, own), (1 - core, mate)):
            row = pl.multiple_of((2 * chip + side) * shard_down, 16)
            copies.append(
                pltpu.make_async_copy(
                    ref.at[j % near], w_down.at[pl.ds(row, shard_down)], sems.at[len(copies)]
                )
            )
    for copy in copies:
        copy.start()
    for copy in plane_copies(chunks, 0):
        copy.wait()

    def put_out(rows, pair):
        w_out[rows, :] = pair

    assemble(0, put_out)
    for copy in plane_copies(1, 0):
        copy.start()

    for a in range(0, length, 128):
        row = pad_ref[:, a : a + 128].astype(F32)
        valid_ref[a : a + 128, :] = jnp.broadcast_to(row, (128, 128)).T
    spot = lax.broadcasted_iota(jnp.int32, (count, 128), 0)
    valid_ref[length:, :] = jnp.where(spot < preds, 1.0, 0.0)
    for ref, scr in ((x_q, xq_scr), (cot_q, cotq_scr)):
        scr[...] = jnp.zeros(scr.shape, F32)
        scr[:preds, :] = ref[...]
    blocks = [(0, length // 2), (length // 2, length), (length, length + count)]

    def pick(ref_c, ref_q, a, b):
        return ref_c[a:b, :] if b <= length else ref_q[...]

    def put(ref_c, ref_q, a, b, value):
        if b <= length:
            ref_c[a:b, :] = value
        else:
            ref_q[...] = value[: ref_q.shape[0]]

    def norm(x):
        mean = jnp.mean(x, axis=-1, keepdims=True)
        centered = x - mean
        inv = lax.rsqrt(jnp.mean(centered * centered, axis=-1, keepdims=True) + EPS)
        return centered * inv, inv

    def norm_grad(up, normed, inv, gain):
        grad = up * gain
        proj = jnp.mean(grad, axis=-1, keepdims=True) + normed * jnp.mean(
            grad * normed, axis=-1, keepdims=True
        )
        return inv * (grad - proj)

    sq_scr[...] = jnp.zeros(sq_scr.shape, F32)
    six_out[...] = jnp.zeros(six_out.shape, F32)
    up_out[...] = jnp.zeros(up_out.shape, F32)

    def count_in(k, x, a, b):
        row = k + (1 if b > length else 0)
        sq_scr[row : row + 1, :] += jnp.sum(x * x * valid_ref[a:b, :1], axis=0, keepdims=True)

    def add_row(row, x):
        six_out[row : row + 1, :] += jnp.sum(x, axis=0, keepdims=True)

    for a, b in blocks:
        attn = bias_out
        for t in range(seqs):
            part = w_out[t * wide : (t + 1) * wide, :]
            attn = attn + (
                dot_tn(ctx_c[t, :, a:b], part) if b <= length else dot_nn(ctx_q[t], part)
            )
        x = pick(x_c, xq_scr, a, b)
        count_in(0, x, a, b)
        count_in(2, attn, a, b)
        normed, inv = norm(x + attn)
        one = normed * gain_one + shift_one
        norm_scr[a:b, :] = normed
        inv_scr[a:b, :] = jnp.broadcast_to(inv, (b - a, 128))
        one_scr[a:b, :] = one
        low_scr[a:b, :] = one.astype(BF16)

    for copy in copies:
        copy.wait()
    sum_scr[...] = jnp.zeros(sum_scr.shape, F32)

    def up_step(i, carry):
        cols = pl.ds(pl.multiple_of(i * COLS, COLS), COLS)
        slot = lax.rem(i + 1, 2)
        for copy in plane_copies(i, slot):
            copy.wait()

        def put_up(rows, pair):
            w_up[rows, cols] = pair

        assemble(slot, put_up)

        @pl.when(i + 2 < chunks)
        def _():
            for copy in plane_copies(i + 2, slot):
                copy.start()

        for a, b in blocks:
            u = dot_nn(low_scr[a:b, :], w_up[:, cols]) + bias_up[:, cols]
            cdf = 0.5 * (1.0 + lax.erf(u * math.sqrt(0.5)))
            act = (u * cdf).astype(BF16)
            act_scr[a:b, cols] = act
            slope_scr[a:b, cols] = cdf + u * (
                jnp.exp(-0.5 * u * u) * (1.0 / math.sqrt(2.0 * math.pi))
            )
            sum_scr[a:b, :] += dot_nn(act, w_down[cols, :])
        return carry

    lax.fori_loop(0, chunks, up_step, 0)

    for a, b in blocks:
        ffn = sum_scr[a:b, :] + bias_down
        count_in(4, ffn, a, b)
        normed, inv = norm(one_scr[a:b, :] + ffn)
        ok = valid_ref[a:b, :1]
        put(outc_scr, outq_scr, a, b, (normed * gain_two + shift_two) * ok)
        up = pick(cot_c, cotq_scr, a, b) * ok
        add_row(4, up * normed)
        add_row(5, up)
        grad = norm_grad(up, normed, inv, gain_two)
        low = grad.astype(BF16)
        add_row(3, low.astype(F32))
        sum_scr[a:b, :] = grad
        grad_scr[a:b, :] = low
    leaving = [
        pltpu.make_async_copy(outc_scr, out_c, out_sems.at[0]),
        pltpu.make_async_copy(outq_scr, out_q, out_sems.at[1]),
    ]
    for copy in leaving:
        copy.start()

    def start(copy_of, h):
        @pl.when(core == h)
        def _():
            copy_of(keep_out).start()

        @pl.when(core != h)
        def _():
            copy_of(give_out).start()

    def up_copy(i, out):
        h, at = i // 2, lax.rem(i, 2) if not isinstance(i, int) else i % 2
        cols = pl.ds(pl.multiple_of(at * COLS, COLS) if not isinstance(i, int) else at * COLS, COLS)
        return pltpu.make_async_copy(
            parts_scr.at[h, :, cols], out.at[:, cols], out_sems.at[2 + i]
        )

    down_rows = 2 * shard * (COLS // (2 * shard_down))
    down_cols = pl.ds(half_ff + half, half_ff)

    def down_copy(i, h, out):
        start = i * down_rows
        rows = pl.ds(start if isinstance(i, int) else pl.multiple_of(start, down_rows), down_rows)
        return pltpu.make_async_copy(
            parts_scr.at[h, rows, down_cols],
            out.at[rows, down_cols],
            out_sems.at[2 + chunks * (1 + h) + i],
        )

    def back_step(i, carry):
        cols = pl.ds(pl.multiple_of(i * COLS, COLS), COLS)
        for a, b in blocks:
            low = (
                dot_nt(grad_scr[a:b, :], w_down[cols, :]) * slope_scr[a:b, cols]
            ).astype(BF16)
            pre_scr[a:b, :] = low
            up_out[:, cols] += jnp.sum(low.astype(F32), axis=0, keepdims=True)
            sum_scr[a:b, :] += dot_nt(low, w_up[:, cols])
        at = pl.ds(pl.multiple_of(lax.rem(i, 2) * COLS, COLS), COLS)
        parts_scr[i // 2, :, at] = dot_tn(low_scr[...], pre_scr[...]).astype(BF16)
        start(lambda out: up_copy(i, out), i // 2)
        grads = dot_tn(act_scr[:, cols], grad_scr[...]).astype(BF16)
        for h in range(2):
            for chip in range(COLS // (2 * shard_down)):
                to = pl.ds(pl.multiple_of(i * down_rows, down_rows) + chip * 2 * shard, 2 * shard)
                for g in range(shard_down // shard):
                    row = 2 * shard_down * chip + 2 * shard * g
                    col = half_ff + half * (1 + g)
                    parts_scr[h, to, col : col + half] = grads[
                        row : row + 2 * shard, h * half : (h + 1) * half
                    ]
            start(lambda out: down_copy(i, h, out), h)
        return carry

    lax.fori_loop(0, chunks, back_step, 0)
    leaving += [up_copy(i, keep_out) for i in range(chunks)]
    leaving += [down_copy(i, h, keep_out) for i in range(chunks) for h in range(2)]

    for a, b in blocks:
        up = sum_scr[a:b, :]
        normed = norm_scr[a:b, :]
        add_row(1, up * normed)
        add_row(2, up)
        grad = norm_grad(up, normed, inv_scr[a:b, :1], gain_one)
        low = grad.astype(BF16)
        add_row(0, low.astype(F32))
        put(res_c, res_q, a, b, grad)
        grad_scr[a:b, :] = low
    for t in range(seqs):
        rows = slice(t * wide, (t + 1) * wide)
        part = w_out[rows, :]
        gctx_c[t] = dot_nt(part, grad_scr[:length, :]).astype(BF16)
        gctx_q[t] = dot_nt(grad_scr[length:, :], part).astype(BF16)
        grads = (
            dot_nn(ctx_c[t], grad_scr[:length, :]) + dot_tn(ctx_q[t], grad_scr[length:, :])
        ).astype(BF16)
        for h in range(2):
            parts_scr[h, rows, half_ff : half_ff + half] = grads[:, h * half : (h + 1) * half]
    tail = pl.ds(half_ff, half)

    def tail_copy(h, out):
        return pltpu.make_async_copy(
            parts_scr.at[h, :, tail], out.at[:, tail], out_sems.at[2 + 3 * chunks + h]
        )

    for h in range(2):
        start(lambda out: tail_copy(h, out), h)
    leaving += [tail_copy(h, keep_out) for h in range(2)]
    sq_scr[6:7, :] = jnp.sum(
        jnp.where(lax.broadcasted_iota(jnp.int32, (length, COLS), 1) == 0, valid_ref[:length, :1], 0.0),
        axis=0,
        keepdims=True,
    )
    sums_ref[...] = jnp.broadcast_to(jnp.sum(sq_scr[...], axis=1, keepdims=True), sums_ref.shape)
    for copy in leaving:
        copy.wait()


def mid_call(ctx_c, ctx_q, x_c, x_q, cot_c, cot_q, pad, six, bias_up, planes):
    seqs, wide, length = ctx_c.shape
    count = ctx_q.shape[1]
    preds = x_q.shape[0]
    total = length + count
    near, shard, cols = planes[0].shape
    chips = 2 * near
    ff = cols - COLS
    chunks = ff // COLS
    vm = pl.BlockSpec(memory_space=pltpu.VMEM)
    anywhere = pl.BlockSpec(memory_space=pl.ANY)
    parts = jax.ShapeDtypeStruct((COLS, (cols + ff) // 2), BF16)
    return pl.pallas_call(
        functools.partial(mid_kernel, seqs),
        out_shape=(
            jax.ShapeDtypeStruct(x_c.shape, F32),
            jax.ShapeDtypeStruct((count, COLS), F32),
            jax.ShapeDtypeStruct(ctx_c.shape, BF16),
            jax.ShapeDtypeStruct(ctx_q.shape, BF16),
            jax.ShapeDtypeStruct((6, COLS), F32),
            jax.ShapeDtypeStruct((1, ff), F32),
            jax.ShapeDtypeStruct((8, 128), F32),
            jax.ShapeDtypeStruct(x_c.shape, F32),
            jax.ShapeDtypeStruct((preds, COLS), F32),
            parts,
            parts,
        ),
        in_specs=[vm] * 9 + [anywhere] * 8,
        out_specs=(vm,) * 7 + (anywhere,) * 4,
        scratch_shapes=[
            pltpu.VMEM((COLS, ff), BF16),
            pltpu.VMEM((COLS, COLS), BF16),
            pltpu.VMEM((ff, COLS), BF16),
            pltpu.VMEM((total, COLS), F32),
            pltpu.VMEM((total, COLS), F32),
            pltpu.VMEM((total, 128), F32),
            pltpu.VMEM((total, COLS), BF16),
            pltpu.VMEM((total, ff), BF16),
            pltpu.VMEM((total, ff), F32),
            pltpu.VMEM((total, COLS), F32),
            pltpu.VMEM((total, COLS), BF16),
            pltpu.VMEM((total, COLS), BF16),
            pltpu.VMEM((2, 2, chips, shard, COLS), BF16),
            pltpu.VMEM(x_c.shape, F32),
            pltpu.VMEM((preds, COLS), F32),
            pltpu.VMEM((2,) + parts.shape, BF16),
            pltpu.VMEM((8, COLS), F32),
            pltpu.VMEM((total, 128), F32),
            pltpu.VMEM((count, COLS), F32),
            pltpu.VMEM((count, COLS), F32),
            pltpu.SemaphoreType.DMA((2 * chips,)),
            pltpu.SemaphoreType.DMA((2, 4)),
            pltpu.SemaphoreType.DMA((4 + 3 * chunks,)),
        ],
        compiler_params=pltpu.CompilerParams(vmem_limit_bytes=63 << 20),
        cost_estimate=cost_of(45),
        name="feed_forward",
    )(ctx_c, ctx_q, x_c, x_q, cot_c, cot_q, pad, six, bias_up, *planes)


def proj_kernel(own, keys, x_ref, w_ref, bq_ref, bv_ref, qt_ref, q_ref, k_ref, kt_ref, v_ref, vt_ref):
    wide = own * HEAD_DIM
    rows = x_ref.shape[0]
    for a in range(0, rows, 256):
        b = min(a + 256, rows)
        parts = [(0, bq_ref, qt_ref, q_ref)]
        if b <= keys:
            parts += [(1, None, kt_ref, k_ref), (2, bv_ref, vt_ref, v_ref)]
        y = dot_nn(x_ref[a:b, :], w_ref[:, : len(parts) * wide])
        for n, bias, flat_ref, head_ref in parts:
            part = y[:, n * wide : (n + 1) * wide]
            if bias is not None:
                part = part + bias[...]
            flat_ref[:, a:b] = part.T.astype(BF16)
            for h in range(own):
                head_ref[h, a:b, :] = part[:, h * HEAD_DIM : (h + 1) * HEAD_DIM].astype(BF16)


def proj_call(own, keys, x, w, bq, bv):
    rows = x.shape[0]
    wide = own * HEAD_DIM
    vm = pl.BlockSpec(memory_space=pltpu.VMEM)
    flat = lambda n: jax.ShapeDtypeStruct((wide, n), BF16)
    head = lambda n: jax.ShapeDtypeStruct((own, n, HEAD_DIM), BF16)
    return pl.pallas_call(
        functools.partial(proj_kernel, own, keys),
        out_shape=(flat(rows), head(rows), head(keys), flat(keys), head(keys), flat(keys)),
        in_specs=[vm] * 4,
        out_specs=(vm,) * 6,
        compiler_params=pltpu.CompilerParams(vmem_limit_bytes=20 << 20),
        cost_estimate=cost_of(5),
        name="project",
    )(x, w, bq, bv)


def grads_kernel(
    keys,
    x_ref,
    w_ref,
    dq_ref,
    dk_ref,
    dv_ref,
    offs_ref,
    qoffs_ref,
    bucket_ref,
    six_ref,
    up_ref,
    squares_ref,
    gc_ref,
    gq_ref,
    gw_ref,
    vec_ref,
    shared_ref,
    part_scr,
):
    s = lax.axis_index("seq")
    wide = dq_ref.shape[1]
    seqs, length = gc_ref.shape[:2]
    shard = gw_ref.shape[1]
    for n, ref in enumerate((dq_ref, dk_ref, dv_ref)):
        part_scr[:, n * wide : (n + 1) * wide] = dot_tn(x_ref[: ref.shape[0], :], ref[...])
    for j in range(gw_ref.shape[0]):
        gw_ref[j] = part_scr[j * shard : (j + 1) * shard, :].astype(BF16)
    blocks = vec_ref.shape[0]
    n_one, n_up = six_ref.shape[1] // blocks, up_ref.shape[1] // blocks
    n_qv = 2 * n_one
    vec_ref[...] = jnp.zeros(vec_ref.shape, F32)
    sums = [jnp.sum(ref[...].astype(F32), axis=0, keepdims=True) for ref in (dq_ref, dv_ref)]
    for d in range(blocks):
        vec_ref[d, :6, :n_one] = six_ref[:, d * n_one : (d + 1) * n_one]
        vec_ref[d, 6:7, :n_up] = up_ref[:, d * n_up : (d + 1) * n_up]
        kind, start = divmod(d * n_qv, seqs * wide)
        owner, start = divmod(start, wide)
        piece = sums[kind][:, start : start + n_qv]
        vec_ref[d, 7:8, :n_qv] = jnp.where(s == owner, piece, 0.0)
    own = offs_ref.shape[0]
    table = jnp.zeros((own, BUCKETS), F32)
    for row, ref in ((1, offs_ref), (0, qoffs_ref)):
        hot = (
            lax.broadcasted_iota(jnp.int32, (BUCKETS, ref.shape[1]), 0)
            == bucket_ref[row : row + 1, :]
        ).astype(F32)
        table += lax.dot_general(
            ref[...],
            hot,
            (((1,), (1,)), ((), ())),
            precision=lax.Precision.HIGHEST,
            preferred_element_type=F32,
        )
    shared_ref[...] = jnp.zeros(shared_ref.shape, F32)
    for h in range(own):
        shared_ref[pl.ds(s * own + h, 1), :BUCKETS] = table[h : h + 1]
    shared_ref[16:24, :] = squares_ref[...]
    w_q = w_ref[:, :wide]
    w_k = w_ref[:, wide : 2 * wide]
    w_v = w_ref[:, 2 * wide :]
    step = 256
    for t in range(seqs):
        for a in range(0, length, step):
            at = slice(t * length + a, t * length + a + step)
            gc_ref[t, a : a + step, :] = (
                dot_nt(dq_ref[at, :], w_q) + dot_nt(dk_ref[at, :], w_k) + dot_nt(dv_ref[at, :], w_v)
            ).astype(BF16)
    count = gq_ref.shape[1]
    for t in range(seqs):
        at = slice(keys + t * count, keys + (t + 1) * count)
        gq_ref[t] = dot_nt(dq_ref[at, :], w_q).astype(BF16)


def grads_call(
    seqs, length, count, blocks, x, w, dq, dk, dv, offs, qoffs, buckets, six, up, squares
):
    wide = dq.shape[1]
    shard = x.shape[1] // blocks
    vm = pl.BlockSpec(memory_space=pltpu.VMEM)
    return pl.pallas_call(
        functools.partial(grads_kernel, seqs * length),
        out_shape=(
            jax.ShapeDtypeStruct((seqs, length, x.shape[1]), BF16),
            jax.ShapeDtypeStruct((seqs, count, x.shape[1]), BF16),
            jax.ShapeDtypeStruct((blocks, shard, 3 * wide), BF16),
            jax.ShapeDtypeStruct((blocks, 8, 128), F32),
            jax.ShapeDtypeStruct((24, 128), F32),
        ),
        in_specs=[vm] * 11,
        out_specs=(vm,) * 5,
        scratch_shapes=[pltpu.VMEM((x.shape[1], 3 * wide), F32)],
        compiler_params=pltpu.CompilerParams(vmem_limit_bytes=28 << 20),
        cost_estimate=cost_of(6),
        name="weight_grads",
    )(x, w, dq, dk, dv, offs, qoffs, buckets, six, up, squares)


MESH = pl.DeviceIdType.MESH
ROWS_Q = 384
SLOT_Q = 80


def greet(devices):
    barrier = pltpu.get_barrier_semaphore()
    for device in devices:
        pl.semaphore_signal(barrier, inc=1, device_id=device, device_id_type=MESH)
    pl.semaphore_wait(barrier, len(devices))


def remote(src, dst, send_sem, recv_sem, k, device):
    return pltpu.make_async_remote_copy(
        src_ref=src,
        dst_ref=dst,
        send_sem=send_sem.at[k],
        recv_sem=recv_sem.at[k],
        device_id=device,
        device_id_type=MESH,
    )


def start_kernel(
    dps,
    seqs,
    c_ref,
    q_ref,
    w_ref,
    v_ref,
    seg_ref,
    order_ref,
    pad_ref,
    pred_ref,
    x_out,
    w_out,
    v_out,
    i_out,
    q_scr,
    send_sem,
    recv_sem,
):
    dp = lax.axis_index("dp")
    s = lax.axis_index("seq")
    length = c_ref.shape[0]
    count = q_scr.shape[0]
    mate = s + 1 - 2 * lax.rem(s, 2)
    across = lax.rem(s + 2, seqs)
    level = dp + 1 - 2 * lax.rem(dp, 2)
    stacks = dps // 2
    greet(
        [(dp, lax.rem(s + r, seqs)) for r in range(1, seqs)]
        + [(level, s)]
        + [(lax.rem(dp + 2 * r, dps), s) for r in range(1, stacks)]
    )

    def at_c(owner):
        return pl.ds(pl.multiple_of(owner * length, length), length)

    def at_q(owner):
        return pl.ds(pl.multiple_of(seqs * length + owner * count, 16), count)

    k = 0

    def push(src, dst, device):
        nonlocal k
        copy = remote(src, dst, send_sem, recv_sem, k, device)
        copy.start()
        k += 1
        return copy

    i_out[s] = jnp.zeros(i_out.shape[1:], jnp.int32)
    for n, ref in enumerate((seg_ref, order_ref, pad_ref)):
        i_out[s, n : n + 1, :] = ref[...]
    i_out[s, 3:4, :] = jnp.full((1, length), -1, jnp.int32)
    i_out[s, 3:4, : pred_ref.shape[1]] = pred_ref[...]
    small = []
    for r in range(1, seqs):
        to = lax.rem(s + r, seqs)
        small.append(push(w_ref.at[to], w_out.at[dp, s], (dp, to)))
        small.append(push(v_ref, v_out.at[dp, s], (dp, to)))
        small.append(push(i_out.at[s], i_out.at[s], (dp, to)))
    x_out[at_c(s), :] = c_ref[...].astype(BF16)
    far = [push(x_out.at[at_c(s)], x_out.at[at_c(s)], (dp, across))]
    q_scr[...] = jnp.zeros(q_scr.shape, F32)
    q_scr[: q_ref.shape[0], :] = q_ref[...]
    x_out[at_q(s), :] = q_scr[...].astype(BF16)
    far.append(push(x_out.at[at_q(s)], x_out.at[at_q(s)], (dp, across)))
    near = [push(x_out.at[at(s)], x_out.at[at(s)], (dp, mate)) for at in (at_c, at_q)]
    w_out[dp, s] = w_ref[s]
    v_out[dp, s] = v_ref[...]
    rest = seqs * (length + count)
    x_out[rest:, :] = jnp.zeros((x_out.shape[0] - rest, x_out.shape[1]), BF16)
    for copy in small:
        copy.wait_recv()
    wide, flat = [], []
    for r in range(1, stacks):
        to = lax.rem(dp + 2 * r, dps)
        wide.append([push(ref.at[dp], ref.at[dp], (to, s)) for ref in (w_out, v_out)])
    flat += [push(ref.at[dp], ref.at[dp], (level, s)) for ref in (w_out, v_out)]
    for r in range(1, stacks):
        source = lax.rem(dp + dps - 2 * r, dps)
        for copy, ref in zip(wide[r - 1], (w_out, v_out)):
            copy.wait_recv()
            flat.append(push(ref.at[source], ref.at[source], (level, s)))
    pass_on = []
    for copy, at in zip(far, (at_c, at_q)):
        copy.wait_recv()
        pass_on.append(push(x_out.at[at(across)], x_out.at[at(across)], (dp, mate)))
    for copy in near + flat + pass_on:
        copy.wait_recv()
    for copy in small + far + near + flat + pass_on + sum(wide, []):
        copy.wait_send()


def start_call(dps, seqs, content, query, w, v, metas, slot_q):
    copies = 3 * (seqs - 1) + 4 + 2 * (dps // 2 - 1) + dps + 2
    length, width = content.shape
    vmem = pl.BlockSpec(memory_space=pltpu.VMEM)
    return pl.pallas_call(
        functools.partial(start_kernel, dps, seqs),
        out_shape=(
            jax.ShapeDtypeStruct((seqs * length + ROWS_Q, width), BF16),
            jax.ShapeDtypeStruct((dps,) + w.shape, BF16),
            jax.ShapeDtypeStruct((dps, seqs) + v.shape, F32),
            jax.ShapeDtypeStruct((seqs, 8, length), jnp.int32),
        ),
        in_specs=[vmem] * 8,
        out_specs=(vmem,) * 4,
        scratch_shapes=[
            pltpu.VMEM((slot_q, width), F32),
            pltpu.SemaphoreType.DMA((copies,)),
            pltpu.SemaphoreType.DMA((copies,)),
        ],
        compiler_params=pltpu.CompilerParams(
            collective_id=0, has_side_effects=True, vmem_limit_bytes=16 << 20
        ),
        cost_estimate=cost_of(30),
        name="gather_rows",
    )(content, query, w, v, *metas)


def swap_kernel(seqs, c_of, q_of, c_ref, q_ref, c_out, q_out, send_sem, recv_sem, here_sem):
    dp = lax.axis_index("dp")
    s = lax.axis_index("seq")
    greet([(dp, lax.rem(s + r, seqs)) for r in range(1, seqs)])
    copies = []
    for r in range(1, seqs):
        to = lax.rem(s + r, seqs)
        k = 2 * (r - 1)
        copies.append(remote(c_of(c_ref, to), c_out.at[s], send_sem, recv_sem, k, (dp, to)))
        copies.append(remote(q_of(q_ref, to), q_out.at[s], send_sem, recv_sem, k + 1, (dp, to)))
    for copy in copies:
        copy.start()
    here = [
        pltpu.make_async_copy(c_of(c_ref, s), c_out.at[s], here_sem.at[0]),
        pltpu.make_async_copy(q_of(q_ref, s), q_out.at[s], here_sem.at[1]),
    ]
    for copy in here:
        copy.start()
    for copy in here + copies:
        copy.wait()


def swap_call(seqs, c, q, c_of, q_of, c_shape, q_shape, ident, name):
    vmem = pl.BlockSpec(memory_space=pltpu.VMEM)
    return pl.pallas_call(
        functools.partial(swap_kernel, seqs, c_of, q_of),
        out_shape=(
            jax.ShapeDtypeStruct((seqs,) + c_shape, c.dtype),
            jax.ShapeDtypeStruct((seqs,) + q_shape, q.dtype),
        ),
        in_specs=[vmem] * 2,
        out_specs=(vmem,) * 2,
        scratch_shapes=[
            pltpu.SemaphoreType.DMA((2 * (seqs - 1),)),
            pltpu.SemaphoreType.DMA((2 * (seqs - 1),)),
            pltpu.SemaphoreType.DMA((2,)),
        ],
        compiler_params=pltpu.CompilerParams(collective_id=ident, has_side_effects=True),
        cost_estimate=cost_of(12),
        name=name,
    )(c, q)


def end_kernel(
    dps,
    seqs,
    gc_ref,
    gq_ref,
    w_ref,
    v_ref,
    sh_ref,
    gc_out,
    gq_out,
    w_out,
    v_out,
    sh_out,
    c_mate,
    q_mate,
    c_far,
    q_far,
    c_send,
    q_send,
    w_flat,
    v_flat,
    sh_flat,
    w_send,
    v_send,
    sh_send,
    w_got,
    v_got,
    sh_got,
    w_sum,
    v_sum,
    sh_sum,
    v_last,
    sh_last,
    send_sem,
    recv_sem,
):
    dp = lax.axis_index("dp")
    s = lax.axis_index("seq")
    core = lax.rem(s, 2)
    mate = s + 1 - 2 * core
    across = lax.rem(s + 2, seqs)
    side = lax.rem(dp, 2)
    level = dp + 1 - 2 * side
    stacks = dps // 2
    greet(
        [(dp, lax.rem(s + r, seqs)) for r in range(1, seqs)]
        + [(level, s)]
        + [(lax.rem(dp + 2 * r, dps), s) for r in range(1, stacks)]
    )
    k = 0

    def push(src, dst, device):
        nonlocal k
        copy = remote(src, dst, send_sem, recv_sem, k, device)
        copy.start()
        k += 1
        return copy

    def each(ref, step, fn):
        def body(i, carry):
            fn(pl.ds(pl.multiple_of(i * step, step), step))
            return carry

        lax.fori_loop(0, ref.shape[-2] // step, body, 0)

    first = []
    for i in range(2):
        to = lax.rem(mate + 2 * (1 - i), seqs)
        for src, dst in ((gc_ref, c_mate), (gq_ref, q_mate)):
            first.append(push(src.at[to], dst.at[i], (dp, mate)))
    flat = []
    for r in list(range(1, stacks)) + [0]:
        to = lax.rem(level + 2 * r, dps)
        flat.append(
            [push(src.at[to], dst.at[r], (level, s)) for src, dst in ((w_ref, w_flat), (v_ref, v_flat))]
        )
    shared = push(sh_ref, sh_flat, (level, s))
    cross = []
    for (src, got, buf, far, copy) in (
        (gc_ref, c_mate, c_send, c_far, first[0]),
        (gq_ref, q_mate, q_send, q_far, first[1]),
    ):
        copy.wait_recv()

        def add(rows, src=src, got=got, buf=buf):
            buf[rows, :] = (
                src[across, rows, :].astype(F32) + got[0, rows, :].astype(F32)
            ).astype(BF16)

        each(buf, 16, add)
        cross.append(push(buf, far, (dp, across)))
    shared.wait_recv()
    sh_send[...] = sh_ref[...] + sh_flat[...]
    tall = []
    for r in range(1, stacks):
        for copy in flat[r - 1]:
            copy.wait_recv()
        to = lax.rem(dp + 2 * r, dps)

        def add_pair(rows, to=to, r=r):
            for t in range(seqs):
                w_send[r - 1, t, rows, :] = (
                    w_ref[to, t, rows, :].astype(F32) + w_flat[r, t, rows, :].astype(F32)
                ).astype(BF16)

        each(w_sum, 24, add_pair)
        v_send[r - 1] = v_ref[to] + v_flat[r]
        for src, dst in (
            (w_send.at[r - 1], w_got.at[r - 1]),
            (v_send.at[r - 1], v_got.at[r - 1]),
            (sh_send, sh_got.at[r - 1]),
        ):
            tall.append(push(src, dst, (to, s)))
    for copy in flat[stacks - 1] + tall:
        copy.wait_recv()

    def add_w(rows):
        for t in range(seqs):
            total = w_ref[dp, t, rows, :].astype(F32) + w_flat[0, t, rows, :].astype(F32)
            for r in range(1, stacks):
                total += w_got[r - 1, t, rows, :].astype(F32)
            w_sum[t, rows, :] = total

    each(w_sum, 24, add_w)
    total = v_ref[dp] + v_flat[0]
    for r in range(1, stacks):
        total += v_got[r - 1]
    v_sum[...] = total
    total = sh_send[...]
    for r in range(1, stacks):
        total += sh_got[r - 1]
    sh_sum[...] = total
    last = []
    for r in range(1, seqs):
        to = lax.rem(s + r, seqs)
        last.append(push(w_sum.at[to], w_out.at[s], (dp, to)))
        last.append(push(v_sum.at[to], v_last.at[r - 1], (dp, to)))
        last.append(push(sh_sum, sh_last.at[r - 1], (dp, to)))
    w_out[s] = w_sum[s]
    for copy in first[2:] + cross:
        copy.wait_recv()
    for (src, got, far, out) in (
        (gc_ref, c_mate, c_far, gc_out),
        (gq_ref, q_mate, q_far, gq_out),
    ):

        def total_of(rows, src=src, got=got, far=far, out=out):
            out[rows, :] = (
                src[s, rows, :].astype(F32)
                + got[1, rows, :].astype(F32)
                + far[rows, :].astype(F32)
            )

        each(out, 16, total_of)
    for copy in last:
        copy.wait_recv()
    total = v_sum[s]
    for r in range(1, seqs):
        total += v_last[r - 1]
    v_out[...] = total
    total = sh_sum[...]
    for r in range(1, seqs):
        total += sh_last[r - 1]
    sh_out[...] = total
    for copy in first + sum(flat, []) + [shared] + cross + tall + last:
        copy.wait_send()


def end_call(dps, seqs, gc, gq, w, v, sh):
    stacks = dps // 2
    copies = 4 + 2 * stacks + 1 + 2 + 3 * (stacks - 1) + 3 * (seqs - 1)
    vm = pl.BlockSpec(memory_space=pltpu.VMEM)
    cshape, qshape, wshape, vshape = gc.shape[1:], gq.shape[1:], w.shape[1:], v.shape[1:]
    return pl.pallas_call(
        functools.partial(end_kernel, dps, seqs),
        out_shape=(
            jax.ShapeDtypeStruct(cshape, F32),
            jax.ShapeDtypeStruct(qshape, F32),
            jax.ShapeDtypeStruct(wshape, F32),
            jax.ShapeDtypeStruct(vshape[1:], F32),
            jax.ShapeDtypeStruct(sh.shape, F32),
        ),
        in_specs=[vm] * 5,
        out_specs=(vm,) * 5,
        scratch_shapes=[
            pltpu.VMEM((2,) + cshape, BF16),
            pltpu.VMEM((2,) + qshape, BF16),
            pltpu.VMEM(cshape, BF16),
            pltpu.VMEM(qshape, BF16),
            pltpu.VMEM(cshape, BF16),
            pltpu.VMEM(qshape, BF16),
            pltpu.VMEM((stacks,) + wshape, BF16),
            pltpu.VMEM((stacks,) + vshape, F32),
            pltpu.VMEM(sh.shape, F32),
            pltpu.VMEM((stacks - 1,) + wshape, BF16),
            pltpu.VMEM((stacks - 1,) + vshape, F32),
            pltpu.VMEM(sh.shape, F32),
            pltpu.VMEM((stacks - 1,) + wshape, BF16),
            pltpu.VMEM((stacks - 1,) + vshape, F32),
            pltpu.VMEM((stacks - 1,) + sh.shape, F32),
            pltpu.VMEM(wshape, F32),
            pltpu.VMEM(vshape, F32),
            pltpu.VMEM(sh.shape, F32),
            pltpu.VMEM((seqs - 1,) + vshape[1:], F32),
            pltpu.VMEM((seqs - 1,) + sh.shape, F32),
            pltpu.SemaphoreType.DMA((copies,)),
            pltpu.SemaphoreType.DMA((copies,)),
        ],
        compiler_params=pltpu.CompilerParams(
            collective_id=3, has_side_effects=True, vmem_limit_bytes=24 << 20
        ),
        cost_estimate=cost_of(30),
        name="sum_rows",
    )(gc, gq, w, v, sh)


def flip_perm(count, bit):
    return [(i, i ^ bit) for i in range(count)]


AXES = ("dp", "seq")


def tie(values, *others):
    return lax.optimization_barrier((values, others))[0]


def give_to(cur, count, bit):
    return lax.ppermute(cur, AXES, flip_perm(count, bit))


def local_fast(
    content,
    query_stream,
    segment_ids,
    pad_mask,
    predicted,
    order,
    rel_bucket,
    qkv_weight,
    qv_bias,
    out_weight,
    out_bias,
    attn_gain,
    attn_shift,
    up_weight,
    up_bias,
    down_weight,
    down_bias,
    ffn_gain,
    ffn_shift,
    rel_table,
    content_cot,
    query_cot,
):
    dps, seqs = lax.axis_size("dp"), lax.axis_size("seq")
    count = dps * seqs
    s = lax.axis_index("seq")
    own = HEADS // seqs
    wide = own * HEAD_DIM
    length = content.shape[1]
    preds = query_stream.shape[1]
    shard = qkv_weight.shape[0]

    vec = jnp.concatenate(
        [
            member.astype(F32)
            for member in (
                qv_bias,
                up_bias,
                out_bias,
                attn_gain,
                attn_shift,
                down_bias,
                ffn_gain,
                ffn_shift,
            )
        ]
    )
    vec = jnp.pad(vec, (0, 1024 - vec.shape[0])).reshape(8, 128)
    buckets = jnp.stack(
        [
            jnp.pad(rel_bucket, (0, 1), constant_values=BUCKETS),
            jnp.pad(rel_bucket, (1, 0), constant_values=BUCKETS),
        ]
    )
    w_parts = jnp.transpose(
        qkv_weight.reshape(shard, 3, seqs, wide), (2, 0, 1, 3)
    ).reshape(seqs, shard, 3 * wide)
    tops = (UP_TOP, DOWN_TOP)

    def send(pair, bits):
        return tuple(give_to(x, count, bit) for x, bit in zip(pair, bits))

    def heap(*pairs):
        return tuple(jnp.concatenate(x) for x in zip(*pairs))

    zs_low = (jnp.concatenate([up_weight, out_weight], axis=1)[None], down_weight[None])
    flying = send(zs_low, (16, 16))
    x_all, w_all, v_all, i_all = start_call(
        dps,
        seqs,
        content[0],
        query_stream[0],
        w_parts,
        vec,
        (segment_ids, order, pad_mask, predicted),
        SLOT_Q,
    )
    w_qkv = w_all.reshape(MODEL_WIDTH, 3 * wide)
    parts_all = v_all.reshape(count, 1024)
    n_qv, n_up, n_one = qv_bias.shape[0], up_bias.shape[0], out_bias.shape[0]
    cut_up, cut_end = n_qv + n_up, n_qv + n_up + 6 * n_one
    bias_qv = parts_all[:, :n_qv].reshape(count * n_qv)
    bias_up = parts_all[:, n_qv:cut_up].reshape(1, count * n_up)
    six = jnp.transpose(parts_all[:, cut_up:cut_end].reshape(count, 6, n_one), (1, 0, 2)).reshape(
        6, count * n_one
    )
    seg_all = i_all[:, 0].reshape(seqs * length)
    pad_all = i_all[:, 2].reshape(seqs * length)
    span = key_spans(seg_all, pad_all)

    bits = [tuple(2 * top[n] for top in tops) for n in range(2)]
    zs_low = heap(zs_low, tie(flying, i_all))
    flying = send(zs_low, (8, 8)), send(zs_low, bits[0])
    first = (s * own).astype(jnp.int32)[None]
    ints = tie(i_all, zs_low)
    tiles, qbias, kmeta, rseg, rlim, hot, shift = bias_call(
        own, ROWS_Q, SLOT_Q, first, buckets, rel_table, ints
    )

    bq = lax.dynamic_slice_in_dim(bias_qv[:MODEL_WIDTH], s * wide, wide)
    bv = lax.dynamic_slice_in_dim(bias_qv[MODEL_WIDTH:], s * wide, wide)
    zs_high, side_low = tie(flying, tiles)
    column = heap(zs_low, zs_high)
    side_high, far_low = send(zs_high, bits[0]), send(column, bits[1])
    x_all = tie(x_all, column)
    q_t, q3, k3, k_t, v3, v_t = proj_call(
        own, seqs * length, x_all, w_qkv, bq[None], bv[None]
    )
    side_high = tie(side_high, q_t)
    side = heap(side_low, side_high)
    far_high = send(side, bits[1])
    close = heap(column, side)
    q_t = tie(q_t, side)

    ctx_t, ctx_rows, lse = fwd_call(span, q_t, k3, v_t, kmeta, rseg, rlim, tiles, qbias)

    far_low, far_high = tie((far_low, far_high), ctx_rows)
    far = heap(far_low, far_high)
    mates, far_mates = send(close, (1, 1)), send(far, (1, 1))
    ctx_rows = tie(ctx_rows, far)
    planes = sum(zip(close, far, mates, far_mates), ())

    def from_lanes(ref, t):
        return ref.at[:, pl.ds(pl.multiple_of(t * length, length), length)]

    def from_query(ref, t):
        return ref.at[pl.ds(pl.multiple_of(t * SLOT_Q, 16), SLOT_Q)]

    ctx_c, ctx_q = swap_call(
        seqs,
        ctx_t,
        ctx_rows,
        from_lanes,
        from_query,
        (wide, length),
        (SLOT_Q, wide),
        1,
        "swap_context",
    )
    (
        res_c,
        res_q,
        give_c,
        give_q,
        six_sums,
        up_sums,
        squares,
        out_c,
        out_q,
        keep,
        give,
    ) = mid_call(
        ctx_c,
        ctx_q,
        content[0],
        query_stream[0],
        content_cot[0],
        query_cot[0],
        pad_mask,
        six,
        bias_up,
        planes,
    )
    core = s % 2
    spot = (lax.axis_index(AXES) // 2) % 4
    flying = give_to(give, count, 1)

    def both(mine, got):
        total = mine.astype(F32) + got.astype(F32)
        return total.astype(BF16).reshape((2, 2, 4, mine.shape[0] // 16, mine.shape[1]))

    def block(x, index):
        return lax.dynamic_index_in_dim(x, index, 2, keepdims=False)

    def from_slot(ref, t):
        return ref.at[t]

    g_c, g_q = swap_call(
        seqs,
        give_c,
        give_q,
        from_slot,
        from_slot,
        (wide, length),
        (SLOT_Q, wide),
        2,
        "swap_grads",
    )
    flying = tie(flying, g_c)
    pairs = both(keep, flying)
    gone = tuple(block(pairs, spot ^ r) for r in (1, 2, 3))
    flying = tuple(give_to(x, count, 2 * r) for x, r in zip(gone, (1, 2, 3)))
    stay = block(pairs, spot)
    g_c = tie(g_c, stay, gone)
    dq, dk, dv, offs, qoffs = bwd_call(
        span,
        q_t,
        q3,
        k3,
        k_t,
        v3,
        ctx_t,
        g_c,
        g_q.reshape(seqs * SLOT_Q, wide),
        lse,
        kmeta,
        rseg,
        rlim,
        tiles,
        hot,
        shift,
        qbias,
    )
    grad_c, grad_q, grad_w, vec_grads, shared = grads_call(
        seqs,
        length,
        SLOT_Q,
        count,
        x_all,
        w_qkv,
        dq,
        dk,
        dv,
        offs,
        qoffs,
        buckets,
        six_sums,
        up_sums,
        squares,
    )
    flying = tie(flying, grad_c)

    def total_of(kept, got):
        total = kept.astype(F32)
        for x in got:
            total += x.astype(F32)
        return total

    def split(x, bit):
        mine = (lax.axis_index(AXES) // bit) % 2
        axis = x.ndim - 3
        away = lax.dynamic_index_in_dim(x, 1 - mine, axis, keepdims=False).astype(BF16)
        return away, lax.dynamic_index_in_dim(x, mine, axis, keepdims=False)

    gone, stay = split(total_of(stay, flying), 8)
    flying = give_to(gone, count, 8)
    grad_c = tie(grad_c, stay, gone)
    sum_c, sum_q, sum_w, sum_v, sum_shared = end_call(
        dps,
        seqs,
        grad_c,
        grad_q,
        grad_w.reshape(dps, seqs, shard, 3 * wide),
        vec_grads.reshape(dps, seqs, 8, 128),
        shared,
    )
    flying, sum_c, sum_q, sum_w, sum_v, sum_shared = tie(
        (flying, sum_c, sum_q, sum_w, sum_v, sum_shared)
    )
    gone, stay = split(total_of(stay, (flying,)), 16)
    flying = give_to(gone, count, 16)
    pair = total_of(stay, (flying,))
    half_ff, half = up_weight.shape[1] // 2, MODEL_WIDTH // 2
    wide_up = half_ff + half
    first, second = pair[:shard], pair[shard:]
    low_cols, high_cols = pair[:, wide_up : wide_up + half_ff // 2], pair[:, wide_up + half_ff // 2 :]

    def pick(a, b):
        return jnp.where(core == 0, a, b), jnp.where(core == 0, b, a)

    rows_mine, rows_away = pick(first[:, :wide_up], second[:, :wide_up])
    cols_mine, cols_away = pick(low_cols, high_cols)
    rows_got = give_to(rows_away, count, 1)
    cols_got = give_to(cols_away, count, 1)
    rows_low, rows_high = pick(rows_mine, rows_got)
    grad_up_own = jnp.concatenate([rows_low[:, :half_ff], rows_high[:, :half_ff]], axis=1)
    grad_out_own = jnp.concatenate([rows_low[:, half_ff:], rows_high[:, half_ff:]], axis=1)

    def unfold(x):
        return jnp.concatenate([x[:, :half], x[:, half:]], axis=0)

    cols_low, cols_high = pick(unfold(cols_mine), unfold(cols_got))
    grad_down_own = jnp.concatenate([cols_low, cols_high], axis=1)
    grad_content = res_c + sum_c
    grad_query = res_q[:preds] + sum_q[:preds]
    grad_qkv_own = jnp.transpose(sum_w.reshape(seqs, shard, 3, wide), (1, 2, 0, 3)).reshape(
        shard, 3 * MODEL_WIDTH
    )
    mine = [sum_v[7, :n_qv], sum_v[6, :n_up]] + [sum_v[i, :n_one] for i in range(6)]
    table_sum = sum_shared[:HEADS, :BUCKETS].T
    totals = sum_shared[16:23, 0]
    content_count = totals[6] * MODEL_WIDTH
    query_count = float(dps * preds * seqs * MODEL_WIDTH)
    each = jnp.stack([content_count, jnp.float32(query_count)])
    stats = jnp.sqrt(totals[:6] / jnp.concatenate([each, each, each]))
    return (
        out_c[None],
        out_q[None],
        grad_content[None],
        grad_query[None],
        grad_qkv_own,
        mine[0],
        grad_out_own,
        mine[2],
        mine[3],
        mine[4],
        grad_up_own,
        mine[1],
        grad_down_own,
        mine[5],
        mine[6],
        mine[7],
        table_sum,
        stats,
    )


def pick_local(mesh):
    sizes = dict(mesh.shape)
    return local_fast if (sizes["dp"], sizes["seq"]) == (8, 4) else local_general


def solution(mesh):
    in_specs = (
        P("dp", "seq", None),
        P("dp", "seq", None),
        P("dp", "seq"),
        P("dp", "seq"),
        P("dp", "seq"),
        P("dp", "seq"),
        P(),
        P(("dp", "seq"), None),
        P(("dp", "seq")),
        P(("dp", "seq"), None),
        P(("dp", "seq")),
        P(("dp", "seq")),
        P(("dp", "seq")),
        P(("dp", "seq"), None),
        P(("dp", "seq")),
        P(("dp", "seq"), None),
        P(("dp", "seq")),
        P(("dp", "seq")),
        P(("dp", "seq")),
        P(),
        P("dp", "seq", None),
        P("dp", "seq", None),
    )
    out_specs = (
        P("dp", "seq", None),
        P("dp", "seq", None),
        P("dp", "seq", None),
        P("dp", "seq", None),
        P(("dp", "seq"), None),
        P(("dp", "seq")),
        P(("dp", "seq"), None),
        P(("dp", "seq")),
        P(("dp", "seq")),
        P(("dp", "seq")),
        P(("dp", "seq"), None),
        P(("dp", "seq")),
        P(("dp", "seq"), None),
        P(("dp", "seq")),
        P(("dp", "seq")),
        P(("dp", "seq")),
        P(),
        P(),
    )
    local = pick_local(mesh)
    return jax.shard_map(local, mesh=mesh, in_specs=in_specs, out_specs=out_specs, check_vma=False)
```

```python
import functools
import math

import jax
import jax.numpy as jnp
from jax import lax
from jax.experimental import pallas as pl
from jax.experimental.pallas import tpu as pltpu
from jax.sharding import PartitionSpec as P

MODEL_WIDTH = 768
HEADS = 12
HEAD_DIM = 64
BUCKETS = 32
SEQ_LEN = 2048


EPS = 1e-05
NEG = -1000000000.0
SCALE = 0.125


def exact_gelu(values):
    return jax.nn.gelu(values, approximate=False)


def norm_fwd(residual, gain_vec, shift_vec):
    row_mean = jnp.mean(residual, axis=-1, keepdims=True)
    centered = residual - row_mean
    inv_std = lax.rsqrt(jnp.mean(centered * centered, axis=-1, keepdims=True) + EPS)
    normed = centered * inv_std
    return (normed * gain_vec + shift_vec, normed, inv_std)


def norm_back(upstream, normed, inv_std, gain_vec):
    grad_norm = upstream * gain_vec
    projected = jnp.mean(grad_norm, axis=-1, keepdims=True) + normed * jnp.mean(
        grad_norm * normed, axis=-1, keepdims=True
    )
    return (
        inv_std * (grad_norm - projected),
        jnp.sum(upstream * normed, axis=(0, 1)),
        jnp.sum(upstream, axis=(0, 1)),
    )


def bucket_edges(rel_bucket):
    entry_count = rel_bucket.shape[0]
    matches = rel_bucket[None, :] == jnp.arange(BUCKETS, dtype=jnp.int32)[:, None]
    places = jnp.arange(entry_count, dtype=jnp.int32)[None, :]
    starts = jnp.min(jnp.where(matches, places, entry_count), axis=1)
    counts = jnp.sum(matches.astype(jnp.int32), axis=1)
    return (starts, starts + counts)


def build_mask(
    query_pos, query_seg, query_limit, content_row, key_pos, key_seg, key_order, key_pad
):
    inside = (
        (query_seg[:, None] == key_seg[None, :])
        & (key_pad[None, :] == 1)
        & (key_order[None, :] <= query_limit[:, None])
    )
    itself = (key_pos[None, :] == query_pos[:, None]) & content_row[:, None]
    return (inside | itself, key_pos[None, :] - query_pos[:, None] + (SEQ_LEN - 1))


def masked_scores(query_heads, key_heads, table_low, edges, allowed, offsets):
    raw_scores = (
        jnp.einsum("rhd,lhd->hrl", query_heads, key_heads, preferred_element_type=jnp.float32)
        * SCALE
    )
    starts, ends = edges
    spread = offsets[..., None]
    onehot = ((spread >= starts) & (spread < ends)).astype(jnp.bfloat16)
    bias = jnp.einsum("rlb,bh->hrl", onehot, table_low, preferred_element_type=jnp.float32)
    return (jnp.where(allowed[None], raw_scores + bias, NEG), onehot)


def attend_forward(packed, table_low, edges, content_row):
    queries, key_values, key_seg, key_order, key_pad, query_pos, query_seg, query_limit = packed
    row_count = queries.shape[0]
    length = key_values.shape[0]
    key_pos = jnp.arange(length, dtype=jnp.int32)
    allowed, offsets = build_mask(
        query_pos, query_seg, query_limit, content_row, key_pos, key_seg, key_order, key_pad
    )
    query_heads = queries.reshape(row_count, HEADS, HEAD_DIM)
    key_heads = key_values[:, :MODEL_WIDTH].reshape(length, HEADS, HEAD_DIM)
    value_heads = key_values[:, MODEL_WIDTH:].reshape(length, HEADS, HEAD_DIM)
    scores, onehot = masked_scores(query_heads, key_heads, table_low, edges, allowed, offsets)
    row_max = jnp.max(scores, axis=-1, keepdims=True)
    expo_vals = jnp.exp(scores - row_max)
    row_total = jnp.sum(expo_vals, axis=-1, keepdims=True)
    probs_low = (expo_vals / row_total).astype(jnp.bfloat16)
    context = jnp.einsum("hrl,lhd->rhd", probs_low, value_heads, preferred_element_type=jnp.float32)
    return (
        context.reshape(row_count, MODEL_WIDTH),
        jnp.transpose((row_max + jnp.log(row_total))[..., 0]),
    )


def attend_backward(packed, table_low, edges, content_row):
    (
        queries,
        key_values,
        key_seg,
        key_order,
        key_pad,
        query_pos,
        query_seg,
        query_limit,
        row_lse,
        grad_context,
    ) = packed
    row_count = queries.shape[0]
    length = key_values.shape[0]
    key_pos = jnp.arange(length, dtype=jnp.int32)
    allowed, offsets = build_mask(
        query_pos, query_seg, query_limit, content_row, key_pos, key_seg, key_order, key_pad
    )
    query_heads = queries.reshape(row_count, HEADS, HEAD_DIM)
    key_heads = key_values[:, :MODEL_WIDTH].reshape(length, HEADS, HEAD_DIM)
    value_heads = key_values[:, MODEL_WIDTH:].reshape(length, HEADS, HEAD_DIM)
    scores, onehot = masked_scores(query_heads, key_heads, table_low, edges, allowed, offsets)
    probs = jnp.exp(scores - jnp.transpose(row_lse)[..., None])
    grad_heads = grad_context.reshape(row_count, HEADS, HEAD_DIM)
    grad_probs = jnp.einsum(
        "rhd,lhd->hrl", grad_heads, value_heads, preferred_element_type=jnp.float32
    )
    row_delta = jnp.sum(probs * grad_probs, axis=-1)
    grad_scores = (probs * (grad_probs - row_delta[..., None])).astype(jnp.bfloat16)
    grad_query = (
        jnp.einsum("hrl,lhd->rhd", grad_scores, key_heads, preferred_element_type=jnp.float32)
        * SCALE
    )
    grad_table = jnp.einsum("hrl,rlb->bh", grad_scores, onehot, preferred_element_type=jnp.float32)
    results = (grad_query.reshape(row_count, MODEL_WIDTH), grad_table, jnp.transpose(row_delta))
    probs_low = probs.astype(jnp.bfloat16)
    grad_key = (
        jnp.einsum("hrl,rhd->lhd", grad_scores, query_heads, preferred_element_type=jnp.float32)
        * SCALE
    )
    grad_value = jnp.einsum(
        "hrl,rhd->lhd", probs_low, grad_heads, preferred_element_type=jnp.float32
    )
    results = results + (
        jnp.concatenate(
            [grad_key.reshape(length, MODEL_WIDTH), grad_value.reshape(length, MODEL_WIDTH)],
            axis=-1,
        ),
    )
    return results


def local_general(
    content,
    query_stream,
    segment_ids,
    pad_mask,
    predicted,
    order,
    rel_bucket,
    qkv_weight,
    qv_bias,
    out_weight,
    out_bias,
    attn_gain,
    attn_shift,
    up_weight,
    up_bias,
    down_weight,
    down_bias,
    ffn_gain,
    ffn_shift,
    rel_table,
    content_cot,
    query_cot,
):
    seq_count = content.shape[0]
    shard_length = content.shape[1]
    pred_count = query_stream.shape[1]
    row_count = shard_length + pred_count
    group_size = lax.axis_size("seq")
    edges = bucket_edges(rel_bucket)
    shards = (
        lax.all_gather(qkv_weight, ("dp", "seq"), axis=0, tiled=True),
        lax.all_gather(out_weight, ("dp", "seq"), axis=0, tiled=True),
        lax.all_gather(up_weight, ("dp", "seq"), axis=0, tiled=True),
        lax.all_gather(down_weight, ("dp", "seq"), axis=0, tiled=True),
        lax.all_gather(qv_bias, ("dp", "seq"), axis=0, tiled=True),
        lax.all_gather(out_bias, ("dp", "seq"), axis=0, tiled=True),
        lax.all_gather(attn_gain, ("dp", "seq"), axis=0, tiled=True),
        lax.all_gather(attn_shift, ("dp", "seq"), axis=0, tiled=True),
        lax.all_gather(up_bias, ("dp", "seq"), axis=0, tiled=True),
        lax.all_gather(down_bias, ("dp", "seq"), axis=0, tiled=True),
        lax.all_gather(ffn_gain, ("dp", "seq"), axis=0, tiled=True),
        lax.all_gather(ffn_shift, ("dp", "seq"), axis=0, tiled=True),
    )
    query_key_value_weight, w_out, w_up, w_down = (shards[0], shards[1], shards[2], shards[3])
    bias_qv, bias_out, first_norm_gain, shift_one, bias_up, bias_down, gain_two, shift_two = [
        member.astype(jnp.float32) for member in shards[4:]
    ]
    all_rows = jnp.concatenate([content, query_stream], axis=1)
    reduced_precision_rows = all_rows.astype(jnp.bfloat16)
    queries = (
        jnp.einsum(
            "srd,de->sre",
            reduced_precision_rows,
            query_key_value_weight[:, :MODEL_WIDTH],
            preferred_element_type=jnp.float32,
        )
        + bias_qv[:MODEL_WIDTH]
    ).astype(jnp.bfloat16)
    value_shift = jnp.concatenate([jnp.zeros((MODEL_WIDTH,), jnp.float32), bias_qv[MODEL_WIDTH:]])
    key_values = (
        jnp.einsum(
            "zci,ip->zcp",
            reduced_precision_rows[:, :shard_length],
            query_key_value_weight[:, MODEL_WIDTH:],
            preferred_element_type=jnp.float32,
        )
        + value_shift
    ).astype(jnp.bfloat16)
    full_pairs, full_seg, full_order, full_pad = (
        lax.all_gather(key_values, "seq", axis=1, tiled=True),
        lax.all_gather(segment_ids, "seq", axis=1, tiled=True),
        lax.all_gather(order, "seq", axis=1, tiled=True),
        lax.all_gather(pad_mask, "seq", axis=1, tiled=True),
    )
    content_pos = lax.axis_index("seq") * shard_length + jnp.arange(shard_length, dtype=jnp.int32)
    query_pos = jnp.concatenate(
        [jnp.broadcast_to(content_pos[None, :], (seq_count, shard_length)), predicted], axis=1
    )
    query_seg = jnp.concatenate(
        [segment_ids, jnp.take_along_axis(full_seg, predicted, axis=1)], axis=1
    )
    query_limit = jnp.concatenate(
        [order, jnp.take_along_axis(full_order, predicted, axis=1) - 1], axis=1
    )
    content_row = jnp.arange(row_count, dtype=jnp.int32) < shard_length
    row_meta = (full_seg, full_order, full_pad, query_pos, query_seg, query_limit)

    def forward_one(packed):
        return attend_forward(packed, rel_table, edges, content_row)

    context, row_lse = lax.map(forward_one, (queries, full_pairs) + row_meta)
    context_low = context.astype(jnp.bfloat16)
    attn_out = (
        jnp.einsum("sre,ed->srd", context_low, w_out, preferred_element_type=jnp.float32) + bias_out
    )
    hidden_one, normed_one, inv_one = norm_fwd(all_rows + attn_out, first_norm_gain, shift_one)
    hidden_low = hidden_one.astype(jnp.bfloat16)
    pre_act = (
        jnp.einsum("srd,df->srf", hidden_low, w_up, preferred_element_type=jnp.float32) + bias_up
    )
    activ, gelu_pull = jax.vjp(exact_gelu, pre_act)
    activ_low = activ.astype(jnp.bfloat16)
    ffn_out = (
        jnp.einsum("srf,fd->srd", activ_low, w_down, preferred_element_type=jnp.float32) + bias_down
    )
    hidden_two, normed_two, inv_two = norm_fwd(hidden_one + ffn_out, gain_two, shift_two)
    pad_float = pad_mask.astype(jnp.float32)
    row_valid = jnp.concatenate(
        [pad_float, jnp.ones((seq_count, pred_count), jnp.float32)], axis=1
    )[..., None]
    outputs = hidden_two * row_valid
    pad_weight = pad_float[..., None]
    local_sums = jnp.stack(
        [
            jnp.sum(pad_weight * content * content),
            jnp.sum(query_stream * query_stream),
            jnp.sum(pad_weight * attn_out[:, :shard_length] * attn_out[:, :shard_length]),
            jnp.sum(attn_out[:, shard_length:] * attn_out[:, shard_length:]),
            jnp.sum(pad_weight * ffn_out[:, :shard_length] * ffn_out[:, :shard_length]),
            jnp.sum(ffn_out[:, shard_length:] * ffn_out[:, shard_length:]),
            jnp.sum(pad_float),
        ]
    )
    back_weights = (
        lax.all_gather(qkv_weight, ("dp", "seq"), axis=0, tiled=True),
        lax.all_gather(out_weight, ("dp", "seq"), axis=0, tiled=True),
        lax.all_gather(up_weight, ("dp", "seq"), axis=0, tiled=True),
        lax.all_gather(down_weight, ("dp", "seq"), axis=0, tiled=True),
        lax.all_gather(attn_gain, ("dp", "seq"), axis=0, tiled=True),
        lax.all_gather(ffn_gain, ("dp", "seq"), axis=0, tiled=True),
    )
    back_pairs = lax.all_gather(key_values, "seq", axis=1, tiled=True)
    backward_query_key_value, back_out, back_up, back_down = (
        back_weights[0],
        back_weights[1],
        back_weights[2],
        back_weights[3],
    )
    back_gain_one = back_weights[4].astype(jnp.float32)
    back_gain_two = back_weights[5].astype(jnp.float32)
    upstream = jnp.concatenate([content_cot, query_cot], axis=1) * row_valid
    grad_res_two, grad_gain_two, grad_shift_two = norm_back(
        upstream, normed_two, inv_two, back_gain_two
    )
    grad_ffn = grad_res_two.astype(jnp.bfloat16)
    grad_bias_down = jnp.sum(grad_ffn, axis=(0, 1), dtype=jnp.float32)
    grad_down = jnp.einsum("srf,srd->fd", activ_low, grad_ffn, preferred_element_type=jnp.float32)
    grad_activ = jnp.einsum("srd,fd->srf", grad_ffn, back_down, preferred_element_type=jnp.float32)
    grad_pre = gelu_pull(grad_activ)[0].astype(jnp.bfloat16)
    grad_bias_up = jnp.sum(grad_pre, axis=(0, 1), dtype=jnp.float32)
    grad_up = jnp.einsum("srd,srf->df", hidden_low, grad_pre, preferred_element_type=jnp.float32)
    grad_hidden = grad_res_two + jnp.einsum(
        "srf,df->srd", grad_pre, back_up, preferred_element_type=jnp.float32
    )
    grad_res_one, grad_gain_one, grad_shift_one = norm_back(
        grad_hidden, normed_one, inv_one, back_gain_one
    )
    grad_attn = grad_res_one.astype(jnp.bfloat16)
    grad_bias_out = jnp.sum(grad_attn, axis=(0, 1), dtype=jnp.float32)
    grad_out = jnp.einsum("sre,srd->ed", context_low, grad_attn, preferred_element_type=jnp.float32)
    grad_context = jnp.einsum(
        "srd,ed->sre", grad_attn, back_out, preferred_element_type=jnp.float32
    ).astype(jnp.bfloat16)

    def backward_all(packed):
        return attend_backward(packed, rel_table, edges, content_row)

    grad_queries, grad_tables, per_row_delta, grad_pairs = lax.map(
        backward_all, (queries, back_pairs) + row_meta + (row_lse, grad_context)
    )
    paired_gradients = lax.psum_scatter(
        grad_pairs.astype(jnp.bfloat16), "seq", scatter_dimension=1, tiled=True
    )
    query_grads = grad_queries.astype(jnp.bfloat16)
    grad_bias_qv = jnp.concatenate(
        [
            jnp.sum(query_grads, axis=(0, 1), dtype=jnp.float32),
            jnp.sum(paired_gradients[..., MODEL_WIDTH:], axis=(0, 1), dtype=jnp.float32),
        ]
    )
    grad_qkv = jnp.concatenate(
        [
            jnp.einsum(
                "srd,sre->de",
                reduced_precision_rows,
                query_grads,
                preferred_element_type=jnp.float32,
            ),
            jnp.einsum(
                "cvi,cvp->ip",
                reduced_precision_rows[:, :shard_length],
                paired_gradients,
                preferred_element_type=jnp.float32,
            ),
        ],
        axis=1,
    )
    grad_rows = grad_res_one + jnp.einsum(
        "sre,de->srd",
        query_grads,
        backward_query_key_value[:, :MODEL_WIDTH],
        preferred_element_type=jnp.float32,
    )
    grad_content = grad_rows[:, :shard_length] + jnp.einsum(
        "zwv,bv->zwb",
        paired_gradients,
        backward_query_key_value[:, MODEL_WIDTH:],
        preferred_element_type=jnp.float32,
    )
    grad_query = grad_rows[:, shard_length:]
    owned = (
        lax.psum_scatter(grad_qkv, ("dp", "seq"), scatter_dimension=0, tiled=True),
        lax.psum_scatter(grad_out, ("dp", "seq"), scatter_dimension=0, tiled=True),
        lax.psum_scatter(grad_up, ("dp", "seq"), scatter_dimension=0, tiled=True),
        lax.psum_scatter(grad_down, ("dp", "seq"), scatter_dimension=0, tiled=True),
        lax.psum_scatter(grad_bias_qv, ("dp", "seq"), scatter_dimension=0, tiled=True),
        lax.psum_scatter(grad_bias_out, ("dp", "seq"), scatter_dimension=0, tiled=True),
        lax.psum_scatter(grad_gain_one, ("dp", "seq"), scatter_dimension=0, tiled=True),
        lax.psum_scatter(grad_shift_one, ("dp", "seq"), scatter_dimension=0, tiled=True),
        lax.psum_scatter(grad_bias_up, ("dp", "seq"), scatter_dimension=0, tiled=True),
        lax.psum_scatter(grad_bias_down, ("dp", "seq"), scatter_dimension=0, tiled=True),
        lax.psum_scatter(grad_gain_two, ("dp", "seq"), scatter_dimension=0, tiled=True),
        lax.psum_scatter(grad_shift_two, ("dp", "seq"), scatter_dimension=0, tiled=True),
    )
    table_sum, totals = lax.psum((jnp.sum(grad_tables, axis=0), local_sums), ("dp", "seq"))
    content_count = totals[6] * MODEL_WIDTH
    query_count = float(seq_count * lax.axis_size("dp") * pred_count * group_size * MODEL_WIDTH)
    stats = jnp.sqrt(
        jnp.stack(
            [
                totals[0] / content_count,
                totals[1] / query_count,
                totals[2] / content_count,
                totals[3] / query_count,
                totals[4] / content_count,
                totals[5] / query_count,
            ]
        )
    )
    return (
        outputs[:, :shard_length],
        outputs[:, shard_length:],
        grad_content,
        grad_query,
        owned[0],
        owned[4],
        owned[1],
        owned[5],
        owned[6],
        owned[7],
        owned[2],
        owned[8],
        owned[3],
        owned[9],
        owned[10],
        owned[11],
        table_sum,
        stats,
    )


LOG2E = math.log2(math.e)
TILE = 256
KEYS = 512
HALF = 128
REACH = 11
DIAGS = 2 * REACH + 1
FAR = 7
WIDE = SEQ_LEN + HALF
MASKED = -1e30
F32 = jnp.float32
BF16 = jnp.bfloat16


def dot_nn(a, b):
    return jnp.dot(a, b, preferred_element_type=F32)


def dot_nt(a, b):
    return lax.dot_general(a, b, (((1,), (1,)), ((), ())), preferred_element_type=F32)


def dot_tn(a, b):
    return lax.dot_general(a, b, (((0,), (0,)), ((), ())), preferred_element_type=F32)


def cost_of(micros):
    return pl.CostEstimate(
        flops=int(micros * 1.0e9), bytes_accessed=int(micros * 1.0e6), transcendentals=0
    )


def bias_kernel(
    rows_q,
    own,
    slot_q,
    heads_ref,
    bucket_ref,
    table_ref,
    ints_ref,
    tile_out,
    qbias_out,
    kmeta_ref,
    rseg_ref,
    rlim_ref,
    hot_ref,
    shift_ref,
    vec_scr,
    ahead_scr,
    fold_scr,
    tile_scr,
    qbias_scr,
    sems,
):
    seqs, length = ints_ref.shape[0], ints_ref.shape[2]
    first = heads_ref[0]
    hot = (
        lax.broadcasted_iota(jnp.int32, (BUCKETS, 2 * SEQ_LEN), 0) == bucket_ref[0:1, :]
    ).astype(BF16)
    vec_scr[...] = dot_tn(table_ref[...], hot)
    hot = (
        lax.broadcasted_iota(jnp.int32, (BUCKETS, 2 * SEQ_LEN), 0) == bucket_ref[1:2, :]
    ).astype(BF16)
    ahead_scr[...] = dot_tn(table_ref[...], hot) * LOG2E
    copies = []
    for h in range(own):
        row = ahead_scr[pl.ds(first + h, 1), :]
        for e in range(REACH - FAR):
            tile_scr[h, e] = jnp.zeros((HALF, HALF), F32)
            tile_scr[h, DIAGS - 1 - e] = jnp.zeros((HALF, HALF), F32)
        for e in range(-FAR, FAR + 1):
            start = HALF * (15 + e)
            skew = pltpu.roll(
                jnp.broadcast_to(row[:, start : start + 2 * HALF], (HALF, 2 * HALF)),
                0,
                1,
                stride=1,
                stride_axis=0,
            )
            tile_scr[h, e + REACH] = skew[:, HALF:].T
        copies.append(pltpu.make_async_copy(tile_scr.at[h], tile_out.at[h], sems.at[h]))
        copies[-1].start()
        vec = vec_scr[pl.ds(first + h, 1), :]
        fold_scr[h] = jnp.concatenate(
            [vec[:, HALF * i : HALF * i + WIDE] for i in range(16)], axis=0
        ).astype(BF16)

    place = lax.broadcasted_iota(jnp.int32, (1, length), 1)
    lane = lax.broadcasted_iota(jnp.int32, (HALF, HALF), 1)
    segs, orders = [], []
    for t in range(seqs):
        seg = ints_ref[t, 0:1, :]
        seg = jnp.where(ints_ref[t, 2:3, :] == 1, seg, -2 - t * length - place)
        order = ints_ref[t, 1:2, :]
        rseg_ref[:, t * length : (t + 1) * length] = seg
        rlim_ref[:, t * length : (t + 1) * length] = order
        for n, row in ((0, seg.astype(F32)), (1, order.astype(F32))):
            for i in range(length // HALF):
                part = row[:, i * HALF : (i + 1) * HALF]
                (segs, orders)[n].append(part)
                kmeta_ref[n, t * length + i * HALF : t * length + (i + 1) * HALF, :] = (
                    jnp.broadcast_to(part, (HALF, HALF)).T.astype(jnp.int32)
                )
    segs = jnp.concatenate(segs, axis=0)
    orders = jnp.concatenate(orders, axis=0)
    preds = [ints_ref[t, 3:4, :slot_q].astype(F32) for t in range(seqs)]
    preds.append(jnp.full((1, rows_q - seqs * slot_q), -1.0, F32))
    preds = jnp.concatenate(preds, axis=1)
    high = lax.Precision.HIGHEST
    for t in range(rows_q // HALF):
        at = slice(t * HALF, (t + 1) * HALF)
        spots = jnp.broadcast_to(preds[:, at], (HALF, HALF)).T.astype(jnp.int32)
        group = jnp.right_shift(spots, 7)
        inside = jnp.bitwise_and(spots, HALF - 1)
        pick = (lane == group)[:, :16].astype(F32)
        for rows, ref, less in ((segs, rseg_ref, 0.0), (orders, rlim_ref, 1.0)):
            spread = jnp.dot(pick, rows, precision=high, preferred_element_type=F32)
            found = jnp.take_along_axis(spread, inside, axis=1) - less
            ref[:, length * seqs + t * HALF : length * seqs + (t + 1) * HALF] = found.T[
                0:1, :
            ].astype(jnp.int32)
        hot_ref[at, :] = (lane == 15 - group)[:, :16].astype(BF16)
        shift_ref[at, :] = HALF - 1 - inside

    for h in range(own):
        for t in range(rows_q // HALF):
            at = slice(t * HALF, (t + 1) * HALF)
            turn = lane + shift_ref[at, :]
            wrap = turn >= HALF
            idx = jnp.where(wrap, turn - HALF, turn)
            spread = dot_nn(hot_ref[at, :], fold_scr[h])
            prev = jnp.take_along_axis(spread[:, :HALF], idx, axis=1)
            for j in range(SEQ_LEN // HALF):
                cur = jnp.take_along_axis(
                    spread[:, (j + 1) * HALF : (j + 2) * HALF], idx, axis=1
                )
                out = jnp.where(wrap, cur, prev) * LOG2E
                qbias_scr[h, j * HALF : (j + 1) * HALF, at] = out.T
                prev = cur
        copies.append(pltpu.make_async_copy(qbias_scr.at[h], qbias_out.at[h], sems.at[own + h]))
        copies[-1].start()
    for copy in copies:
        copy.wait()


def bias_call(own, rows_q, slot_q, first, buckets, table, ints):
    vm = pl.BlockSpec(memory_space=pltpu.VMEM)
    tiles = jax.ShapeDtypeStruct((own, DIAGS, HALF, HALF), F32)
    qbias = jax.ShapeDtypeStruct((own, SEQ_LEN, rows_q), F32)
    rows = jax.ShapeDtypeStruct((1, SEQ_LEN + rows_q), jnp.int32)
    return pl.pallas_call(
        functools.partial(bias_kernel, rows_q, own, slot_q),
        out_shape=(
            tiles,
            qbias,
            jax.ShapeDtypeStruct((2, SEQ_LEN, HALF), jnp.int32),
            rows,
            rows,
            jax.ShapeDtypeStruct((rows_q, 16), BF16),
            jax.ShapeDtypeStruct((rows_q, HALF), jnp.int32),
        ),
        in_specs=[pl.BlockSpec(memory_space=pltpu.SMEM)] + [vm] * 3,
        out_specs=(pl.BlockSpec(memory_space=pltpu.HBM),) * 2 + (vm,) * 5,
        scratch_shapes=[
            pltpu.VMEM((table.shape[1], 2 * SEQ_LEN), F32),
            pltpu.VMEM((table.shape[1], 2 * SEQ_LEN), F32),
            pltpu.VMEM((own, 16, WIDE), BF16),
            pltpu.VMEM(tiles.shape, F32),
            pltpu.VMEM(qbias.shape, F32),
            pltpu.SemaphoreType.DMA((2 * own,)),
        ],
        compiler_params=pltpu.CompilerParams(vmem_limit_bytes=58 << 20),
        cost_estimate=cost_of(12),
        name="bias_tiles",
    )(first, buckets, table, ints)


def bias_block(tile_ref, h, e):
    return jnp.concatenate(
        [
            jnp.concatenate([tile_ref[h, e + i], tile_ref[h, e + i - 1]], axis=1)
            for i in range(KEYS // HALF)
        ],
        axis=0,
    )


def mask_block(kmeta_ref, rseg_ref, rlim_ref, krow, rcol, width):
    kseg = kmeta_ref[0, pl.ds(krow, KEYS), :]
    kord = kmeta_ref[1, pl.ds(krow, KEYS), :]
    parts = []
    for w in range(width // HALF):
        rseg = rseg_ref[:, pl.ds(rcol + w * HALF, HALF)]
        rlim = rlim_ref[:, pl.ds(rcol + w * HALF, HALF)]
        ok = (kseg == rseg) & (kord <= rlim)
        parts.append(jnp.where(ok, 0.0, MASKED))
    return parts[0] if len(parts) == 1 else jnp.concatenate(parts, axis=1)


def fwd_kernel(
    own,
    rows_q,
    span_ref,
    qt_ref,
    k_ref,
    vt_ref,
    kmeta_ref,
    rseg_ref,
    rlim_ref,
    tile_ref,
    qbias_ref,
    ctx_ref,
    rows_ref,
    lse_ref,
    s_scr,
    qbias_scr,
    qbias_sem,
):
    late = pltpu.make_async_copy(qbias_ref, qbias_scr, qbias_sem.at[0])
    late.start()

    def run(rcol, width, lo, steps, bias_of):
        heads = range(own)

        def fold(op, x):
            rows = [x[i * 8 : (i + 1) * 8] for i in range(x.shape[0] // 8)]
            while len(rows) > 1:
                rows = [op(rows[i], rows[i + 1]) for i in range(0, len(rows), 2)]
            return rows[0]

        def score(step, tops):
            kt = lo + step * (KEYS // TILE)
            krow = pl.multiple_of(kt * TILE, TILE)
            mask = mask_block(kmeta_ref, rseg_ref, rlim_ref, krow, rcol, width)
            new = []
            for h in heads:
                s = jnp.dot(
                    k_ref[h, pl.ds(krow, KEYS), :],
                    qt_ref[h * HEAD_DIM : (h + 1) * HEAD_DIM, pl.ds(rcol, width)],
                    preferred_element_type=F32,
                )
                s = s * (SCALE * LOG2E) + (bias_of(h, kt) + mask)
                s_scr[h, pl.ds(krow, KEYS), :width] = s
                new.append(jnp.maximum(tops[h], fold(jnp.maximum, s)))
            return tuple(new)

        tops = lax.fori_loop(
            0, steps, score, tuple(jnp.full((8, width), MASKED, F32) for _ in heads)
        )
        tops = [jnp.max(t, axis=0, keepdims=True) for t in tops]

        def weigh(step, carry):
            kt = lo + step * (KEYS // TILE)
            krow = pl.multiple_of(kt * TILE, TILE)
            sums, accs = carry
            new_sums, new_accs = [], []
            for h in heads:
                p = jnp.exp2(s_scr[h, pl.ds(krow, KEYS), :width] - tops[h])
                new_sums.append(sums[h] + fold(jnp.add, p))
                new_accs.append(
                    accs[h]
                    + jnp.dot(
                        vt_ref[h * HEAD_DIM : (h + 1) * HEAD_DIM, pl.ds(krow, KEYS)],
                        p.astype(BF16),
                        preferred_element_type=F32,
                    )
                )
            return tuple(new_sums), tuple(new_accs)

        sums, accs = lax.fori_loop(
            0,
            steps,
            weigh,
            (
                tuple(jnp.zeros((8, width), F32) for _ in heads),
                tuple(jnp.zeros((HEAD_DIM, width), F32) for _ in heads),
            ),
        )
        outs = []
        for h in heads:
            total = jnp.sum(sums[h], axis=0, keepdims=True)
            outs.append(accs[h] / total)
            lse_ref[h : h + 1, pl.ds(rcol, width)] = tops[h] + jnp.log2(total)
        out = jnp.concatenate(outs, axis=0)
        ctx_ref[:, pl.ds(rcol, width)] = out.astype(BF16)
        return out

    def content_tile(qt, carry):
        def bias_of(h, kt):
            return bias_block(tile_ref, h, 2 * (kt - qt) + REACH)

        run(pl.multiple_of(qt * TILE, TILE), TILE, span_ref[0, qt], span_ref[1, qt], bias_of)
        return carry

    lax.fori_loop(0, SEQ_LEN // TILE, content_tile, 0)

    def query_bias(h, kt):
        return qbias_scr[h, pl.ds(pl.multiple_of(kt * TILE, TILE), KEYS), :]

    late.wait()
    last = SEQ_LEN // TILE
    out = run(SEQ_LEN, rows_q, span_ref[0, last], span_ref[1, last], query_bias)
    rows_ref[...] = out.T.astype(BF16)


def fwd_call(span, qt, k3, vt, kmeta, rseg, rlim, tiles, qbias):
    own = k3.shape[0]
    rows = qt.shape[1]
    rows_q = rows - SEQ_LEN
    vm = pl.BlockSpec(memory_space=pltpu.VMEM)
    return pl.pallas_call(
        functools.partial(fwd_kernel, own, rows_q),
        out_shape=(
            jax.ShapeDtypeStruct((own * HEAD_DIM, rows), BF16),
            jax.ShapeDtypeStruct((rows_q, own * HEAD_DIM), BF16),
            jax.ShapeDtypeStruct((own, rows), F32),
        ),
        in_specs=[pl.BlockSpec(memory_space=pltpu.SMEM)]
        + [vm] * 7
        + [pl.BlockSpec(memory_space=pltpu.HBM)],
        scratch_shapes=[
            pltpu.VMEM((own, SEQ_LEN, max(rows_q, TILE)), F32),
            pltpu.VMEM(qbias.shape, F32),
            pltpu.SemaphoreType.DMA((1,)),
        ],
        compiler_params=pltpu.CompilerParams(vmem_limit_bytes=46 << 20),
        cost_estimate=cost_of(32),
        name="attend",
    )(span, qt, k3, vt, kmeta, rseg, rlim, tiles, qbias)


def bwd_kernel(
    own,
    rows_q,
    span_ref,
    qt_ref,
    k_ref,
    kt_ref,
    v_ref,
    ctx_ref,
    gc_ref,
    gq_ref,
    lse_ref,
    kmeta_ref,
    rseg_ref,
    rlim_ref,
    tile_ref,
    hot_ref,
    shift_ref,
    qbias_ref,
    dq_ref,
    dk_ref,
    dv_ref,
    offs_ref,
    qoffs_ref,
    dk_scr,
    dv_scr,
    dq_scr,
    diag_scr,
    ds_scr,
    delta_scr,
    gt_ref,
    qbias_scr,
    qbias_sem,
):
    late = pltpu.make_async_copy(qbias_ref, qbias_scr, qbias_sem.at[0])
    late.start()
    seqs, length = gc_ref.shape[0], gc_ref.shape[2]
    for t in range(seqs):
        for a in range(0, length, TILE):
            block = gc_ref[t, :, a : a + TILE]
            gt_ref[:, t * length + a : t * length + a + TILE] = block
    used = gq_ref.shape[0]
    block = jnp.concatenate(
        [gq_ref[...].astype(F32), jnp.zeros((rows_q - used, gq_ref.shape[1]), F32)], axis=0
    )
    gt_ref[:, SEQ_LEN:] = block.T.astype(BF16)
    dk_scr[...] = jnp.zeros(dk_scr.shape, F32)
    dv_scr[...] = jnp.zeros(dv_scr.shape, F32)
    diag_scr[...] = jnp.zeros(diag_scr.shape, F32)
    ds_scr[...] = jnp.zeros(ds_scr.shape, BF16)
    for h in range(own):
        part = slice(h * HEAD_DIM, (h + 1) * HEAD_DIM)
        delta_scr[h : h + 1, :] = jnp.sum(
            ctx_ref[part, :].astype(F32) * gt_ref[part, :].astype(F32), axis=0, keepdims=True
        )

    def run(rcol, width, lo, steps, bias_of, keep):
        dq_scr[...] = jnp.zeros(dq_scr.shape, F32)

        def body(step, carry):
            kt = lo + step * (KEYS // TILE)
            krow = pl.multiple_of(kt * TILE, TILE)
            mask = mask_block(kmeta_ref, rseg_ref, rlim_ref, krow, rcol, width)
            for h in range(own):
                part = slice(h * HEAD_DIM, (h + 1) * HEAD_DIM)
                s = jnp.dot(
                    k_ref[h, pl.ds(krow, KEYS), :],
                    qt_ref[part, pl.ds(rcol, width)],
                    preferred_element_type=F32,
                )
                s = s * (SCALE * LOG2E) + (bias_of(h, kt) + mask)
                p = jnp.exp2(s - lse_ref[h : h + 1, pl.ds(rcol, width)])
                gp = jnp.dot(
                    v_ref[h, pl.ds(krow, KEYS), :],
                    gt_ref[part, pl.ds(rcol, width)],
                    preferred_element_type=F32,
                )
                ds = p * (gp - delta_scr[h : h + 1, pl.ds(rcol, width)])
                low = ds.astype(BF16)
                keep(h, kt, ds, low)
                dv_scr[part, pl.ds(krow, KEYS)] += dot_nt(
                    gt_ref[part, pl.ds(rcol, width)], p.astype(BF16)
                )
                dk_scr[part, pl.ds(krow, KEYS)] += dot_nt(qt_ref[part, pl.ds(rcol, width)], low)
                dq_scr[h, :, :width] += jnp.dot(
                    kt_ref[part, pl.ds(krow, KEYS)], low, preferred_element_type=F32
                )
            return carry

        lax.fori_loop(0, steps, body, 0)
        grad = jnp.concatenate([dq_scr[h, :, :width] for h in range(own)], axis=0)
        dq_ref[pl.ds(rcol, width), :] = (grad * SCALE).T.astype(BF16)

    def content_tile(qt, carry):
        def bias_of(h, kt):
            return bias_block(tile_ref, h, 2 * (kt - qt) + REACH)

        def keep(h, kt, ds, low):
            e = 2 * (kt - qt) + REACH
            subs = [ds[i * HALF : (i + 1) * HALF] for i in range(KEYS // HALF)]
            diag_scr[h, e - 1] += subs[0][:, HALF:]
            for i, sub in enumerate(subs):
                here = sub[:, :HALF]
                if i + 1 < len(subs):
                    here = here + subs[i + 1][:, HALF:]
                diag_scr[h, e + i] += here

        run(pl.multiple_of(qt * TILE, TILE), TILE, span_ref[0, qt], span_ref[1, qt], bias_of, keep)
        return carry

    lax.fori_loop(0, SEQ_LEN // TILE, content_tile, 0)

    def query_bias(h, kt):
        return qbias_scr[h, pl.ds(pl.multiple_of(kt * TILE, TILE), KEYS), :]

    def query_keep(h, kt, ds, low):
        ds_scr[h, pl.ds(pl.multiple_of(kt * TILE, TILE), KEYS), :] = low

    late.wait()
    last = SEQ_LEN // TILE
    run(SEQ_LEN, rows_q, span_ref[0, last], span_ref[1, last], query_bias, query_keep)

    for a in range(0, SEQ_LEN, TILE):
        at = slice(a, a + TILE)
        dk_ref[at, :] = (dk_scr[:, at] * SCALE).T.astype(BF16)
        dv_ref[at, :] = dv_scr[:, at].T.astype(BF16)

    offs_ref[...] = jnp.zeros(offs_ref.shape, F32)
    qoffs_ref[...] = jnp.zeros(qoffs_ref.shape, F32)
    lane = lax.broadcasted_iota(jnp.int32, (HALF, HALF), 1)
    turn = lax.broadcasted_iota(jnp.int32, (HALF, HALF), 0) - lane
    over = turn < 0
    turn = jnp.where(over, turn + HALF, turn)
    for h in range(own):
        for e in range(REACH - FAR, REACH + FAR + 1):
            skew = jnp.take_along_axis(diag_scr[h, e], turn, axis=1)
            start = HALF * (15 + e - REACH)
            offs_ref[h : h + 1, start : start + HALF] += jnp.sum(
                jnp.where(over, skew, 0.0), axis=0, keepdims=True
            )
            offs_ref[h : h + 1, start + HALF : start + 2 * HALF] += jnp.sum(
                jnp.where(over, 0.0, skew), axis=0, keepdims=True
            )

    for h in range(own):
        total = jnp.zeros((16, WIDE), F32)
        for t in range(rows_q // HALF):
            shift = shift_ref[t * HALF : (t + 1) * HALF, :]
            place = lane - shift
            low_side = place < 0
            idx = jnp.where(low_side, place + HALF, place)
            prev = jnp.zeros((HALF, HALF), F32)
            pieces = []
            for j in range(SEQ_LEN // HALF + 1):
                if j < SEQ_LEN // HALF:
                    block = ds_scr[h, j * HALF : (j + 1) * HALF, t * HALF : (t + 1) * HALF]
                    cur = jnp.take_along_axis(block.astype(F32).T, idx, axis=1)
                else:
                    cur = jnp.zeros((HALF, HALF), F32)
                pieces.append(jnp.where(low_side, prev, cur).astype(BF16))
                prev = cur
            total += dot_tn(
                hot_ref[t * HALF : (t + 1) * HALF, :], jnp.concatenate(pieces, axis=1)
            )
        for i in range(16):
            qoffs_ref[h : h + 1, HALF * i : HALF * i + WIDE] += total[i : i + 1, :]


def bwd_call(
    span, qt, k3, kt, v3, ctx, g_c, g_q, lse, kmeta, rseg, rlim, tiles, hot, shift, qbias
):
    own = k3.shape[0]
    rows = qt.shape[1]
    rows_q = rows - SEQ_LEN
    vm = pl.BlockSpec(memory_space=pltpu.VMEM)
    return pl.pallas_call(
        functools.partial(bwd_kernel, own, rows_q),
        out_shape=(
            jax.ShapeDtypeStruct((rows, own * HEAD_DIM), BF16),
            jax.ShapeDtypeStruct((SEQ_LEN, own * HEAD_DIM), BF16),
            jax.ShapeDtypeStruct((SEQ_LEN, own * HEAD_DIM), BF16),
            jax.ShapeDtypeStruct((own, 2 * SEQ_LEN), F32),
            jax.ShapeDtypeStruct((own, 2 * SEQ_LEN), F32),
        ),
        in_specs=[pl.BlockSpec(memory_space=pltpu.SMEM)]
        + [vm] * 14
        + [pl.BlockSpec(memory_space=pltpu.HBM)],
        scratch_shapes=[
            pltpu.VMEM((own * HEAD_DIM, SEQ_LEN), F32),
            pltpu.VMEM((own * HEAD_DIM, SEQ_LEN), F32),
            pltpu.VMEM((own, HEAD_DIM, max(rows_q, TILE)), F32),
            pltpu.VMEM((own, DIAGS, HALF, HALF), F32),
            pltpu.VMEM((own, SEQ_LEN, rows_q), BF16),
            pltpu.VMEM((own, rows), F32),
            pltpu.VMEM((own * HEAD_DIM, rows), BF16),
            pltpu.VMEM(qbias.shape, F32),
            pltpu.SemaphoreType.DMA((1,)),
        ],
        compiler_params=pltpu.CompilerParams(vmem_limit_bytes=42 << 20),
        cost_estimate=cost_of(58),
        name="attend_back",
    )(span, qt, k3, kt, v3, ctx, g_c, g_q, lse, kmeta, rseg, rlim, tiles, hot, shift, qbias)


def key_spans(segment, pad_mask):
    length = segment.shape[0]
    real = pad_mask == 1
    head_seg = segment[::TILE]
    tail_seg = segment[TILE - 1 :: TILE]
    starts = jnp.sum((segment[None, :] < head_seg[:, None]).astype(jnp.int32), axis=1)
    first = jnp.arange(0, length, TILE, dtype=jnp.int32)
    lo = jnp.where(real[::TILE], starts, first) // TILE
    hi = jnp.where(real[TILE - 1 :: TILE], tail_seg, first + TILE - 1) // TILE
    count = jnp.sum(pad_mask)
    lo = jnp.concatenate([lo, jnp.zeros((1,), jnp.int32)])
    hi = jnp.concatenate([hi, jnp.maximum(count - 1, 0)[None] // TILE])
    per = KEYS // TILE
    steps = (hi - lo + per) // per
    lo = jnp.minimum(lo, length // TILE - steps * per)
    return jnp.stack([lo, steps]).astype(jnp.int32)


COLS = 768
UP_TOP = (2, 1)
DOWN_TOP = (1, 2)


def place_of(j, top):
    return (
        8 * (j % 2)
        + 4 * ((j // 2) % 2)
        + top[0] * ((j // 4) % 2)
        + top[1] * (j // 8)
    )


def mid_kernel(
    seqs,
    ctx_c,
    ctx_q,
    x_c,
    x_q,
    cot_c,
    cot_q,
    pad_ref,
    six_ref,
    bias_up,
    uo_own,
    uo_own_far,
    uo_mate,
    uo_mate_far,
    down_own,
    down_own_far,
    down_mate,
    down_mate_far,
    res_c,
    res_q,
    gctx_c,
    gctx_q,
    six_out,
    up_out,
    sums_ref,
    out_c,
    out_q,
    keep_out,
    give_out,
    w_up,
    w_out,
    w_down,
    one_scr,
    norm_scr,
    inv_scr,
    low_scr,
    act_scr,
    slope_scr,
    sum_scr,
    grad_scr,
    pre_scr,
    plane_scr,
    outc_scr,
    outq_scr,
    parts_scr,
    sq_scr,
    valid_ref,
    xq_scr,
    cotq_scr,
    sems,
    plane_sems,
    out_sems,
):
    core = lax.rem(lax.axis_index("seq"), 2)
    this = lax.axis_index("dp") * (seqs // 2) + lax.axis_index("seq") // 2
    near, shard = uo_own.shape[0], uo_own.shape[1]
    chips = 2 * near
    shard_down = down_own.shape[1]
    length = x_c.shape[0]
    preds = x_q.shape[0]
    count = xq_scr.shape[0]
    ff = w_up.shape[1]
    chunks = ff // COLS
    wide = ctx_c.shape[1]
    half_ff, half = ff // 2, COLS // 2
    bias_out, gain_one, shift_one, bias_down, gain_two, shift_two = [
        six_ref[i : i + 1, :] for i in range(6)
    ]

    def plane_copies(chunk, slot):
        start = chunk * COLS
        if not isinstance(start, int):
            start = pl.multiple_of(start, COLS)
        return [
            pltpu.make_async_copy(
                ref.at[:, :, pl.ds(start, COLS)],
                plane_scr.at[slot, n // 2, pl.ds(near * (n % 2), near)],
                plane_sems.at[slot, n],
            )
            for n, ref in enumerate((uo_own, uo_own_far, uo_mate, uo_mate_far))
        ]

    def assemble(slot, put_rows):
        def body(j, carry):
            chip = this ^ place_of(j, UP_TOP)
            first = plane_scr[slot, core, j].astype(F32)
            second = plane_scr[slot, 1 - core, j].astype(F32)
            pair = jnp.concatenate([first, second], axis=0).astype(BF16)
            put_rows(pl.ds(pl.multiple_of(2 * shard * chip, 16), 2 * shard), pair)
            return carry

        lax.fori_loop(0, chips, body, 0)

    for chunk, slot in ((chunks, 0), (0, 1)):
        for copy in plane_copies(chunk, slot):
            copy.start()
    copies = []
    for j in range(chips):
        chip = this ^ place_of(j, DOWN_TOP)
        own, mate = ((down_own, down_mate), (down_own_far, down_mate_far))[j // near]
        for side, ref in ((core, own), (1 - core, mate)):
            row = pl.multiple_of((2 * chip + side) * shard_down, 16)
            copies.append(
                pltpu.make_async_copy(
                    ref.at[j % near], w_down.at[pl.ds(row, shard_down)], sems.at[len(copies)]
                )
            )
    for copy in copies:
        copy.start()
    for copy in plane_copies(chunks, 0):
        copy.wait()

    def put_out(rows, pair):
        w_out[rows, :] = pair

    assemble(0, put_out)
    for copy in plane_copies(1, 0):
        copy.start()

    for a in range(0, length, 128):
        row = pad_ref[:, a : a + 128].astype(F32)
        valid_ref[a : a + 128, :] = jnp.broadcast_to(row, (128, 128)).T
    spot = lax.broadcasted_iota(jnp.int32, (count, 128), 0)
    valid_ref[length:, :] = jnp.where(spot < preds, 1.0, 0.0)
    for ref, scr in ((x_q, xq_scr), (cot_q, cotq_scr)):
        scr[...] = jnp.zeros(scr.shape, F32)
        scr[:preds, :] = ref[...]
    blocks = [(0, length // 2), (length // 2, length), (length, length + count)]
    total = length + count
    cut = (total // 2 + 15) // 16 * 16
    halves = [(0, cut), (cut, total)]

    def pick(ref_c, ref_q, a, b):
        return ref_c[a:b, :] if b <= length else ref_q[...]

    def put(ref_c, ref_q, a, b, value):
        if b <= length:
            ref_c[a:b, :] = value
        else:
            ref_q[...] = value[: ref_q.shape[0]]

    def norm(x):
        mean = jnp.mean(x, axis=-1, keepdims=True)
        centered = x - mean
        inv = lax.rsqrt(jnp.mean(centered * centered, axis=-1, keepdims=True) + EPS)
        return centered * inv, inv

    def norm_grad(up, normed, inv, gain):
        grad = up * gain
        proj = jnp.mean(grad, axis=-1, keepdims=True) + normed * jnp.mean(
            grad * normed, axis=-1, keepdims=True
        )
        return inv * (grad - proj)

    sq_scr[...] = jnp.zeros(sq_scr.shape, F32)
    six_out[...] = jnp.zeros(six_out.shape, F32)
    up_out[...] = jnp.zeros(up_out.shape, F32)

    def count_in(k, x, a, b):
        row = k + (1 if b > length else 0)
        sq_scr[row : row + 1, :] += jnp.sum(x * x * valid_ref[a:b, :1], axis=0, keepdims=True)

    def add_row(row, x):
        six_out[row : row + 1, :] += jnp.sum(x, axis=0, keepdims=True)

    for a, b in blocks:
        attn = bias_out
        for t in range(seqs):
            part = w_out[t * wide : (t + 1) * wide, :]
            attn = attn + (
                dot_tn(ctx_c[t, :, a:b], part) if b <= length else dot_nn(ctx_q[t], part)
            )
        x = pick(x_c, xq_scr, a, b)
        count_in(0, x, a, b)
        count_in(2, attn, a, b)
        normed, inv = norm(x + attn)
        one = normed * gain_one + shift_one
        norm_scr[a:b, :] = normed
        inv_scr[a:b, :] = jnp.broadcast_to(inv, (b - a, 128))
        one_scr[a:b, :] = one
        low_scr[a:b, :] = one.astype(BF16)

    for copy in copies:
        copy.wait()
    sum_scr[...] = jnp.zeros(sum_scr.shape, F32)

    def up_step(i, carry):
        cols = pl.ds(pl.multiple_of(i * COLS, COLS), COLS)
        slot = lax.rem(i + 1, 2)
        for copy in plane_copies(i, slot):
            copy.wait()

        def put_up(rows, pair):
            w_up[rows, cols] = pair

        assemble(slot, put_up)

        @pl.when(i + 2 < chunks)
        def _():
            for copy in plane_copies(i + 2, slot):
                copy.start()

        for a, b in halves:
            u = dot_nn(low_scr[a:b, :], w_up[:, cols]) + bias_up[:, cols]
            cdf = 0.5 * (1.0 + lax.erf(u * math.sqrt(0.5)))
            act = (u * cdf).astype(BF16)
            act_scr[a:b, cols] = act
            slope_scr[a:b, cols] = cdf + u * (
                jnp.exp(-0.5 * u * u) * (1.0 / math.sqrt(2.0 * math.pi))
            )
            sum_scr[a:b, :] += dot_nn(act, w_down[cols, :])
        return carry

    lax.fori_loop(0, chunks, up_step, 0)

    for a, b in blocks:
        ffn = sum_scr[a:b, :] + bias_down
        count_in(4, ffn, a, b)
        normed, inv = norm(one_scr[a:b, :] + ffn)
        ok = valid_ref[a:b, :1]
        put(outc_scr, outq_scr, a, b, (normed * gain_two + shift_two) * ok)
        up = pick(cot_c, cotq_scr, a, b) * ok
        add_row(4, up * normed)
        add_row(5, up)
        grad = norm_grad(up, normed, inv, gain_two)
        low = grad.astype(BF16)
        add_row(3, low.astype(F32))
        sum_scr[a:b, :] = grad
        grad_scr[a:b, :] = low
    leaving = [
        pltpu.make_async_copy(outc_scr, out_c, out_sems.at[0]),
        pltpu.make_async_copy(outq_scr, out_q, out_sems.at[1]),
    ]
    for copy in leaving:
        copy.start()

    def start(copy_of, h):
        @pl.when(core == h)
        def _():
            copy_of(keep_out).start()

        @pl.when(core != h)
        def _():
            copy_of(give_out).start()

    def up_copy(i, out):
        h, at = i // 2, lax.rem(i, 2) if not isinstance(i, int) else i % 2
        cols = pl.ds(pl.multiple_of(at * COLS, COLS) if not isinstance(i, int) else at * COLS, COLS)
        return pltpu.make_async_copy(
            parts_scr.at[h, :, cols], out.at[:, cols], out_sems.at[2 + i]
        )

    down_rows = 2 * shard * (COLS // (2 * shard_down))
    down_cols = pl.ds(half_ff + half, half_ff)

    def down_copy(i, h, out):
        start = i * down_rows
        rows = pl.ds(start if isinstance(i, int) else pl.multiple_of(start, down_rows), down_rows)
        return pltpu.make_async_copy(
            parts_scr.at[h, rows, down_cols],
            out.at[rows, down_cols],
            out_sems.at[2 + chunks * (1 + h) + i],
        )

    def back_step(i, carry):
        cols = pl.ds(pl.multiple_of(i * COLS, COLS), COLS)
        for a, b in halves:
            low = (
                dot_nt(grad_scr[a:b, :], w_down[cols, :]) * slope_scr[a:b, cols]
            ).astype(BF16)
            pre_scr[a:b, :] = low
            up_out[:, cols] += jnp.sum(low.astype(F32), axis=0, keepdims=True)
            sum_scr[a:b, :] += dot_nt(low, w_up[:, cols])
        at = pl.ds(pl.multiple_of(lax.rem(i, 2) * COLS, COLS), COLS)
        parts_scr[i // 2, :, at] = dot_tn(low_scr[...], pre_scr[...]).astype(BF16)
        start(lambda out: up_copy(i, out), i // 2)
        grads = dot_tn(act_scr[:, cols], grad_scr[...]).astype(BF16)
        for h in range(2):
            for chip in range(COLS // (2 * shard_down)):
                to = pl.ds(pl.multiple_of(i * down_rows, down_rows) + chip * 2 * shard, 2 * shard)
                for g in range(shard_down // shard):
                    row = 2 * shard_down * chip + 2 * shard * g
                    col = half_ff + half * (1 + g)
                    parts_scr[h, to, col : col + half] = grads[
                        row : row + 2 * shard, h * half : (h + 1) * half
                    ]
            start(lambda out: down_copy(i, h, out), h)
        return carry

    lax.fori_loop(0, chunks, back_step, 0)
    leaving += [up_copy(i, keep_out) for i in range(chunks)]
    leaving += [down_copy(i, h, keep_out) for i in range(chunks) for h in range(2)]

    for a, b in blocks:
        up = sum_scr[a:b, :]
        normed = norm_scr[a:b, :]
        add_row(1, up * normed)
        add_row(2, up)
        grad = norm_grad(up, normed, inv_scr[a:b, :1], gain_one)
        low = grad.astype(BF16)
        add_row(0, low.astype(F32))
        put(res_c, res_q, a, b, grad)
        grad_scr[a:b, :] = low
    for t in range(seqs):
        rows = slice(t * wide, (t + 1) * wide)
        part = w_out[rows, :]
        gctx_c[t] = dot_nt(part, grad_scr[:length, :]).astype(BF16)
        gctx_q[t] = dot_nt(grad_scr[length:, :], part).astype(BF16)
        grads = (
            dot_nn(ctx_c[t], grad_scr[:length, :]) + dot_tn(ctx_q[t], grad_scr[length:, :])
        ).astype(BF16)
        for h in range(2):
            parts_scr[h, rows, half_ff : half_ff + half] = grads[:, h * half : (h + 1) * half]
    tail = pl.ds(half_ff, half)

    def tail_copy(h, out):
        return pltpu.make_async_copy(
            parts_scr.at[h, :, tail], out.at[:, tail], out_sems.at[2 + 3 * chunks + h]
        )

    for h in range(2):
        start(lambda out: tail_copy(h, out), h)
    leaving += [tail_copy(h, keep_out) for h in range(2)]
    sq_scr[6:7, :] = jnp.sum(
        jnp.where(lax.broadcasted_iota(jnp.int32, (length, COLS), 1) == 0, valid_ref[:length, :1], 0.0),
        axis=0,
        keepdims=True,
    )
    sums_ref[...] = jnp.broadcast_to(jnp.sum(sq_scr[...], axis=1, keepdims=True), sums_ref.shape)
    for copy in leaving:
        copy.wait()


def mid_call(ctx_c, ctx_q, x_c, x_q, cot_c, cot_q, pad, six, bias_up, planes):
    seqs, wide, length = ctx_c.shape
    count = ctx_q.shape[1]
    preds = x_q.shape[0]
    total = length + count
    near, shard, cols = planes[0].shape
    chips = 2 * near
    ff = cols - COLS
    chunks = ff // COLS
    vm = pl.BlockSpec(memory_space=pltpu.VMEM)
    anywhere = pl.BlockSpec(memory_space=pl.ANY)
    parts = jax.ShapeDtypeStruct((COLS, (cols + ff) // 2), BF16)
    return pl.pallas_call(
        functools.partial(mid_kernel, seqs),
        out_shape=(
            jax.ShapeDtypeStruct(x_c.shape, F32),
            jax.ShapeDtypeStruct((count, COLS), F32),
            jax.ShapeDtypeStruct(ctx_c.shape, BF16),
            jax.ShapeDtypeStruct(ctx_q.shape, BF16),
            jax.ShapeDtypeStruct((6, COLS), F32),
            jax.ShapeDtypeStruct((1, ff), F32),
            jax.ShapeDtypeStruct((8, 128), F32),
            jax.ShapeDtypeStruct(x_c.shape, F32),
            jax.ShapeDtypeStruct((preds, COLS), F32),
            parts,
            parts,
        ),
        in_specs=[vm] * 9 + [anywhere] * 8,
        out_specs=(vm,) * 7 + (anywhere,) * 4,
        scratch_shapes=[
            pltpu.VMEM((COLS, ff), BF16),
            pltpu.VMEM((COLS, COLS), BF16),
            pltpu.VMEM((ff, COLS), BF16),
            pltpu.VMEM((total, COLS), F32),
            pltpu.VMEM((total, COLS), F32),
            pltpu.VMEM((total, 128), F32),
            pltpu.VMEM((total, COLS), BF16),
            pltpu.VMEM((total, ff), BF16),
            pltpu.VMEM((total, ff), F32),
            pltpu.VMEM((total, COLS), F32),
            pltpu.VMEM((total, COLS), BF16),
            pltpu.VMEM((total, COLS), BF16),
            pltpu.VMEM((2, 2, chips, shard, COLS), BF16),
            pltpu.VMEM(x_c.shape, F32),
            pltpu.VMEM((preds, COLS), F32),
            pltpu.VMEM((2,) + parts.shape, BF16),
            pltpu.VMEM((8, COLS), F32),
            pltpu.VMEM((total, 128), F32),
            pltpu.VMEM((count, COLS), F32),
            pltpu.VMEM((count, COLS), F32),
            pltpu.SemaphoreType.DMA((2 * chips,)),
            pltpu.SemaphoreType.DMA((2, 4)),
            pltpu.SemaphoreType.DMA((4 + 3 * chunks,)),
        ],
        compiler_params=pltpu.CompilerParams(vmem_limit_bytes=63 << 20),
        cost_estimate=cost_of(45),
        name="feed_forward",
    )(ctx_c, ctx_q, x_c, x_q, cot_c, cot_q, pad, six, bias_up, *planes)


def proj_kernel(own, keys, x_ref, w_ref, bq_ref, bv_ref, qt_ref, k_ref, kt_ref, v_ref, vt_ref):
    wide = own * HEAD_DIM
    rows = x_ref.shape[0]
    for a in range(0, rows, 256):
        b = min(a + 256, rows)
        parts = [(0, bq_ref, qt_ref, None)]
        if b <= keys:
            parts += [(1, None, kt_ref, k_ref), (2, bv_ref, vt_ref, v_ref)]
        y = dot_nn(x_ref[a:b, :], w_ref[:, : len(parts) * wide])
        for n, bias, flat_ref, head_ref in parts:
            part = y[:, n * wide : (n + 1) * wide]
            if bias is not None:
                part = part + bias[...]
            flat_ref[:, a:b] = part.T.astype(BF16)
            for h in range(own if head_ref is not None else 0):
                head_ref[h, a:b, :] = part[:, h * HEAD_DIM : (h + 1) * HEAD_DIM].astype(BF16)


def proj_call(own, keys, x, w, bq, bv):
    rows = x.shape[0]
    wide = own * HEAD_DIM
    vm = pl.BlockSpec(memory_space=pltpu.VMEM)
    flat = lambda n: jax.ShapeDtypeStruct((wide, n), BF16)
    head = lambda n: jax.ShapeDtypeStruct((own, n, HEAD_DIM), BF16)
    return pl.pallas_call(
        functools.partial(proj_kernel, own, keys),
        out_shape=(flat(rows), head(keys), flat(keys), head(keys), flat(keys)),
        in_specs=[vm] * 4,
        out_specs=(vm,) * 5,
        compiler_params=pltpu.CompilerParams(vmem_limit_bytes=20 << 20),
        cost_estimate=cost_of(5),
        name="project",
    )(x, w, bq, bv)


def grads_kernel(
    keys,
    x_ref,
    w_ref,
    dq_ref,
    dk_ref,
    dv_ref,
    offs_ref,
    qoffs_ref,
    bucket_ref,
    six_ref,
    up_ref,
    squares_ref,
    gc_ref,
    gq_ref,
    gw_ref,
    vec_ref,
    shared_ref,
    part_scr,
):
    s = lax.axis_index("seq")
    wide = dq_ref.shape[1]
    seqs, length = gc_ref.shape[:2]
    shard = gw_ref.shape[1]
    for n, ref in enumerate((dq_ref, dk_ref, dv_ref)):
        part_scr[:, n * wide : (n + 1) * wide] = dot_tn(x_ref[: ref.shape[0], :], ref[...])
    for j in range(gw_ref.shape[0]):
        gw_ref[j] = part_scr[j * shard : (j + 1) * shard, :].astype(BF16)
    blocks = vec_ref.shape[0]
    n_one, n_up = six_ref.shape[1] // blocks, up_ref.shape[1] // blocks
    n_qv = 2 * n_one
    vec_ref[...] = jnp.zeros(vec_ref.shape, F32)
    sums = [jnp.sum(ref[...].astype(F32), axis=0, keepdims=True) for ref in (dq_ref, dv_ref)]
    for d in range(blocks):
        vec_ref[d, :6, :n_one] = six_ref[:, d * n_one : (d + 1) * n_one]
        vec_ref[d, 6:7, :n_up] = up_ref[:, d * n_up : (d + 1) * n_up]
        kind, start = divmod(d * n_qv, seqs * wide)
        owner, start = divmod(start, wide)
        piece = sums[kind][:, start : start + n_qv]
        vec_ref[d, 7:8, :n_qv] = jnp.where(s == owner, piece, 0.0)
    own = offs_ref.shape[0]
    table = jnp.zeros((own, BUCKETS), F32)
    for row, ref in ((1, offs_ref), (0, qoffs_ref)):
        hot = (
            lax.broadcasted_iota(jnp.int32, (BUCKETS, ref.shape[1]), 0)
            == bucket_ref[row : row + 1, :]
        ).astype(F32)
        table += lax.dot_general(
            ref[...],
            hot,
            (((1,), (1,)), ((), ())),
            precision=lax.Precision.HIGHEST,
            preferred_element_type=F32,
        )
    shared_ref[...] = jnp.zeros(shared_ref.shape, F32)
    for h in range(own):
        shared_ref[pl.ds(s * own + h, 1), :BUCKETS] = table[h : h + 1]
    shared_ref[16:24, :] = squares_ref[...]
    w_q = w_ref[:, :wide]
    w_k = w_ref[:, wide : 2 * wide]
    w_v = w_ref[:, 2 * wide :]
    step = 256
    for t in range(seqs):
        for a in range(0, length, step):
            at = slice(t * length + a, t * length + a + step)
            gc_ref[t, a : a + step, :] = (
                dot_nt(dq_ref[at, :], w_q) + dot_nt(dk_ref[at, :], w_k) + dot_nt(dv_ref[at, :], w_v)
            ).astype(BF16)
    count = gq_ref.shape[1]
    for t in range(seqs):
        at = slice(keys + t * count, keys + (t + 1) * count)
        gq_ref[t] = dot_nt(dq_ref[at, :], w_q).astype(BF16)


def grads_call(
    seqs, length, count, blocks, x, w, dq, dk, dv, offs, qoffs, buckets, six, up, squares
):
    wide = dq.shape[1]
    shard = x.shape[1] // blocks
    vm = pl.BlockSpec(memory_space=pltpu.VMEM)
    return pl.pallas_call(
        functools.partial(grads_kernel, seqs * length),
        out_shape=(
            jax.ShapeDtypeStruct((seqs, length, x.shape[1]), BF16),
            jax.ShapeDtypeStruct((seqs, count, x.shape[1]), BF16),
            jax.ShapeDtypeStruct((blocks, shard, 3 * wide), BF16),
            jax.ShapeDtypeStruct((blocks, 8, 128), F32),
            jax.ShapeDtypeStruct((24, 128), F32),
        ),
        in_specs=[vm] * 11,
        out_specs=(vm,) * 5,
        scratch_shapes=[pltpu.VMEM((x.shape[1], 3 * wide), F32)],
        compiler_params=pltpu.CompilerParams(vmem_limit_bytes=28 << 20),
        cost_estimate=cost_of(6),
        name="weight_grads",
    )(x, w, dq, dk, dv, offs, qoffs, buckets, six, up, squares)


MESH = pl.DeviceIdType.MESH
ROWS_Q = 384
SLOT_Q = 80


def greet(devices):
    barrier = pltpu.get_barrier_semaphore()
    for device in devices:
        pl.semaphore_signal(barrier, inc=1, device_id=device, device_id_type=MESH)
    pl.semaphore_wait(barrier, len(devices))


def remote(src, dst, send_sem, recv_sem, k, device):
    return pltpu.make_async_remote_copy(
        src_ref=src,
        dst_ref=dst,
        send_sem=send_sem.at[k],
        recv_sem=recv_sem.at[k],
        device_id=device,
        device_id_type=MESH,
    )


def start_kernel(
    dps,
    seqs,
    c_ref,
    q_ref,
    w_ref,
    v_ref,
    seg_ref,
    order_ref,
    pad_ref,
    pred_ref,
    x_out,
    w_out,
    v_out,
    i_out,
    c_scr,
    q_scr,
    qlow_scr,
    zero_scr,
    send_sem,
    recv_sem,
    here_sem,
):
    dp = lax.axis_index("dp")
    s = lax.axis_index("seq")
    length = c_ref.shape[0]
    count = q_scr.shape[0]
    mate = s + 1 - 2 * lax.rem(s, 2)
    across = lax.rem(s + 2, seqs)
    level = dp + 1 - 2 * lax.rem(dp, 2)
    stacks = dps // 2
    greet(
        [(dp, lax.rem(s + r, seqs)) for r in range(1, seqs)]
        + [(level, s)]
        + [(lax.rem(dp + 2 * r, dps), s) for r in range(1, stacks)]
    )

    def at_c(owner):
        return pl.ds(pl.multiple_of(owner * length, length), length)

    def at_q(owner):
        return pl.ds(pl.multiple_of(seqs * length + owner * count, 16), count)

    k = 0

    def push(src, dst, device):
        nonlocal k
        copy = remote(src, dst, send_sem, recv_sem, k, device)
        copy.start()
        k += 1
        return copy

    i_out[s] = jnp.zeros(i_out.shape[1:], jnp.int32)
    for n, ref in enumerate((seg_ref, order_ref, pad_ref)):
        i_out[s, n : n + 1, :] = ref[...]
    i_out[s, 3:4, :] = jnp.full((1, length), -1, jnp.int32)
    i_out[s, 3:4, : pred_ref.shape[1]] = pred_ref[...]
    small = []
    for r in range(1, seqs):
        to = lax.rem(s + r, seqs)
        small.append(push(w_ref.at[to], w_out.at[dp, s], (dp, to)))
        small.append(push(v_ref, v_out.at[dp, s], (dp, to)))
        small.append(push(i_out.at[s], i_out.at[s], (dp, to)))
    c_scr[...] = c_ref[...].astype(BF16)
    far = [push(c_scr, x_out.at[at_c(s)], (dp, across))]
    q_scr[...] = jnp.zeros(q_scr.shape, F32)
    q_scr[: q_ref.shape[0], :] = q_ref[...]
    qlow_scr[...] = q_scr[...].astype(BF16)
    far.append(push(qlow_scr, x_out.at[at_q(s)], (dp, across)))
    near = [
        push(scr, x_out.at[at(s)], (dp, mate)) for scr, at in ((c_scr, at_c), (qlow_scr, at_q))
    ]
    v_out[dp, s] = v_ref[...]
    zero_scr[...] = jnp.zeros(zero_scr.shape, BF16)
    here = [
        pltpu.make_async_copy(src, dst, here_sem.at[n])
        for n, (src, dst) in enumerate(
            (
                (w_ref.at[s], w_out.at[dp, s]),
                (c_scr, x_out.at[at_c(s)]),
                (qlow_scr, x_out.at[at_q(s)]),
                (zero_scr, x_out.at[pl.ds(seqs * (length + count), zero_scr.shape[0])]),
            )
        )
    ]
    for copy in here:
        copy.start()
    for copy in here:
        copy.wait()
    for copy in small:
        copy.wait_recv()
    wide, flat = [], []
    for r in range(1, stacks):
        to = lax.rem(dp + 2 * r, dps)
        wide.append([push(ref.at[dp], ref.at[dp], (to, s)) for ref in (w_out, v_out)])
    flat += [push(ref.at[dp], ref.at[dp], (level, s)) for ref in (w_out, v_out)]
    for r in range(1, stacks):
        source = lax.rem(dp + dps - 2 * r, dps)
        for copy, ref in zip(wide[r - 1], (w_out, v_out)):
            copy.wait_recv()
            flat.append(push(ref.at[source], ref.at[source], (level, s)))
    pass_on = []
    for copy, at in zip(far, (at_c, at_q)):
        copy.wait_recv()
        pass_on.append(push(x_out.at[at(across)], x_out.at[at(across)], (dp, mate)))
    for copy in near + flat + pass_on:
        copy.wait_recv()
    for copy in small + far + near + flat + pass_on + sum(wide, []):
        copy.wait_send()


def start_call(dps, seqs, content, query, w, v, metas, slot_q):
    copies = 3 * (seqs - 1) + 4 + 2 * (dps // 2 - 1) + dps + 2
    length, width = content.shape
    vmem = pl.BlockSpec(memory_space=pltpu.VMEM)
    return pl.pallas_call(
        functools.partial(start_kernel, dps, seqs),
        out_shape=(
            jax.ShapeDtypeStruct((seqs * length + ROWS_Q, width), BF16),
            jax.ShapeDtypeStruct((dps,) + w.shape, BF16),
            jax.ShapeDtypeStruct((dps, seqs) + v.shape, F32),
            jax.ShapeDtypeStruct((seqs, 8, length), jnp.int32),
        ),
        in_specs=[vmem] * 8,
        out_specs=(pl.BlockSpec(memory_space=pltpu.HBM),) * 2 + (vmem,) * 2,
        scratch_shapes=[
            pltpu.VMEM((length, width), BF16),
            pltpu.VMEM((slot_q, width), F32),
            pltpu.VMEM((slot_q, width), BF16),
            pltpu.VMEM((ROWS_Q - seqs * slot_q, width), BF16),
            pltpu.SemaphoreType.DMA((copies,)),
            pltpu.SemaphoreType.DMA((copies,)),
            pltpu.SemaphoreType.DMA((4,)),
        ],
        compiler_params=pltpu.CompilerParams(
            collective_id=0, has_side_effects=True, vmem_limit_bytes=16 << 20
        ),
        cost_estimate=cost_of(30),
        name="gather_rows",
    )(content, query, w, v, *metas)


def swap_kernel(seqs, c_of, q_of, c_ref, q_ref, c_out, q_out, send_sem, recv_sem, here_sem):
    dp = lax.axis_index("dp")
    s = lax.axis_index("seq")
    greet([(dp, lax.rem(s + r, seqs)) for r in range(1, seqs)])
    copies = []
    for r in range(1, seqs):
        to = lax.rem(s + r, seqs)
        k = 2 * (r - 1)
        copies.append(remote(c_of(c_ref, to), c_out.at[s], send_sem, recv_sem, k, (dp, to)))
        copies.append(remote(q_of(q_ref, to), q_out.at[s], send_sem, recv_sem, k + 1, (dp, to)))
    for copy in copies:
        copy.start()
    here = [
        pltpu.make_async_copy(c_of(c_ref, s), c_out.at[s], here_sem.at[0]),
        pltpu.make_async_copy(q_of(q_ref, s), q_out.at[s], here_sem.at[1]),
    ]
    for copy in here:
        copy.start()
    for copy in here + copies:
        copy.wait()


def swap_call(seqs, c, q, c_of, q_of, c_shape, q_shape, ident, name):
    vmem = pl.BlockSpec(memory_space=pltpu.VMEM)
    return pl.pallas_call(
        functools.partial(swap_kernel, seqs, c_of, q_of),
        out_shape=(
            jax.ShapeDtypeStruct((seqs,) + c_shape, c.dtype),
            jax.ShapeDtypeStruct((seqs,) + q_shape, q.dtype),
        ),
        in_specs=[vmem] * 2,
        out_specs=(vmem,) * 2,
        scratch_shapes=[
            pltpu.SemaphoreType.DMA((2 * (seqs - 1),)),
            pltpu.SemaphoreType.DMA((2 * (seqs - 1),)),
            pltpu.SemaphoreType.DMA((2,)),
        ],
        compiler_params=pltpu.CompilerParams(collective_id=ident, has_side_effects=True),
        cost_estimate=cost_of(12),
        name=name,
    )(c, q)


def end_kernel(
    dps,
    seqs,
    gc_ref,
    gq_ref,
    w_ref,
    v_ref,
    sh_ref,
    gc_out,
    gq_out,
    w_out,
    v_out,
    sh_out,
    c_mate,
    q_mate,
    c_far,
    q_far,
    c_send,
    q_send,
    w_flat,
    v_flat,
    sh_flat,
    w_send,
    v_send,
    sh_send,
    w_got,
    v_got,
    sh_got,
    w_sum,
    v_sum,
    sh_sum,
    v_last,
    sh_last,
    send_sem,
    recv_sem,
):
    dp = lax.axis_index("dp")
    s = lax.axis_index("seq")
    core = lax.rem(s, 2)
    mate = s + 1 - 2 * core
    across = lax.rem(s + 2, seqs)
    side = lax.rem(dp, 2)
    level = dp + 1 - 2 * side
    stacks = dps // 2
    greet(
        [(dp, lax.rem(s + r, seqs)) for r in range(1, seqs)]
        + [(level, s)]
        + [(lax.rem(dp + 2 * r, dps), s) for r in range(1, stacks)]
    )
    k = 0

    def push(src, dst, device):
        nonlocal k
        copy = remote(src, dst, send_sem, recv_sem, k, device)
        copy.start()
        k += 1
        return copy

    def each(ref, step, fn):
        def body(i, carry):
            fn(pl.ds(pl.multiple_of(i * step, step), step))
            return carry

        lax.fori_loop(0, ref.shape[-2] // step, body, 0)

    first = []
    for i in range(2):
        to = lax.rem(mate + 2 * (1 - i), seqs)
        for src, dst in ((gc_ref, c_mate), (gq_ref, q_mate)):
            first.append(push(src.at[to], dst.at[i], (dp, mate)))
    flat = []
    for r in list(range(1, stacks)) + [0]:
        to = lax.rem(level + 2 * r, dps)
        flat.append(
            [push(src.at[to], dst.at[r], (level, s)) for src, dst in ((w_ref, w_flat), (v_ref, v_flat))]
        )
    shared = push(sh_ref, sh_flat, (level, s))
    cross = []
    for (src, got, buf, far, copy) in (
        (gc_ref, c_mate, c_send, c_far, first[0]),
        (gq_ref, q_mate, q_send, q_far, first[1]),
    ):
        copy.wait_recv()

        def add(rows, src=src, got=got, buf=buf):
            buf[rows, :] = (
                src[across, rows, :].astype(F32) + got[0, rows, :].astype(F32)
            ).astype(BF16)

        each(buf, 16, add)
        cross.append(push(buf, far, (dp, across)))
    shared.wait_recv()
    sh_send[...] = sh_ref[...] + sh_flat[...]
    tall = []
    for r in range(1, stacks):
        for copy in flat[r - 1]:
            copy.wait_recv()
        to = lax.rem(dp + 2 * r, dps)

        def add_pair(rows, to=to, r=r):
            for t in range(seqs):
                w_send[r - 1, t, rows, :] = (
                    w_ref[to, t, rows, :].astype(F32) + w_flat[r, t, rows, :].astype(F32)
                ).astype(BF16)

        each(w_sum, 24, add_pair)
        v_send[r - 1] = v_ref[to] + v_flat[r]
        for src, dst in (
            (w_send.at[r - 1], w_got.at[r - 1]),
            (v_send.at[r - 1], v_got.at[r - 1]),
            (sh_send, sh_got.at[r - 1]),
        ):
            tall.append(push(src, dst, (to, s)))
    for copy in flat[stacks - 1] + tall:
        copy.wait_recv()

    def add_w(rows):
        for t in range(seqs):
            total = w_ref[dp, t, rows, :].astype(F32) + w_flat[0, t, rows, :].astype(F32)
            for r in range(1, stacks):
                total += w_got[r - 1, t, rows, :].astype(F32)
            w_sum[t, rows, :] = total

    each(w_sum, 24, add_w)
    total = v_ref[dp] + v_flat[0]
    for r in range(1, stacks):
        total += v_got[r - 1]
    v_sum[...] = total
    total = sh_send[...]
    for r in range(1, stacks):
        total += sh_got[r - 1]
    sh_sum[...] = total
    last = []
    for r in range(1, seqs):
        to = lax.rem(s + r, seqs)
        last.append(push(w_sum.at[to], w_out.at[s], (dp, to)))
        last.append(push(v_sum.at[to], v_last.at[r - 1], (dp, to)))
        last.append(push(sh_sum, sh_last.at[r - 1], (dp, to)))
    w_out[s] = w_sum[s]
    for copy in first[2:] + cross:
        copy.wait_recv()
    for (src, got, far, out) in (
        (gc_ref, c_mate, c_far, gc_out),
        (gq_ref, q_mate, q_far, gq_out),
    ):

        def total_of(rows, src=src, got=got, far=far, out=out):
            out[rows, :] = (
                src[s, rows, :].astype(F32)
                + got[1, rows, :].astype(F32)
                + far[rows, :].astype(F32)
            )

        each(out, 16, total_of)
    for copy in last:
        copy.wait_recv()
    total = v_sum[s]
    for r in range(1, seqs):
        total += v_last[r - 1]
    v_out[...] = total
    total = sh_sum[...]
    for r in range(1, seqs):
        total += sh_last[r - 1]
    sh_out[...] = total
    for copy in first + sum(flat, []) + [shared] + cross + tall + last:
        copy.wait_send()


def end_call(dps, seqs, gc, gq, w, v, sh):
    stacks = dps // 2
    copies = 4 + 2 * stacks + 1 + 2 + 3 * (stacks - 1) + 3 * (seqs - 1)
    vm = pl.BlockSpec(memory_space=pltpu.VMEM)
    cshape, qshape, wshape, vshape = gc.shape[1:], gq.shape[1:], w.shape[1:], v.shape[1:]
    return pl.pallas_call(
        functools.partial(end_kernel, dps, seqs),
        out_shape=(
            jax.ShapeDtypeStruct(cshape, F32),
            jax.ShapeDtypeStruct(qshape, F32),
            jax.ShapeDtypeStruct(wshape, F32),
            jax.ShapeDtypeStruct(vshape[1:], F32),
            jax.ShapeDtypeStruct(sh.shape, F32),
        ),
        in_specs=[vm] * 5,
        out_specs=(vm,) * 5,
        scratch_shapes=[
            pltpu.VMEM((2,) + cshape, BF16),
            pltpu.VMEM((2,) + qshape, BF16),
            pltpu.VMEM(cshape, BF16),
            pltpu.VMEM(qshape, BF16),
            pltpu.VMEM(cshape, BF16),
            pltpu.VMEM(qshape, BF16),
            pltpu.VMEM((stacks,) + wshape, BF16),
            pltpu.VMEM((stacks,) + vshape, F32),
            pltpu.VMEM(sh.shape, F32),
            pltpu.VMEM((stacks - 1,) + wshape, BF16),
            pltpu.VMEM((stacks - 1,) + vshape, F32),
            pltpu.VMEM(sh.shape, F32),
            pltpu.VMEM((stacks - 1,) + wshape, BF16),
            pltpu.VMEM((stacks - 1,) + vshape, F32),
            pltpu.VMEM((stacks - 1,) + sh.shape, F32),
            pltpu.VMEM(wshape, F32),
            pltpu.VMEM(vshape, F32),
            pltpu.VMEM(sh.shape, F32),
            pltpu.VMEM((seqs - 1,) + vshape[1:], F32),
            pltpu.VMEM((seqs - 1,) + sh.shape, F32),
            pltpu.SemaphoreType.DMA((copies,)),
            pltpu.SemaphoreType.DMA((copies,)),
        ],
        compiler_params=pltpu.CompilerParams(
            collective_id=3, has_side_effects=True, vmem_limit_bytes=24 << 20
        ),
        cost_estimate=cost_of(30),
        name="sum_rows",
    )(gc, gq, w, v, sh)


def flip_perm(count, bit):
    return [(i, i ^ bit) for i in range(count)]


AXES = ("dp", "seq")


def tie(values, *others):
    return lax.optimization_barrier((values, others))[0]


def give_to(cur, count, bit):
    return lax.ppermute(cur, AXES, flip_perm(count, bit))


def local_fast(
    content,
    query_stream,
    segment_ids,
    pad_mask,
    predicted,
    order,
    rel_bucket,
    qkv_weight,
    qv_bias,
    out_weight,
    out_bias,
    attn_gain,
    attn_shift,
    up_weight,
    up_bias,
    down_weight,
    down_bias,
    ffn_gain,
    ffn_shift,
    rel_table,
    content_cot,
    query_cot,
):
    dps, seqs = lax.axis_size("dp"), lax.axis_size("seq")
    count = dps * seqs
    s = lax.axis_index("seq")
    own = HEADS // seqs
    wide = own * HEAD_DIM
    length = content.shape[1]
    preds = query_stream.shape[1]
    shard = qkv_weight.shape[0]

    vec = jnp.concatenate(
        [
            member.astype(F32)
            for member in (
                qv_bias,
                up_bias,
                out_bias,
                attn_gain,
                attn_shift,
                down_bias,
                ffn_gain,
                ffn_shift,
            )
        ]
    )
    vec = jnp.pad(vec, (0, 1024 - vec.shape[0])).reshape(8, 128)
    buckets = jnp.stack(
        [
            jnp.pad(rel_bucket, (0, 1), constant_values=BUCKETS),
            jnp.pad(rel_bucket, (1, 0), constant_values=BUCKETS),
        ]
    )
    w_parts = jnp.transpose(
        qkv_weight.reshape(shard, 3, seqs, wide), (2, 0, 1, 3)
    ).reshape(seqs, shard, 3 * wide)
    tops = (UP_TOP, DOWN_TOP)

    def send(pair, bits):
        return tuple(give_to(x, count, bit) for x, bit in zip(pair, bits))

    def heap(*pairs):
        return tuple(jnp.concatenate(x) for x in zip(*pairs))

    zs_low = (jnp.concatenate([up_weight, out_weight], axis=1)[None], down_weight[None])
    flying = send(zs_low, (16, 16))
    x_all, w_all, v_all, i_all = start_call(
        dps,
        seqs,
        content[0],
        query_stream[0],
        w_parts,
        vec,
        (segment_ids, order, pad_mask, predicted),
        SLOT_Q,
    )
    w_qkv = w_all.reshape(MODEL_WIDTH, 3 * wide)
    parts_all = v_all.reshape(count, 1024)
    n_qv, n_up, n_one = qv_bias.shape[0], up_bias.shape[0], out_bias.shape[0]
    cut_up, cut_end = n_qv + n_up, n_qv + n_up + 6 * n_one
    bias_qv = parts_all[:, :n_qv].reshape(count * n_qv)
    bias_up = parts_all[:, n_qv:cut_up].reshape(1, count * n_up)
    six = jnp.transpose(parts_all[:, cut_up:cut_end].reshape(count, 6, n_one), (1, 0, 2)).reshape(
        6, count * n_one
    )
    seg_all = i_all[:, 0].reshape(seqs * length)
    pad_all = i_all[:, 2].reshape(seqs * length)
    span = key_spans(seg_all, pad_all)

    bits = [tuple(2 * top[n] for top in tops) for n in range(2)]
    zs_low = heap(zs_low, tie(flying, i_all))
    flying = send(zs_low, (8, 8)), send(zs_low, bits[0])
    first = (s * own).astype(jnp.int32)[None]
    ints = tie(i_all, zs_low)
    tiles, qbias, kmeta, rseg, rlim, hot, shift = bias_call(
        own, ROWS_Q, SLOT_Q, first, buckets, rel_table, ints
    )

    bq = lax.dynamic_slice_in_dim(bias_qv[:MODEL_WIDTH], s * wide, wide)
    bv = lax.dynamic_slice_in_dim(bias_qv[MODEL_WIDTH:], s * wide, wide)
    zs_high, side_low = tie(flying, tiles)
    column = heap(zs_low, zs_high)
    side_high, far_low = send(zs_high, bits[0]), send(column, bits[1])
    x_all = tie(x_all, column)
    q_t, k3, k_t, v3, v_t = proj_call(
        own, seqs * length, x_all, w_qkv, bq[None], bv[None]
    )
    side_high = tie(side_high, q_t)
    side = heap(side_low, side_high)
    far_high = send(side, bits[1])
    close = heap(column, side)
    q_t = tie(q_t, side)

    ctx_t, ctx_rows, lse = fwd_call(span, q_t, k3, v_t, kmeta, rseg, rlim, tiles, qbias)

    far_low, far_high = tie((far_low, far_high), ctx_rows)
    far = heap(far_low, far_high)
    mates, far_mates = send(close, (1, 1)), send(far, (1, 1))
    ctx_rows = tie(ctx_rows, far)
    planes = sum(zip(close, far, mates, far_mates), ())

    def from_lanes(ref, t):
        return ref.at[:, pl.ds(pl.multiple_of(t * length, length), length)]

    def from_query(ref, t):
        return ref.at[pl.ds(pl.multiple_of(t * SLOT_Q, 16), SLOT_Q)]

    ctx_c, ctx_q = swap_call(
        seqs,
        ctx_t,
        ctx_rows,
        from_lanes,
        from_query,
        (wide, length),
        (SLOT_Q, wide),
        1,
        "swap_context",
    )
    (
        res_c,
        res_q,
        give_c,
        give_q,
        six_sums,
        up_sums,
        squares,
        out_c,
        out_q,
        keep,
        give,
    ) = mid_call(
        ctx_c,
        ctx_q,
        content[0],
        query_stream[0],
        content_cot[0],
        query_cot[0],
        pad_mask,
        six,
        bias_up,
        planes,
    )
    core = s % 2
    spot = (lax.axis_index(AXES) // 2) % 4
    flying = give_to(give, count, 1)

    def both(mine, got):
        total = mine.astype(F32) + got.astype(F32)
        return total.astype(BF16).reshape((2, 2, 4, mine.shape[0] // 16, mine.shape[1]))

    def total_of(kept, got):
        total = kept.astype(F32)
        for x in got:
            total += x.astype(F32)
        return total

    def split(x, bit):
        mine = (lax.axis_index(AXES) // bit) % 2
        axis = 0
        away = lax.dynamic_index_in_dim(x, 1 - mine, axis, keepdims=False).astype(BF16)
        return away, lax.dynamic_index_in_dim(x, mine, axis, keepdims=False)

    def block(x, index):
        return lax.dynamic_index_in_dim(x, index, 2, keepdims=False)

    def from_slot(ref, t):
        return ref.at[t]

    g_c, g_q = swap_call(
        seqs,
        give_c,
        give_q,
        from_slot,
        from_slot,
        (wide, length),
        (SLOT_Q, wide),
        2,
        "swap_grads",
    )
    flying = tie(flying, g_c)
    pairs = both(keep, flying)
    cut = pairs.shape[-1] - MODEL_WIDTH
    main, rest = pairs[..., :cut], pairs[..., cut:]
    rest_gone, rest_stay = split(rest, 16)
    gone = tuple(block(main, spot ^ r) for r in (1, 2, 3)) + (rest_gone,)
    flying = tuple(give_to(x, count, bit) for x, bit in zip(gone, (2, 4, 6, 16)))
    stay = (block(main, spot), rest_stay)
    g_c = tie(g_c, stay, gone)
    dq, dk, dv, offs, qoffs = bwd_call(
        span,
        q_t,
        k3,
        k_t,
        v3,
        ctx_t,
        g_c,
        g_q.reshape(seqs * SLOT_Q, wide),
        lse,
        kmeta,
        rseg,
        rlim,
        tiles,
        hot,
        shift,
        qbias,
    )
    flying = tie(flying, dq)

    main_gone, main_stay = split(total_of(stay[0], flying[:3]), 16)
    rest_gone, rest_stay = split(total_of(stay[1], flying[3:]), 8)
    gone, stay = (main_gone, rest_gone), (main_stay, rest_stay)
    flying = (give_to(main_gone, count, 16), give_to(rest_gone, count, 8))
    dq = tie(dq, stay, gone)
    grad_c, grad_q, grad_w, vec_grads, shared = grads_call(
        seqs,
        length,
        SLOT_Q,
        count,
        x_all,
        w_qkv,
        dq,
        dk,
        dv,
        offs,
        qoffs,
        buckets,
        six_sums,
        up_sums,
        squares,
    )
    sum_c, sum_q, sum_w, sum_v, sum_shared = end_call(
        dps,
        seqs,
        grad_c,
        grad_q,
        grad_w.reshape(dps, seqs, shard, 3 * wide),
        vec_grads.reshape(dps, seqs, 8, 128),
        shared,
    )
    flying, sum_c, sum_q, sum_w, sum_v, sum_shared = tie(
        (flying, sum_c, sum_q, sum_w, sum_v, sum_shared)
    )
    main_gone, main_stay = split(total_of(stay[0], flying[:1]), 8)
    rest = total_of(stay[1], flying[1:])
    near = [lax.dynamic_index_in_dim(rest, spot ^ r, 0, keepdims=False) for r in range(4)]
    flying = [give_to(main_gone, count, 8)]
    flying += [give_to(near[r].astype(BF16), count, 2 * r) for r in (1, 2, 3)]
    pair = jnp.concatenate(
        [total_of(main_stay, flying[:1]), total_of(near[0], flying[1:])], axis=1
    )
    half_ff, half = up_weight.shape[1] // 2, MODEL_WIDTH // 2
    wide_up = half_ff + half
    first, second = pair[:shard], pair[shard:]
    low_cols, high_cols = pair[:, wide_up : wide_up + half_ff // 2], pair[:, wide_up + half_ff // 2 :]

    def pick(a, b):
        return jnp.where(core == 0, a, b), jnp.where(core == 0, b, a)

    rows_mine, rows_away = pick(first[:, :wide_up], second[:, :wide_up])
    cols_mine, cols_away = pick(low_cols, high_cols)
    rows_got = give_to(rows_away, count, 1)
    cols_got = give_to(cols_away, count, 1)
    rows_low, rows_high = pick(rows_mine, rows_got)
    grad_up_own = jnp.concatenate([rows_low[:, :half_ff], rows_high[:, :half_ff]], axis=1)
    grad_out_own = jnp.concatenate([rows_low[:, half_ff:], rows_high[:, half_ff:]], axis=1)

    def unfold(x):
        return jnp.concatenate([x[:, :half], x[:, half:]], axis=0)

    cols_low, cols_high = pick(unfold(cols_mine), unfold(cols_got))
    grad_down_own = jnp.concatenate([cols_low, cols_high], axis=1)
    grad_content = res_c + sum_c
    grad_query = res_q[:preds] + sum_q[:preds]
    grad_qkv_own = jnp.transpose(sum_w.reshape(seqs, shard, 3, wide), (1, 2, 0, 3)).reshape(
        shard, 3 * MODEL_WIDTH
    )
    mine = [sum_v[7, :n_qv], sum_v[6, :n_up]] + [sum_v[i, :n_one] for i in range(6)]
    table_sum = sum_shared[:HEADS, :BUCKETS].T
    totals = sum_shared[16:23, 0]
    content_count = totals[6] * MODEL_WIDTH
    query_count = float(dps * preds * seqs * MODEL_WIDTH)
    each = jnp.stack([content_count, jnp.float32(query_count)])
    stats = jnp.sqrt(totals[:6] / jnp.concatenate([each, each, each]))
    return (
        out_c[None],
        out_q[None],
        grad_content[None],
        grad_query[None],
        grad_qkv_own,
        mine[0],
        grad_out_own,
        mine[2],
        mine[3],
        mine[4],
        grad_up_own,
        mine[1],
        grad_down_own,
        mine[5],
        mine[6],
        mine[7],
        table_sum,
        stats,
    )


def pick_local(mesh):
    sizes = dict(mesh.shape)
    return local_fast if (sizes["dp"], sizes["seq"]) == (8, 4) else local_general


def solution(mesh):
    in_specs = (
        P("dp", "seq", None),
        P("dp", "seq", None),
        P("dp", "seq"),
        P("dp", "seq"),
        P("dp", "seq"),
        P("dp", "seq"),
        P(),
        P(("dp", "seq"), None),
        P(("dp", "seq")),
        P(("dp", "seq"), None),
        P(("dp", "seq")),
        P(("dp", "seq")),
        P(("dp", "seq")),
        P(("dp", "seq"), None),
        P(("dp", "seq")),
        P(("dp", "seq"), None),
        P(("dp", "seq")),
        P(("dp", "seq")),
        P(("dp", "seq")),
        P(),
        P("dp", "seq", None),
        P("dp", "seq", None),
    )
    out_specs = (
        P("dp", "seq", None),
        P("dp", "seq", None),
        P("dp", "seq", None),
        P("dp", "seq", None),
        P(("dp", "seq"), None),
        P(("dp", "seq")),
        P(("dp", "seq"), None),
        P(("dp", "seq")),
        P(("dp", "seq")),
        P(("dp", "seq")),
        P(("dp", "seq"), None),
        P(("dp", "seq")),
        P(("dp", "seq"), None),
        P(("dp", "seq")),
        P(("dp", "seq")),
        P(("dp", "seq")),
        P(),
        P(),
    )
    local = pick_local(mesh)
    return jax.shard_map(local, mesh=mesh, in_specs=in_specs, out_specs=out_specs, check_vma=False)
```

```python
import functools
import math

import jax
import jax.numpy as jnp
from jax import lax
from jax.experimental import pallas as pl
from jax.experimental.pallas import tpu as pltpu
from jax.sharding import PartitionSpec as P

MODEL_WIDTH = 768
HEADS = 12
HEAD_DIM = 64
BUCKETS = 32
SEQ_LEN = 2048


EPS = 1e-05
NEG = -1000000000.0
SCALE = 0.125


def exact_gelu(values):
    return jax.nn.gelu(values, approximate=False)


def norm_fwd(residual, gain_vec, shift_vec):
    row_mean = jnp.mean(residual, axis=-1, keepdims=True)
    centered = residual - row_mean
    inv_std = lax.rsqrt(jnp.mean(centered * centered, axis=-1, keepdims=True) + EPS)
    normed = centered * inv_std
    return (normed * gain_vec + shift_vec, normed, inv_std)


def norm_back(upstream, normed, inv_std, gain_vec):
    grad_norm = upstream * gain_vec
    projected = jnp.mean(grad_norm, axis=-1, keepdims=True) + normed * jnp.mean(
        grad_norm * normed, axis=-1, keepdims=True
    )
    return (
        inv_std * (grad_norm - projected),
        jnp.sum(upstream * normed, axis=(0, 1)),
        jnp.sum(upstream, axis=(0, 1)),
    )


def bucket_edges(rel_bucket):
    entry_count = rel_bucket.shape[0]
    matches = rel_bucket[None, :] == jnp.arange(BUCKETS, dtype=jnp.int32)[:, None]
    places = jnp.arange(entry_count, dtype=jnp.int32)[None, :]
    starts = jnp.min(jnp.where(matches, places, entry_count), axis=1)
    counts = jnp.sum(matches.astype(jnp.int32), axis=1)
    return (starts, starts + counts)


def build_mask(
    query_pos, query_seg, query_limit, content_row, key_pos, key_seg, key_order, key_pad
):
    inside = (
        (query_seg[:, None] == key_seg[None, :])
        & (key_pad[None, :] == 1)
        & (key_order[None, :] <= query_limit[:, None])
    )
    itself = (key_pos[None, :] == query_pos[:, None]) & content_row[:, None]
    return (inside | itself, key_pos[None, :] - query_pos[:, None] + (SEQ_LEN - 1))


def masked_scores(query_heads, key_heads, table_low, edges, allowed, offsets):
    raw_scores = (
        jnp.einsum("rhd,lhd->hrl", query_heads, key_heads, preferred_element_type=jnp.float32)
        * SCALE
    )
    starts, ends = edges
    spread = offsets[..., None]
    onehot = ((spread >= starts) & (spread < ends)).astype(jnp.bfloat16)
    bias = jnp.einsum("rlb,bh->hrl", onehot, table_low, preferred_element_type=jnp.float32)
    return (jnp.where(allowed[None], raw_scores + bias, NEG), onehot)


def attend_forward(packed, table_low, edges, content_row):
    queries, key_values, key_seg, key_order, key_pad, query_pos, query_seg, query_limit = packed
    row_count = queries.shape[0]
    length = key_values.shape[0]
    key_pos = jnp.arange(length, dtype=jnp.int32)
    allowed, offsets = build_mask(
        query_pos, query_seg, query_limit, content_row, key_pos, key_seg, key_order, key_pad
    )
    query_heads = queries.reshape(row_count, HEADS, HEAD_DIM)
    key_heads = key_values[:, :MODEL_WIDTH].reshape(length, HEADS, HEAD_DIM)
    value_heads = key_values[:, MODEL_WIDTH:].reshape(length, HEADS, HEAD_DIM)
    scores, onehot = masked_scores(query_heads, key_heads, table_low, edges, allowed, offsets)
    row_max = jnp.max(scores, axis=-1, keepdims=True)
    expo_vals = jnp.exp(scores - row_max)
    row_total = jnp.sum(expo_vals, axis=-1, keepdims=True)
    probs_low = (expo_vals / row_total).astype(jnp.bfloat16)
    context = jnp.einsum("hrl,lhd->rhd", probs_low, value_heads, preferred_element_type=jnp.float32)
    return (
        context.reshape(row_count, MODEL_WIDTH),
        jnp.transpose((row_max + jnp.log(row_total))[..., 0]),
    )


def attend_backward(packed, table_low, edges, content_row):
    (
        queries,
        key_values,
        key_seg,
        key_order,
        key_pad,
        query_pos,
        query_seg,
        query_limit,
        row_lse,
        grad_context,
    ) = packed
    row_count = queries.shape[0]
    length = key_values.shape[0]
    key_pos = jnp.arange(length, dtype=jnp.int32)
    allowed, offsets = build_mask(
        query_pos, query_seg, query_limit, content_row, key_pos, key_seg, key_order, key_pad
    )
    query_heads = queries.reshape(row_count, HEADS, HEAD_DIM)
    key_heads = key_values[:, :MODEL_WIDTH].reshape(length, HEADS, HEAD_DIM)
    value_heads = key_values[:, MODEL_WIDTH:].reshape(length, HEADS, HEAD_DIM)
    scores, onehot = masked_scores(query_heads, key_heads, table_low, edges, allowed, offsets)
    probs = jnp.exp(scores - jnp.transpose(row_lse)[..., None])
    grad_heads = grad_context.reshape(row_count, HEADS, HEAD_DIM)
    grad_probs = jnp.einsum(
        "rhd,lhd->hrl", grad_heads, value_heads, preferred_element_type=jnp.float32
    )
    row_delta = jnp.sum(probs * grad_probs, axis=-1)
    grad_scores = (probs * (grad_probs - row_delta[..., None])).astype(jnp.bfloat16)
    grad_query = (
        jnp.einsum("hrl,lhd->rhd", grad_scores, key_heads, preferred_element_type=jnp.float32)
        * SCALE
    )
    grad_table = jnp.einsum("hrl,rlb->bh", grad_scores, onehot, preferred_element_type=jnp.float32)
    results = (grad_query.reshape(row_count, MODEL_WIDTH), grad_table, jnp.transpose(row_delta))
    probs_low = probs.astype(jnp.bfloat16)
    grad_key = (
        jnp.einsum("hrl,rhd->lhd", grad_scores, query_heads, preferred_element_type=jnp.float32)
        * SCALE
    )
    grad_value = jnp.einsum(
        "hrl,rhd->lhd", probs_low, grad_heads, preferred_element_type=jnp.float32
    )
    results = results + (
        jnp.concatenate(
            [grad_key.reshape(length, MODEL_WIDTH), grad_value.reshape(length, MODEL_WIDTH)],
            axis=-1,
        ),
    )
    return results


def local_general(
    content,
    query_stream,
    segment_ids,
    pad_mask,
    predicted,
    order,
    rel_bucket,
    qkv_weight,
    qv_bias,
    out_weight,
    out_bias,
    attn_gain,
    attn_shift,
    up_weight,
    up_bias,
    down_weight,
    down_bias,
    ffn_gain,
    ffn_shift,
    rel_table,
    content_cot,
    query_cot,
):
    seq_count = content.shape[0]
    shard_length = content.shape[1]
    pred_count = query_stream.shape[1]
    row_count = shard_length + pred_count
    group_size = lax.axis_size("seq")
    edges = bucket_edges(rel_bucket)
    shards = (
        lax.all_gather(qkv_weight, ("dp", "seq"), axis=0, tiled=True),
        lax.all_gather(out_weight, ("dp", "seq"), axis=0, tiled=True),
        lax.all_gather(up_weight, ("dp", "seq"), axis=0, tiled=True),
        lax.all_gather(down_weight, ("dp", "seq"), axis=0, tiled=True),
        lax.all_gather(qv_bias, ("dp", "seq"), axis=0, tiled=True),
        lax.all_gather(out_bias, ("dp", "seq"), axis=0, tiled=True),
        lax.all_gather(attn_gain, ("dp", "seq"), axis=0, tiled=True),
        lax.all_gather(attn_shift, ("dp", "seq"), axis=0, tiled=True),
        lax.all_gather(up_bias, ("dp", "seq"), axis=0, tiled=True),
        lax.all_gather(down_bias, ("dp", "seq"), axis=0, tiled=True),
        lax.all_gather(ffn_gain, ("dp", "seq"), axis=0, tiled=True),
        lax.all_gather(ffn_shift, ("dp", "seq"), axis=0, tiled=True),
    )
    query_key_value_weight, w_out, w_up, w_down = (shards[0], shards[1], shards[2], shards[3])
    bias_qv, bias_out, first_norm_gain, shift_one, bias_up, bias_down, gain_two, shift_two = [
        member.astype(jnp.float32) for member in shards[4:]
    ]
    all_rows = jnp.concatenate([content, query_stream], axis=1)
    reduced_precision_rows = all_rows.astype(jnp.bfloat16)
    queries = (
        jnp.einsum(
            "srd,de->sre",
            reduced_precision_rows,
            query_key_value_weight[:, :MODEL_WIDTH],
            preferred_element_type=jnp.float32,
        )
        + bias_qv[:MODEL_WIDTH]
    ).astype(jnp.bfloat16)
    value_shift = jnp.concatenate([jnp.zeros((MODEL_WIDTH,), jnp.float32), bias_qv[MODEL_WIDTH:]])
    key_values = (
        jnp.einsum(
            "zci,ip->zcp",
            reduced_precision_rows[:, :shard_length],
            query_key_value_weight[:, MODEL_WIDTH:],
            preferred_element_type=jnp.float32,
        )
        + value_shift
    ).astype(jnp.bfloat16)
    full_pairs, full_seg, full_order, full_pad = (
        lax.all_gather(key_values, "seq", axis=1, tiled=True),
        lax.all_gather(segment_ids, "seq", axis=1, tiled=True),
        lax.all_gather(order, "seq", axis=1, tiled=True),
        lax.all_gather(pad_mask, "seq", axis=1, tiled=True),
    )
    content_pos = lax.axis_index("seq") * shard_length + jnp.arange(shard_length, dtype=jnp.int32)
    query_pos = jnp.concatenate(
        [jnp.broadcast_to(content_pos[None, :], (seq_count, shard_length)), predicted], axis=1
    )
    query_seg = jnp.concatenate(
        [segment_ids, jnp.take_along_axis(full_seg, predicted, axis=1)], axis=1
    )
    query_limit = jnp.concatenate(
        [order, jnp.take_along_axis(full_order, predicted, axis=1) - 1], axis=1
    )
    content_row = jnp.arange(row_count, dtype=jnp.int32) < shard_length
    row_meta = (full_seg, full_order, full_pad, query_pos, query_seg, query_limit)

    def forward_one(packed):
        return attend_forward(packed, rel_table, edges, content_row)

    context, row_lse = lax.map(forward_one, (queries, full_pairs) + row_meta)
    context_low = context.astype(jnp.bfloat16)
    attn_out = (
        jnp.einsum("sre,ed->srd", context_low, w_out, preferred_element_type=jnp.float32) + bias_out
    )
    hidden_one, normed_one, inv_one = norm_fwd(all_rows + attn_out, first_norm_gain, shift_one)
    hidden_low = hidden_one.astype(jnp.bfloat16)
    pre_act = (
        jnp.einsum("srd,df->srf", hidden_low, w_up, preferred_element_type=jnp.float32) + bias_up
    )
    activ, gelu_pull = jax.vjp(exact_gelu, pre_act)
    activ_low = activ.astype(jnp.bfloat16)
    ffn_out = (
        jnp.einsum("srf,fd->srd", activ_low, w_down, preferred_element_type=jnp.float32) + bias_down
    )
    hidden_two, normed_two, inv_two = norm_fwd(hidden_one + ffn_out, gain_two, shift_two)
    pad_float = pad_mask.astype(jnp.float32)
    row_valid = jnp.concatenate(
        [pad_float, jnp.ones((seq_count, pred_count), jnp.float32)], axis=1
    )[..., None]
    outputs = hidden_two * row_valid
    pad_weight = pad_float[..., None]
    local_sums = jnp.stack(
        [
            jnp.sum(pad_weight * content * content),
            jnp.sum(query_stream * query_stream),
            jnp.sum(pad_weight * attn_out[:, :shard_length] * attn_out[:, :shard_length]),
            jnp.sum(attn_out[:, shard_length:] * attn_out[:, shard_length:]),
            jnp.sum(pad_weight * ffn_out[:, :shard_length] * ffn_out[:, :shard_length]),
            jnp.sum(ffn_out[:, shard_length:] * ffn_out[:, shard_length:]),
            jnp.sum(pad_float),
        ]
    )
    back_weights = (
        lax.all_gather(qkv_weight, ("dp", "seq"), axis=0, tiled=True),
        lax.all_gather(out_weight, ("dp", "seq"), axis=0, tiled=True),
        lax.all_gather(up_weight, ("dp", "seq"), axis=0, tiled=True),
        lax.all_gather(down_weight, ("dp", "seq"), axis=0, tiled=True),
        lax.all_gather(attn_gain, ("dp", "seq"), axis=0, tiled=True),
        lax.all_gather(ffn_gain, ("dp", "seq"), axis=0, tiled=True),
    )
    back_pairs = lax.all_gather(key_values, "seq", axis=1, tiled=True)
    backward_query_key_value, back_out, back_up, back_down = (
        back_weights[0],
        back_weights[1],
        back_weights[2],
        back_weights[3],
    )
    back_gain_one = back_weights[4].astype(jnp.float32)
    back_gain_two = back_weights[5].astype(jnp.float32)
    upstream = jnp.concatenate([content_cot, query_cot], axis=1) * row_valid
    grad_res_two, grad_gain_two, grad_shift_two = norm_back(
        upstream, normed_two, inv_two, back_gain_two
    )
    grad_ffn = grad_res_two.astype(jnp.bfloat16)
    grad_bias_down = jnp.sum(grad_ffn, axis=(0, 1), dtype=jnp.float32)
    grad_down = jnp.einsum("srf,srd->fd", activ_low, grad_ffn, preferred_element_type=jnp.float32)
    grad_activ = jnp.einsum("srd,fd->srf", grad_ffn, back_down, preferred_element_type=jnp.float32)
    grad_pre = gelu_pull(grad_activ)[0].astype(jnp.bfloat16)
    grad_bias_up = jnp.sum(grad_pre, axis=(0, 1), dtype=jnp.float32)
    grad_up = jnp.einsum("srd,srf->df", hidden_low, grad_pre, preferred_element_type=jnp.float32)
    grad_hidden = grad_res_two + jnp.einsum(
        "srf,df->srd", grad_pre, back_up, preferred_element_type=jnp.float32
    )
    grad_res_one, grad_gain_one, grad_shift_one = norm_back(
        grad_hidden, normed_one, inv_one, back_gain_one
    )
    grad_attn = grad_res_one.astype(jnp.bfloat16)
    grad_bias_out = jnp.sum(grad_attn, axis=(0, 1), dtype=jnp.float32)
    grad_out = jnp.einsum("sre,srd->ed", context_low, grad_attn, preferred_element_type=jnp.float32)
    grad_context = jnp.einsum(
        "srd,ed->sre", grad_attn, back_out, preferred_element_type=jnp.float32
    ).astype(jnp.bfloat16)

    def backward_all(packed):
        return attend_backward(packed, rel_table, edges, content_row)

    grad_queries, grad_tables, per_row_delta, grad_pairs = lax.map(
        backward_all, (queries, back_pairs) + row_meta + (row_lse, grad_context)
    )
    paired_gradients = lax.psum_scatter(
        grad_pairs.astype(jnp.bfloat16), "seq", scatter_dimension=1, tiled=True
    )
    query_grads = grad_queries.astype(jnp.bfloat16)
    grad_bias_qv = jnp.concatenate(
        [
            jnp.sum(query_grads, axis=(0, 1), dtype=jnp.float32),
            jnp.sum(paired_gradients[..., MODEL_WIDTH:], axis=(0, 1), dtype=jnp.float32),
        ]
    )
    grad_qkv = jnp.concatenate(
        [
            jnp.einsum(
                "srd,sre->de",
                reduced_precision_rows,
                query_grads,
                preferred_element_type=jnp.float32,
            ),
            jnp.einsum(
                "cvi,cvp->ip",
                reduced_precision_rows[:, :shard_length],
                paired_gradients,
                preferred_element_type=jnp.float32,
            ),
        ],
        axis=1,
    )
    grad_rows = grad_res_one + jnp.einsum(
        "sre,de->srd",
        query_grads,
        backward_query_key_value[:, :MODEL_WIDTH],
        preferred_element_type=jnp.float32,
    )
    grad_content = grad_rows[:, :shard_length] + jnp.einsum(
        "zwv,bv->zwb",
        paired_gradients,
        backward_query_key_value[:, MODEL_WIDTH:],
        preferred_element_type=jnp.float32,
    )
    grad_query = grad_rows[:, shard_length:]
    owned = (
        lax.psum_scatter(grad_qkv, ("dp", "seq"), scatter_dimension=0, tiled=True),
        lax.psum_scatter(grad_out, ("dp", "seq"), scatter_dimension=0, tiled=True),
        lax.psum_scatter(grad_up, ("dp", "seq"), scatter_dimension=0, tiled=True),
        lax.psum_scatter(grad_down, ("dp", "seq"), scatter_dimension=0, tiled=True),
        lax.psum_scatter(grad_bias_qv, ("dp", "seq"), scatter_dimension=0, tiled=True),
        lax.psum_scatter(grad_bias_out, ("dp", "seq"), scatter_dimension=0, tiled=True),
        lax.psum_scatter(grad_gain_one, ("dp", "seq"), scatter_dimension=0, tiled=True),
        lax.psum_scatter(grad_shift_one, ("dp", "seq"), scatter_dimension=0, tiled=True),
        lax.psum_scatter(grad_bias_up, ("dp", "seq"), scatter_dimension=0, tiled=True),
        lax.psum_scatter(grad_bias_down, ("dp", "seq"), scatter_dimension=0, tiled=True),
        lax.psum_scatter(grad_gain_two, ("dp", "seq"), scatter_dimension=0, tiled=True),
        lax.psum_scatter(grad_shift_two, ("dp", "seq"), scatter_dimension=0, tiled=True),
    )
    table_sum, totals = lax.psum((jnp.sum(grad_tables, axis=0), local_sums), ("dp", "seq"))
    content_count = totals[6] * MODEL_WIDTH
    query_count = float(seq_count * lax.axis_size("dp") * pred_count * group_size * MODEL_WIDTH)
    stats = jnp.sqrt(
        jnp.stack(
            [
                totals[0] / content_count,
                totals[1] / query_count,
                totals[2] / content_count,
                totals[3] / query_count,
                totals[4] / content_count,
                totals[5] / query_count,
            ]
        )
    )
    return (
        outputs[:, :shard_length],
        outputs[:, shard_length:],
        grad_content,
        grad_query,
        owned[0],
        owned[4],
        owned[1],
        owned[5],
        owned[6],
        owned[7],
        owned[2],
        owned[8],
        owned[3],
        owned[9],
        owned[10],
        owned[11],
        table_sum,
        stats,
    )


LOG2E = math.log2(math.e)
TILE = 256
KEYS = 512
HALF = 128
REACH = 11
DIAGS = 2 * REACH + 1
FAR = 7
WIDE = SEQ_LEN + HALF
MASKED = -1e30
F32 = jnp.float32
BF16 = jnp.bfloat16


def dot_nn(a, b):
    return jnp.dot(a, b, preferred_element_type=F32)


def dot_nt(a, b):
    return lax.dot_general(a, b, (((1,), (1,)), ((), ())), preferred_element_type=F32)


def dot_tn(a, b):
    return lax.dot_general(a, b, (((0,), (0,)), ((), ())), preferred_element_type=F32)


def cost_of(micros):
    return pl.CostEstimate(
        flops=int(micros * 1.0e9), bytes_accessed=int(micros * 1.0e6), transcendentals=0
    )


def bias_kernel(
    rows_q,
    own,
    slot_q,
    heads_ref,
    bucket_ref,
    table_ref,
    ints_ref,
    tile_out,
    qbias_out,
    kmeta_ref,
    rseg_ref,
    rlim_ref,
    hot_ref,
    shift_ref,
    vec_scr,
    ahead_scr,
    fold_scr,
    tile_scr,
    qbias_scr,
    sems,
):
    seqs, length = ints_ref.shape[0], ints_ref.shape[2]
    first = heads_ref[0]
    hot = (
        lax.broadcasted_iota(jnp.int32, (BUCKETS, 2 * SEQ_LEN), 0) == bucket_ref[0:1, :]
    ).astype(BF16)
    vec_scr[...] = dot_tn(table_ref[...], hot)
    hot = (
        lax.broadcasted_iota(jnp.int32, (BUCKETS, 2 * SEQ_LEN), 0) == bucket_ref[1:2, :]
    ).astype(BF16)
    ahead_scr[...] = dot_tn(table_ref[...], hot) * LOG2E
    copies = []
    for h in range(own):
        row = ahead_scr[pl.ds(first + h, 1), :]
        for e in range(REACH - FAR):
            tile_scr[h, e] = jnp.zeros((HALF, HALF), F32)
            tile_scr[h, DIAGS - 1 - e] = jnp.zeros((HALF, HALF), F32)
        for e in range(-FAR, FAR + 1):
            start = HALF * (15 + e)
            skew = pltpu.roll(
                jnp.broadcast_to(row[:, start : start + 2 * HALF], (HALF, 2 * HALF)),
                0,
                1,
                stride=1,
                stride_axis=0,
            )
            tile_scr[h, e + REACH] = skew[:, HALF:].T
        copies.append(pltpu.make_async_copy(tile_scr.at[h], tile_out.at[h], sems.at[h]))
        copies[-1].start()
        vec = vec_scr[pl.ds(first + h, 1), :]
        fold_scr[h] = jnp.concatenate(
            [vec[:, HALF * i : HALF * i + WIDE] for i in range(16)], axis=0
        ).astype(BF16)

    place = lax.broadcasted_iota(jnp.int32, (1, length), 1)
    lane = lax.broadcasted_iota(jnp.int32, (HALF, HALF), 1)
    segs, orders = [], []
    for t in range(seqs):
        seg = ints_ref[t, 0:1, :]
        seg = jnp.where(ints_ref[t, 2:3, :] == 1, seg, -2 - t * length - place)
        order = ints_ref[t, 1:2, :]
        rseg_ref[:, t * length : (t + 1) * length] = seg
        rlim_ref[:, t * length : (t + 1) * length] = order
        for n, row in ((0, seg.astype(F32)), (1, order.astype(F32))):
            for i in range(length // HALF):
                part = row[:, i * HALF : (i + 1) * HALF]
                (segs, orders)[n].append(part)
                kmeta_ref[n, t * length + i * HALF : t * length + (i + 1) * HALF, :] = (
                    jnp.broadcast_to(part, (HALF, HALF)).T.astype(jnp.int32)
                )
    segs = jnp.concatenate(segs, axis=0)
    orders = jnp.concatenate(orders, axis=0)
    preds = [ints_ref[t, 3:4, :slot_q].astype(F32) for t in range(seqs)]
    preds.append(jnp.full((1, rows_q - seqs * slot_q), -1.0, F32))
    preds = jnp.concatenate(preds, axis=1)
    high = lax.Precision.HIGHEST
    for t in range(rows_q // HALF):
        at = slice(t * HALF, (t + 1) * HALF)
        spots = jnp.broadcast_to(preds[:, at], (HALF, HALF)).T.astype(jnp.int32)
        group = jnp.right_shift(spots, 7)
        inside = jnp.bitwise_and(spots, HALF - 1)
        pick = (lane == group)[:, :16].astype(F32)
        for rows, ref, less in ((segs, rseg_ref, 0.0), (orders, rlim_ref, 1.0)):
            spread = jnp.dot(pick, rows, precision=high, preferred_element_type=F32)
            found = jnp.take_along_axis(spread, inside, axis=1) - less
            ref[:, length * seqs + t * HALF : length * seqs + (t + 1) * HALF] = found.T[
                0:1, :
            ].astype(jnp.int32)
        hot_ref[at, :] = (lane == 15 - group)[:, :16].astype(BF16)
        shift_ref[at, :] = HALF - 1 - inside

    for h in range(own):
        for t in range(rows_q // HALF):
            at = slice(t * HALF, (t + 1) * HALF)
            turn = lane + shift_ref[at, :]
            wrap = turn >= HALF
            idx = jnp.where(wrap, turn - HALF, turn)
            spread = dot_nn(hot_ref[at, :], fold_scr[h])
            prev = jnp.take_along_axis(spread[:, :HALF], idx, axis=1)
            for j in range(SEQ_LEN // HALF):
                cur = jnp.take_along_axis(
                    spread[:, (j + 1) * HALF : (j + 2) * HALF], idx, axis=1
                )
                out = jnp.where(wrap, cur, prev) * LOG2E
                qbias_scr[h, j * HALF : (j + 1) * HALF, at] = out.T
                prev = cur
        copies.append(pltpu.make_async_copy(qbias_scr.at[h], qbias_out.at[h], sems.at[own + h]))
        copies[-1].start()
    for copy in copies:
        copy.wait()


def bias_call(own, rows_q, slot_q, first, buckets, table, ints):
    vm = pl.BlockSpec(memory_space=pltpu.VMEM)
    tiles = jax.ShapeDtypeStruct((own, DIAGS, HALF, HALF), F32)
    qbias = jax.ShapeDtypeStruct((own, SEQ_LEN, rows_q), F32)
    rows = jax.ShapeDtypeStruct((1, SEQ_LEN + rows_q), jnp.int32)
    return pl.pallas_call(
        functools.partial(bias_kernel, rows_q, own, slot_q),
        out_shape=(
            tiles,
            qbias,
            jax.ShapeDtypeStruct((2, SEQ_LEN, HALF), jnp.int32),
            rows,
            rows,
            jax.ShapeDtypeStruct((rows_q, 16), BF16),
            jax.ShapeDtypeStruct((rows_q, HALF), jnp.int32),
        ),
        in_specs=[pl.BlockSpec(memory_space=pltpu.SMEM)] + [vm] * 3,
        out_specs=(pl.BlockSpec(memory_space=pltpu.HBM),) * 2 + (vm,) * 5,
        scratch_shapes=[
            pltpu.VMEM((table.shape[1], 2 * SEQ_LEN), F32),
            pltpu.VMEM((table.shape[1], 2 * SEQ_LEN), F32),
            pltpu.VMEM((own, 16, WIDE), BF16),
            pltpu.VMEM(tiles.shape, F32),
            pltpu.VMEM(qbias.shape, F32),
            pltpu.SemaphoreType.DMA((2 * own,)),
        ],
        compiler_params=pltpu.CompilerParams(vmem_limit_bytes=58 << 20),
        cost_estimate=cost_of(12),
        name="bias_tiles",
    )(first, buckets, table, ints)


def bias_block(tile_ref, h, e):
    return jnp.concatenate(
        [
            jnp.concatenate([tile_ref[h, e + i], tile_ref[h, e + i - 1]], axis=1)
            for i in range(KEYS // HALF)
        ],
        axis=0,
    )


def mask_block(kmeta_ref, rseg_ref, rlim_ref, krow, rcol, width):
    kseg = kmeta_ref[0, pl.ds(krow, KEYS), :]
    kord = kmeta_ref[1, pl.ds(krow, KEYS), :]
    parts = []
    for w in range(width // HALF):
        rseg = rseg_ref[:, pl.ds(rcol + w * HALF, HALF)]
        rlim = rlim_ref[:, pl.ds(rcol + w * HALF, HALF)]
        ok = (kseg == rseg) & (kord <= rlim)
        parts.append(jnp.where(ok, 0.0, MASKED))
    return parts[0] if len(parts) == 1 else jnp.concatenate(parts, axis=1)


def fwd_kernel(
    own,
    rows_q,
    span_ref,
    qt_ref,
    k_ref,
    vt_ref,
    kmeta_ref,
    rseg_ref,
    rlim_ref,
    tile_ref,
    qbias_ref,
    ctx_ref,
    rows_ref,
    lse_ref,
    s_scr,
    qbias_scr,
    qbias_sem,
):
    late = pltpu.make_async_copy(qbias_ref, qbias_scr, qbias_sem.at[0])
    late.start()

    def run(rcol, width, lo, steps, bias_of):
        heads = range(own)

        def fold(op, x):
            rows = [x[i * 8 : (i + 1) * 8] for i in range(x.shape[0] // 8)]
            while len(rows) > 1:
                rows = [op(rows[i], rows[i + 1]) for i in range(0, len(rows), 2)]
            return rows[0]

        def score(step, tops):
            kt = lo + step * (KEYS // TILE)
            krow = pl.multiple_of(kt * TILE, TILE)
            mask = mask_block(kmeta_ref, rseg_ref, rlim_ref, krow, rcol, width)
            new = []
            for h in heads:
                s = jnp.dot(
                    k_ref[h, pl.ds(krow, KEYS), :],
                    qt_ref[h * HEAD_DIM : (h + 1) * HEAD_DIM, pl.ds(rcol, width)],
                    preferred_element_type=F32,
                )
                s = s * (SCALE * LOG2E) + (bias_of(h, kt) + mask)
                s_scr[h, pl.ds(krow, KEYS), :width] = s
                new.append(jnp.maximum(tops[h], fold(jnp.maximum, s)))
            return tuple(new)

        tops = lax.fori_loop(
            0, steps, score, tuple(jnp.full((8, width), MASKED, F32) for _ in heads)
        )
        tops = [jnp.max(t, axis=0, keepdims=True) for t in tops]

        def weigh(step, carry):
            kt = lo + step * (KEYS // TILE)
            krow = pl.multiple_of(kt * TILE, TILE)
            sums, accs = carry
            new_sums, new_accs = [], []
            for h in heads:
                p = jnp.exp2(s_scr[h, pl.ds(krow, KEYS), :width] - tops[h])
                new_sums.append(sums[h] + fold(jnp.add, p))
                new_accs.append(
                    accs[h]
                    + jnp.dot(
                        vt_ref[h * HEAD_DIM : (h + 1) * HEAD_DIM, pl.ds(krow, KEYS)],
                        p.astype(BF16),
                        preferred_element_type=F32,
                    )
                )
            return tuple(new_sums), tuple(new_accs)

        sums, accs = lax.fori_loop(
            0,
            steps,
            weigh,
            (
                tuple(jnp.zeros((8, width), F32) for _ in heads),
                tuple(jnp.zeros((HEAD_DIM, width), F32) for _ in heads),
            ),
        )
        outs = []
        for h in heads:
            total = jnp.sum(sums[h], axis=0, keepdims=True)
            outs.append(accs[h] / total)
            lse_ref[h : h + 1, pl.ds(rcol, width)] = tops[h] + jnp.log2(total)
        out = jnp.concatenate(outs, axis=0)
        ctx_ref[:, pl.ds(rcol, width)] = out.astype(BF16)
        return out

    def content_tile(qt, carry):
        def bias_of(h, kt):
            return bias_block(tile_ref, h, 2 * (kt - qt) + REACH)

        run(pl.multiple_of(qt * TILE, TILE), TILE, span_ref[0, qt], span_ref[1, qt], bias_of)
        return carry

    lax.fori_loop(0, SEQ_LEN // TILE, content_tile, 0)

    def query_bias(h, kt):
        return qbias_scr[h, pl.ds(pl.multiple_of(kt * TILE, TILE), KEYS), :]

    late.wait()
    last = SEQ_LEN // TILE
    out = run(SEQ_LEN, rows_q, span_ref[0, last], span_ref[1, last], query_bias)
    rows_ref[...] = out.T.astype(BF16)


def fwd_call(span, qt, k3, vt, kmeta, rseg, rlim, tiles, qbias):
    own = k3.shape[0]
    rows = qt.shape[1]
    rows_q = rows - SEQ_LEN
    vm = pl.BlockSpec(memory_space=pltpu.VMEM)
    return pl.pallas_call(
        functools.partial(fwd_kernel, own, rows_q),
        out_shape=(
            jax.ShapeDtypeStruct((own * HEAD_DIM, rows), BF16),
            jax.ShapeDtypeStruct((rows_q, own * HEAD_DIM), BF16),
            jax.ShapeDtypeStruct((own, rows), F32),
        ),
        in_specs=[pl.BlockSpec(memory_space=pltpu.SMEM)]
        + [vm] * 7
        + [pl.BlockSpec(memory_space=pltpu.HBM)],
        scratch_shapes=[
            pltpu.VMEM((own, SEQ_LEN, max(rows_q, TILE)), F32),
            pltpu.VMEM(qbias.shape, F32),
            pltpu.SemaphoreType.DMA((1,)),
        ],
        compiler_params=pltpu.CompilerParams(vmem_limit_bytes=46 << 20),
        cost_estimate=cost_of(32),
        name="attend",
    )(span, qt, k3, vt, kmeta, rseg, rlim, tiles, qbias)


def bwd_kernel(
    own,
    rows_q,
    span_ref,
    qt_ref,
    k_ref,
    kt_ref,
    v_ref,
    ctx_ref,
    gc_ref,
    gq_ref,
    lse_ref,
    kmeta_ref,
    rseg_ref,
    rlim_ref,
    tile_ref,
    hot_ref,
    shift_ref,
    qbias_ref,
    dq_ref,
    dk_ref,
    dv_ref,
    offs_ref,
    qoffs_ref,
    dk_scr,
    dv_scr,
    dq_scr,
    diag_scr,
    ds_scr,
    delta_scr,
    gt_ref,
    qbias_scr,
    qbias_sem,
):
    late = pltpu.make_async_copy(qbias_ref, qbias_scr, qbias_sem.at[0])
    late.start()
    seqs, length = gc_ref.shape[0], gc_ref.shape[2]
    for t in range(seqs):
        for a in range(0, length, TILE):
            block = gc_ref[t, :, a : a + TILE]
            gt_ref[:, t * length + a : t * length + a + TILE] = block
    used = gq_ref.shape[0]
    block = jnp.concatenate(
        [gq_ref[...].astype(F32), jnp.zeros((rows_q - used, gq_ref.shape[1]), F32)], axis=0
    )
    gt_ref[:, SEQ_LEN:] = block.T.astype(BF16)
    dk_scr[...] = jnp.zeros(dk_scr.shape, F32)
    dv_scr[...] = jnp.zeros(dv_scr.shape, F32)
    diag_scr[...] = jnp.zeros(diag_scr.shape, F32)
    ds_scr[...] = jnp.zeros(ds_scr.shape, BF16)
    for h in range(own):
        part = slice(h * HEAD_DIM, (h + 1) * HEAD_DIM)
        delta_scr[h : h + 1, :] = jnp.sum(
            ctx_ref[part, :].astype(F32) * gt_ref[part, :].astype(F32), axis=0, keepdims=True
        )

    def run(rcol, width, lo, steps, bias_of, keep):
        dq_scr[...] = jnp.zeros(dq_scr.shape, F32)

        def body(step, carry):
            kt = lo + step * (KEYS // TILE)
            krow = pl.multiple_of(kt * TILE, TILE)
            mask = mask_block(kmeta_ref, rseg_ref, rlim_ref, krow, rcol, width)
            for h in range(own):
                part = slice(h * HEAD_DIM, (h + 1) * HEAD_DIM)
                s = jnp.dot(
                    k_ref[h, pl.ds(krow, KEYS), :],
                    qt_ref[part, pl.ds(rcol, width)],
                    preferred_element_type=F32,
                )
                s = s * (SCALE * LOG2E) + (bias_of(h, kt) + mask)
                p = jnp.exp2(s - lse_ref[h : h + 1, pl.ds(rcol, width)])
                gp = jnp.dot(
                    v_ref[h, pl.ds(krow, KEYS), :],
                    gt_ref[part, pl.ds(rcol, width)],
                    preferred_element_type=F32,
                )
                ds = p * (gp - delta_scr[h : h + 1, pl.ds(rcol, width)])
                low = ds.astype(BF16)
                keep(h, kt, ds, low)
                dv_scr[part, pl.ds(krow, KEYS)] += dot_nt(
                    gt_ref[part, pl.ds(rcol, width)], p.astype(BF16)
                )
                dk_scr[part, pl.ds(krow, KEYS)] += dot_nt(qt_ref[part, pl.ds(rcol, width)], low)
                dq_scr[h, :, :width] += jnp.dot(
                    kt_ref[part, pl.ds(krow, KEYS)], low, preferred_element_type=F32
                )
            return carry

        lax.fori_loop(0, steps, body, 0)
        grad = jnp.concatenate([dq_scr[h, :, :width] for h in range(own)], axis=0)
        dq_ref[pl.ds(rcol, width), :] = (grad * SCALE).T.astype(BF16)

    def content_tile(qt, carry):
        def bias_of(h, kt):
            return bias_block(tile_ref, h, 2 * (kt - qt) + REACH)

        def keep(h, kt, ds, low):
            e = 2 * (kt - qt) + REACH
            subs = [ds[i * HALF : (i + 1) * HALF] for i in range(KEYS // HALF)]
            diag_scr[h, e - 1] += subs[0][:, HALF:]
            for i, sub in enumerate(subs):
                here = sub[:, :HALF]
                if i + 1 < len(subs):
                    here = here + subs[i + 1][:, HALF:]
                diag_scr[h, e + i] += here

        run(pl.multiple_of(qt * TILE, TILE), TILE, span_ref[0, qt], span_ref[1, qt], bias_of, keep)
        return carry

    lax.fori_loop(0, SEQ_LEN // TILE, content_tile, 0)

    def query_bias(h, kt):
        return qbias_scr[h, pl.ds(pl.multiple_of(kt * TILE, TILE), KEYS), :]

    def query_keep(h, kt, ds, low):
        ds_scr[h, pl.ds(pl.multiple_of(kt * TILE, TILE), KEYS), :] = low

    late.wait()
    last = SEQ_LEN // TILE
    run(SEQ_LEN, rows_q, span_ref[0, last], span_ref[1, last], query_bias, query_keep)

    for a in range(0, SEQ_LEN, TILE):
        at = slice(a, a + TILE)
        dk_ref[at, :] = (dk_scr[:, at] * SCALE).T.astype(BF16)
        dv_ref[at, :] = dv_scr[:, at].T.astype(BF16)

    offs_ref[...] = jnp.zeros(offs_ref.shape, F32)
    qoffs_ref[...] = jnp.zeros(qoffs_ref.shape, F32)
    lane = lax.broadcasted_iota(jnp.int32, (HALF, HALF), 1)
    turn = lax.broadcasted_iota(jnp.int32, (HALF, HALF), 0) - lane
    over = turn < 0
    turn = jnp.where(over, turn + HALF, turn)
    for h in range(own):
        for e in range(REACH - FAR, REACH + FAR + 1):
            skew = jnp.take_along_axis(diag_scr[h, e], turn, axis=1)
            start = HALF * (15 + e - REACH)
            offs_ref[h : h + 1, start : start + HALF] += jnp.sum(
                jnp.where(over, skew, 0.0), axis=0, keepdims=True
            )
            offs_ref[h : h + 1, start + HALF : start + 2 * HALF] += jnp.sum(
                jnp.where(over, 0.0, skew), axis=0, keepdims=True
            )

    for h in range(own):
        total = jnp.zeros((16, WIDE), F32)
        for t in range(rows_q // HALF):
            shift = shift_ref[t * HALF : (t + 1) * HALF, :]
            place = lane - shift
            low_side = place < 0
            idx = jnp.where(low_side, place + HALF, place)
            prev = jnp.zeros((HALF, HALF), F32)
            pieces = []
            for j in range(SEQ_LEN // HALF + 1):
                if j < SEQ_LEN // HALF:
                    block = ds_scr[h, j * HALF : (j + 1) * HALF, t * HALF : (t + 1) * HALF]
                    cur = jnp.take_along_axis(block.astype(F32).T, idx, axis=1)
                else:
                    cur = jnp.zeros((HALF, HALF), F32)
                pieces.append(jnp.where(low_side, prev, cur).astype(BF16))
                prev = cur
            total += dot_tn(
                hot_ref[t * HALF : (t + 1) * HALF, :], jnp.concatenate(pieces, axis=1)
            )
        for i in range(16):
            qoffs_ref[h : h + 1, HALF * i : HALF * i + WIDE] += total[i : i + 1, :]


def bwd_call(
    span, qt, k3, kt, v3, ctx, g_c, g_q, lse, kmeta, rseg, rlim, tiles, hot, shift, qbias
):
    own = k3.shape[0]
    rows = qt.shape[1]
    rows_q = rows - SEQ_LEN
    vm = pl.BlockSpec(memory_space=pltpu.VMEM)
    return pl.pallas_call(
        functools.partial(bwd_kernel, own, rows_q),
        out_shape=(
            jax.ShapeDtypeStruct((rows, own * HEAD_DIM), BF16),
            jax.ShapeDtypeStruct((SEQ_LEN, own * HEAD_DIM), BF16),
            jax.ShapeDtypeStruct((SEQ_LEN, own * HEAD_DIM), BF16),
            jax.ShapeDtypeStruct((own, 2 * SEQ_LEN), F32),
            jax.ShapeDtypeStruct((own, 2 * SEQ_LEN), F32),
        ),
        in_specs=[pl.BlockSpec(memory_space=pltpu.SMEM)]
        + [vm] * 14
        + [pl.BlockSpec(memory_space=pltpu.HBM)],
        scratch_shapes=[
            pltpu.VMEM((own * HEAD_DIM, SEQ_LEN), F32),
            pltpu.VMEM((own * HEAD_DIM, SEQ_LEN), F32),
            pltpu.VMEM((own, HEAD_DIM, max(rows_q, TILE)), F32),
            pltpu.VMEM((own, DIAGS, HALF, HALF), F32),
            pltpu.VMEM((own, SEQ_LEN, rows_q), BF16),
            pltpu.VMEM((own, rows), F32),
            pltpu.VMEM((own * HEAD_DIM, rows), BF16),
            pltpu.VMEM(qbias.shape, F32),
            pltpu.SemaphoreType.DMA((1,)),
        ],
        compiler_params=pltpu.CompilerParams(vmem_limit_bytes=42 << 20),
        cost_estimate=cost_of(58),
        name="attend_back",
    )(span, qt, k3, kt, v3, ctx, g_c, g_q, lse, kmeta, rseg, rlim, tiles, hot, shift, qbias)


def key_spans(segment, pad_mask):
    length = segment.shape[0]
    real = pad_mask == 1
    head_seg = segment[::TILE]
    tail_seg = segment[TILE - 1 :: TILE]
    starts = jnp.sum((segment[None, :] < head_seg[:, None]).astype(jnp.int32), axis=1)
    first = jnp.arange(0, length, TILE, dtype=jnp.int32)
    lo = jnp.where(real[::TILE], starts, first) // TILE
    hi = jnp.where(real[TILE - 1 :: TILE], tail_seg, first + TILE - 1) // TILE
    count = jnp.sum(pad_mask)
    lo = jnp.concatenate([lo, jnp.zeros((1,), jnp.int32)])
    hi = jnp.concatenate([hi, jnp.maximum(count - 1, 0)[None] // TILE])
    per = KEYS // TILE
    steps = (hi - lo + per) // per
    lo = jnp.minimum(lo, length // TILE - steps * per)
    return jnp.stack([lo, steps]).astype(jnp.int32)


COLS = 768
UP_TOP = (2, 1)
DOWN_TOP = (1, 2)


def place_of(j, top):
    return (
        8 * (j % 2)
        + 4 * ((j // 2) % 2)
        + top[0] * ((j // 4) % 2)
        + top[1] * (j // 8)
    )


def mid_kernel(
    seqs,
    n_one,
    n_up,
    ctx_c,
    ctx_q,
    x_c,
    x_q,
    cot_c,
    cot_q,
    pad_ref,
    v_ref,
    uo_own,
    uo_own_far,
    uo_mate,
    uo_mate_far,
    down_own,
    down_own_far,
    down_mate,
    down_mate_far,
    res_c,
    res_q,
    gctx_c,
    gctx_q,
    six_out,
    up_out,
    sums_ref,
    out_c,
    out_q,
    keep_out,
    give_out,
    w_up,
    w_out,
    w_down,
    one_scr,
    norm_scr,
    inv_scr,
    low_scr,
    act_scr,
    slope_scr,
    sum_scr,
    grad_scr,
    pre_scr,
    plane_scr,
    outc_scr,
    outq_scr,
    parts_scr,
    sq_scr,
    valid_ref,
    xq_scr,
    cotq_scr,
    six_ref,
    bias_up,
    sems,
    plane_sems,
    out_sems,
):
    core = lax.rem(lax.axis_index("seq"), 2)
    this = lax.axis_index("dp") * (seqs // 2) + lax.axis_index("seq") // 2
    near, shard = uo_own.shape[0], uo_own.shape[1]
    chips = 2 * near
    shard_down = down_own.shape[1]
    length = x_c.shape[0]
    preds = x_q.shape[0]
    count = xq_scr.shape[0]
    ff = w_up.shape[1]
    chunks = ff // COLS
    wide = ctx_c.shape[1]
    half_ff, half = ff // 2, COLS // 2
    for d in range(v_ref.shape[0]):
        six_ref[:, d * n_one : (d + 1) * n_one] = v_ref[d, :6, :n_one]
        bias_up[:, d * n_up : (d + 1) * n_up] = v_ref[d, 6:7, :n_up]
    bias_out, gain_one, shift_one, bias_down, gain_two, shift_two = [
        six_ref[i : i + 1, :] for i in range(6)
    ]

    def plane_copies(chunk, slot):
        start = chunk * COLS
        if not isinstance(start, int):
            start = pl.multiple_of(start, COLS)
        return [
            pltpu.make_async_copy(
                ref.at[:, :, pl.ds(start, COLS)],
                plane_scr.at[slot, n // 2, pl.ds(near * (n % 2), near)],
                plane_sems.at[slot, n],
            )
            for n, ref in enumerate((uo_own, uo_own_far, uo_mate, uo_mate_far))
        ]

    def assemble(slot, put_rows):
        def body(j, carry):
            chip = this ^ place_of(j, UP_TOP)
            first = plane_scr[slot, core, j].astype(F32)
            second = plane_scr[slot, 1 - core, j].astype(F32)
            pair = jnp.concatenate([first, second], axis=0).astype(BF16)
            put_rows(pl.ds(pl.multiple_of(2 * shard * chip, 16), 2 * shard), pair)
            return carry

        lax.fori_loop(0, chips, body, 0)

    for chunk, slot in ((chunks, 0), (0, 1)):
        for copy in plane_copies(chunk, slot):
            copy.start()
    copies = []
    for j in range(chips):
        chip = this ^ place_of(j, DOWN_TOP)
        own, mate = ((down_own, down_mate), (down_own_far, down_mate_far))[j // near]
        for side, ref in ((core, own), (1 - core, mate)):
            row = pl.multiple_of((2 * chip + side) * shard_down, 16)
            copies.append(
                pltpu.make_async_copy(
                    ref.at[j % near], w_down.at[pl.ds(row, shard_down)], sems.at[len(copies)]
                )
            )
    for copy in copies:
        copy.start()
    for copy in plane_copies(chunks, 0):
        copy.wait()

    def put_out(rows, pair):
        w_out[rows, :] = pair

    assemble(0, put_out)
    for copy in plane_copies(1, 0):
        copy.start()

    for a in range(0, length, 128):
        row = pad_ref[:, a : a + 128].astype(F32)
        valid_ref[a : a + 128, :] = jnp.broadcast_to(row, (128, 128)).T
    spot = lax.broadcasted_iota(jnp.int32, (count, 128), 0)
    valid_ref[length:, :] = jnp.where(spot < preds, 1.0, 0.0)
    for ref, scr in ((x_q, xq_scr), (cot_q, cotq_scr)):
        scr[...] = jnp.zeros(scr.shape, F32)
        scr[:preds, :] = ref[...]
    blocks = [(0, length // 2), (length // 2, length), (length, length + count)]
    total = length + count
    cut = (total // 2 + 15) // 16 * 16
    halves = [(0, cut), (cut, total)]

    def pick(ref_c, ref_q, a, b):
        return ref_c[a:b, :] if b <= length else ref_q[...]

    def put(ref_c, ref_q, a, b, value):
        if b <= length:
            ref_c[a:b, :] = value
        else:
            ref_q[...] = value[: ref_q.shape[0]]

    def norm(x):
        mean = jnp.mean(x, axis=-1, keepdims=True)
        centered = x - mean
        inv = lax.rsqrt(jnp.mean(centered * centered, axis=-1, keepdims=True) + EPS)
        return centered * inv, inv

    def norm_grad(up, normed, inv, gain):
        grad = up * gain
        proj = jnp.mean(grad, axis=-1, keepdims=True) + normed * jnp.mean(
            grad * normed, axis=-1, keepdims=True
        )
        return inv * (grad - proj)

    sq_scr[...] = jnp.zeros(sq_scr.shape, F32)
    six_out[...] = jnp.zeros(six_out.shape, F32)
    up_out[...] = jnp.zeros(up_out.shape, F32)

    def count_in(k, x, a, b):
        row = k + (1 if b > length else 0)
        sq_scr[row : row + 1, :] += jnp.sum(x * x * valid_ref[a:b, :1], axis=0, keepdims=True)

    def add_row(row, x):
        six_out[row : row + 1, :] += jnp.sum(x, axis=0, keepdims=True)

    for a, b in blocks:
        attn = bias_out
        for t in range(seqs):
            part = w_out[t * wide : (t + 1) * wide, :]
            attn = attn + (
                dot_tn(ctx_c[t, :, a:b], part) if b <= length else dot_nn(ctx_q[t], part)
            )
        x = pick(x_c, xq_scr, a, b)
        count_in(0, x, a, b)
        count_in(2, attn, a, b)
        normed, inv = norm(x + attn)
        one = normed * gain_one + shift_one
        norm_scr[a:b, :] = normed
        inv_scr[a:b, :] = jnp.broadcast_to(inv, (b - a, 128))
        one_scr[a:b, :] = one
        low_scr[a:b, :] = one.astype(BF16)

    for copy in copies:
        copy.wait()
    sum_scr[...] = jnp.zeros(sum_scr.shape, F32)

    def up_step(i, carry):
        cols = pl.ds(pl.multiple_of(i * COLS, COLS), COLS)
        slot = lax.rem(i + 1, 2)
        for copy in plane_copies(i, slot):
            copy.wait()

        def put_up(rows, pair):
            w_up[rows, cols] = pair

        assemble(slot, put_up)

        @pl.when(i + 2 < chunks)
        def _():
            for copy in plane_copies(i + 2, slot):
                copy.start()

        for a, b in halves:
            u = dot_nn(low_scr[a:b, :], w_up[:, cols]) + bias_up[:, cols]
            cdf = 0.5 * (1.0 + lax.erf(u * math.sqrt(0.5)))
            act = (u * cdf).astype(BF16)
            act_scr[a:b, cols] = act
            slope_scr[a:b, cols] = cdf + u * (
                jnp.exp(-0.5 * u * u) * (1.0 / math.sqrt(2.0 * math.pi))
            )
            sum_scr[a:b, :] += dot_nn(act, w_down[cols, :])
        return carry

    lax.fori_loop(0, chunks, up_step, 0)

    for a, b in blocks:
        ffn = sum_scr[a:b, :] + bias_down
        count_in(4, ffn, a, b)
        normed, inv = norm(one_scr[a:b, :] + ffn)
        ok = valid_ref[a:b, :1]
        put(outc_scr, outq_scr, a, b, (normed * gain_two + shift_two) * ok)
        up = pick(cot_c, cotq_scr, a, b) * ok
        add_row(4, up * normed)
        add_row(5, up)
        grad = norm_grad(up, normed, inv, gain_two)
        low = grad.astype(BF16)
        add_row(3, low.astype(F32))
        sum_scr[a:b, :] = grad
        grad_scr[a:b, :] = low
    leaving = [
        pltpu.make_async_copy(outc_scr, out_c, out_sems.at[0]),
        pltpu.make_async_copy(outq_scr, out_q, out_sems.at[1]),
    ]
    for copy in leaving:
        copy.start()

    def start(copy_of, h):
        @pl.when(core == h)
        def _():
            copy_of(keep_out).start()

        @pl.when(core != h)
        def _():
            copy_of(give_out).start()

    def up_copy(i, out):
        h, at = i // 2, lax.rem(i, 2) if not isinstance(i, int) else i % 2
        cols = pl.ds(pl.multiple_of(at * COLS, COLS) if not isinstance(i, int) else at * COLS, COLS)
        return pltpu.make_async_copy(
            parts_scr.at[h, :, cols], out.at[:, cols], out_sems.at[2 + i]
        )

    down_rows = 2 * shard * (COLS // (2 * shard_down))
    down_cols = pl.ds(half_ff + half, half_ff)

    def down_copy(i, h, out):
        start = i * down_rows
        rows = pl.ds(start if isinstance(i, int) else pl.multiple_of(start, down_rows), down_rows)
        return pltpu.make_async_copy(
            parts_scr.at[h, rows, down_cols],
            out.at[rows, down_cols],
            out_sems.at[2 + chunks * (1 + h) + i],
        )

    def back_step(i, carry):
        cols = pl.ds(pl.multiple_of(i * COLS, COLS), COLS)
        for a, b in halves:
            low = (
                dot_nt(grad_scr[a:b, :], w_down[cols, :]) * slope_scr[a:b, cols]
            ).astype(BF16)
            pre_scr[a:b, :] = low
            up_out[:, cols] += jnp.sum(low.astype(F32), axis=0, keepdims=True)
            sum_scr[a:b, :] += dot_nt(low, w_up[:, cols])
        at = pl.ds(pl.multiple_of(lax.rem(i, 2) * COLS, COLS), COLS)
        parts_scr[i // 2, :, at] = dot_tn(low_scr[...], pre_scr[...]).astype(BF16)
        start(lambda out: up_copy(i, out), i // 2)
        grads = dot_tn(act_scr[:, cols], grad_scr[...]).astype(BF16)
        for h in range(2):
            for chip in range(COLS // (2 * shard_down)):
                to = pl.ds(pl.multiple_of(i * down_rows, down_rows) + chip * 2 * shard, 2 * shard)
                for g in range(shard_down // shard):
                    row = 2 * shard_down * chip + 2 * shard * g
                    col = half_ff + half * (1 + g)
                    parts_scr[h, to, col : col + half] = grads[
                        row : row + 2 * shard, h * half : (h + 1) * half
                    ]
            start(lambda out: down_copy(i, h, out), h)
        return carry

    lax.fori_loop(0, chunks, back_step, 0)
    leaving += [up_copy(i, keep_out) for i in range(chunks)]
    leaving += [down_copy(i, h, keep_out) for i in range(chunks) for h in range(2)]

    for a, b in blocks:
        up = sum_scr[a:b, :]
        normed = norm_scr[a:b, :]
        add_row(1, up * normed)
        add_row(2, up)
        grad = norm_grad(up, normed, inv_scr[a:b, :1], gain_one)
        low = grad.astype(BF16)
        add_row(0, low.astype(F32))
        put(res_c, res_q, a, b, grad)
        grad_scr[a:b, :] = low
    for t in range(seqs):
        rows = slice(t * wide, (t + 1) * wide)
        part = w_out[rows, :]
        gctx_c[t] = dot_nt(part, grad_scr[:length, :]).astype(BF16)
        gctx_q[t] = dot_nt(grad_scr[length:, :], part).astype(BF16)
        grads = (
            dot_nn(ctx_c[t], grad_scr[:length, :]) + dot_tn(ctx_q[t], grad_scr[length:, :])
        ).astype(BF16)
        for h in range(2):
            parts_scr[h, rows, half_ff : half_ff + half] = grads[:, h * half : (h + 1) * half]
    tail = pl.ds(half_ff, half)

    def tail_copy(h, out):
        return pltpu.make_async_copy(
            parts_scr.at[h, :, tail], out.at[:, tail], out_sems.at[2 + 3 * chunks + h]
        )

    for h in range(2):
        start(lambda out: tail_copy(h, out), h)
    leaving += [tail_copy(h, keep_out) for h in range(2)]
    sq_scr[6:7, :] = jnp.sum(
        jnp.where(lax.broadcasted_iota(jnp.int32, (length, COLS), 1) == 0, valid_ref[:length, :1], 0.0),
        axis=0,
        keepdims=True,
    )
    sums_ref[...] = jnp.broadcast_to(jnp.sum(sq_scr[...], axis=1, keepdims=True), sums_ref.shape)
    for copy in leaving:
        copy.wait()


def mid_call(ctx_c, ctx_q, x_c, x_q, cot_c, cot_q, pad, v_all, n_one, n_up, planes):
    seqs, wide, length = ctx_c.shape
    count = ctx_q.shape[1]
    preds = x_q.shape[0]
    total = length + count
    near, shard, cols = planes[0].shape
    chips = 2 * near
    ff = cols - COLS
    chunks = ff // COLS
    vm = pl.BlockSpec(memory_space=pltpu.VMEM)
    anywhere = pl.BlockSpec(memory_space=pl.ANY)
    parts = jax.ShapeDtypeStruct((COLS, (cols + ff) // 2), BF16)
    return pl.pallas_call(
        functools.partial(mid_kernel, seqs, n_one, n_up),
        out_shape=(
            jax.ShapeDtypeStruct(x_c.shape, F32),
            jax.ShapeDtypeStruct((count, COLS), F32),
            jax.ShapeDtypeStruct(ctx_c.shape, BF16),
            jax.ShapeDtypeStruct(ctx_q.shape, BF16),
            jax.ShapeDtypeStruct((6, COLS), F32),
            jax.ShapeDtypeStruct((1, ff), F32),
            jax.ShapeDtypeStruct((8, 128), F32),
            jax.ShapeDtypeStruct(x_c.shape, F32),
            jax.ShapeDtypeStruct((preds, COLS), F32),
            parts,
            parts,
        ),
        in_specs=[vm] * 8 + [anywhere] * 8,
        out_specs=(vm,) * 7 + (anywhere,) * 4,
        scratch_shapes=[
            pltpu.VMEM((COLS, ff), BF16),
            pltpu.VMEM((COLS, COLS), BF16),
            pltpu.VMEM((ff, COLS), BF16),
            pltpu.VMEM((total, COLS), F32),
            pltpu.VMEM((total, COLS), F32),
            pltpu.VMEM((total, 128), F32),
            pltpu.VMEM((total, COLS), BF16),
            pltpu.VMEM((total, ff), BF16),
            pltpu.VMEM((total, ff), F32),
            pltpu.VMEM((total, COLS), F32),
            pltpu.VMEM((total, COLS), BF16),
            pltpu.VMEM((total, COLS), BF16),
            pltpu.VMEM((2, 2, chips, shard, COLS), BF16),
            pltpu.VMEM(x_c.shape, F32),
            pltpu.VMEM((preds, COLS), F32),
            pltpu.VMEM((2,) + parts.shape, BF16),
            pltpu.VMEM((8, COLS), F32),
            pltpu.VMEM((total, 128), F32),
            pltpu.VMEM((count, COLS), F32),
            pltpu.VMEM((count, COLS), F32),
            pltpu.VMEM((6, COLS), F32),
            pltpu.VMEM((1, ff), F32),
            pltpu.SemaphoreType.DMA((2 * chips,)),
            pltpu.SemaphoreType.DMA((2, 4)),
            pltpu.SemaphoreType.DMA((4 + 3 * chunks,)),
        ],
        compiler_params=pltpu.CompilerParams(vmem_limit_bytes=63 << 20),
        cost_estimate=cost_of(45),
        name="feed_forward",
    )(ctx_c, ctx_q, x_c, x_q, cot_c, cot_q, pad, v_all, *planes)


def proj_kernel(
    own, keys, n_qv, x_ref, w_ref, vec_ref, qt_ref, k_ref, kt_ref, v_ref, vt_ref, bq_ref, bv_ref
):
    wide = own * HEAD_DIM
    first = lax.axis_index("seq") * (wide // n_qv)
    for ref, start in ((bq_ref, first), (bv_ref, first + vec_ref.shape[0] // 2)):
        for i in range(wide // n_qv):
            ref[:, i * n_qv : (i + 1) * n_qv] = vec_ref[start + i, 7:8, :n_qv]
    rows = x_ref.shape[0]
    for a in range(0, rows, 256):
        b = min(a + 256, rows)
        parts = [(0, bq_ref, qt_ref, None)]
        if b <= keys:
            parts += [(1, None, kt_ref, k_ref), (2, bv_ref, vt_ref, v_ref)]
        y = dot_nn(x_ref[a:b, :], w_ref[:, : len(parts) * wide])
        for n, bias, flat_ref, head_ref in parts:
            part = y[:, n * wide : (n + 1) * wide]
            if bias is not None:
                part = part + bias[...]
            flat_ref[:, a:b] = part.T.astype(BF16)
            for h in range(own if head_ref is not None else 0):
                head_ref[h, a:b, :] = part[:, h * HEAD_DIM : (h + 1) * HEAD_DIM].astype(BF16)


def proj_call(own, keys, x, w, vec, n_qv):
    rows = x.shape[0]
    wide = own * HEAD_DIM
    vm = pl.BlockSpec(memory_space=pltpu.VMEM)
    flat = lambda n: jax.ShapeDtypeStruct((wide, n), BF16)
    head = lambda n: jax.ShapeDtypeStruct((own, n, HEAD_DIM), BF16)
    return pl.pallas_call(
        functools.partial(proj_kernel, own, keys, n_qv),
        out_shape=(flat(rows), head(keys), flat(keys), head(keys), flat(keys)),
        in_specs=[vm] * 3,
        out_specs=(vm,) * 5,
        scratch_shapes=[pltpu.VMEM((1, wide), F32)] * 2,
        compiler_params=pltpu.CompilerParams(vmem_limit_bytes=20 << 20),
        cost_estimate=cost_of(5),
        name="project",
    )(x, w, vec)


def grads_kernel(
    keys,
    x_ref,
    w_ref,
    dq_ref,
    dk_ref,
    dv_ref,
    offs_ref,
    qoffs_ref,
    bucket_ref,
    six_ref,
    up_ref,
    squares_ref,
    gc_ref,
    gq_ref,
    gw_ref,
    vec_ref,
    shared_ref,
    part_scr,
):
    s = lax.axis_index("seq")
    wide = dq_ref.shape[1]
    seqs, length = gc_ref.shape[:2]
    shard = gw_ref.shape[1]
    for n, ref in enumerate((dq_ref, dk_ref, dv_ref)):
        part_scr[:, n * wide : (n + 1) * wide] = dot_tn(x_ref[: ref.shape[0], :], ref[...])
    for j in range(gw_ref.shape[0]):
        gw_ref[j] = part_scr[j * shard : (j + 1) * shard, :].astype(BF16)
    blocks = vec_ref.shape[0]
    n_one, n_up = six_ref.shape[1] // blocks, up_ref.shape[1] // blocks
    n_qv = 2 * n_one
    vec_ref[...] = jnp.zeros(vec_ref.shape, F32)
    sums = [jnp.sum(ref[...].astype(F32), axis=0, keepdims=True) for ref in (dq_ref, dv_ref)]
    for d in range(blocks):
        vec_ref[d, :6, :n_one] = six_ref[:, d * n_one : (d + 1) * n_one]
        vec_ref[d, 6:7, :n_up] = up_ref[:, d * n_up : (d + 1) * n_up]
        kind, start = divmod(d * n_qv, seqs * wide)
        owner, start = divmod(start, wide)
        piece = sums[kind][:, start : start + n_qv]
        vec_ref[d, 7:8, :n_qv] = jnp.where(s == owner, piece, 0.0)
    own = offs_ref.shape[0]
    table = jnp.zeros((own, BUCKETS), F32)
    for row, ref in ((1, offs_ref), (0, qoffs_ref)):
        hot = (
            lax.broadcasted_iota(jnp.int32, (BUCKETS, ref.shape[1]), 0)
            == bucket_ref[row : row + 1, :]
        ).astype(F32)
        table += lax.dot_general(
            ref[...],
            hot,
            (((1,), (1,)), ((), ())),
            precision=lax.Precision.HIGHEST,
            preferred_element_type=F32,
        )
    shared_ref[...] = jnp.zeros(shared_ref.shape, F32)
    for h in range(own):
        shared_ref[pl.ds(s * own + h, 1), :BUCKETS] = table[h : h + 1]
    shared_ref[16:24, :] = squares_ref[...]
    w_q = w_ref[:, :wide]
    w_k = w_ref[:, wide : 2 * wide]
    w_v = w_ref[:, 2 * wide :]
    step = 256
    for t in range(seqs):
        for a in range(0, length, step):
            at = slice(t * length + a, t * length + a + step)
            gc_ref[t, a : a + step, :] = (
                dot_nt(dq_ref[at, :], w_q) + dot_nt(dk_ref[at, :], w_k) + dot_nt(dv_ref[at, :], w_v)
            ).astype(BF16)
    count = gq_ref.shape[1]
    for t in range(seqs):
        at = slice(keys + t * count, keys + (t + 1) * count)
        gq_ref[t] = dot_nt(dq_ref[at, :], w_q).astype(BF16)


def grads_call(
    seqs, length, count, blocks, x, w, dq, dk, dv, offs, qoffs, buckets, six, up, squares
):
    wide = dq.shape[1]
    shard = x.shape[1] // blocks
    vm = pl.BlockSpec(memory_space=pltpu.VMEM)
    return pl.pallas_call(
        functools.partial(grads_kernel, seqs * length),
        out_shape=(
            jax.ShapeDtypeStruct((seqs, length, x.shape[1]), BF16),
            jax.ShapeDtypeStruct((seqs, count, x.shape[1]), BF16),
            jax.ShapeDtypeStruct((blocks, shard, 3 * wide), BF16),
            jax.ShapeDtypeStruct((blocks, 8, 128), F32),
            jax.ShapeDtypeStruct((24, 128), F32),
        ),
        in_specs=[vm] * 11,
        out_specs=(vm,) * 5,
        scratch_shapes=[pltpu.VMEM((x.shape[1], 3 * wide), F32)],
        compiler_params=pltpu.CompilerParams(vmem_limit_bytes=28 << 20),
        cost_estimate=cost_of(6),
        name="weight_grads",
    )(x, w, dq, dk, dv, offs, qoffs, buckets, six, up, squares)


MESH = pl.DeviceIdType.MESH
ROWS_Q = 384
SLOT_Q = 80


def greet(devices):
    barrier = pltpu.get_barrier_semaphore()
    for device in devices:
        pl.semaphore_signal(barrier, inc=1, device_id=device, device_id_type=MESH)
    pl.semaphore_wait(barrier, len(devices))


def remote(src, dst, send_sem, recv_sem, k, device):
    return pltpu.make_async_remote_copy(
        src_ref=src,
        dst_ref=dst,
        send_sem=send_sem.at[k],
        recv_sem=recv_sem.at[k],
        device_id=device,
        device_id_type=MESH,
    )


def start_kernel(
    dps,
    seqs,
    c_ref,
    q_ref,
    w_ref,
    v_ref,
    seg_ref,
    order_ref,
    pad_ref,
    pred_ref,
    x_out,
    w_out,
    v_out,
    i_out,
    c_scr,
    q_scr,
    qlow_scr,
    zero_scr,
    send_sem,
    recv_sem,
    here_sem,
):
    dp = lax.axis_index("dp")
    s = lax.axis_index("seq")
    length = c_ref.shape[0]
    count = q_scr.shape[0]
    mate = s + 1 - 2 * lax.rem(s, 2)
    across = lax.rem(s + 2, seqs)
    level = dp + 1 - 2 * lax.rem(dp, 2)
    stacks = dps // 2
    greet(
        [(dp, lax.rem(s + r, seqs)) for r in range(1, seqs)]
        + [(level, s)]
        + [(lax.rem(dp + 2 * r, dps), s) for r in range(1, stacks)]
    )

    def at_c(owner):
        return pl.ds(pl.multiple_of(owner * length, length), length)

    def at_q(owner):
        return pl.ds(pl.multiple_of(seqs * length + owner * count, 16), count)

    k = 0

    def push(src, dst, device):
        nonlocal k
        copy = remote(src, dst, send_sem, recv_sem, k, device)
        copy.start()
        k += 1
        return copy

    i_out[s] = jnp.zeros(i_out.shape[1:], jnp.int32)
    for n, ref in enumerate((seg_ref, order_ref, pad_ref)):
        i_out[s, n : n + 1, :] = ref[...]
    i_out[s, 3:4, :] = jnp.full((1, length), -1, jnp.int32)
    i_out[s, 3:4, : pred_ref.shape[1]] = pred_ref[...]
    small = []
    for r in range(1, seqs):
        to = lax.rem(s + r, seqs)
        small.append(push(w_ref.at[to], w_out.at[dp, s], (dp, to)))
        small.append(push(v_ref, v_out.at[dp, s], (dp, to)))
        small.append(push(i_out.at[s], i_out.at[s], (dp, to)))
    c_scr[...] = c_ref[...].astype(BF16)
    far = [push(c_scr, x_out.at[at_c(s)], (dp, across))]
    q_scr[...] = jnp.zeros(q_scr.shape, F32)
    q_scr[: q_ref.shape[0], :] = q_ref[...]
    qlow_scr[...] = q_scr[...].astype(BF16)
    far.append(push(qlow_scr, x_out.at[at_q(s)], (dp, across)))
    near = [
        push(scr, x_out.at[at(s)], (dp, mate)) for scr, at in ((c_scr, at_c), (qlow_scr, at_q))
    ]
    v_out[dp, s] = v_ref[...]
    zero_scr[...] = jnp.zeros(zero_scr.shape, BF16)
    here = [
        pltpu.make_async_copy(src, dst, here_sem.at[n])
        for n, (src, dst) in enumerate(
            (
                (w_ref.at[s], w_out.at[dp, s]),
                (c_scr, x_out.at[at_c(s)]),
                (qlow_scr, x_out.at[at_q(s)]),
                (zero_scr, x_out.at[pl.ds(seqs * (length + count), zero_scr.shape[0])]),
            )
        )
    ]
    for copy in here:
        copy.start()
    for copy in here:
        copy.wait()
    for copy in small:
        copy.wait_recv()
    wide, flat = [], []
    for r in range(1, stacks):
        to = lax.rem(dp + 2 * r, dps)
        wide.append([push(ref.at[dp], ref.at[dp], (to, s)) for ref in (w_out, v_out)])
    flat += [push(ref.at[dp], ref.at[dp], (level, s)) for ref in (w_out, v_out)]
    for r in range(1, stacks):
        source = lax.rem(dp + dps - 2 * r, dps)
        for copy, ref in zip(wide[r - 1], (w_out, v_out)):
            copy.wait_recv()
            flat.append(push(ref.at[source], ref.at[source], (level, s)))
    pass_on = []
    for copy, at in zip(far, (at_c, at_q)):
        copy.wait_recv()
        pass_on.append(push(x_out.at[at(across)], x_out.at[at(across)], (dp, mate)))
    for copy in near + flat + pass_on:
        copy.wait_recv()
    for copy in small + far + near + flat + pass_on + sum(wide, []):
        copy.wait_send()


def start_call(dps, seqs, content, query, w, v, metas, slot_q):
    copies = 3 * (seqs - 1) + 4 + 2 * (dps // 2 - 1) + dps + 2
    length, width = content.shape
    vmem = pl.BlockSpec(memory_space=pltpu.VMEM)
    return pl.pallas_call(
        functools.partial(start_kernel, dps, seqs),
        out_shape=(
            jax.ShapeDtypeStruct((seqs * length + ROWS_Q, width), BF16),
            jax.ShapeDtypeStruct((dps,) + w.shape, BF16),
            jax.ShapeDtypeStruct((dps, seqs) + v.shape, F32),
            jax.ShapeDtypeStruct((seqs, 8, length), jnp.int32),
        ),
        in_specs=[vmem] * 8,
        out_specs=(pl.BlockSpec(memory_space=pltpu.HBM),) * 2 + (vmem,) * 2,
        scratch_shapes=[
            pltpu.VMEM((length, width), BF16),
            pltpu.VMEM((slot_q, width), F32),
            pltpu.VMEM((slot_q, width), BF16),
            pltpu.VMEM((ROWS_Q - seqs * slot_q, width), BF16),
            pltpu.SemaphoreType.DMA((copies,)),
            pltpu.SemaphoreType.DMA((copies,)),
            pltpu.SemaphoreType.DMA((4,)),
        ],
        compiler_params=pltpu.CompilerParams(
            collective_id=0, has_side_effects=True, vmem_limit_bytes=16 << 20
        ),
        cost_estimate=cost_of(30),
        name="gather_rows",
    )(content, query, w, v, *metas)


def swap_kernel(seqs, c_of, q_of, c_ref, q_ref, c_out, q_out, send_sem, recv_sem, here_sem):
    dp = lax.axis_index("dp")
    s = lax.axis_index("seq")
    greet([(dp, lax.rem(s + r, seqs)) for r in range(1, seqs)])
    copies = []
    for r in range(1, seqs):
        to = lax.rem(s + r, seqs)
        k = 2 * (r - 1)
        copies.append(remote(c_of(c_ref, to), c_out.at[s], send_sem, recv_sem, k, (dp, to)))
        copies.append(remote(q_of(q_ref, to), q_out.at[s], send_sem, recv_sem, k + 1, (dp, to)))
    for copy in copies:
        copy.start()
    here = [
        pltpu.make_async_copy(c_of(c_ref, s), c_out.at[s], here_sem.at[0]),
        pltpu.make_async_copy(q_of(q_ref, s), q_out.at[s], here_sem.at[1]),
    ]
    for copy in here:
        copy.start()
    for copy in here + copies:
        copy.wait()


def swap_call(seqs, c, q, c_of, q_of, c_shape, q_shape, ident, name):
    vmem = pl.BlockSpec(memory_space=pltpu.VMEM)
    return pl.pallas_call(
        functools.partial(swap_kernel, seqs, c_of, q_of),
        out_shape=(
            jax.ShapeDtypeStruct((seqs,) + c_shape, c.dtype),
            jax.ShapeDtypeStruct((seqs,) + q_shape, q.dtype),
        ),
        in_specs=[vmem] * 2,
        out_specs=(vmem,) * 2,
        scratch_shapes=[
            pltpu.SemaphoreType.DMA((2 * (seqs - 1),)),
            pltpu.SemaphoreType.DMA((2 * (seqs - 1),)),
            pltpu.SemaphoreType.DMA((2,)),
        ],
        compiler_params=pltpu.CompilerParams(collective_id=ident, has_side_effects=True),
        cost_estimate=cost_of(12),
        name=name,
    )(c, q)


def end_kernel(
    dps,
    seqs,
    gc_ref,
    gq_ref,
    w_ref,
    v_ref,
    sh_ref,
    gc_out,
    gq_out,
    w_out,
    v_out,
    sh_out,
    c_mate,
    q_mate,
    c_far,
    q_far,
    c_send,
    q_send,
    w_flat,
    v_flat,
    sh_flat,
    w_send,
    v_send,
    sh_send,
    w_got,
    v_got,
    sh_got,
    w_sum,
    v_sum,
    sh_sum,
    v_last,
    sh_last,
    send_sem,
    recv_sem,
):
    dp = lax.axis_index("dp")
    s = lax.axis_index("seq")
    core = lax.rem(s, 2)
    mate = s + 1 - 2 * core
    across = lax.rem(s + 2, seqs)
    side = lax.rem(dp, 2)
    level = dp + 1 - 2 * side
    stacks = dps // 2
    greet(
        [(dp, lax.rem(s + r, seqs)) for r in range(1, seqs)]
        + [(level, s)]
        + [(lax.rem(dp + 2 * r, dps), s) for r in range(1, stacks)]
    )
    k = 0

    def push(src, dst, device):
        nonlocal k
        copy = remote(src, dst, send_sem, recv_sem, k, device)
        copy.start()
        k += 1
        return copy

    def each(ref, step, fn):
        def body(i, carry):
            fn(pl.ds(pl.multiple_of(i * step, step), step))
            return carry

        lax.fori_loop(0, ref.shape[-2] // step, body, 0)

    first = []
    for i in range(2):
        to = lax.rem(mate + 2 * (1 - i), seqs)
        for src, dst in ((gc_ref, c_mate), (gq_ref, q_mate)):
            first.append(push(src.at[to], dst.at[i], (dp, mate)))
    flat = []
    for r in list(range(1, stacks)) + [0]:
        to = lax.rem(level + 2 * r, dps)
        flat.append(
            [push(src.at[to], dst.at[r], (level, s)) for src, dst in ((w_ref, w_flat), (v_ref, v_flat))]
        )
    shared = push(sh_ref, sh_flat, (level, s))
    cross = []
    for (src, got, buf, far, copy) in (
        (gc_ref, c_mate, c_send, c_far, first[0]),
        (gq_ref, q_mate, q_send, q_far, first[1]),
    ):
        copy.wait_recv()

        def add(rows, src=src, got=got, buf=buf):
            buf[rows, :] = (
                src[across, rows, :].astype(F32) + got[0, rows, :].astype(F32)
            ).astype(BF16)

        each(buf, 16, add)
        cross.append(push(buf, far, (dp, across)))
    shared.wait_recv()
    sh_send[...] = sh_ref[...] + sh_flat[...]
    tall = []
    for r in range(1, stacks):
        for copy in flat[r - 1]:
            copy.wait_recv()
        to = lax.rem(dp + 2 * r, dps)

        def add_pair(rows, to=to, r=r):
            for t in range(seqs):
                w_send[r - 1, t, rows, :] = (
                    w_ref[to, t, rows, :].astype(F32) + w_flat[r, t, rows, :].astype(F32)
                ).astype(BF16)

        each(w_sum, 24, add_pair)
        v_send[r - 1] = v_ref[to] + v_flat[r]
        for src, dst in (
            (w_send.at[r - 1], w_got.at[r - 1]),
            (v_send.at[r - 1], v_got.at[r - 1]),
            (sh_send, sh_got.at[r - 1]),
        ):
            tall.append(push(src, dst, (to, s)))
    for copy in flat[stacks - 1] + tall:
        copy.wait_recv()

    def add_w(rows):
        for t in range(seqs):
            total = w_ref[dp, t, rows, :].astype(F32) + w_flat[0, t, rows, :].astype(F32)
            for r in range(1, stacks):
                total += w_got[r - 1, t, rows, :].astype(F32)
            w_sum[t, rows, :] = total

    each(w_sum, 24, add_w)
    total = v_ref[dp] + v_flat[0]
    for r in range(1, stacks):
        total += v_got[r - 1]
    v_sum[...] = total
    total = sh_send[...]
    for r in range(1, stacks):
        total += sh_got[r - 1]
    sh_sum[...] = total
    last = []
    for r in range(1, seqs):
        to = lax.rem(s + r, seqs)
        last.append(push(w_sum.at[to], w_out.at[s], (dp, to)))
        last.append(push(v_sum.at[to], v_last.at[r - 1], (dp, to)))
        last.append(push(sh_sum, sh_last.at[r - 1], (dp, to)))
    w_out[s] = w_sum[s]
    for copy in first[2:] + cross:
        copy.wait_recv()
    for (src, got, far, out) in (
        (gc_ref, c_mate, c_far, gc_out),
        (gq_ref, q_mate, q_far, gq_out),
    ):

        def total_of(rows, src=src, got=got, far=far, out=out):
            out[rows, :] = (
                src[s, rows, :].astype(F32)
                + got[1, rows, :].astype(F32)
                + far[rows, :].astype(F32)
            )

        each(out, 16, total_of)
    for copy in last:
        copy.wait_recv()
    total = v_sum[s]
    for r in range(1, seqs):
        total += v_last[r - 1]
    v_out[...] = total
    total = sh_sum[...]
    for r in range(1, seqs):
        total += sh_last[r - 1]
    sh_out[...] = total
    for copy in first + sum(flat, []) + [shared] + cross + tall + last:
        copy.wait_send()


def end_call(dps, seqs, gc, gq, w, v, sh):
    stacks = dps // 2
    copies = 4 + 2 * stacks + 1 + 2 + 3 * (stacks - 1) + 3 * (seqs - 1)
    vm = pl.BlockSpec(memory_space=pltpu.VMEM)
    cshape, qshape, wshape, vshape = gc.shape[1:], gq.shape[1:], w.shape[1:], v.shape[1:]
    return pl.pallas_call(
        functools.partial(end_kernel, dps, seqs),
        out_shape=(
            jax.ShapeDtypeStruct(cshape, F32),
            jax.ShapeDtypeStruct(qshape, F32),
            jax.ShapeDtypeStruct(wshape, F32),
            jax.ShapeDtypeStruct(vshape[1:], F32),
            jax.ShapeDtypeStruct(sh.shape, F32),
        ),
        in_specs=[vm] * 5,
        out_specs=(vm,) * 5,
        scratch_shapes=[
            pltpu.VMEM((2,) + cshape, BF16),
            pltpu.VMEM((2,) + qshape, BF16),
            pltpu.VMEM(cshape, BF16),
            pltpu.VMEM(qshape, BF16),
            pltpu.VMEM(cshape, BF16),
            pltpu.VMEM(qshape, BF16),
            pltpu.VMEM((stacks,) + wshape, BF16),
            pltpu.VMEM((stacks,) + vshape, F32),
            pltpu.VMEM(sh.shape, F32),
            pltpu.VMEM((stacks - 1,) + wshape, BF16),
            pltpu.VMEM((stacks - 1,) + vshape, F32),
            pltpu.VMEM(sh.shape, F32),
            pltpu.VMEM((stacks - 1,) + wshape, BF16),
            pltpu.VMEM((stacks - 1,) + vshape, F32),
            pltpu.VMEM((stacks - 1,) + sh.shape, F32),
            pltpu.VMEM(wshape, F32),
            pltpu.VMEM(vshape, F32),
            pltpu.VMEM(sh.shape, F32),
            pltpu.VMEM((seqs - 1,) + vshape[1:], F32),
            pltpu.VMEM((seqs - 1,) + sh.shape, F32),
            pltpu.SemaphoreType.DMA((copies,)),
            pltpu.SemaphoreType.DMA((copies,)),
        ],
        compiler_params=pltpu.CompilerParams(
            collective_id=3, has_side_effects=True, vmem_limit_bytes=24 << 20
        ),
        cost_estimate=cost_of(30),
        name="sum_rows",
    )(gc, gq, w, v, sh)


def flip_perm(count, bit):
    return [(i, i ^ bit) for i in range(count)]


AXES = ("dp", "seq")


def tie(values, *others):
    return lax.optimization_barrier((values, others))[0]


def give_to(cur, count, bit):
    return lax.ppermute(cur, AXES, flip_perm(count, bit))


def local_fast(
    content,
    query_stream,
    segment_ids,
    pad_mask,
    predicted,
    order,
    rel_bucket,
    qkv_weight,
    qv_bias,
    out_weight,
    out_bias,
    attn_gain,
    attn_shift,
    up_weight,
    up_bias,
    down_weight,
    down_bias,
    ffn_gain,
    ffn_shift,
    rel_table,
    content_cot,
    query_cot,
):
    dps, seqs = lax.axis_size("dp"), lax.axis_size("seq")
    count = dps * seqs
    s = lax.axis_index("seq")
    own = HEADS // seqs
    wide = own * HEAD_DIM
    length = content.shape[1]
    preds = query_stream.shape[1]
    shard = qkv_weight.shape[0]

    rows = (out_bias, attn_gain, attn_shift, down_bias, ffn_gain, ffn_shift, up_bias, qv_bias)
    fill = [jnp.zeros((128 - row.shape[0],), row.dtype) for row in rows]
    vec = jnp.concatenate([x for pair in zip(rows, fill) for x in pair])
    vec = vec.astype(F32).reshape(8, 128)
    buckets = jnp.stack(
        [
            jnp.pad(rel_bucket, (0, 1), constant_values=BUCKETS),
            jnp.pad(rel_bucket, (1, 0), constant_values=BUCKETS),
        ]
    )
    w_parts = jnp.transpose(
        qkv_weight.reshape(shard, 3, seqs, wide), (2, 0, 1, 3)
    ).reshape(seqs, shard, 3 * wide)
    tops = (UP_TOP, DOWN_TOP)

    def send(pair, bits):
        return tuple(give_to(x, count, bit) for x, bit in zip(pair, bits))

    def heap(*pairs):
        return tuple(jnp.concatenate(x) for x in zip(*pairs))

    zs_low = (jnp.concatenate([up_weight, out_weight], axis=1)[None], down_weight[None])
    flying = send(zs_low, (16, 16))
    x_all, w_all, v_all, i_all = start_call(
        dps,
        seqs,
        content[0],
        query_stream[0],
        w_parts,
        vec,
        (segment_ids, order, pad_mask, predicted),
        SLOT_Q,
    )
    w_qkv = w_all.reshape(MODEL_WIDTH, 3 * wide)
    n_qv, n_up, n_one = qv_bias.shape[0], up_bias.shape[0], out_bias.shape[0]
    v_all = v_all.reshape(count, 8, 128)
    seg_all = i_all[:, 0].reshape(seqs * length)
    pad_all = i_all[:, 2].reshape(seqs * length)
    span = key_spans(seg_all, pad_all)

    bits = [tuple(2 * top[n] for top in tops) for n in range(2)]
    zs_low = heap(zs_low, tie(flying, i_all))
    flying = send(zs_low, (8, 8)), send(zs_low, bits[0])
    first = (s * own).astype(jnp.int32)[None]
    ints = tie(i_all, zs_low)
    tiles, qbias, kmeta, rseg, rlim, hot, shift = bias_call(
        own, ROWS_Q, SLOT_Q, first, buckets, rel_table, ints
    )

    zs_high, side_low = tie(flying, tiles)
    column = heap(zs_low, zs_high)
    side_high, far_low = send(zs_high, bits[0]), send(column, bits[1])
    x_all = tie(x_all, column)
    q_t, k3, k_t, v3, v_t = proj_call(
        own, seqs * length, x_all, w_qkv, v_all, n_qv
    )
    side_high = tie(side_high, q_t)
    side = heap(side_low, side_high)
    far_high = send(side, bits[1])
    close = heap(column, side)
    q_t = tie(q_t, side)

    ctx_t, ctx_rows, lse = fwd_call(span, q_t, k3, v_t, kmeta, rseg, rlim, tiles, qbias)

    far_low, far_high = tie((far_low, far_high), ctx_rows)
    far = heap(far_low, far_high)
    mates, far_mates = send(close, (1, 1)), send(far, (1, 1))
    ctx_rows = tie(ctx_rows, far)
    planes = sum(zip(close, far, mates, far_mates), ())

    def from_lanes(ref, t):
        return ref.at[:, pl.ds(pl.multiple_of(t * length, length), length)]

    def from_query(ref, t):
        return ref.at[pl.ds(pl.multiple_of(t * SLOT_Q, 16), SLOT_Q)]

    ctx_c, ctx_q = swap_call(
        seqs,
        ctx_t,
        ctx_rows,
        from_lanes,
        from_query,
        (wide, length),
        (SLOT_Q, wide),
        1,
        "swap_context",
    )
    (
        res_c,
        res_q,
        give_c,
        give_q,
        six_sums,
        up_sums,
        squares,
        out_c,
        out_q,
        keep,
        give,
    ) = mid_call(
        ctx_c,
        ctx_q,
        content[0],
        query_stream[0],
        content_cot[0],
        query_cot[0],
        pad_mask,
        v_all,
        n_one,
        n_up,
        planes,
    )
    core = s % 2
    spot = (lax.axis_index(AXES) // 2) % 4
    flying = give_to(give, count, 1)

    def both(mine, got):
        total = mine.astype(F32) + got.astype(F32)
        return total.astype(BF16).reshape((2, 2, 4, mine.shape[0] // 16, mine.shape[1]))

    def total_of(kept, got):
        total = kept.astype(F32)
        for x in got:
            total += x.astype(F32)
        return total

    def split(x, bit):
        mine = (lax.axis_index(AXES) // bit) % 2
        axis = 0
        away = lax.dynamic_index_in_dim(x, 1 - mine, axis, keepdims=False).astype(BF16)
        return away, lax.dynamic_index_in_dim(x, mine, axis, keepdims=False)

    def block(x, index):
        return lax.dynamic_index_in_dim(x, index, 2, keepdims=False)

    def from_slot(ref, t):
        return ref.at[t]

    g_c, g_q = swap_call(
        seqs,
        give_c,
        give_q,
        from_slot,
        from_slot,
        (wide, length),
        (SLOT_Q, wide),
        2,
        "swap_grads",
    )
    flying = tie(flying, g_c)
    pairs = both(keep, flying)
    cut = pairs.shape[-1] - MODEL_WIDTH
    main, rest = pairs[..., :cut], pairs[..., cut:]
    rest_gone, rest_stay = split(rest, 16)
    gone = tuple(block(main, spot ^ r) for r in (1, 2, 3)) + (rest_gone,)
    flying = tuple(give_to(x, count, bit) for x, bit in zip(gone, (2, 4, 6, 16)))
    stay = (block(main, spot), rest_stay)
    g_c = tie(g_c, stay, gone)
    dq, dk, dv, offs, qoffs = bwd_call(
        span,
        q_t,
        k3,
        k_t,
        v3,
        ctx_t,
        g_c,
        g_q.reshape(seqs * SLOT_Q, wide),
        lse,
        kmeta,
        rseg,
        rlim,
        tiles,
        hot,
        shift,
        qbias,
    )
    flying = tie(flying, dq)

    main_gone, main_stay = split(total_of(stay[0], flying[:3]), 16)
    rest_gone, rest_stay = split(total_of(stay[1], flying[3:]), 8)
    gone, stay = (main_gone, rest_gone), (main_stay, rest_stay)
    flying = (give_to(main_gone, count, 16), give_to(rest_gone, count, 8))
    dq = tie(dq, stay, gone)
    grad_c, grad_q, grad_w, vec_grads, shared = grads_call(
        seqs,
        length,
        SLOT_Q,
        count,
        x_all,
        w_qkv,
        dq,
        dk,
        dv,
        offs,
        qoffs,
        buckets,
        six_sums,
        up_sums,
        squares,
    )
    sum_c, sum_q, sum_w, sum_v, sum_shared = end_call(
        dps,
        seqs,
        grad_c,
        grad_q,
        grad_w.reshape(dps, seqs, shard, 3 * wide),
        vec_grads.reshape(dps, seqs, 8, 128),
        shared,
    )
    flying, sum_c, sum_q, sum_w, sum_v, sum_shared = tie(
        (flying, sum_c, sum_q, sum_w, sum_v, sum_shared)
    )
    main_gone, main_stay = split(total_of(stay[0], flying[:1]), 8)
    rest = total_of(stay[1], flying[1:])
    near = [lax.dynamic_index_in_dim(rest, spot ^ r, 0, keepdims=False) for r in range(4)]
    flying = [give_to(main_gone, count, 8)]
    flying += [give_to(near[r].astype(BF16), count, 2 * r) for r in (1, 2, 3)]
    sum_c, sum_q, sum_w, sum_v, sum_shared = tie(
        (sum_c, sum_q, sum_w, sum_v, sum_shared), main_gone, near
    )
    grad_content = res_c + sum_c
    grad_query = res_q[:preds] + sum_q[:preds]
    grad_qkv_own = jnp.transpose(sum_w.reshape(seqs, shard, 3, wide), (1, 2, 0, 3)).reshape(
        shard, 3 * MODEL_WIDTH
    )
    mine = [sum_v[7, :n_qv], sum_v[6, :n_up]] + [sum_v[i, :n_one] for i in range(6)]
    table_sum = sum_shared[:HEADS, :BUCKETS].T
    totals = sum_shared[16:23, 0]
    content_count = totals[6] * MODEL_WIDTH
    query_count = float(dps * preds * seqs * MODEL_WIDTH)
    each = jnp.stack([content_count, jnp.float32(query_count)])
    stats = jnp.sqrt(totals[:6] / jnp.concatenate([each, each, each]))
    flying = tie(flying, grad_content, grad_query, grad_qkv_own, mine, table_sum, stats)
    pair = jnp.concatenate(
        [total_of(main_stay, flying[:1]), total_of(near[0], flying[1:])], axis=1
    )
    half_ff, half = up_weight.shape[1] // 2, MODEL_WIDTH // 2
    wide_up = half_ff + half
    first, second = pair[:shard], pair[shard:]
    low_cols, high_cols = pair[:, wide_up : wide_up + half_ff // 2], pair[:, wide_up + half_ff // 2 :]

    def pick(a, b):
        return jnp.where(core == 0, a, b), jnp.where(core == 0, b, a)

    rows_mine, rows_away = pick(first[:, :wide_up], second[:, :wide_up])
    cols_mine, cols_away = pick(low_cols, high_cols)
    got = give_to(
        jnp.concatenate([rows_away, cols_away[:shard], cols_away[shard:]], axis=1), count, 1
    )
    rows_got = got[:, :wide_up]
    cols_got = jnp.concatenate(
        [got[:, wide_up : wide_up + half_ff // 2], got[:, wide_up + half_ff // 2 :]], axis=0
    )
    rows_low, rows_high = pick(rows_mine, rows_got)
    grad_up_own = jnp.concatenate([rows_low[:, :half_ff], rows_high[:, :half_ff]], axis=1)
    grad_out_own = jnp.concatenate([rows_low[:, half_ff:], rows_high[:, half_ff:]], axis=1)

    def unfold(x):
        return jnp.concatenate([x[:, :half], x[:, half:]], axis=0)

    cols_low, cols_high = pick(unfold(cols_mine), unfold(cols_got))
    grad_down_own = jnp.concatenate([cols_low, cols_high], axis=1)
    return (
        out_c[None],
        out_q[None],
        grad_content[None],
        grad_query[None],
        grad_qkv_own,
        mine[0],
        grad_out_own,
        mine[2],
        mine[3],
        mine[4],
        grad_up_own,
        mine[1],
        grad_down_own,
        mine[5],
        mine[6],
        mine[7],
        table_sum,
        stats,
    )


def pick_local(mesh):
    sizes = dict(mesh.shape)
    return local_fast if (sizes["dp"], sizes["seq"]) == (8, 4) else local_general


def solution(mesh):
    in_specs = (
        P("dp", "seq", None),
        P("dp", "seq", None),
        P("dp", "seq"),
        P("dp", "seq"),
        P("dp", "seq"),
        P("dp", "seq"),
        P(),
        P(("dp", "seq"), None),
        P(("dp", "seq")),
        P(("dp", "seq"), None),
        P(("dp", "seq")),
        P(("dp", "seq")),
        P(("dp", "seq")),
        P(("dp", "seq"), None),
        P(("dp", "seq")),
        P(("dp", "seq"), None),
        P(("dp", "seq")),
        P(("dp", "seq")),
        P(("dp", "seq")),
        P(),
        P("dp", "seq", None),
        P("dp", "seq", None),
    )
    out_specs = (
        P("dp", "seq", None),
        P("dp", "seq", None),
        P("dp", "seq", None),
        P("dp", "seq", None),
        P(("dp", "seq"), None),
        P(("dp", "seq")),
        P(("dp", "seq"), None),
        P(("dp", "seq")),
        P(("dp", "seq")),
        P(("dp", "seq")),
        P(("dp", "seq"), None),
        P(("dp", "seq")),
        P(("dp", "seq"), None),
        P(("dp", "seq")),
        P(("dp", "seq")),
        P(("dp", "seq")),
        P(),
        P(),
    )
    local = pick_local(mesh)
    return jax.shard_map(local, mesh=mesh, in_specs=in_specs, out_specs=out_specs, check_vma=False)
```

```python
import functools
import math

import jax
import jax.numpy as jnp
from jax import lax
from jax.experimental import pallas as pl
from jax.experimental.pallas import tpu as pltpu
from jax.sharding import PartitionSpec as P

MODEL_WIDTH = 768
HEADS = 12
HEAD_DIM = 64
BUCKETS = 32
SEQ_LEN = 2048


EPS = 1e-05
NEG = -1000000000.0
SCALE = 0.125


def exact_gelu(values):
    return jax.nn.gelu(values, approximate=False)


def norm_fwd(residual, gain_vec, shift_vec):
    row_mean = jnp.mean(residual, axis=-1, keepdims=True)
    centered = residual - row_mean
    inv_std = lax.rsqrt(jnp.mean(centered * centered, axis=-1, keepdims=True) + EPS)
    normed = centered * inv_std
    return (normed * gain_vec + shift_vec, normed, inv_std)


def norm_back(upstream, normed, inv_std, gain_vec):
    grad_norm = upstream * gain_vec
    projected = jnp.mean(grad_norm, axis=-1, keepdims=True) + normed * jnp.mean(
        grad_norm * normed, axis=-1, keepdims=True
    )
    return (
        inv_std * (grad_norm - projected),
        jnp.sum(upstream * normed, axis=(0, 1)),
        jnp.sum(upstream, axis=(0, 1)),
    )


def bucket_edges(rel_bucket):
    entry_count = rel_bucket.shape[0]
    matches = rel_bucket[None, :] == jnp.arange(BUCKETS, dtype=jnp.int32)[:, None]
    places = jnp.arange(entry_count, dtype=jnp.int32)[None, :]
    starts = jnp.min(jnp.where(matches, places, entry_count), axis=1)
    counts = jnp.sum(matches.astype(jnp.int32), axis=1)
    return (starts, starts + counts)


def build_mask(
    query_pos, query_seg, query_limit, content_row, key_pos, key_seg, key_order, key_pad
):
    inside = (
        (query_seg[:, None] == key_seg[None, :])
        & (key_pad[None, :] == 1)
        & (key_order[None, :] <= query_limit[:, None])
    )
    itself = (key_pos[None, :] == query_pos[:, None]) & content_row[:, None]
    return (inside | itself, key_pos[None, :] - query_pos[:, None] + (SEQ_LEN - 1))


def masked_scores(query_heads, key_heads, table_low, edges, allowed, offsets):
    raw_scores = (
        jnp.einsum("rhd,lhd->hrl", query_heads, key_heads, preferred_element_type=jnp.float32)
        * SCALE
    )
    starts, ends = edges
    spread = offsets[..., None]
    onehot = ((spread >= starts) & (spread < ends)).astype(jnp.bfloat16)
    bias = jnp.einsum("rlb,bh->hrl", onehot, table_low, preferred_element_type=jnp.float32)
    return (jnp.where(allowed[None], raw_scores + bias, NEG), onehot)


def attend_forward(packed, table_low, edges, content_row):
    queries, key_values, key_seg, key_order, key_pad, query_pos, query_seg, query_limit = packed
    row_count = queries.shape[0]
    length = key_values.shape[0]
    key_pos = jnp.arange(length, dtype=jnp.int32)
    allowed, offsets = build_mask(
        query_pos, query_seg, query_limit, content_row, key_pos, key_seg, key_order, key_pad
    )
    query_heads = queries.reshape(row_count, HEADS, HEAD_DIM)
    key_heads = key_values[:, :MODEL_WIDTH].reshape(length, HEADS, HEAD_DIM)
    value_heads = key_values[:, MODEL_WIDTH:].reshape(length, HEADS, HEAD_DIM)
    scores, onehot = masked_scores(query_heads, key_heads, table_low, edges, allowed, offsets)
    row_max = jnp.max(scores, axis=-1, keepdims=True)
    expo_vals = jnp.exp(scores - row_max)
    row_total = jnp.sum(expo_vals, axis=-1, keepdims=True)
    probs_low = (expo_vals / row_total).astype(jnp.bfloat16)
    context = jnp.einsum("hrl,lhd->rhd", probs_low, value_heads, preferred_element_type=jnp.float32)
    return (
        context.reshape(row_count, MODEL_WIDTH),
        jnp.transpose((row_max + jnp.log(row_total))[..., 0]),
    )


def attend_backward(packed, table_low, edges, content_row):
    (
        queries,
        key_values,
        key_seg,
        key_order,
        key_pad,
        query_pos,
        query_seg,
        query_limit,
        row_lse,
        grad_context,
    ) = packed
    row_count = queries.shape[0]
    length = key_values.shape[0]
    key_pos = jnp.arange(length, dtype=jnp.int32)
    allowed, offsets = build_mask(
        query_pos, query_seg, query_limit, content_row, key_pos, key_seg, key_order, key_pad
    )
    query_heads = queries.reshape(row_count, HEADS, HEAD_DIM)
    key_heads = key_values[:, :MODEL_WIDTH].reshape(length, HEADS, HEAD_DIM)
    value_heads = key_values[:, MODEL_WIDTH:].reshape(length, HEADS, HEAD_DIM)
    scores, onehot = masked_scores(query_heads, key_heads, table_low, edges, allowed, offsets)
    probs = jnp.exp(scores - jnp.transpose(row_lse)[..., None])
    grad_heads = grad_context.reshape(row_count, HEADS, HEAD_DIM)
    grad_probs = jnp.einsum(
        "rhd,lhd->hrl", grad_heads, value_heads, preferred_element_type=jnp.float32
    )
    row_delta = jnp.sum(probs * grad_probs, axis=-1)
    grad_scores = (probs * (grad_probs - row_delta[..., None])).astype(jnp.bfloat16)
    grad_query = (
        jnp.einsum("hrl,lhd->rhd", grad_scores, key_heads, preferred_element_type=jnp.float32)
        * SCALE
    )
    grad_table = jnp.einsum("hrl,rlb->bh", grad_scores, onehot, preferred_element_type=jnp.float32)
    results = (grad_query.reshape(row_count, MODEL_WIDTH), grad_table, jnp.transpose(row_delta))
    probs_low = probs.astype(jnp.bfloat16)
    grad_key = (
        jnp.einsum("hrl,rhd->lhd", grad_scores, query_heads, preferred_element_type=jnp.float32)
        * SCALE
    )
    grad_value = jnp.einsum(
        "hrl,rhd->lhd", probs_low, grad_heads, preferred_element_type=jnp.float32
    )
    results = results + (
        jnp.concatenate(
            [grad_key.reshape(length, MODEL_WIDTH), grad_value.reshape(length, MODEL_WIDTH)],
            axis=-1,
        ),
    )
    return results


def local_general(
    content,
    query_stream,
    segment_ids,
    pad_mask,
    predicted,
    order,
    rel_bucket,
    qkv_weight,
    qv_bias,
    out_weight,
    out_bias,
    attn_gain,
    attn_shift,
    up_weight,
    up_bias,
    down_weight,
    down_bias,
    ffn_gain,
    ffn_shift,
    rel_table,
    content_cot,
    query_cot,
):
    seq_count = content.shape[0]
    shard_length = content.shape[1]
    pred_count = query_stream.shape[1]
    row_count = shard_length + pred_count
    group_size = lax.axis_size("seq")
    edges = bucket_edges(rel_bucket)
    shards = (
        lax.all_gather(qkv_weight, ("dp", "seq"), axis=0, tiled=True),
        lax.all_gather(out_weight, ("dp", "seq"), axis=0, tiled=True),
        lax.all_gather(up_weight, ("dp", "seq"), axis=0, tiled=True),
        lax.all_gather(down_weight, ("dp", "seq"), axis=0, tiled=True),
        lax.all_gather(qv_bias, ("dp", "seq"), axis=0, tiled=True),
        lax.all_gather(out_bias, ("dp", "seq"), axis=0, tiled=True),
        lax.all_gather(attn_gain, ("dp", "seq"), axis=0, tiled=True),
        lax.all_gather(attn_shift, ("dp", "seq"), axis=0, tiled=True),
        lax.all_gather(up_bias, ("dp", "seq"), axis=0, tiled=True),
        lax.all_gather(down_bias, ("dp", "seq"), axis=0, tiled=True),
        lax.all_gather(ffn_gain, ("dp", "seq"), axis=0, tiled=True),
        lax.all_gather(ffn_shift, ("dp", "seq"), axis=0, tiled=True),
    )
    query_key_value_weight, w_out, w_up, w_down = (shards[0], shards[1], shards[2], shards[3])
    bias_qv, bias_out, first_norm_gain, shift_one, bias_up, bias_down, gain_two, shift_two = [
        member.astype(jnp.float32) for member in shards[4:]
    ]
    all_rows = jnp.concatenate([content, query_stream], axis=1)
    reduced_precision_rows = all_rows.astype(jnp.bfloat16)
    queries = (
        jnp.einsum(
            "srd,de->sre",
            reduced_precision_rows,
            query_key_value_weight[:, :MODEL_WIDTH],
            preferred_element_type=jnp.float32,
        )
        + bias_qv[:MODEL_WIDTH]
    ).astype(jnp.bfloat16)
    value_shift = jnp.concatenate([jnp.zeros((MODEL_WIDTH,), jnp.float32), bias_qv[MODEL_WIDTH:]])
    key_values = (
        jnp.einsum(
            "zci,ip->zcp",
            reduced_precision_rows[:, :shard_length],
            query_key_value_weight[:, MODEL_WIDTH:],
            preferred_element_type=jnp.float32,
        )
        + value_shift
    ).astype(jnp.bfloat16)
    full_pairs, full_seg, full_order, full_pad = (
        lax.all_gather(key_values, "seq", axis=1, tiled=True),
        lax.all_gather(segment_ids, "seq", axis=1, tiled=True),
        lax.all_gather(order, "seq", axis=1, tiled=True),
        lax.all_gather(pad_mask, "seq", axis=1, tiled=True),
    )
    content_pos = lax.axis_index("seq") * shard_length + jnp.arange(shard_length, dtype=jnp.int32)
    query_pos = jnp.concatenate(
        [jnp.broadcast_to(content_pos[None, :], (seq_count, shard_length)), predicted], axis=1
    )
    query_seg = jnp.concatenate(
        [segment_ids, jnp.take_along_axis(full_seg, predicted, axis=1)], axis=1
    )
    query_limit = jnp.concatenate(
        [order, jnp.take_along_axis(full_order, predicted, axis=1) - 1], axis=1
    )
    content_row = jnp.arange(row_count, dtype=jnp.int32) < shard_length
    row_meta = (full_seg, full_order, full_pad, query_pos, query_seg, query_limit)

    def forward_one(packed):
        return attend_forward(packed, rel_table, edges, content_row)

    context, row_lse = lax.map(forward_one, (queries, full_pairs) + row_meta)
    context_low = context.astype(jnp.bfloat16)
    attn_out = (
        jnp.einsum("sre,ed->srd", context_low, w_out, preferred_element_type=jnp.float32) + bias_out
    )
    hidden_one, normed_one, inv_one = norm_fwd(all_rows + attn_out, first_norm_gain, shift_one)
    hidden_low = hidden_one.astype(jnp.bfloat16)
    pre_act = (
        jnp.einsum("srd,df->srf", hidden_low, w_up, preferred_element_type=jnp.float32) + bias_up
    )
    activ, gelu_pull = jax.vjp(exact_gelu, pre_act)
    activ_low = activ.astype(jnp.bfloat16)
    ffn_out = (
        jnp.einsum("srf,fd->srd", activ_low, w_down, preferred_element_type=jnp.float32) + bias_down
    )
    hidden_two, normed_two, inv_two = norm_fwd(hidden_one + ffn_out, gain_two, shift_two)
    pad_float = pad_mask.astype(jnp.float32)
    row_valid = jnp.concatenate(
        [pad_float, jnp.ones((seq_count, pred_count), jnp.float32)], axis=1
    )[..., None]
    outputs = hidden_two * row_valid
    pad_weight = pad_float[..., None]
    local_sums = jnp.stack(
        [
            jnp.sum(pad_weight * content * content),
            jnp.sum(query_stream * query_stream),
            jnp.sum(pad_weight * attn_out[:, :shard_length] * attn_out[:, :shard_length]),
            jnp.sum(attn_out[:, shard_length:] * attn_out[:, shard_length:]),
            jnp.sum(pad_weight * ffn_out[:, :shard_length] * ffn_out[:, :shard_length]),
            jnp.sum(ffn_out[:, shard_length:] * ffn_out[:, shard_length:]),
            jnp.sum(pad_float),
        ]
    )
    back_weights = (
        lax.all_gather(qkv_weight, ("dp", "seq"), axis=0, tiled=True),
        lax.all_gather(out_weight, ("dp", "seq"), axis=0, tiled=True),
        lax.all_gather(up_weight, ("dp", "seq"), axis=0, tiled=True),
        lax.all_gather(down_weight, ("dp", "seq"), axis=0, tiled=True),
        lax.all_gather(attn_gain, ("dp", "seq"), axis=0, tiled=True),
        lax.all_gather(ffn_gain, ("dp", "seq"), axis=0, tiled=True),
    )
    back_pairs = lax.all_gather(key_values, "seq", axis=1, tiled=True)
    backward_query_key_value, back_out, back_up, back_down = (
        back_weights[0],
        back_weights[1],
        back_weights[2],
        back_weights[3],
    )
    back_gain_one = back_weights[4].astype(jnp.float32)
    back_gain_two = back_weights[5].astype(jnp.float32)
    upstream = jnp.concatenate([content_cot, query_cot], axis=1) * row_valid
    grad_res_two, grad_gain_two, grad_shift_two = norm_back(
        upstream, normed_two, inv_two, back_gain_two
    )
    grad_ffn = grad_res_two.astype(jnp.bfloat16)
    grad_bias_down = jnp.sum(grad_ffn, axis=(0, 1), dtype=jnp.float32)
    grad_down = jnp.einsum("srf,srd->fd", activ_low, grad_ffn, preferred_element_type=jnp.float32)
    grad_activ = jnp.einsum("srd,fd->srf", grad_ffn, back_down, preferred_element_type=jnp.float32)
    grad_pre = gelu_pull(grad_activ)[0].astype(jnp.bfloat16)
    grad_bias_up = jnp.sum(grad_pre, axis=(0, 1), dtype=jnp.float32)
    grad_up = jnp.einsum("srd,srf->df", hidden_low, grad_pre, preferred_element_type=jnp.float32)
    grad_hidden = grad_res_two + jnp.einsum(
        "srf,df->srd", grad_pre, back_up, preferred_element_type=jnp.float32
    )
    grad_res_one, grad_gain_one, grad_shift_one = norm_back(
        grad_hidden, normed_one, inv_one, back_gain_one
    )
    grad_attn = grad_res_one.astype(jnp.bfloat16)
    grad_bias_out = jnp.sum(grad_attn, axis=(0, 1), dtype=jnp.float32)
    grad_out = jnp.einsum("sre,srd->ed", context_low, grad_attn, preferred_element_type=jnp.float32)
    grad_context = jnp.einsum(
        "srd,ed->sre", grad_attn, back_out, preferred_element_type=jnp.float32
    ).astype(jnp.bfloat16)

    def backward_all(packed):
        return attend_backward(packed, rel_table, edges, content_row)

    grad_queries, grad_tables, per_row_delta, grad_pairs = lax.map(
        backward_all, (queries, back_pairs) + row_meta + (row_lse, grad_context)
    )
    paired_gradients = lax.psum_scatter(
        grad_pairs.astype(jnp.bfloat16), "seq", scatter_dimension=1, tiled=True
    )
    query_grads = grad_queries.astype(jnp.bfloat16)
    grad_bias_qv = jnp.concatenate(
        [
            jnp.sum(query_grads, axis=(0, 1), dtype=jnp.float32),
            jnp.sum(paired_gradients[..., MODEL_WIDTH:], axis=(0, 1), dtype=jnp.float32),
        ]
    )
    grad_qkv = jnp.concatenate(
        [
            jnp.einsum(
                "srd,sre->de",
                reduced_precision_rows,
                query_grads,
                preferred_element_type=jnp.float32,
            ),
            jnp.einsum(
                "cvi,cvp->ip",
                reduced_precision_rows[:, :shard_length],
                paired_gradients,
                preferred_element_type=jnp.float32,
            ),
        ],
        axis=1,
    )
    grad_rows = grad_res_one + jnp.einsum(
        "sre,de->srd",
        query_grads,
        backward_query_key_value[:, :MODEL_WIDTH],
        preferred_element_type=jnp.float32,
    )
    grad_content = grad_rows[:, :shard_length] + jnp.einsum(
        "zwv,bv->zwb",
        paired_gradients,
        backward_query_key_value[:, MODEL_WIDTH:],
        preferred_element_type=jnp.float32,
    )
    grad_query = grad_rows[:, shard_length:]
    owned = (
        lax.psum_scatter(grad_qkv, ("dp", "seq"), scatter_dimension=0, tiled=True),
        lax.psum_scatter(grad_out, ("dp", "seq"), scatter_dimension=0, tiled=True),
        lax.psum_scatter(grad_up, ("dp", "seq"), scatter_dimension=0, tiled=True),
        lax.psum_scatter(grad_down, ("dp", "seq"), scatter_dimension=0, tiled=True),
        lax.psum_scatter(grad_bias_qv, ("dp", "seq"), scatter_dimension=0, tiled=True),
        lax.psum_scatter(grad_bias_out, ("dp", "seq"), scatter_dimension=0, tiled=True),
        lax.psum_scatter(grad_gain_one, ("dp", "seq"), scatter_dimension=0, tiled=True),
        lax.psum_scatter(grad_shift_one, ("dp", "seq"), scatter_dimension=0, tiled=True),
        lax.psum_scatter(grad_bias_up, ("dp", "seq"), scatter_dimension=0, tiled=True),
        lax.psum_scatter(grad_bias_down, ("dp", "seq"), scatter_dimension=0, tiled=True),
        lax.psum_scatter(grad_gain_two, ("dp", "seq"), scatter_dimension=0, tiled=True),
        lax.psum_scatter(grad_shift_two, ("dp", "seq"), scatter_dimension=0, tiled=True),
    )
    table_sum, totals = lax.psum((jnp.sum(grad_tables, axis=0), local_sums), ("dp", "seq"))
    content_count = totals[6] * MODEL_WIDTH
    query_count = float(seq_count * lax.axis_size("dp") * pred_count * group_size * MODEL_WIDTH)
    stats = jnp.sqrt(
        jnp.stack(
            [
                totals[0] / content_count,
                totals[1] / query_count,
                totals[2] / content_count,
                totals[3] / query_count,
                totals[4] / content_count,
                totals[5] / query_count,
            ]
        )
    )
    return (
        outputs[:, :shard_length],
        outputs[:, shard_length:],
        grad_content,
        grad_query,
        owned[0],
        owned[4],
        owned[1],
        owned[5],
        owned[6],
        owned[7],
        owned[2],
        owned[8],
        owned[3],
        owned[9],
        owned[10],
        owned[11],
        table_sum,
        stats,
    )


LOG2E = math.log2(math.e)
TILE = 256
KEYS = 512
HALF = 128
REACH = 11
DIAGS = 2 * REACH + 1
FAR = 7
WIDE = SEQ_LEN + HALF
MASKED = -1e30
F32 = jnp.float32
BF16 = jnp.bfloat16


def dot_nn(a, b):
    return jnp.dot(a, b, preferred_element_type=F32)


def dot_nt(a, b):
    return lax.dot_general(a, b, (((1,), (1,)), ((), ())), preferred_element_type=F32)


def dot_tn(a, b):
    return lax.dot_general(a, b, (((0,), (0,)), ((), ())), preferred_element_type=F32)


def cost_of(micros):
    return pl.CostEstimate(
        flops=int(micros * 1.0e9), bytes_accessed=int(micros * 1.0e6), transcendentals=0
    )


def bias_kernel(
    rows_q,
    own,
    slot_q,
    heads_ref,
    bucket_ref,
    table_ref,
    ints_ref,
    tile_out,
    qbias_out,
    kmeta_ref,
    rseg_ref,
    rlim_ref,
    hot_ref,
    shift_ref,
    vec_scr,
    ahead_scr,
    fold_scr,
    tile_scr,
    qbias_scr,
    sems,
):
    seqs, length = ints_ref.shape[0], ints_ref.shape[2]
    first = heads_ref[0]
    hot = (
        lax.broadcasted_iota(jnp.int32, (BUCKETS, 2 * SEQ_LEN), 0) == bucket_ref[0:1, :]
    ).astype(BF16)
    vec_scr[...] = dot_tn(table_ref[...], hot)
    hot = (
        lax.broadcasted_iota(jnp.int32, (BUCKETS, 2 * SEQ_LEN), 0) == bucket_ref[1:2, :]
    ).astype(BF16)
    ahead_scr[...] = dot_tn(table_ref[...], hot) * LOG2E
    copies = []
    for h in range(own):
        row = ahead_scr[pl.ds(first + h, 1), :]
        for e in range(REACH - FAR):
            tile_scr[h, e] = jnp.zeros((HALF, HALF), F32)
            tile_scr[h, DIAGS - 1 - e] = jnp.zeros((HALF, HALF), F32)
        for e in range(-FAR, FAR + 1):
            start = HALF * (15 + e)
            skew = pltpu.roll(
                jnp.broadcast_to(row[:, start : start + 2 * HALF], (HALF, 2 * HALF)),
                0,
                1,
                stride=1,
                stride_axis=0,
            )
            tile_scr[h, e + REACH] = skew[:, HALF:].T
        copies.append(pltpu.make_async_copy(tile_scr.at[h], tile_out.at[h], sems.at[h]))
        copies[-1].start()
        vec = vec_scr[pl.ds(first + h, 1), :]
        fold_scr[h] = jnp.concatenate(
            [vec[:, HALF * i : HALF * i + WIDE] for i in range(16)], axis=0
        ).astype(BF16)

    place = lax.broadcasted_iota(jnp.int32, (1, length), 1)
    lane = lax.broadcasted_iota(jnp.int32, (HALF, HALF), 1)
    segs, orders = [], []
    for t in range(seqs):
        seg = ints_ref[t, 0:1, :]
        seg = jnp.where(ints_ref[t, 2:3, :] == 1, seg, -2 - t * length - place)
        order = ints_ref[t, 1:2, :]
        rseg_ref[:, t * length : (t + 1) * length] = seg
        rlim_ref[:, t * length : (t + 1) * length] = order
        for n, row in ((0, seg.astype(F32)), (1, order.astype(F32))):
            for i in range(length // HALF):
                part = row[:, i * HALF : (i + 1) * HALF]
                (segs, orders)[n].append(part)
                kmeta_ref[n, t * length + i * HALF : t * length + (i + 1) * HALF, :] = (
                    jnp.broadcast_to(part, (HALF, HALF)).T.astype(jnp.int32)
                )
    segs = jnp.concatenate(segs, axis=0)
    orders = jnp.concatenate(orders, axis=0)
    preds = [ints_ref[t, 3:4, :slot_q].astype(F32) for t in range(seqs)]
    preds.append(jnp.full((1, rows_q - seqs * slot_q), -1.0, F32))
    preds = jnp.concatenate(preds, axis=1)
    high = lax.Precision.HIGHEST
    for t in range(rows_q // HALF):
        at = slice(t * HALF, (t + 1) * HALF)
        spots = jnp.broadcast_to(preds[:, at], (HALF, HALF)).T.astype(jnp.int32)
        group = jnp.right_shift(spots, 7)
        inside = jnp.bitwise_and(spots, HALF - 1)
        pick = (lane == group)[:, :16].astype(F32)
        for rows, ref, less in ((segs, rseg_ref, 0.0), (orders, rlim_ref, 1.0)):
            spread = jnp.dot(pick, rows, precision=high, preferred_element_type=F32)
            found = jnp.take_along_axis(spread, inside, axis=1) - less
            ref[:, length * seqs + t * HALF : length * seqs + (t + 1) * HALF] = found.T[
                0:1, :
            ].astype(jnp.int32)
        hot_ref[at, :] = (lane == 15 - group)[:, :16].astype(BF16)
        shift_ref[at, :] = HALF - 1 - inside

    for h in range(own):
        for t in range(rows_q // HALF):
            at = slice(t * HALF, (t + 1) * HALF)
            turn = lane + shift_ref[at, :]
            wrap = turn >= HALF
            idx = jnp.where(wrap, turn - HALF, turn)
            spread = dot_nn(hot_ref[at, :], fold_scr[h])
            prev = jnp.take_along_axis(spread[:, :HALF], idx, axis=1)
            for j in range(SEQ_LEN // HALF):
                cur = jnp.take_along_axis(
                    spread[:, (j + 1) * HALF : (j + 2) * HALF], idx, axis=1
                )
                out = jnp.where(wrap, cur, prev) * LOG2E
                qbias_scr[h, j * HALF : (j + 1) * HALF, at] = out.T
                prev = cur
        copies.append(pltpu.make_async_copy(qbias_scr.at[h], qbias_out.at[h], sems.at[own + h]))
        copies[-1].start()
    for copy in copies:
        copy.wait()


def bias_call(own, rows_q, slot_q, first, buckets, table, ints):
    vm = pl.BlockSpec(memory_space=pltpu.VMEM)
    tiles = jax.ShapeDtypeStruct((own, DIAGS, HALF, HALF), F32)
    qbias = jax.ShapeDtypeStruct((own, SEQ_LEN, rows_q), F32)
    rows = jax.ShapeDtypeStruct((1, SEQ_LEN + rows_q), jnp.int32)
    return pl.pallas_call(
        functools.partial(bias_kernel, rows_q, own, slot_q),
        out_shape=(
            tiles,
            qbias,
            jax.ShapeDtypeStruct((2, SEQ_LEN, HALF), jnp.int32),
            rows,
            rows,
            jax.ShapeDtypeStruct((rows_q, 16), BF16),
            jax.ShapeDtypeStruct((rows_q, HALF), jnp.int32),
        ),
        in_specs=[pl.BlockSpec(memory_space=pltpu.SMEM)] + [vm] * 3,
        out_specs=(pl.BlockSpec(memory_space=pltpu.HBM),) * 2 + (vm,) * 5,
        scratch_shapes=[
            pltpu.VMEM((table.shape[1], 2 * SEQ_LEN), F32),
            pltpu.VMEM((table.shape[1], 2 * SEQ_LEN), F32),
            pltpu.VMEM((own, 16, WIDE), BF16),
            pltpu.VMEM(tiles.shape, F32),
            pltpu.VMEM(qbias.shape, F32),
            pltpu.SemaphoreType.DMA((2 * own,)),
        ],
        compiler_params=pltpu.CompilerParams(vmem_limit_bytes=58 << 20),
        cost_estimate=cost_of(12),
        name="bias_tiles",
    )(first, buckets, table, ints)


def bias_block(tile_ref, h, e):
    return jnp.concatenate(
        [
            jnp.concatenate([tile_ref[h, e + i], tile_ref[h, e + i - 1]], axis=1)
            for i in range(KEYS // HALF)
        ],
        axis=0,
    )


def mask_block(kmeta_ref, rseg_ref, rlim_ref, krow, rcol, width):
    kseg = kmeta_ref[0, pl.ds(krow, KEYS), :]
    kord = kmeta_ref[1, pl.ds(krow, KEYS), :]
    parts = []
    for w in range(width // HALF):
        rseg = rseg_ref[:, pl.ds(rcol + w * HALF, HALF)]
        rlim = rlim_ref[:, pl.ds(rcol + w * HALF, HALF)]
        ok = (kseg == rseg) & (kord <= rlim)
        parts.append(jnp.where(ok, 0.0, MASKED))
    return parts[0] if len(parts) == 1 else jnp.concatenate(parts, axis=1)


def fwd_kernel(
    own,
    rows_q,
    span_ref,
    qt_ref,
    k_ref,
    vt_ref,
    kmeta_ref,
    rseg_ref,
    rlim_ref,
    tile_ref,
    qbias_ref,
    ctx_ref,
    rows_ref,
    lse_ref,
    s_scr,
    qbias_scr,
    qbias_sem,
):
    late = pltpu.make_async_copy(qbias_ref, qbias_scr, qbias_sem.at[0])
    late.start()

    def run(rcol, width, lo, steps, bias_of):
        heads = range(own)

        def fold(op, x):
            rows = [x[i * 8 : (i + 1) * 8] for i in range(x.shape[0] // 8)]
            while len(rows) > 1:
                rows = [op(rows[i], rows[i + 1]) for i in range(0, len(rows), 2)]
            return rows[0]

        def score(step, tops):
            kt = lo + step * (KEYS // TILE)
            krow = pl.multiple_of(kt * TILE, TILE)
            mask = mask_block(kmeta_ref, rseg_ref, rlim_ref, krow, rcol, width)
            new = []
            for h in heads:
                s = jnp.dot(
                    k_ref[h, pl.ds(krow, KEYS), :],
                    qt_ref[h * HEAD_DIM : (h + 1) * HEAD_DIM, pl.ds(rcol, width)],
                    preferred_element_type=F32,
                )
                s = s * (SCALE * LOG2E) + (bias_of(h, kt) + mask)
                s_scr[h, pl.ds(krow, KEYS), :width] = s
                new.append(jnp.maximum(tops[h], fold(jnp.maximum, s)))
            return tuple(new)

        tops = lax.fori_loop(
            0, steps, score, tuple(jnp.full((8, width), MASKED, F32) for _ in heads)
        )
        tops = [jnp.max(t, axis=0, keepdims=True) for t in tops]

        def weigh(step, carry):
            kt = lo + step * (KEYS // TILE)
            krow = pl.multiple_of(kt * TILE, TILE)
            sums, accs = carry
            new_sums, new_accs = [], []
            for h in heads:
                p = jnp.exp2(s_scr[h, pl.ds(krow, KEYS), :width] - tops[h])
                new_sums.append(sums[h] + fold(jnp.add, p))
                new_accs.append(
                    accs[h]
                    + jnp.dot(
                        vt_ref[h * HEAD_DIM : (h + 1) * HEAD_DIM, pl.ds(krow, KEYS)],
                        p.astype(BF16),
                        preferred_element_type=F32,
                    )
                )
            return tuple(new_sums), tuple(new_accs)

        sums, accs = lax.fori_loop(
            0,
            steps,
            weigh,
            (
                tuple(jnp.zeros((8, width), F32) for _ in heads),
                tuple(jnp.zeros((HEAD_DIM, width), F32) for _ in heads),
            ),
        )
        outs = []
        for h in heads:
            total = jnp.sum(sums[h], axis=0, keepdims=True)
            outs.append(accs[h] / total)
            lse_ref[h : h + 1, pl.ds(rcol, width)] = tops[h] + jnp.log2(total)
        out = jnp.concatenate(outs, axis=0)
        ctx_ref[:, pl.ds(rcol, width)] = out.astype(BF16)
        return out

    def content_tile(qt, carry):
        def bias_of(h, kt):
            return bias_block(tile_ref, h, 2 * (kt - qt) + REACH)

        run(pl.multiple_of(qt * TILE, TILE), TILE, span_ref[0, qt], span_ref[1, qt], bias_of)
        return carry

    lax.fori_loop(0, SEQ_LEN // TILE, content_tile, 0)

    def query_bias(h, kt):
        return qbias_scr[h, pl.ds(pl.multiple_of(kt * TILE, TILE), KEYS), :]

    late.wait()
    last = SEQ_LEN // TILE
    out = run(SEQ_LEN, rows_q, span_ref[0, last], span_ref[1, last], query_bias)
    rows_ref[...] = out.T.astype(BF16)


def fwd_call(span, qt, k3, vt, kmeta, rseg, rlim, tiles, qbias):
    own = k3.shape[0]
    rows = qt.shape[1]
    rows_q = rows - SEQ_LEN
    vm = pl.BlockSpec(memory_space=pltpu.VMEM)
    return pl.pallas_call(
        functools.partial(fwd_kernel, own, rows_q),
        out_shape=(
            jax.ShapeDtypeStruct((own * HEAD_DIM, rows), BF16),
            jax.ShapeDtypeStruct((rows_q, own * HEAD_DIM), BF16),
            jax.ShapeDtypeStruct((own, rows), F32),
        ),
        in_specs=[pl.BlockSpec(memory_space=pltpu.SMEM)]
        + [vm] * 7
        + [pl.BlockSpec(memory_space=pltpu.HBM)],
        scratch_shapes=[
            pltpu.VMEM((own, SEQ_LEN, max(rows_q, TILE)), F32),
            pltpu.VMEM(qbias.shape, F32),
            pltpu.SemaphoreType.DMA((1,)),
        ],
        compiler_params=pltpu.CompilerParams(vmem_limit_bytes=40 << 20),
        cost_estimate=cost_of(32),
        name="attend",
    )(span, qt, k3, vt, kmeta, rseg, rlim, tiles, qbias)


def bwd_kernel(
    own,
    rows_q,
    span_ref,
    qt_ref,
    k_ref,
    kt_ref,
    v_ref,
    ctx_ref,
    gc_ref,
    gq_ref,
    lse_ref,
    kmeta_ref,
    rseg_ref,
    rlim_ref,
    tile_ref,
    hot_ref,
    shift_ref,
    qbias_ref,
    dq_ref,
    dk_ref,
    dv_ref,
    offs_ref,
    qoffs_ref,
    dk_scr,
    dv_scr,
    dq_scr,
    diag_scr,
    ds_scr,
    delta_scr,
    gt_ref,
    qbias_scr,
    qbias_sem,
):
    late = pltpu.make_async_copy(qbias_ref, qbias_scr, qbias_sem.at[0])
    late.start()
    seqs, length = gc_ref.shape[0], gc_ref.shape[2]
    for t in range(seqs):
        for a in range(0, length, TILE):
            block = gc_ref[t, :, a : a + TILE]
            gt_ref[:, t * length + a : t * length + a + TILE] = block
    used = gq_ref.shape[0]
    block = jnp.concatenate(
        [gq_ref[...].astype(F32), jnp.zeros((rows_q - used, gq_ref.shape[1]), F32)], axis=0
    )
    gt_ref[:, SEQ_LEN:] = block.T.astype(BF16)
    dk_scr[...] = jnp.zeros(dk_scr.shape, F32)
    dv_scr[...] = jnp.zeros(dv_scr.shape, F32)
    diag_scr[...] = jnp.zeros(diag_scr.shape, F32)
    ds_scr[...] = jnp.zeros(ds_scr.shape, BF16)
    for h in range(own):
        part = slice(h * HEAD_DIM, (h + 1) * HEAD_DIM)
        delta_scr[h : h + 1, :] = jnp.sum(
            ctx_ref[part, :].astype(F32) * gt_ref[part, :].astype(F32), axis=0, keepdims=True
        )

    def run(rcol, width, lo, steps, bias_of, keep):
        dq_scr[...] = jnp.zeros(dq_scr.shape, F32)

        def body(step, carry):
            kt = lo + step * (KEYS // TILE)
            krow = pl.multiple_of(kt * TILE, TILE)
            mask = mask_block(kmeta_ref, rseg_ref, rlim_ref, krow, rcol, width)
            for h in range(own):
                part = slice(h * HEAD_DIM, (h + 1) * HEAD_DIM)
                s = jnp.dot(
                    k_ref[h, pl.ds(krow, KEYS), :],
                    qt_ref[part, pl.ds(rcol, width)],
                    preferred_element_type=F32,
                )
                s = s * (SCALE * LOG2E) + (bias_of(h, kt) + mask)
                p = jnp.exp2(s - lse_ref[h : h + 1, pl.ds(rcol, width)])
                gp = jnp.dot(
                    v_ref[h, pl.ds(krow, KEYS), :],
                    gt_ref[part, pl.ds(rcol, width)],
                    preferred_element_type=F32,
                )
                ds = p * (gp - delta_scr[h : h + 1, pl.ds(rcol, width)])
                low = ds.astype(BF16)
                keep(h, kt, ds, low)
                dv_scr[part, pl.ds(krow, KEYS)] += dot_nt(
                    gt_ref[part, pl.ds(rcol, width)], p.astype(BF16)
                )
                dk_scr[part, pl.ds(krow, KEYS)] += dot_nt(qt_ref[part, pl.ds(rcol, width)], low)
                dq_scr[h, :, :width] += jnp.dot(
                    kt_ref[part, pl.ds(krow, KEYS)], low, preferred_element_type=F32
                )
            return carry

        lax.fori_loop(0, steps, body, 0)
        grad = jnp.concatenate([dq_scr[h, :, :width] for h in range(own)], axis=0)
        dq_ref[pl.ds(rcol, width), :] = (grad * SCALE).T.astype(BF16)

    def content_tile(qt, carry):
        def bias_of(h, kt):
            return bias_block(tile_ref, h, 2 * (kt - qt) + REACH)

        def keep(h, kt, ds, low):
            e = 2 * (kt - qt) + REACH
            subs = [ds[i * HALF : (i + 1) * HALF] for i in range(KEYS // HALF)]
            diag_scr[h, e - 1] += subs[0][:, HALF:]
            for i, sub in enumerate(subs):
                here = sub[:, :HALF]
                if i + 1 < len(subs):
                    here = here + subs[i + 1][:, HALF:]
                diag_scr[h, e + i] += here

        run(pl.multiple_of(qt * TILE, TILE), TILE, span_ref[0, qt], span_ref[1, qt], bias_of, keep)
        return carry

    lax.fori_loop(0, SEQ_LEN // TILE, content_tile, 0)

    def query_bias(h, kt):
        return qbias_scr[h, pl.ds(pl.multiple_of(kt * TILE, TILE), KEYS), :]

    def query_keep(h, kt, ds, low):
        ds_scr[h, pl.ds(pl.multiple_of(kt * TILE, TILE), KEYS), :] = low

    late.wait()
    last = SEQ_LEN // TILE
    run(SEQ_LEN, rows_q, span_ref[0, last], span_ref[1, last], query_bias, query_keep)

    for a in range(0, SEQ_LEN, TILE):
        at = slice(a, a + TILE)
        dk_ref[at, :] = (dk_scr[:, at] * SCALE).T.astype(BF16)
        dv_ref[at, :] = dv_scr[:, at].T.astype(BF16)

    offs_ref[...] = jnp.zeros(offs_ref.shape, F32)
    qoffs_ref[...] = jnp.zeros(qoffs_ref.shape, F32)
    lane = lax.broadcasted_iota(jnp.int32, (HALF, HALF), 1)
    turn = lax.broadcasted_iota(jnp.int32, (HALF, HALF), 0) - lane
    over = turn < 0
    turn = jnp.where(over, turn + HALF, turn)
    for h in range(own):
        for e in range(REACH - FAR, REACH + FAR + 1):
            skew = jnp.take_along_axis(diag_scr[h, e], turn, axis=1)
            start = HALF * (15 + e - REACH)
            offs_ref[h : h + 1, start : start + HALF] += jnp.sum(
                jnp.where(over, skew, 0.0), axis=0, keepdims=True
            )
            offs_ref[h : h + 1, start + HALF : start + 2 * HALF] += jnp.sum(
                jnp.where(over, 0.0, skew), axis=0, keepdims=True
            )

    for h in range(own):
        total = jnp.zeros((16, WIDE), F32)
        for t in range(rows_q // HALF):
            shift = shift_ref[t * HALF : (t + 1) * HALF, :]
            place = lane - shift
            low_side = place < 0
            idx = jnp.where(low_side, place + HALF, place)
            prev = jnp.zeros((HALF, HALF), F32)
            pieces = []
            for j in range(SEQ_LEN // HALF + 1):
                if j < SEQ_LEN // HALF:
                    block = ds_scr[h, j * HALF : (j + 1) * HALF, t * HALF : (t + 1) * HALF]
                    cur = jnp.take_along_axis(block.astype(F32).T, idx, axis=1)
                else:
                    cur = jnp.zeros((HALF, HALF), F32)
                pieces.append(jnp.where(low_side, prev, cur).astype(BF16))
                prev = cur
            total += dot_tn(
                hot_ref[t * HALF : (t + 1) * HALF, :], jnp.concatenate(pieces, axis=1)
            )
        for i in range(16):
            qoffs_ref[h : h + 1, HALF * i : HALF * i + WIDE] += total[i : i + 1, :]


def bwd_call(
    span, qt, k3, kt, v3, ctx, g_c, g_q, lse, kmeta, rseg, rlim, tiles, hot, shift, qbias
):
    own = k3.shape[0]
    rows = qt.shape[1]
    rows_q = rows - SEQ_LEN
    vm = pl.BlockSpec(memory_space=pltpu.VMEM)
    return pl.pallas_call(
        functools.partial(bwd_kernel, own, rows_q),
        out_shape=(
            jax.ShapeDtypeStruct((rows, own * HEAD_DIM), BF16),
            jax.ShapeDtypeStruct((SEQ_LEN, own * HEAD_DIM), BF16),
            jax.ShapeDtypeStruct((SEQ_LEN, own * HEAD_DIM), BF16),
            jax.ShapeDtypeStruct((own, 2 * SEQ_LEN), F32),
            jax.ShapeDtypeStruct((own, 2 * SEQ_LEN), F32),
        ),
        in_specs=[pl.BlockSpec(memory_space=pltpu.SMEM)]
        + [vm] * 14
        + [pl.BlockSpec(memory_space=pltpu.HBM)],
        scratch_shapes=[
            pltpu.VMEM((own * HEAD_DIM, SEQ_LEN), F32),
            pltpu.VMEM((own * HEAD_DIM, SEQ_LEN), F32),
            pltpu.VMEM((own, HEAD_DIM, max(rows_q, TILE)), F32),
            pltpu.VMEM((own, DIAGS, HALF, HALF), F32),
            pltpu.VMEM((own, SEQ_LEN, rows_q), BF16),
            pltpu.VMEM((own, rows), F32),
            pltpu.VMEM((own * HEAD_DIM, rows), BF16),
            pltpu.VMEM(qbias.shape, F32),
            pltpu.SemaphoreType.DMA((1,)),
        ],
        compiler_params=pltpu.CompilerParams(vmem_limit_bytes=42 << 20),
        cost_estimate=cost_of(58),
        name="attend_back",
    )(span, qt, k3, kt, v3, ctx, g_c, g_q, lse, kmeta, rseg, rlim, tiles, hot, shift, qbias)


def key_spans(segment, pad_mask):
    length = segment.shape[0]
    real = pad_mask == 1
    head_seg = segment[::TILE]
    tail_seg = segment[TILE - 1 :: TILE]
    starts = jnp.sum((segment[None, :] < head_seg[:, None]).astype(jnp.int32), axis=1)
    first = jnp.arange(0, length, TILE, dtype=jnp.int32)
    lo = jnp.where(real[::TILE], starts, first) // TILE
    hi = jnp.where(real[TILE - 1 :: TILE], tail_seg, first + TILE - 1) // TILE
    count = jnp.sum(pad_mask)
    lo = jnp.concatenate([lo, jnp.zeros((1,), jnp.int32)])
    hi = jnp.concatenate([hi, jnp.maximum(count - 1, 0)[None] // TILE])
    per = KEYS // TILE
    steps = (hi - lo + per) // per
    lo = jnp.minimum(lo, length // TILE - steps * per)
    return jnp.stack([lo, steps]).astype(jnp.int32)


COLS = 768
UP_TOP = (2, 1)
DOWN_TOP = (1, 2)


def place_of(j, top):
    return (
        8 * (j % 2)
        + 4 * ((j // 2) % 2)
        + top[0] * ((j // 4) % 2)
        + top[1] * (j // 8)
    )


def mid_kernel(
    seqs,
    n_one,
    n_up,
    ctx_c,
    ctx_q,
    x_c,
    x_q,
    cot_c,
    cot_q,
    pad_ref,
    v_ref,
    uo_own,
    uo_own_far,
    uo_mate,
    uo_mate_far,
    down_own,
    down_own_far,
    down_mate,
    down_mate_far,
    res_c,
    res_q,
    gctx_c,
    gctx_q,
    six_out,
    up_out,
    sums_ref,
    out_c,
    out_q,
    keep_out,
    give_out,
    w_up,
    w_out,
    w_down,
    one_scr,
    norm_scr,
    inv_scr,
    low_scr,
    act_scr,
    slope_scr,
    sum_scr,
    grad_scr,
    pre_scr,
    plane_scr,
    outc_scr,
    outq_scr,
    parts_scr,
    sq_scr,
    valid_ref,
    xq_scr,
    cotq_scr,
    six_ref,
    bias_up,
    sems,
    plane_sems,
    out_sems,
):
    core = lax.rem(lax.axis_index("seq"), 2)
    this = lax.axis_index("dp") * (seqs // 2) + lax.axis_index("seq") // 2
    near, shard = uo_own.shape[0], uo_own.shape[1]
    chips = 2 * near
    shard_down = down_own.shape[1]
    length = x_c.shape[0]
    preds = x_q.shape[0]
    count = xq_scr.shape[0]
    ff = w_up.shape[1]
    chunks = ff // COLS
    wide = ctx_c.shape[1]
    half_ff, half = ff // 2, COLS // 2
    for d in range(v_ref.shape[0]):
        six_ref[:, d * n_one : (d + 1) * n_one] = v_ref[d, :6, :n_one]
        bias_up[:, d * n_up : (d + 1) * n_up] = v_ref[d, 6:7, :n_up]
    bias_out, gain_one, shift_one, bias_down, gain_two, shift_two = [
        six_ref[i : i + 1, :] for i in range(6)
    ]

    def plane_copies(chunk, slot):
        start = chunk * COLS
        if not isinstance(start, int):
            start = pl.multiple_of(start, COLS)
        return [
            pltpu.make_async_copy(
                ref.at[:, :, pl.ds(start, COLS)],
                plane_scr.at[slot, n // 2, pl.ds(near * (n % 2), near)],
                plane_sems.at[slot, n],
            )
            for n, ref in enumerate((uo_own, uo_own_far, uo_mate, uo_mate_far))
        ]

    def assemble(slot, put_rows):
        def body(j, carry):
            chip = this ^ place_of(j, UP_TOP)
            first = plane_scr[slot, core, j].astype(F32)
            second = plane_scr[slot, 1 - core, j].astype(F32)
            pair = jnp.concatenate([first, second], axis=0).astype(BF16)
            put_rows(pl.ds(pl.multiple_of(2 * shard * chip, 16), 2 * shard), pair)
            return carry

        lax.fori_loop(0, chips, body, 0)

    for chunk, slot in ((chunks, 0), (0, 1)):
        for copy in plane_copies(chunk, slot):
            copy.start()
    copies = []
    for j in range(chips):
        chip = this ^ place_of(j, DOWN_TOP)
        own, mate = ((down_own, down_mate), (down_own_far, down_mate_far))[j // near]
        for side, ref in ((core, own), (1 - core, mate)):
            row = pl.multiple_of((2 * chip + side) * shard_down, 16)
            copies.append(
                pltpu.make_async_copy(
                    ref.at[j % near], w_down.at[pl.ds(row, shard_down)], sems.at[len(copies)]
                )
            )
    for copy in copies:
        copy.start()
    for copy in plane_copies(chunks, 0):
        copy.wait()

    def put_out(rows, pair):
        w_out[rows, :] = pair

    assemble(0, put_out)
    for copy in plane_copies(1, 0):
        copy.start()

    for a in range(0, length, 128):
        row = pad_ref[:, a : a + 128].astype(F32)
        valid_ref[a : a + 128, :] = jnp.broadcast_to(row, (128, 128)).T
    spot = lax.broadcasted_iota(jnp.int32, (count, 128), 0)
    valid_ref[length:, :] = jnp.where(spot < preds, 1.0, 0.0)
    for ref, scr in ((x_q, xq_scr), (cot_q, cotq_scr)):
        scr[...] = jnp.zeros(scr.shape, F32)
        scr[:preds, :] = ref[...]
    blocks = [(0, length // 2), (length // 2, length), (length, length + count)]
    total = length + count
    cut = (total // 2 + 15) // 16 * 16
    halves = [(0, cut), (cut, total)]

    def pick(ref_c, ref_q, a, b):
        return ref_c[a:b, :] if b <= length else ref_q[...]

    def put(ref_c, ref_q, a, b, value):
        if b <= length:
            ref_c[a:b, :] = value
        else:
            ref_q[...] = value[: ref_q.shape[0]]

    def norm(x):
        mean = jnp.mean(x, axis=-1, keepdims=True)
        centered = x - mean
        inv = lax.rsqrt(jnp.mean(centered * centered, axis=-1, keepdims=True) + EPS)
        return centered * inv, inv

    def norm_grad(up, normed, inv, gain):
        grad = up * gain
        proj = jnp.mean(grad, axis=-1, keepdims=True) + normed * jnp.mean(
            grad * normed, axis=-1, keepdims=True
        )
        return inv * (grad - proj)

    sq_scr[...] = jnp.zeros(sq_scr.shape, F32)
    six_out[...] = jnp.zeros(six_out.shape, F32)
    up_out[...] = jnp.zeros(up_out.shape, F32)

    def count_in(k, x, a, b):
        row = k + (1 if b > length else 0)
        sq_scr[row : row + 1, :] += jnp.sum(x * x * valid_ref[a:b, :1], axis=0, keepdims=True)

    def add_row(row, x):
        six_out[row : row + 1, :] += jnp.sum(x, axis=0, keepdims=True)

    for a, b in blocks:
        attn = bias_out
        for t in range(seqs):
            part = w_out[t * wide : (t + 1) * wide, :]
            attn = attn + (
                dot_tn(ctx_c[t, :, a:b], part) if b <= length else dot_nn(ctx_q[t], part)
            )
        x = pick(x_c, xq_scr, a, b)
        count_in(0, x, a, b)
        count_in(2, attn, a, b)
        normed, inv = norm(x + attn)
        one = normed * gain_one + shift_one
        norm_scr[a:b, :] = normed
        inv_scr[a:b, :] = jnp.broadcast_to(inv, (b - a, 128))
        one_scr[a:b, :] = one
        low_scr[a:b, :] = one.astype(BF16)

    for copy in copies:
        copy.wait()
    sum_scr[...] = jnp.zeros(sum_scr.shape, F32)

    def up_step(i, carry):
        cols = pl.ds(pl.multiple_of(i * COLS, COLS), COLS)
        slot = lax.rem(i + 1, 2)
        for copy in plane_copies(i, slot):
            copy.wait()

        def put_up(rows, pair):
            w_up[rows, cols] = pair

        assemble(slot, put_up)

        @pl.when(i + 2 < chunks)
        def _():
            for copy in plane_copies(i + 2, slot):
                copy.start()

        for a, b in halves:
            u = dot_nn(low_scr[a:b, :], w_up[:, cols]) + bias_up[:, cols]
            cdf = 0.5 * (1.0 + lax.erf(u * math.sqrt(0.5)))
            act = (u * cdf).astype(BF16)
            act_scr[a:b, cols] = act
            slope_scr[a:b, cols] = cdf + u * (
                jnp.exp(-0.5 * u * u) * (1.0 / math.sqrt(2.0 * math.pi))
            )
            sum_scr[a:b, :] += dot_nn(act, w_down[cols, :])
        return carry

    lax.fori_loop(0, chunks, up_step, 0)

    for a, b in blocks:
        ffn = sum_scr[a:b, :] + bias_down
        count_in(4, ffn, a, b)
        normed, inv = norm(one_scr[a:b, :] + ffn)
        ok = valid_ref[a:b, :1]
        put(outc_scr, outq_scr, a, b, (normed * gain_two + shift_two) * ok)
        up = pick(cot_c, cotq_scr, a, b) * ok
        add_row(4, up * normed)
        add_row(5, up)
        grad = norm_grad(up, normed, inv, gain_two)
        low = grad.astype(BF16)
        add_row(3, low.astype(F32))
        sum_scr[a:b, :] = grad
        grad_scr[a:b, :] = low
    leaving = [
        pltpu.make_async_copy(outc_scr, out_c, out_sems.at[0]),
        pltpu.make_async_copy(outq_scr, out_q, out_sems.at[1]),
    ]
    for copy in leaving:
        copy.start()

    def start(copy_of, h):
        @pl.when(core == h)
        def _():
            copy_of(keep_out).start()

        @pl.when(core != h)
        def _():
            copy_of(give_out).start()

    def up_copy(i, out):
        h, at = i // 2, lax.rem(i, 2) if not isinstance(i, int) else i % 2
        cols = pl.ds(pl.multiple_of(at * COLS, COLS) if not isinstance(i, int) else at * COLS, COLS)
        return pltpu.make_async_copy(
            parts_scr.at[h, :, cols], out.at[:, cols], out_sems.at[2 + i]
        )

    down_rows = 2 * shard * (COLS // (2 * shard_down))
    down_cols = pl.ds(half_ff + half, half_ff)

    def down_copy(i, h, out):
        start = i * down_rows
        rows = pl.ds(start if isinstance(i, int) else pl.multiple_of(start, down_rows), down_rows)
        return pltpu.make_async_copy(
            parts_scr.at[h, rows, down_cols],
            out.at[rows, down_cols],
            out_sems.at[2 + chunks * (1 + h) + i],
        )

    def back_step(i, carry):
        cols = pl.ds(pl.multiple_of(i * COLS, COLS), COLS)
        for a, b in halves:
            low = (
                dot_nt(grad_scr[a:b, :], w_down[cols, :]) * slope_scr[a:b, cols]
            ).astype(BF16)
            pre_scr[a:b, :] = low
            up_out[:, cols] += jnp.sum(low.astype(F32), axis=0, keepdims=True)
            sum_scr[a:b, :] += dot_nt(low, w_up[:, cols])
        at = pl.ds(pl.multiple_of(lax.rem(i, 2) * COLS, COLS), COLS)
        parts_scr[i // 2, :, at] = dot_tn(low_scr[...], pre_scr[...]).astype(BF16)
        start(lambda out: up_copy(i, out), i // 2)
        grads = dot_tn(act_scr[:, cols], grad_scr[...]).astype(BF16)
        for h in range(2):
            for chip in range(COLS // (2 * shard_down)):
                to = pl.ds(pl.multiple_of(i * down_rows, down_rows) + chip * 2 * shard, 2 * shard)
                for g in range(shard_down // shard):
                    row = 2 * shard_down * chip + 2 * shard * g
                    col = half_ff + half * (1 + g)
                    parts_scr[h, to, col : col + half] = grads[
                        row : row + 2 * shard, h * half : (h + 1) * half
                    ]
            start(lambda out: down_copy(i, h, out), h)
        return carry

    lax.fori_loop(0, chunks, back_step, 0)
    leaving += [up_copy(i, keep_out) for i in range(chunks)]
    leaving += [down_copy(i, h, keep_out) for i in range(chunks) for h in range(2)]

    for a, b in blocks:
        up = sum_scr[a:b, :]
        normed = norm_scr[a:b, :]
        add_row(1, up * normed)
        add_row(2, up)
        grad = norm_grad(up, normed, inv_scr[a:b, :1], gain_one)
        low = grad.astype(BF16)
        add_row(0, low.astype(F32))
        put(res_c, res_q, a, b, grad)
        grad_scr[a:b, :] = low
    for t in range(seqs):
        rows = slice(t * wide, (t + 1) * wide)
        part = w_out[rows, :]
        gctx_c[t] = dot_nt(part, grad_scr[:length, :]).astype(BF16)
        gctx_q[t] = dot_nt(grad_scr[length:, :], part).astype(BF16)
        grads = (
            dot_nn(ctx_c[t], grad_scr[:length, :]) + dot_tn(ctx_q[t], grad_scr[length:, :])
        ).astype(BF16)
        for h in range(2):
            parts_scr[h, rows, half_ff : half_ff + half] = grads[:, h * half : (h + 1) * half]
    tail = pl.ds(half_ff, half)

    def tail_copy(h, out):
        return pltpu.make_async_copy(
            parts_scr.at[h, :, tail], out.at[:, tail], out_sems.at[2 + 3 * chunks + h]
        )

    for h in range(2):
        start(lambda out: tail_copy(h, out), h)
    leaving += [tail_copy(h, keep_out) for h in range(2)]
    sq_scr[6:7, :] = jnp.sum(
        jnp.where(lax.broadcasted_iota(jnp.int32, (length, COLS), 1) == 0, valid_ref[:length, :1], 0.0),
        axis=0,
        keepdims=True,
    )
    sums_ref[...] = jnp.broadcast_to(jnp.sum(sq_scr[...], axis=1, keepdims=True), sums_ref.shape)
    for copy in leaving:
        copy.wait()


def mid_call(ctx_c, ctx_q, x_c, x_q, cot_c, cot_q, pad, v_all, n_one, n_up, planes):
    seqs, wide, length = ctx_c.shape
    count = ctx_q.shape[1]
    preds = x_q.shape[0]
    total = length + count
    near, shard, cols = planes[0].shape
    chips = 2 * near
    ff = cols - COLS
    chunks = ff // COLS
    vm = pl.BlockSpec(memory_space=pltpu.VMEM)
    anywhere = pl.BlockSpec(memory_space=pl.ANY)
    parts = jax.ShapeDtypeStruct((COLS, (cols + ff) // 2), BF16)
    return pl.pallas_call(
        functools.partial(mid_kernel, seqs, n_one, n_up),
        out_shape=(
            jax.ShapeDtypeStruct(x_c.shape, F32),
            jax.ShapeDtypeStruct((count, COLS), F32),
            jax.ShapeDtypeStruct(ctx_c.shape, BF16),
            jax.ShapeDtypeStruct(ctx_q.shape, BF16),
            jax.ShapeDtypeStruct((6, COLS), F32),
            jax.ShapeDtypeStruct((1, ff), F32),
            jax.ShapeDtypeStruct((8, 128), F32),
            jax.ShapeDtypeStruct(x_c.shape, F32),
            jax.ShapeDtypeStruct((preds, COLS), F32),
            parts,
            parts,
        ),
        in_specs=[vm] * 8 + [anywhere] * 8,
        out_specs=(vm,) * 7 + (anywhere,) * 4,
        scratch_shapes=[
            pltpu.VMEM((COLS, ff), BF16),
            pltpu.VMEM((COLS, COLS), BF16),
            pltpu.VMEM((ff, COLS), BF16),
            pltpu.VMEM((total, COLS), F32),
            pltpu.VMEM((total, COLS), F32),
            pltpu.VMEM((total, 128), F32),
            pltpu.VMEM((total, COLS), BF16),
            pltpu.VMEM((total, ff), BF16),
            pltpu.VMEM((total, ff), F32),
            pltpu.VMEM((total, COLS), F32),
            pltpu.VMEM((total, COLS), BF16),
            pltpu.VMEM((total, COLS), BF16),
            pltpu.VMEM((2, 2, chips, shard, COLS), BF16),
            pltpu.VMEM(x_c.shape, F32),
            pltpu.VMEM((preds, COLS), F32),
            pltpu.VMEM((2,) + parts.shape, BF16),
            pltpu.VMEM((8, COLS), F32),
            pltpu.VMEM((total, 128), F32),
            pltpu.VMEM((count, COLS), F32),
            pltpu.VMEM((count, COLS), F32),
            pltpu.VMEM((6, COLS), F32),
            pltpu.VMEM((1, ff), F32),
            pltpu.SemaphoreType.DMA((2 * chips,)),
            pltpu.SemaphoreType.DMA((2, 4)),
            pltpu.SemaphoreType.DMA((4 + 3 * chunks,)),
        ],
        compiler_params=pltpu.CompilerParams(vmem_limit_bytes=63 << 20),
        cost_estimate=cost_of(45),
        name="feed_forward",
    )(ctx_c, ctx_q, x_c, x_q, cot_c, cot_q, pad, v_all, *planes)


def proj_kernel(
    own, keys, n_qv, x_ref, w_ref, vec_ref, qt_ref, k_ref, kt_ref, v_ref, vt_ref, bq_ref, bv_ref
):
    wide = own * HEAD_DIM
    first = lax.axis_index("seq") * (wide // n_qv)
    for ref, start in ((bq_ref, first), (bv_ref, first + vec_ref.shape[0] // 2)):
        for i in range(wide // n_qv):
            ref[:, i * n_qv : (i + 1) * n_qv] = vec_ref[start + i, 7:8, :n_qv]
    rows = x_ref.shape[0]
    for a in range(0, rows, 256):
        b = min(a + 256, rows)
        parts = [(0, bq_ref, qt_ref, None)]
        if b <= keys:
            parts += [(1, None, kt_ref, k_ref), (2, bv_ref, vt_ref, v_ref)]
        y = dot_nn(x_ref[a:b, :], w_ref[:, : len(parts) * wide])
        for n, bias, flat_ref, head_ref in parts:
            part = y[:, n * wide : (n + 1) * wide]
            if bias is not None:
                part = part + bias[...]
            flat_ref[:, a:b] = part.T.astype(BF16)
            for h in range(own if head_ref is not None else 0):
                head_ref[h, a:b, :] = part[:, h * HEAD_DIM : (h + 1) * HEAD_DIM].astype(BF16)


def proj_call(own, keys, x, w, vec, n_qv):
    rows = x.shape[0]
    wide = own * HEAD_DIM
    vm = pl.BlockSpec(memory_space=pltpu.VMEM)
    flat = lambda n: jax.ShapeDtypeStruct((wide, n), BF16)
    head = lambda n: jax.ShapeDtypeStruct((own, n, HEAD_DIM), BF16)
    return pl.pallas_call(
        functools.partial(proj_kernel, own, keys, n_qv),
        out_shape=(flat(rows), head(keys), flat(keys), head(keys), flat(keys)),
        in_specs=[vm] * 3,
        out_specs=(vm,) * 5,
        scratch_shapes=[pltpu.VMEM((1, wide), F32)] * 2,
        compiler_params=pltpu.CompilerParams(vmem_limit_bytes=20 << 20),
        cost_estimate=cost_of(5),
        name="project",
    )(x, w, vec)


def grads_kernel(
    keys,
    x_ref,
    w_ref,
    dq_ref,
    dk_ref,
    dv_ref,
    offs_ref,
    qoffs_ref,
    bucket_ref,
    six_ref,
    up_ref,
    squares_ref,
    gc_ref,
    gq_ref,
    gw_ref,
    vec_ref,
    shared_ref,
    part_scr,
):
    s = lax.axis_index("seq")
    wide = dq_ref.shape[1]
    seqs, length = gc_ref.shape[:2]
    shard = gw_ref.shape[1]
    for n, ref in enumerate((dq_ref, dk_ref, dv_ref)):
        part_scr[:, n * wide : (n + 1) * wide] = dot_tn(x_ref[: ref.shape[0], :], ref[...])
    for j in range(gw_ref.shape[0]):
        gw_ref[j] = part_scr[j * shard : (j + 1) * shard, :].astype(BF16)
    blocks = vec_ref.shape[0]
    n_one, n_up = six_ref.shape[1] // blocks, up_ref.shape[1] // blocks
    n_qv = 2 * n_one
    vec_ref[...] = jnp.zeros(vec_ref.shape, F32)
    sums = [jnp.sum(ref[...].astype(F32), axis=0, keepdims=True) for ref in (dq_ref, dv_ref)]
    for d in range(blocks):
        vec_ref[d, :6, :n_one] = six_ref[:, d * n_one : (d + 1) * n_one]
        vec_ref[d, 6:7, :n_up] = up_ref[:, d * n_up : (d + 1) * n_up]
        kind, start = divmod(d * n_qv, seqs * wide)
        owner, start = divmod(start, wide)
        piece = sums[kind][:, start : start + n_qv]
        vec_ref[d, 7:8, :n_qv] = jnp.where(s == owner, piece, 0.0)
    own = offs_ref.shape[0]
    table = jnp.zeros((own, BUCKETS), F32)
    for row, ref in ((1, offs_ref), (0, qoffs_ref)):
        hot = (
            lax.broadcasted_iota(jnp.int32, (BUCKETS, ref.shape[1]), 0)
            == bucket_ref[row : row + 1, :]
        ).astype(F32)
        table += lax.dot_general(
            ref[...],
            hot,
            (((1,), (1,)), ((), ())),
            precision=lax.Precision.HIGHEST,
            preferred_element_type=F32,
        )
    shared_ref[...] = jnp.zeros(shared_ref.shape, F32)
    for h in range(own):
        shared_ref[pl.ds(s * own + h, 1), :BUCKETS] = table[h : h + 1]
    shared_ref[16:24, :] = squares_ref[...]
    w_q = w_ref[:, :wide]
    w_k = w_ref[:, wide : 2 * wide]
    w_v = w_ref[:, 2 * wide :]
    step = 256
    for t in range(seqs):
        for a in range(0, length, step):
            at = slice(t * length + a, t * length + a + step)
            gc_ref[t, a : a + step, :] = (
                dot_nt(dq_ref[at, :], w_q) + dot_nt(dk_ref[at, :], w_k) + dot_nt(dv_ref[at, :], w_v)
            ).astype(BF16)
    count = gq_ref.shape[1]
    for t in range(seqs):
        at = slice(keys + t * count, keys + (t + 1) * count)
        gq_ref[t] = dot_nt(dq_ref[at, :], w_q).astype(BF16)


def grads_call(
    seqs, length, count, blocks, x, w, dq, dk, dv, offs, qoffs, buckets, six, up, squares
):
    wide = dq.shape[1]
    shard = x.shape[1] // blocks
    vm = pl.BlockSpec(memory_space=pltpu.VMEM)
    return pl.pallas_call(
        functools.partial(grads_kernel, seqs * length),
        out_shape=(
            jax.ShapeDtypeStruct((seqs, length, x.shape[1]), BF16),
            jax.ShapeDtypeStruct((seqs, count, x.shape[1]), BF16),
            jax.ShapeDtypeStruct((blocks, shard, 3 * wide), BF16),
            jax.ShapeDtypeStruct((blocks, 8, 128), F32),
            jax.ShapeDtypeStruct((24, 128), F32),
        ),
        in_specs=[vm] * 11,
        out_specs=(vm,) * 5,
        scratch_shapes=[pltpu.VMEM((x.shape[1], 3 * wide), F32)],
        compiler_params=pltpu.CompilerParams(vmem_limit_bytes=28 << 20),
        cost_estimate=cost_of(6),
        name="weight_grads",
    )(x, w, dq, dk, dv, offs, qoffs, buckets, six, up, squares)


MESH = pl.DeviceIdType.MESH
ROWS_Q = 384
SLOT_Q = 80


def greet(devices):
    barrier = pltpu.get_barrier_semaphore()
    for device in devices:
        pl.semaphore_signal(barrier, inc=1, device_id=device, device_id_type=MESH)
    pl.semaphore_wait(barrier, len(devices))


def remote(src, dst, send_sem, recv_sem, k, device):
    return pltpu.make_async_remote_copy(
        src_ref=src,
        dst_ref=dst,
        send_sem=send_sem.at[k],
        recv_sem=recv_sem.at[k],
        device_id=device,
        device_id_type=MESH,
    )


def start_kernel(
    dps,
    seqs,
    c_ref,
    q_ref,
    w_ref,
    v_ref,
    seg_ref,
    order_ref,
    pad_ref,
    pred_ref,
    x_out,
    w_out,
    v_out,
    i_out,
    c_scr,
    q_scr,
    qlow_scr,
    zero_scr,
    send_sem,
    recv_sem,
    here_sem,
):
    dp = lax.axis_index("dp")
    s = lax.axis_index("seq")
    length = c_ref.shape[0]
    count = q_scr.shape[0]
    mate = s + 1 - 2 * lax.rem(s, 2)
    across = lax.rem(s + 2, seqs)
    level = dp + 1 - 2 * lax.rem(dp, 2)
    stacks = dps // 2
    greet(
        [(dp, lax.rem(s + r, seqs)) for r in range(1, seqs)]
        + [(level, s)]
        + [(lax.rem(dp + 2 * r, dps), s) for r in range(1, stacks)]
    )

    def at_c(owner):
        return pl.ds(pl.multiple_of(owner * length, length), length)

    def at_q(owner):
        return pl.ds(pl.multiple_of(seqs * length + owner * count, 16), count)

    k = 0

    def push(src, dst, device):
        nonlocal k
        copy = remote(src, dst, send_sem, recv_sem, k, device)
        copy.start()
        k += 1
        return copy

    i_out[s] = jnp.zeros(i_out.shape[1:], jnp.int32)
    for n, ref in enumerate((seg_ref, order_ref, pad_ref)):
        i_out[s, n : n + 1, :] = ref[...]
    i_out[s, 3:4, :] = jnp.full((1, length), -1, jnp.int32)
    i_out[s, 3:4, : pred_ref.shape[1]] = pred_ref[...]
    small = []
    for r in range(1, seqs):
        to = lax.rem(s + r, seqs)
        small.append(push(w_ref.at[to], w_out.at[dp, s], (dp, to)))
        small.append(push(v_ref, v_out.at[dp, s], (dp, to)))
        small.append(push(i_out.at[s], i_out.at[s], (dp, to)))
    c_scr[...] = c_ref[...].astype(BF16)
    far = [push(c_scr, x_out.at[at_c(s)], (dp, across))]
    q_scr[...] = jnp.zeros(q_scr.shape, F32)
    q_scr[: q_ref.shape[0], :] = q_ref[...]
    qlow_scr[...] = q_scr[...].astype(BF16)
    far.append(push(qlow_scr, x_out.at[at_q(s)], (dp, across)))
    near = [
        push(scr, x_out.at[at(s)], (dp, mate)) for scr, at in ((c_scr, at_c), (qlow_scr, at_q))
    ]
    v_out[dp, s] = v_ref[...]
    zero_scr[...] = jnp.zeros(zero_scr.shape, BF16)
    here = [
        pltpu.make_async_copy(src, dst, here_sem.at[n])
        for n, (src, dst) in enumerate(
            (
                (w_ref.at[s], w_out.at[dp, s]),
                (c_scr, x_out.at[at_c(s)]),
                (qlow_scr, x_out.at[at_q(s)]),
                (zero_scr, x_out.at[pl.ds(seqs * (length + count), zero_scr.shape[0])]),
            )
        )
    ]
    for copy in here:
        copy.start()
    for copy in here:
        copy.wait()
    for copy in small:
        copy.wait_recv()
    wide, flat = [], []
    for r in range(1, stacks):
        to = lax.rem(dp + 2 * r, dps)
        wide.append([push(ref.at[dp], ref.at[dp], (to, s)) for ref in (w_out, v_out)])
    flat += [push(ref.at[dp], ref.at[dp], (level, s)) for ref in (w_out, v_out)]
    for r in range(1, stacks):
        source = lax.rem(dp + dps - 2 * r, dps)
        for copy, ref in zip(wide[r - 1], (w_out, v_out)):
            copy.wait_recv()
            flat.append(push(ref.at[source], ref.at[source], (level, s)))
    pass_on = []
    for copy, at in zip(far, (at_c, at_q)):
        copy.wait_recv()
        pass_on.append(push(x_out.at[at(across)], x_out.at[at(across)], (dp, mate)))
    for copy in near + flat + pass_on:
        copy.wait_recv()
    for copy in small + far + near + flat + pass_on + sum(wide, []):
        copy.wait_send()


def start_call(dps, seqs, content, query, w, v, metas, slot_q):
    copies = 3 * (seqs - 1) + 4 + 2 * (dps // 2 - 1) + dps + 2
    length, width = content.shape
    vmem = pl.BlockSpec(memory_space=pltpu.VMEM)
    return pl.pallas_call(
        functools.partial(start_kernel, dps, seqs),
        out_shape=(
            jax.ShapeDtypeStruct((seqs * length + ROWS_Q, width), BF16),
            jax.ShapeDtypeStruct((dps,) + w.shape, BF16),
            jax.ShapeDtypeStruct((dps, seqs) + v.shape, F32),
            jax.ShapeDtypeStruct((seqs, 8, length), jnp.int32),
        ),
        in_specs=[vmem] * 8,
        out_specs=(pl.BlockSpec(memory_space=pltpu.HBM),) * 2 + (vmem,) * 2,
        scratch_shapes=[
            pltpu.VMEM((length, width), BF16),
            pltpu.VMEM((slot_q, width), F32),
            pltpu.VMEM((slot_q, width), BF16),
            pltpu.VMEM((ROWS_Q - seqs * slot_q, width), BF16),
            pltpu.SemaphoreType.DMA((copies,)),
            pltpu.SemaphoreType.DMA((copies,)),
            pltpu.SemaphoreType.DMA((4,)),
        ],
        compiler_params=pltpu.CompilerParams(
            collective_id=0, has_side_effects=True, vmem_limit_bytes=16 << 20
        ),
        cost_estimate=cost_of(30),
        name="gather_rows",
    )(content, query, w, v, *metas)


def swap_kernel(seqs, c_of, q_of, c_ref, q_ref, c_out, q_out, send_sem, recv_sem, here_sem):
    dp = lax.axis_index("dp")
    s = lax.axis_index("seq")
    greet([(dp, lax.rem(s + r, seqs)) for r in range(1, seqs)])
    copies = []
    for r in range(1, seqs):
        to = lax.rem(s + r, seqs)
        k = 2 * (r - 1)
        copies.append(remote(c_of(c_ref, to), c_out.at[s], send_sem, recv_sem, k, (dp, to)))
        copies.append(remote(q_of(q_ref, to), q_out.at[s], send_sem, recv_sem, k + 1, (dp, to)))
    for copy in copies:
        copy.start()
    here = [
        pltpu.make_async_copy(c_of(c_ref, s), c_out.at[s], here_sem.at[0]),
        pltpu.make_async_copy(q_of(q_ref, s), q_out.at[s], here_sem.at[1]),
    ]
    for copy in here:
        copy.start()
    for copy in here + copies:
        copy.wait()


def swap_call(seqs, c, q, c_of, q_of, c_shape, q_shape, ident, name):
    vmem = pl.BlockSpec(memory_space=pltpu.VMEM)
    return pl.pallas_call(
        functools.partial(swap_kernel, seqs, c_of, q_of),
        out_shape=(
            jax.ShapeDtypeStruct((seqs,) + c_shape, c.dtype),
            jax.ShapeDtypeStruct((seqs,) + q_shape, q.dtype),
        ),
        in_specs=[vmem] * 2,
        out_specs=(vmem,) * 2,
        scratch_shapes=[
            pltpu.SemaphoreType.DMA((2 * (seqs - 1),)),
            pltpu.SemaphoreType.DMA((2 * (seqs - 1),)),
            pltpu.SemaphoreType.DMA((2,)),
        ],
        compiler_params=pltpu.CompilerParams(collective_id=ident, has_side_effects=True),
        cost_estimate=cost_of(12),
        name=name,
    )(c, q)


def end_kernel(
    dps,
    seqs,
    gc_ref,
    gq_ref,
    w_ref,
    v_ref,
    sh_ref,
    gc_out,
    gq_out,
    w_out,
    v_out,
    sh_out,
    c_mate,
    q_mate,
    c_far,
    q_far,
    c_send,
    q_send,
    w_flat,
    v_flat,
    sh_flat,
    w_send,
    v_send,
    sh_send,
    w_got,
    v_got,
    sh_got,
    w_sum,
    v_sum,
    sh_sum,
    v_last,
    sh_last,
    send_sem,
    recv_sem,
):
    dp = lax.axis_index("dp")
    s = lax.axis_index("seq")
    core = lax.rem(s, 2)
    mate = s + 1 - 2 * core
    across = lax.rem(s + 2, seqs)
    side = lax.rem(dp, 2)
    level = dp + 1 - 2 * side
    stacks = dps // 2
    greet(
        [(dp, lax.rem(s + r, seqs)) for r in range(1, seqs)]
        + [(level, s)]
        + [(lax.rem(dp + 2 * r, dps), s) for r in range(1, stacks)]
    )
    k = 0

    def push(src, dst, device):
        nonlocal k
        copy = remote(src, dst, send_sem, recv_sem, k, device)
        copy.start()
        k += 1
        return copy

    def each(ref, step, fn):
        def body(i, carry):
            fn(pl.ds(pl.multiple_of(i * step, step), step))
            return carry

        lax.fori_loop(0, ref.shape[-2] // step, body, 0)

    first = []
    for i in range(2):
        to = lax.rem(mate + 2 * (1 - i), seqs)
        for src, dst in ((gc_ref, c_mate), (gq_ref, q_mate)):
            first.append(push(src.at[to], dst.at[i], (dp, mate)))
    flat = []
    for r in list(range(1, stacks)) + [0]:
        to = lax.rem(level + 2 * r, dps)
        flat.append(
            [push(src.at[to], dst.at[r], (level, s)) for src, dst in ((w_ref, w_flat), (v_ref, v_flat))]
        )
    shared = push(sh_ref, sh_flat, (level, s))
    cross = []
    for (src, got, buf, far, copy) in (
        (gc_ref, c_mate, c_send, c_far, first[0]),
        (gq_ref, q_mate, q_send, q_far, first[1]),
    ):
        copy.wait_recv()

        def add(rows, src=src, got=got, buf=buf):
            buf[rows, :] = (
                src[across, rows, :].astype(F32) + got[0, rows, :].astype(F32)
            ).astype(BF16)

        each(buf, 16, add)
        cross.append(push(buf, far, (dp, across)))
    shared.wait_recv()
    sh_send[...] = sh_ref[...] + sh_flat[...]
    tall = []
    for r in range(1, stacks):
        for copy in flat[r - 1]:
            copy.wait_recv()
        to = lax.rem(dp + 2 * r, dps)

        def add_pair(rows, to=to, r=r):
            for t in range(seqs):
                w_send[r - 1, t, rows, :] = (
                    w_ref[to, t, rows, :].astype(F32) + w_flat[r, t, rows, :].astype(F32)
                ).astype(BF16)

        each(w_sum, 24, add_pair)
        v_send[r - 1] = v_ref[to] + v_flat[r]
        for src, dst in (
            (w_send.at[r - 1], w_got.at[r - 1]),
            (v_send.at[r - 1], v_got.at[r - 1]),
            (sh_send, sh_got.at[r - 1]),
        ):
            tall.append(push(src, dst, (to, s)))
    for copy in flat[stacks - 1] + tall:
        copy.wait_recv()

    def add_w(rows):
        for t in range(seqs):
            total = w_ref[dp, t, rows, :].astype(F32) + w_flat[0, t, rows, :].astype(F32)
            for r in range(1, stacks):
                total += w_got[r - 1, t, rows, :].astype(F32)
            w_sum[t, rows, :] = total

    each(w_sum, 24, add_w)
    total = v_ref[dp] + v_flat[0]
    for r in range(1, stacks):
        total += v_got[r - 1]
    v_sum[...] = total
    total = sh_send[...]
    for r in range(1, stacks):
        total += sh_got[r - 1]
    sh_sum[...] = total
    last = []
    for r in range(1, seqs):
        to = lax.rem(s + r, seqs)
        last.append(push(w_sum.at[to], w_out.at[s], (dp, to)))
        last.append(push(v_sum.at[to], v_last.at[r - 1], (dp, to)))
        last.append(push(sh_sum, sh_last.at[r - 1], (dp, to)))
    w_out[s] = w_sum[s]
    for copy in first[2:] + cross:
        copy.wait_recv()
    for (src, got, far, out) in (
        (gc_ref, c_mate, c_far, gc_out),
        (gq_ref, q_mate, q_far, gq_out),
    ):

        def total_of(rows, src=src, got=got, far=far, out=out):
            out[rows, :] = (
                src[s, rows, :].astype(F32)
                + got[1, rows, :].astype(F32)
                + far[rows, :].astype(F32)
            )

        each(out, 16, total_of)
    for copy in last:
        copy.wait_recv()
    total = v_sum[s]
    for r in range(1, seqs):
        total += v_last[r - 1]
    v_out[...] = total
    total = sh_sum[...]
    for r in range(1, seqs):
        total += sh_last[r - 1]
    sh_out[...] = total
    for copy in first + sum(flat, []) + [shared] + cross + tall + last:
        copy.wait_send()


def end_call(dps, seqs, gc, gq, w, v, sh):
    stacks = dps // 2
    copies = 4 + 2 * stacks + 1 + 2 + 3 * (stacks - 1) + 3 * (seqs - 1)
    vm = pl.BlockSpec(memory_space=pltpu.VMEM)
    cshape, qshape, wshape, vshape = gc.shape[1:], gq.shape[1:], w.shape[1:], v.shape[1:]
    return pl.pallas_call(
        functools.partial(end_kernel, dps, seqs),
        out_shape=(
            jax.ShapeDtypeStruct(cshape, F32),
            jax.ShapeDtypeStruct(qshape, F32),
            jax.ShapeDtypeStruct(wshape, F32),
            jax.ShapeDtypeStruct(vshape[1:], F32),
            jax.ShapeDtypeStruct(sh.shape, F32),
        ),
        in_specs=[vm] * 5,
        out_specs=(vm,) * 5,
        scratch_shapes=[
            pltpu.VMEM((2,) + cshape, BF16),
            pltpu.VMEM((2,) + qshape, BF16),
            pltpu.VMEM(cshape, BF16),
            pltpu.VMEM(qshape, BF16),
            pltpu.VMEM(cshape, BF16),
            pltpu.VMEM(qshape, BF16),
            pltpu.VMEM((stacks,) + wshape, BF16),
            pltpu.VMEM((stacks,) + vshape, F32),
            pltpu.VMEM(sh.shape, F32),
            pltpu.VMEM((stacks - 1,) + wshape, BF16),
            pltpu.VMEM((stacks - 1,) + vshape, F32),
            pltpu.VMEM(sh.shape, F32),
            pltpu.VMEM((stacks - 1,) + wshape, BF16),
            pltpu.VMEM((stacks - 1,) + vshape, F32),
            pltpu.VMEM((stacks - 1,) + sh.shape, F32),
            pltpu.VMEM(wshape, F32),
            pltpu.VMEM(vshape, F32),
            pltpu.VMEM(sh.shape, F32),
            pltpu.VMEM((seqs - 1,) + vshape[1:], F32),
            pltpu.VMEM((seqs - 1,) + sh.shape, F32),
            pltpu.SemaphoreType.DMA((copies,)),
            pltpu.SemaphoreType.DMA((copies,)),
        ],
        compiler_params=pltpu.CompilerParams(
            collective_id=3, has_side_effects=True, vmem_limit_bytes=24 << 20
        ),
        cost_estimate=cost_of(30),
        name="sum_rows",
    )(gc, gq, w, v, sh)


def flip_perm(count, bit):
    return [(i, i ^ bit) for i in range(count)]


AXES = ("dp", "seq")


def tie(values, *others):
    return lax.optimization_barrier((values, others))[0]


def give_to(cur, count, bit):
    return lax.ppermute(cur, AXES, flip_perm(count, bit))


def local_fast(
    content,
    query_stream,
    segment_ids,
    pad_mask,
    predicted,
    order,
    rel_bucket,
    qkv_weight,
    qv_bias,
    out_weight,
    out_bias,
    attn_gain,
    attn_shift,
    up_weight,
    up_bias,
    down_weight,
    down_bias,
    ffn_gain,
    ffn_shift,
    rel_table,
    content_cot,
    query_cot,
):
    dps, seqs = lax.axis_size("dp"), lax.axis_size("seq")
    count = dps * seqs
    s = lax.axis_index("seq")
    own = HEADS // seqs
    wide = own * HEAD_DIM
    length = content.shape[1]
    preds = query_stream.shape[1]
    shard = qkv_weight.shape[0]

    rows = (out_bias, attn_gain, attn_shift, down_bias, ffn_gain, ffn_shift, up_bias, qv_bias)
    fill = [jnp.zeros((128 - row.shape[0],), row.dtype) for row in rows]
    vec = jnp.concatenate([x for pair in zip(rows, fill) for x in pair])
    vec = vec.astype(F32).reshape(8, 128)
    buckets = jnp.stack(
        [
            jnp.pad(rel_bucket, (0, 1), constant_values=BUCKETS),
            jnp.pad(rel_bucket, (1, 0), constant_values=BUCKETS),
        ]
    )
    w_parts = jnp.transpose(
        qkv_weight.reshape(shard, 3, seqs, wide), (2, 0, 1, 3)
    ).reshape(seqs, shard, 3 * wide)
    tops = (UP_TOP, DOWN_TOP)

    def send(pair, bits):
        return tuple(give_to(x, count, bit) for x, bit in zip(pair, bits))

    def heap(*pairs):
        return tuple(jnp.concatenate(x) for x in zip(*pairs))

    zs_low = (jnp.concatenate([up_weight, out_weight], axis=1)[None], down_weight[None])
    flying = send(zs_low, (16, 16))
    x_all, w_all, v_all, i_all = start_call(
        dps,
        seqs,
        content[0],
        query_stream[0],
        w_parts,
        vec,
        (segment_ids, order, pad_mask, predicted),
        SLOT_Q,
    )
    w_qkv = w_all.reshape(MODEL_WIDTH, 3 * wide)
    n_qv, n_up, n_one = qv_bias.shape[0], up_bias.shape[0], out_bias.shape[0]
    v_all = v_all.reshape(count, 8, 128)
    seg_all = i_all[:, 0].reshape(seqs * length)
    pad_all = i_all[:, 2].reshape(seqs * length)
    span = key_spans(seg_all, pad_all)

    bits = [tuple(2 * top[n] for top in tops) for n in range(2)]
    zs_low = heap(zs_low, tie(flying, i_all))
    flying = send(zs_low, (8, 8)), send(zs_low, bits[0]), give_to(zs_low[0], count, bits[1][0])
    first = (s * own).astype(jnp.int32)[None]
    ints = tie(i_all, zs_low)
    tiles, qbias, kmeta, rseg, rlim, hot, shift = bias_call(
        own, ROWS_Q, SLOT_Q, first, buckets, rel_table, ints
    )

    zs_high, side_low, far_first = tie(flying, tiles)
    column = heap(zs_low, zs_high)
    side_high, far_low = send(zs_high, bits[0]), send((zs_high[0], column[1]), bits[1])
    x_all = tie(x_all, column)
    q_t, k3, k_t, v3, v_t = proj_call(
        own, seqs * length, x_all, w_qkv, v_all, n_qv
    )
    side_high = tie(side_high, q_t)
    side = heap(side_low, side_high)
    far_high = send(side, bits[1])
    close = heap(column, side)
    q_t = tie(q_t, side)

    ctx_t, ctx_rows, lse = fwd_call(span, q_t, k3, v_t, kmeta, rseg, rlim, tiles, qbias)

    far_low, far_high = tie((far_low, far_high), ctx_rows)
    far = (
        jnp.concatenate([far_first, far_low[0], far_high[0]]),
        jnp.concatenate([far_low[1], far_high[1]]),
    )
    mates, far_mates = send(close, (1, 1)), send(far, (1, 1))
    ctx_rows = tie(ctx_rows, far)
    planes = sum(zip(close, far, mates, far_mates), ())

    def from_lanes(ref, t):
        return ref.at[:, pl.ds(pl.multiple_of(t * length, length), length)]

    def from_query(ref, t):
        return ref.at[pl.ds(pl.multiple_of(t * SLOT_Q, 16), SLOT_Q)]

    ctx_c, ctx_q = swap_call(
        seqs,
        ctx_t,
        ctx_rows,
        from_lanes,
        from_query,
        (wide, length),
        (SLOT_Q, wide),
        1,
        "swap_context",
    )
    (
        res_c,
        res_q,
        give_c,
        give_q,
        six_sums,
        up_sums,
        squares,
        out_c,
        out_q,
        keep,
        give,
    ) = mid_call(
        ctx_c,
        ctx_q,
        content[0],
        query_stream[0],
        content_cot[0],
        query_cot[0],
        pad_mask,
        v_all,
        n_one,
        n_up,
        planes,
    )
    core = s % 2
    spot = (lax.axis_index(AXES) // 2) % 4
    flying = give_to(give, count, 1)

    def both(mine, got):
        total = mine.astype(F32) + got.astype(F32)
        return total.astype(BF16).reshape((2, 2, 4, mine.shape[0] // 16, mine.shape[1]))

    def total_of(kept, got):
        total = kept.astype(F32)
        for x in got:
            total += x.astype(F32)
        return total

    def split(x, bit):
        mine = (lax.axis_index(AXES) // bit) % 2
        axis = 0
        away = lax.dynamic_index_in_dim(x, 1 - mine, axis, keepdims=False).astype(BF16)
        return away, lax.dynamic_index_in_dim(x, mine, axis, keepdims=False)

    def block(x, index):
        return lax.dynamic_index_in_dim(x, index, 2, keepdims=False)

    def from_slot(ref, t):
        return ref.at[t]

    g_c, g_q = swap_call(
        seqs,
        give_c,
        give_q,
        from_slot,
        from_slot,
        (wide, length),
        (SLOT_Q, wide),
        2,
        "swap_grads",
    )
    flying = tie(flying, g_c)
    pairs = both(keep, flying)
    cut = pairs.shape[-1] - MODEL_WIDTH
    main, rest = pairs[..., :cut], pairs[..., cut:]
    rest_gone, rest_stay = split(rest, 16)
    gone = tuple(block(main, spot ^ r) for r in (1, 2, 3)) + (rest_gone,)
    flying = tuple(give_to(x, count, bit) for x, bit in zip(gone, (2, 4, 6, 16)))
    stay = (block(main, spot), rest_stay)
    g_c = tie(g_c, stay, gone)
    dq, dk, dv, offs, qoffs = bwd_call(
        span,
        q_t,
        k3,
        k_t,
        v3,
        ctx_t,
        g_c,
        g_q.reshape(seqs * SLOT_Q, wide),
        lse,
        kmeta,
        rseg,
        rlim,
        tiles,
        hot,
        shift,
        qbias,
    )
    flying = tie(flying, dq)

    main_gone, main_stay = split(total_of(stay[0], flying[:3]), 16)
    rest_gone, rest_stay = split(total_of(stay[1], flying[3:]), 8)
    gone, stay = (main_gone, rest_gone), (main_stay, rest_stay)
    flying = (give_to(main_gone, count, 16), give_to(rest_gone, count, 8))
    dq = tie(dq, stay, gone)
    grad_c, grad_q, grad_w, vec_grads, shared = grads_call(
        seqs,
        length,
        SLOT_Q,
        count,
        x_all,
        w_qkv,
        dq,
        dk,
        dv,
        offs,
        qoffs,
        buckets,
        six_sums,
        up_sums,
        squares,
    )
    sum_c, sum_q, sum_w, sum_v, sum_shared = end_call(
        dps,
        seqs,
        grad_c,
        grad_q,
        grad_w.reshape(dps, seqs, shard, 3 * wide),
        vec_grads.reshape(dps, seqs, 8, 128),
        shared,
    )
    flying, sum_c, sum_q, sum_w, sum_v, sum_shared = tie(
        (flying, sum_c, sum_q, sum_w, sum_v, sum_shared)
    )
    main_gone, main_stay = split(total_of(stay[0], flying[:1]), 8)
    rest = total_of(stay[1], flying[1:])
    near = [lax.dynamic_index_in_dim(rest, spot ^ r, 0, keepdims=False) for r in range(4)]
    flying = [give_to(main_gone, count, 8)]
    flying += [give_to(near[r].astype(BF16), count, 2 * r) for r in (1, 2, 3)]
    sum_c, sum_q, sum_w, sum_v, sum_shared = tie(
        (sum_c, sum_q, sum_w, sum_v, sum_shared), main_gone, near
    )
    grad_content = res_c + sum_c
    grad_query = res_q[:preds] + sum_q[:preds]
    grad_qkv_own = jnp.transpose(sum_w.reshape(seqs, shard, 3, wide), (1, 2, 0, 3)).reshape(
        shard, 3 * MODEL_WIDTH
    )
    mine = [sum_v[7, :n_qv], sum_v[6, :n_up]] + [sum_v[i, :n_one] for i in range(6)]
    table_sum = sum_shared[:HEADS, :BUCKETS].T
    totals = sum_shared[16:23, 0]
    content_count = totals[6] * MODEL_WIDTH
    query_count = float(dps * preds * seqs * MODEL_WIDTH)
    each = jnp.stack([content_count, jnp.float32(query_count)])
    stats = jnp.sqrt(totals[:6] / jnp.concatenate([each, each, each]))
    flying = tie(flying, grad_content, grad_query, grad_qkv_own, mine, table_sum, stats)
    pair = jnp.concatenate(
        [total_of(main_stay, flying[:1]), total_of(near[0], flying[1:])], axis=1
    )
    half_ff, half = up_weight.shape[1] // 2, MODEL_WIDTH // 2
    wide_up = half_ff + half
    first, second = pair[:shard], pair[shard:]
    low_cols, high_cols = pair[:, wide_up : wide_up + half_ff // 2], pair[:, wide_up + half_ff // 2 :]

    def pick(a, b):
        return jnp.where(core == 0, a, b), jnp.where(core == 0, b, a)

    rows_mine, rows_away = pick(first[:, :wide_up], second[:, :wide_up])
    cols_mine, cols_away = pick(low_cols, high_cols)
    got = give_to(
        jnp.concatenate([rows_away, cols_away[:shard], cols_away[shard:]], axis=1), count, 1
    )
    rows_got = got[:, :wide_up]
    cols_got = jnp.concatenate(
        [got[:, wide_up : wide_up + half_ff // 2], got[:, wide_up + half_ff // 2 :]], axis=0
    )
    rows_low, rows_high = pick(rows_mine, rows_got)
    grad_up_own = jnp.concatenate([rows_low[:, :half_ff], rows_high[:, :half_ff]], axis=1)
    grad_out_own = jnp.concatenate([rows_low[:, half_ff:], rows_high[:, half_ff:]], axis=1)

    def unfold(x):
        return jnp.concatenate([x[:, :half], x[:, half:]], axis=0)

    cols_low, cols_high = pick(unfold(cols_mine), unfold(cols_got))
    grad_down_own = jnp.concatenate([cols_low, cols_high], axis=1)
    return (
        out_c[None],
        out_q[None],
        grad_content[None],
        grad_query[None],
        grad_qkv_own,
        mine[0],
        grad_out_own,
        mine[2],
        mine[3],
        mine[4],
        grad_up_own,
        mine[1],
        grad_down_own,
        mine[5],
        mine[6],
        mine[7],
        table_sum,
        stats,
    )


def pick_local(mesh):
    sizes = dict(mesh.shape)
    return local_fast if (sizes["dp"], sizes["seq"]) == (8, 4) else local_general


def solution(mesh):
    in_specs = (
        P("dp", "seq", None),
        P("dp", "seq", None),
        P("dp", "seq"),
        P("dp", "seq"),
        P("dp", "seq"),
        P("dp", "seq"),
        P(),
        P(("dp", "seq"), None),
        P(("dp", "seq")),
        P(("dp", "seq"), None),
        P(("dp", "seq")),
        P(("dp", "seq")),
        P(("dp", "seq")),
        P(("dp", "seq"), None),
        P(("dp", "seq")),
        P(("dp", "seq"), None),
        P(("dp", "seq")),
        P(("dp", "seq")),
        P(("dp", "seq")),
        P(),
        P("dp", "seq", None),
        P("dp", "seq", None),
    )
    out_specs = (
        P("dp", "seq", None),
        P("dp", "seq", None),
        P("dp", "seq", None),
        P("dp", "seq", None),
        P(("dp", "seq"), None),
        P(("dp", "seq")),
        P(("dp", "seq"), None),
        P(("dp", "seq")),
        P(("dp", "seq")),
        P(("dp", "seq")),
        P(("dp", "seq"), None),
        P(("dp", "seq")),
        P(("dp", "seq"), None),
        P(("dp", "seq")),
        P(("dp", "seq")),
        P(("dp", "seq")),
        P(),
        P(),
    )
    local = pick_local(mesh)
    return jax.shard_map(local, mesh=mesh, in_specs=in_specs, out_specs=out_specs, check_vma=False)
```
